32 devices in a mesh: rep: 16 (over z, x, core), shard: 2 (over y).
Axes of the slice: x: 2, y: 2, z: 4, core: 2. Of those that a mesh axis runs over, the one named last changes fastest.
Arguments:
- patches: bfloat16 [16384, 1280], P(('rep', 'shard')), may hold values from -6 to 6
- lengths: int32 [32, 4], P(('rep', 'shard')), may hold values from 1 to 256, 512 in all within a row
- positions: int32 [2, 16384], P(None, ('rep', 'shard')), may hold values from 0 to 63
- ln1_gain: bfloat16 [1280], P('shard'), may hold values from 0.5 to 1.5
- ln1_bias: bfloat16 [1280], P('shard'), may hold values from -3 to 3
- qkv_weight: bfloat16 [1280, 3840], P('shard'), may hold values from -0.15625 to 0.15625
- qkv_bias: bfloat16 [3840], P('shard'), may hold values from -3 to 3
- proj_weight: bfloat16 [1280, 1280], P('shard'), may hold values from -1.25 to 1.25
- proj_bias: bfloat16 [1280], P('shard'), may hold values from -3 to 3
- ln2_gain: bfloat16 [1280], P('shard'), may hold values from 0.5 to 1.5
- ln2_bias: bfloat16 [1280], P('shard'), may hold values from -3 to 3
- fc1_weight: bfloat16 [1280, 5120], P('shard'), may hold values from -0.15625 to 0.15625
- fc1_bias: bfloat16 [5120], P('shard'), may hold values from -3 to 3
- fc2_weight: bfloat16 [5120, 1280], P('shard'), may hold values from -0.125 to 0.125
- fc2_bias: bfloat16 [1280], P('shard'), may hold values from -3 to 3
- cotangent: bfloat16 [16384, 1280], P(('rep', 'shard')), may hold values from -6 to 6
Outputs:
- layer_out: bfloat16 [16384, 1280], P(('rep', 'shard'))
- d_patches: float32 [16384, 1280], P(('rep', 'shard'))
- d_ln1_gain: float32 [1280], P('shard')
- d_ln1_bias: float32 [1280], P('shard')
- d_qkv_weight: float32 [1280, 3840], P('shard')
- d_qkv_bias: float32 [3840], P('shard')
- d_proj_weight: float32 [1280, 1280], P('shard')
- d_proj_bias: float32 [1280], P('shard')
- d_ln2_gain: float32 [1280], P('shard')
- d_ln2_bias: float32 [1280], P('shard')
- d_fc1_weight: float32 [1280, 5120], P('shard')
- d_fc1_bias: float32 [5120], P('shard')
- d_fc2_weight: float32 [5120, 1280], P('shard')
- d_fc2_bias: float32 [1280], P('shard')
The draws below stay inside these ranges and needn't reach their ends.
Inputs may be any that keep to these rules, and one draw needn't show every extreme that they name: `lengths`: each row's entries sum to 512; its largest entry is 256.
All inputs are finite; a program needn't handle non-finite values.
Results may differ from the reference program's by a relative error of at most 0.012.
The reference program's roundings to bfloat16 on the way count: a program that leaves them out, or rounds other values in their place, can miss the bound.
Values may be sent and summed in bfloat16 or wider, within the bound.
A program may use at most 320 MiB of HBM per device.

```python
import math
import jax
import jax.numpy as jnp
import numpy as np
from jax import lax

D = 1280
HEADS = 16
HEAD = 80
FF = 5120
LEN = 512
PICS = 3
MOST = 256
PACKS = 32
TOKENS = 16384


def with_ends(entries, own_key, smallest, top_value):
    dims = entries.shape
    index_at = [jax.random.randint(jax.random.fold_in(own_key, axis), (), 0, dims[axis]) for axis in range(len(dims))]
    entries = entries.at[tuple(index_at)].set(smallest)
    longest = dims.index(max(dims))
    index_at[longest] = (index_at[longest] + 1) % dims[longest]
    return entries.at[tuple(index_at)].set(top_value)


def shard_levels(own_key, extent, shards, low, high):
    loudness, own = 1.0, jax.random.fold_in(own_key, 6)
    for dim, parts in shards:
        heights = jnp.exp(jax.random.uniform(jax.random.fold_in(own, dim), (parts,), jnp.float32, low / len(shards), high / len(shards)))
        loudness = loudness * jnp.repeat(heights, extent[dim] // parts).reshape([-1 if axis == dim else 1 for axis in range(len(extent))])
    return loudness


def length_profile(amount, total, most, slope):
    portions = [(1 << 20) // math.isqrt(grade ** slope) + 1 for grade in range(2, amount + 1)]
    spare, counts = total - most - (amount - 1), [1] * (amount - 1)
    while spare > 0:
        candidates = [i for i in range(amount - 1) if counts[i] < most]
        whole, budget = sum([portions[i] for i in candidates]), spare
        for i in candidates:
            more = min(most - counts[i], max(1, budget * portions[i] // whole), spare)
            counts[i] = counts[i] + more
            spare = spare - more
    return np.array([most] + counts)


def uneven(stream_key, count, total, bound, lean):
    if count == 2:
        one = jax.random.randint(stream_key, (), max(1, total - bound), min(bound, total - 1) + 1)
        return jnp.stack([one, total - one])
    sizes = jnp.asarray(length_profile(count, total, bound, lean), jnp.int32)
    twos = (count - 1) // 2
    source_of, receiver = sizes[1:1 + 2 * twos:2], sizes[2:2 + 2 * twos:2]
    margin = jnp.minimum(source_of - 1, bound - receiver)
    passed = jax.random.randint(jax.random.fold_in(stream_key, 1), (twos,), 0, 1 << 20) % (margin + 1)
    sizes = sizes.at[1:1 + 2 * twos:2].set(source_of - passed).at[2:2 + 2 * twos:2].set(receiver + passed)
    return sizes[jax.random.permutation(jax.random.fold_in(stream_key, 2), count)]


def bell_draw(rng, dims, deviation, reach, shards=(), kind=jnp.bfloat16):
    values = deviation * jax.random.normal(rng, dims, jnp.float32)
    if shards:
        values = values * shard_levels(rng, dims, shards, -0.22, 0.18)
    return jnp.clip(values, -reach, reach).astype(kind)


def setup_inputs(seed: int = 0) -> dict:
    arg_keys = jax.random.split(jax.random.key(seed), 17)
    patches = bell_draw(arg_keys[0], (TOKENS, D), 1.0, 6.0, ((0, 32),))
    lengths = jax.vmap(lambda own: uneven(own, PICS + 1, LEN, MOST, 1))(jax.random.split(arg_keys[1], PACKS)).reshape((PACKS, PICS + 1)).astype(jnp.int32)
    positions = with_ends(jax.random.randint(arg_keys[2], (2, TOKENS), 0, 64), jax.random.fold_in(arg_keys[2], 1), 0, 63).astype(jnp.int32)
    ln1_gain = jnp.clip(1.0 + 0.1 * jax.random.normal(arg_keys[3], (D,), jnp.float32), 0.5, 1.5).astype(jnp.bfloat16)
    ln1_bias = bell_draw(arg_keys[4], (D,), 0.5, 3.0, ((0, 2),))
    qkv_weight = bell_draw(arg_keys[5], (D, 3 * D), D ** -0.5, 0.15625, ((0, 2),))
    qkv_bias = bell_draw(arg_keys[6], (3 * D,), 0.5, 3.0, ((0, 2),))
    proj_weight = bell_draw(arg_keys[7], (D, D), (D // 64) ** -0.5, 1.25, ((0, 2),))
    proj_bias = bell_draw(arg_keys[8], (D,), 0.5, 3.0, ((0, 2),))
    ln2_gain = jnp.clip(1.0 + 0.1 * jax.random.normal(arg_keys[9], (D,), jnp.float32), 0.5, 1.5).astype(jnp.bfloat16)
    ln2_bias = bell_draw(arg_keys[10], (D,), 0.5, 3.0, ((0, 2),))
    fc1_weight = bell_draw(arg_keys[11], (D, FF), D ** -0.5, 0.15625, ((0, 2),))
    fc1_bias = bell_draw(arg_keys[12], (FF,), 0.5, 3.0, ((0, 2),))
    fc2_weight = bell_draw(arg_keys[13], (FF, D), (FF // 2) ** -0.5, 0.125, ((0, 2),))
    fc2_bias = bell_draw(arg_keys[14], (D,), 0.5, 3.0, ((0, 2),))
    cotangent = bell_draw(arg_keys[15], (TOKENS, D), 1.0, 6.0, ((0, 32),))
    return {"patches": patches, "lengths": lengths, "positions": positions, "ln1_gain": ln1_gain, "ln1_bias": ln1_bias, "qkv_weight": qkv_weight, "qkv_bias": qkv_bias, "proj_weight": proj_weight, "proj_bias": proj_bias, "ln2_gain": ln2_gain, "ln2_bias": ln2_bias, "fc1_weight": fc1_weight, "fc1_bias": fc1_bias, "fc2_weight": fc2_weight, "fc2_bias": fc2_bias, "cotangent": cotangent}


@jax.custom_vjp
def low(v):
    return lax.optimization_barrier(v.astype(jnp.bfloat16)).astype(jnp.float32)

@jax.custom_vjp
def low_back(v):
    return v

def low_keep(v):
    return (low(v), None)

def low_pass(kept, grad):
    return (grad,)

def back_keep(v):
    return (v, None)

def back_low(kept, grad):
    return (low(grad),)
low.defvjp(low_keep, low_pass)
low_back.defvjp(back_keep, back_low)
norm_eps = 1e-06
quick_slope = 1.702
highest = lax.Precision.HIGHEST

def precise_dot(left, right):
    return jnp.dot(left, right, precision=highest, preferred_element_type=jnp.float32)

def layer_norm(matrix, norm_gain, shift):
    center = matrix - lax.optimization_barrier(jnp.mean(matrix, axis=-1, keepdims=True))
    spread = lax.optimization_barrier(jnp.mean(center * center, axis=-1, keepdims=True))
    return center * lax.rsqrt(spread + norm_eps) * norm_gain + shift

def rotary_tables(positions, head_size):
    quarter = head_size // 4
    counter = jnp.arange(quarter, dtype=jnp.float32)
    inverse = jnp.power(jnp.float32(10000.0), -2.0 * counter / (head_size // 2))
    row_angle = positions[0].astype(jnp.float32)[:, None] * inverse[None, :]
    col_angle = positions[1].astype(jnp.float32)[:, None] * inverse[None, :]
    angle = jnp.concatenate([row_angle, col_angle], axis=1)
    angle = jnp.concatenate([angle, angle], axis=1)
    return (jnp.cos(angle), jnp.sin(angle))

def rotate_half(matrix):
    half_size = matrix.shape[-1] // 2
    return jnp.concatenate([-matrix[..., half_size:], matrix[..., :half_size]], axis=-1)

def apply_rotary(matrix, cosine, sine):
    return matrix * cosine[:, None, :] + rotate_half(matrix) * sine[:, None, :]

def picture_ids(lengths, length):
    pic_ends = jnp.cumsum(lengths[:, :-1], axis=1)
    slot_index = jnp.arange(length, dtype=jnp.int32)
    return lax.optimization_barrier(jnp.sum((slot_index[None, :, None] >= pic_ends[:, None, :]).astype(jnp.int32), axis=2))

def reference(patches, lengths, positions, ln1_gain, ln1_bias, qkv_weight, qkv_bias, proj_weight, proj_bias, ln2_gain, ln2_bias, fc1_weight, fc1_bias, fc2_weight, fc2_bias, cotangent):
    pack_count = lengths.shape[0]
    token_count = patches.shape[0]
    idents = picture_ids(lengths, LEN)
    cosine, sine = rotary_tables(positions, HEAD)
    group_size = math.gcd(pack_count, 8)
    group_count = pack_count // group_size
    score_scale = HEAD ** (-0.5)
    id_groups = idents.reshape(group_count, group_size, LEN)
    group_shape = (group_count, group_size, LEN, HEADS, HEAD)

    def attend_group(pieces):
        queries, keys_all, values_all, ident = pieces
        scores = jnp.einsum('gqhd,gkhd->ghqk', queries, keys_all, precision=highest) * score_scale
        scores = low_back(scores)
        same_pic = ident[:, :, None] == ident[:, None, :]
        scores = jnp.where(same_pic[:, None], scores, -1000000000.0)
        top_score = lax.optimization_barrier(jnp.max(scores, axis=3, keepdims=True))
        exp_scores = jnp.exp(scores - top_score)
        probs = low(exp_scores / lax.optimization_barrier(jnp.sum(exp_scores, axis=3, keepdims=True)))
        return jnp.einsum('ghqk,gkhd->gqhd', probs, values_all, precision=highest)

    def forward(input_rows, first_norm_gain, first_norm_bias, w_qkv, b_qkv, w_proj, b_proj, second_norm_gain, second_norm_bias, w_up, b_up, w_down, b_down):
        first_normalized = low(layer_norm(input_rows, first_norm_gain, first_norm_bias))
        qkv_rows = low_back(precise_dot(first_normalized, w_qkv) + b_qkv).reshape(token_count, 3, HEADS, HEAD)
        queries = low(apply_rotary(qkv_rows[:, 0], cosine, sine))
        keys_rot = low(apply_rotary(qkv_rows[:, 1], cosine, sine))
        values_all = low(qkv_rows[:, 2])
        attended = lax.map(jax.checkpoint(attend_group), (queries.reshape(group_shape), keys_rot.reshape(group_shape), values_all.reshape(group_shape), id_groups))
        heads_out = low(low_back(attended.reshape(token_count, D)))
        hidden_rows = input_rows + low_back(precise_dot(heads_out, w_proj) + b_proj)
        second_normalized = low(layer_norm(hidden_rows, second_norm_gain, second_norm_bias))
        up_pre = low_back(precise_dot(second_normalized, w_up) + b_up)
        activation = low(up_pre / (1.0 + jnp.exp(-quick_slope * up_pre)))
        return hidden_rows + low_back(precise_dot(activation, w_down) + b_down)
    floats = tuple((item.astype(jnp.float32) for item in (patches, ln1_gain, ln1_bias, qkv_weight, qkv_bias, proj_weight, proj_bias, ln2_gain, ln2_bias, fc1_weight, fc1_bias, fc2_weight, fc2_bias)))
    out_full, pull = jax.vjp(forward, *floats)
    grads = pull(cotangent.astype(jnp.float32))
    return (out_full.astype(jnp.bfloat16), grads[0], grads[1], grads[2], grads[3], grads[4], grads[5], grads[6], grads[7], grads[8], grads[9], grads[10], grads[11], grads[12])
```

```python
from functools import partial

import jax
import jax.numpy as jnp
from jax import lax
from jax.sharding import PartitionSpec as P

HEADS = 16


norm_eps = 1e-06
quick_slope = 1.702


def apply_layer_norm(matrix):
    center = matrix - jnp.mean(matrix, axis=-1, keepdims=True)
    spread = jnp.mean(center * center, axis=-1, keepdims=True)
    inverse_spread = lax.rsqrt(spread + norm_eps)
    return (center * inverse_spread, inverse_spread)


def norm_gradient_step(normalized_gradient, centered_standard, inverse_spread, norm_gain):
    scaled_rows = normalized_gradient * norm_gain
    return inverse_spread * (
        scaled_rows
        - jnp.mean(scaled_rows, axis=-1, keepdims=True)
        - centered_standard * jnp.mean(scaled_rows * centered_standard, axis=-1, keepdims=True)
    )


def rotary_tables(positions, head_size):
    quarter = head_size // 4
    counter = jnp.arange(quarter, dtype=jnp.float32)
    inverse = jnp.power(jnp.float32(10000.0), -2.0 * counter / (head_size // 2))
    row_angle = positions[0].astype(jnp.float32)[:, None] * inverse[None, :]
    col_angle = positions[1].astype(jnp.float32)[:, None] * inverse[None, :]
    angle = jnp.concatenate([row_angle, col_angle], axis=1)
    angle = jnp.concatenate([angle, angle], axis=1)
    return (jnp.cos(angle), jnp.sin(angle))


def apply_rotary(matrix, cosine, sine):
    half_size = matrix.shape[-1] // 2
    turned = jnp.concatenate([-matrix[..., half_size:], matrix[..., :half_size]], axis=-1)
    return matrix * cosine[:, None, :] + turned * sine[:, None, :]


def rotary_back(grad_rows, cosine, sine):
    half_size = grad_rows.shape[-1] // 2
    sined = grad_rows * sine[:, None, :]
    turned = jnp.concatenate([sined[..., half_size:], -sined[..., :half_size]], axis=-1)
    return grad_rows * cosine[:, None, :] + turned


def masked_scores(queries, keys_rot, ident, score_scale):
    scores = (
        jnp.einsum("qhd,khd->hqk", queries, keys_rot, preferred_element_type=jnp.float32)
        * score_scale
    )
    same_pic = ident[:, None] == ident[None, :]
    return jnp.where(same_pic[None], scores, -1000000000.0)


def attend(pieces, score_scale):
    queries, keys_rot, values_all, ident = pieces
    scores = masked_scores(queries, keys_rot, ident, score_scale)
    top_score = jnp.max(scores, axis=2, keepdims=True)
    exp_scores = jnp.exp(scores - top_score)
    total = jnp.sum(exp_scores, axis=2, keepdims=True)
    probs = (exp_scores / total).astype(jnp.bfloat16)
    attended = jnp.einsum("hqk,khd->qhd", probs, values_all, preferred_element_type=jnp.float32)
    return (attended, (top_score + jnp.log(total))[:, :, 0])


def attend_back(pieces, score_scale):
    queries, keys_rot, values_all, ident, grad_heads, log_total = pieces
    scores = masked_scores(queries, keys_rot, ident, score_scale)
    probs = jnp.exp(scores - log_total[:, :, None])
    grad_probs = jnp.einsum(
        "qhd,khd->hqk", grad_heads, values_all, preferred_element_type=jnp.float32
    )
    inner = jnp.sum(probs * grad_probs, axis=2, keepdims=True)
    grad_scores = (probs * (grad_probs - inner)).astype(jnp.bfloat16)
    grad_query = (
        jnp.einsum("hqk,khd->qhd", grad_scores, keys_rot, preferred_element_type=jnp.float32)
        * score_scale
    )
    grad_key = (
        jnp.einsum("hqk,qhd->khd", grad_scores, queries, preferred_element_type=jnp.float32)
        * score_scale
    )
    grad_value = jnp.einsum(
        "hqk,qhd->khd", probs.astype(jnp.bfloat16), grad_heads, preferred_element_type=jnp.float32
    )
    return (grad_query, grad_key, grad_value)


def row_product(left, right):
    return jnp.einsum("ti,tj->ij", left, right, preferred_element_type=jnp.float32)


def back_product(grad_rows, weight_full):
    return jnp.einsum("tj,ij->ti", grad_rows, weight_full, preferred_element_type=jnp.float32)


def add_low(left, right):
    return (left.astype(jnp.float32) + right.astype(jnp.float32)).astype(jnp.bfloat16)


class Links:
    def __init__(self, n_rep, n_shard):
        self.nz, self.ny, self.n_rep = n_rep // 4, n_shard, n_rep
        rep = lax.axis_index("rep")
        self.y = lax.axis_index("shard")
        self.z, self.x, self.c = rep // 4, (rep // 2) % 2, rep % 2

    def swap_core(self, item):
        return lax.ppermute(item, "rep", [(i, i ^ 1) for i in range(self.n_rep)])

    def swap_x(self, item):
        return lax.ppermute(item, "rep", [(i, i ^ 2) for i in range(self.n_rep)])

    def swap_y(self, item):
        return lax.ppermute(item, "shard", [(0, 1), (1, 0)])

    def send_z(self, item, pairs):
        return lax.ppermute(
            item, "rep", [(a * 4 + k, b * 4 + k) for a, b in pairs for k in range(4)]
        )

    def inward(self, step):
        last = self.nz - 1
        return [(step, step + 1), (last - step, last - step - 1)]

    def outward(self, step):
        return [(b, a) for a, b in self.inward(step)]

    def middle(self):
        half = self.nz // 2
        return [(half - 1, half), (half, half - 1)]

    def in_order(self, index, mine, theirs, axis=0):
        first = jnp.concatenate([mine, theirs], axis=axis)
        second = jnp.concatenate([theirs, mine], axis=axis)
        return jnp.where(index == 0, first, second)

    def reduce_z(self, part):
        for step in range(self.nz // 2 - 1):
            part = add_low(part, self.send_z(part, self.inward(step)))
        part = add_low(part, self.send_z(part, self.middle()))
        for step in reversed(range(self.nz // 2 - 1)):
            moved = self.send_z(part, self.outward(step))
            outer = (self.z == step) | (self.z == self.nz - 1 - step)
            part = jnp.where(outer, moved, part)
        return part

    def gather_z(self, part):
        low = self.z < self.nz // 2
        own = part
        for step in range(self.nz // 2 - 1):
            moved = self.send_z(part, self.inward(step))
            part = jnp.where(
                low, jnp.concatenate([moved, own], 0), jnp.concatenate([own, moved], 0)
            )
        part = self.in_order(jnp.where(low, 0, 1), part, self.send_z(part, self.middle()))
        for step in reversed(range(self.nz // 2 - 1)):
            moved = self.send_z(part, self.outward(step))
            outer = (self.z == step) | (self.z == self.nz - 1 - step)
            part = jnp.where(outer, moved, part)
        return part

    def gather_plane(self, weight):
        rows = weight.shape[0] // self.n_rep
        place = ((self.c * 2 + self.x) * self.nz + self.z) * rows
        part = self.swap_y(lax.dynamic_slice_in_dim(weight, place, rows, 0))
        part = self.gather_z(part)
        part = self.in_order(self.x, part, self.swap_x(part))
        return self.in_order(self.c, part, self.swap_core(part))

    def gather_straight(self, weight):
        rows = weight.shape[0] // 2
        part = self.swap_y(lax.dynamic_slice_in_dim(weight, self.c * rows, rows, 0))
        return self.in_order(self.c, part, self.swap_core(part))

    def gather_weight(self, weight, cuts):
        if self.ny != 2:
            return lax.all_gather(weight, "shard", axis=0, tiled=True)
        pieces = []
        for start, stop, plane in cuts:
            block = weight[:, start:stop]
            pieces.append(self.gather_plane(block) if plane else self.gather_straight(block))
        other = jnp.concatenate(pieces, axis=1)
        return self.in_order(self.y, weight, other)

    def gather_vector(self, vector):
        if self.ny != 2:
            return lax.all_gather(vector, "shard", axis=0, tiled=False)
        return self.in_order(self.y, vector[None], self.swap_y(vector)[None])

    def sum_all(self, vector):
        vector = vector + self.swap_core(vector)
        vector = vector + self.swap_x(vector)
        step = 1
        while step < self.nz:
            vector = vector + self.send_z(vector, [(i, i ^ step) for i in range(self.nz)])
            step *= 2
        step = 1
        while step < self.ny:
            vector = vector + lax.ppermute(
                vector, "shard", [(i, i ^ step) for i in range(self.ny)]
            )
            step *= 2
        return vector

    def pick(self, stacked, index):
        return lax.dynamic_index_in_dim(stacked, index, 0, keepdims=False)

    def reduce_part(self, part):
        if self.ny == 2:
            got = self.swap_y(self.pick(part, 1 - self.y))
            part = add_low(self.pick(part, self.y), got)
        else:
            part = lax.psum_scatter(part, "shard", scatter_dimension=0, tiled=False)
        got = self.swap_x(self.pick(part, 1 - self.x))
        part = add_low(self.pick(part, self.x), got)
        part = self.reduce_z(part)
        part = self.in_order(self.x, part[None], self.swap_x(part)[None])
        return part

    def weight_gradient(self, left, right, chunks):
        half = right.shape[1] // 2
        kept = lax.dynamic_slice_in_dim(right, self.c * half, half, 1)
        sent = lax.dynamic_slice_in_dim(right, (1 - self.c) * half, half, 1)
        both_left = jnp.concatenate([left, self.swap_core(left)], axis=0)
        both_right = jnp.concatenate([kept, self.swap_core(sent)], axis=0)
        product = row_product(both_left, both_right).astype(jnp.bfloat16)
        rows = product.shape[0] // (self.ny * 2 * chunks)
        product = product.reshape(self.ny, 2, chunks, rows, half)
        parts = [self.reduce_part(product[:, :, i]) for i in range(chunks)]
        full = []
        for part in parts:
            full.append(self.in_order(self.c, part, self.swap_core(part), axis=2))
        total = jnp.stack(full, axis=1)
        return total.reshape(2 * chunks * rows, 2 * half).astype(jnp.float32)


def per_device(
    patches,
    lengths,
    positions,
    ln1_gain,
    ln1_bias,
    qkv_weight,
    qkv_bias,
    proj_weight,
    proj_bias,
    ln2_gain,
    ln2_bias,
    fc1_weight,
    fc1_bias,
    fc2_weight,
    fc2_bias,
    cotangent,
    n_rep,
    n_shard,
):
    links = Links(n_rep, n_shard)
    pack_count = lengths.shape[0]
    row_count = patches.shape[0]
    length = row_count // pack_count
    model_width = patches.shape[1]
    head_count = HEADS
    head_size = model_width // head_count
    score_scale = head_size ** (-0.5)
    pic_ends = jnp.cumsum(lengths[:, :-1], axis=1)
    slot_index = jnp.arange(length, dtype=jnp.int32)
    idents = jnp.sum((slot_index[None, :, None] >= pic_ends[:, None, :]).astype(jnp.int32), axis=2)
    cosine, sine = rotary_tables(positions, head_size)
    pack_shape = (pack_count, length, head_count, head_size)

    small = [ln1_gain, ln1_bias, qkv_bias, proj_bias, ln2_gain, ln2_bias, fc1_bias, fc2_bias]
    sizes = [item.shape[0] for item in small]
    gathered = links.gather_vector(jnp.concatenate(small))
    spots = [sum(sizes[:i]) for i in range(len(sizes) + 1)]
    (
        first_norm_gain, first_norm_bias, b_qkv, b_proj,
        second_norm_gain, second_norm_bias, b_up, b_down,
    ) = [
        gathered[:, spots[i] : spots[i + 1]].reshape(-1).astype(jnp.float32)
        for i in range(len(sizes))
    ]

    width = model_width
    w_qkv = links.gather_weight(
        qkv_weight,
        [(0, 1024, True), (1024, 2048, True), (2048, 2816, True), (2816, 3840, False)],
    )
    w_proj = links.gather_weight(proj_weight, [(0, 1024, True), (1024, width, False)])
    ff = fc1_weight.shape[1]
    w_up = links.gather_weight(
        fc1_weight, [(0, 1920, True), (1920, 3840, True), (3840, ff, False)]
    )
    w_down = links.gather_weight(
        fc2_weight, [(0, 512, True), (512, 1024, True), (1024, width, False)]
    )

    input_rows = patches.astype(jnp.float32)
    first_centered_standard, first_inverse_spread = apply_layer_norm(input_rows)
    first_normalized = (first_centered_standard * first_norm_gain + first_norm_bias).astype(
        jnp.bfloat16
    )
    qkv_rows = jnp.dot(first_normalized, w_qkv, preferred_element_type=jnp.float32) + b_qkv
    qkv_rows = qkv_rows.reshape(row_count, 3, head_count, head_size)
    queries = apply_rotary(qkv_rows[:, 0], cosine, sine).astype(jnp.bfloat16).reshape(pack_shape)
    keys_rot = apply_rotary(qkv_rows[:, 1], cosine, sine).astype(jnp.bfloat16).reshape(pack_shape)
    values_all = qkv_rows[:, 2].astype(jnp.bfloat16).reshape(pack_shape)
    attended, log_total = lax.map(
        partial(attend, score_scale=score_scale), (queries, keys_rot, values_all, idents)
    )
    heads_out = attended.reshape(row_count, model_width).astype(jnp.bfloat16)
    hidden_rows = (
        input_rows + jnp.dot(heads_out, w_proj, preferred_element_type=jnp.float32) + b_proj
    )
    second_centered_standard, second_inverse_spread = apply_layer_norm(hidden_rows)
    second_normalized = (second_centered_standard * second_norm_gain + second_norm_bias).astype(
        jnp.bfloat16
    )
    up_pre = jnp.dot(second_normalized, w_up, preferred_element_type=jnp.float32) + b_up
    sigmoid_up = 1.0 / (1.0 + jnp.exp(-quick_slope * up_pre))
    activation = (up_pre * sigmoid_up).astype(jnp.bfloat16)

    d_w_down = links.weight_gradient(activation, cotangent, 4)
    out_full = (
        hidden_rows + jnp.dot(activation, w_down, preferred_element_type=jnp.float32) + b_down
    )
    layer_out = out_full.astype(jnp.bfloat16)
    grad_out = cotangent.astype(jnp.float32)
    d_b_down = jnp.sum(grad_out, axis=0)
    grad_act = back_product(cotangent, w_down)
    slope_up = sigmoid_up + quick_slope * up_pre * sigmoid_up * (1.0 - sigmoid_up)
    grad_pre = (grad_act * slope_up).astype(jnp.bfloat16)
    d_w_up = links.weight_gradient(second_normalized, grad_pre, 4)
    d_b_up = jnp.sum(grad_pre.astype(jnp.float32), axis=0)
    second_normalized_gradient = back_product(grad_pre, w_up)
    second_gain_gradient = jnp.sum(second_normalized_gradient * second_centered_standard, axis=0)
    d_bias_two = jnp.sum(second_normalized_gradient, axis=0)
    grad_hidden = grad_out + norm_gradient_step(
        second_normalized_gradient,
        second_centered_standard,
        second_inverse_spread,
        second_norm_gain,
    )
    grad_branch = grad_hidden.astype(jnp.bfloat16)
    d_w_proj = links.weight_gradient(heads_out, grad_branch, 1)
    d_b_proj = jnp.sum(grad_branch.astype(jnp.float32), axis=0)
    grad_heads = back_product(grad_branch, w_proj).astype(jnp.bfloat16).reshape(pack_shape)
    grad_query, grad_key, grad_value = lax.map(
        partial(attend_back, score_scale=score_scale),
        (queries, keys_rot, values_all, idents, grad_heads, log_total),
    )
    rows_shape = (row_count, head_count, head_size)
    grad_query = rotary_back(grad_query.reshape(rows_shape), cosine, sine)
    grad_key = rotary_back(grad_key.reshape(rows_shape), cosine, sine)
    grad_qkv = (
        jnp.stack([grad_query, grad_key, grad_value.reshape(rows_shape)], axis=1)
        .reshape(row_count, 3 * model_width)
        .astype(jnp.bfloat16)
    )
    d_w_qkv = links.weight_gradient(first_normalized, grad_qkv, 4)
    d_b_qkv = jnp.sum(grad_qkv.astype(jnp.float32), axis=0)
    first_normalized_gradient = back_product(grad_qkv, w_qkv)
    first_gain_gradient = jnp.sum(first_normalized_gradient * first_centered_standard, axis=0)
    d_bias_one = jnp.sum(first_normalized_gradient, axis=0)
    d_patches = grad_hidden + norm_gradient_step(
        first_normalized_gradient,
        first_centered_standard,
        first_inverse_spread,
        first_norm_gain,
    )

    def own_parts(vectors):
        lens = [item.shape[0] for item in vectors]
        total = links.sum_all(jnp.concatenate(vectors))
        result, start = [], 0
        for size in lens:
            own = size // n_shard
            result.append(lax.dynamic_slice_in_dim(total, start + links.y * own, own, 0))
            start += size
        return result

    m_gain, m_bias, m_upb, m_downb = own_parts(
        [second_gain_gradient, d_bias_two, d_b_up, d_b_down]
    )
    a_gain, a_bias, a_qkvb, a_projb = own_parts(
        [first_gain_gradient, d_bias_one, d_b_qkv, d_b_proj]
    )
    return (
        layer_out,
        d_patches,
        a_gain,
        a_bias,
        d_w_qkv,
        a_qkvb,
        d_w_proj,
        a_projb,
        m_gain,
        m_bias,
        d_w_up,
        m_upb,
        d_w_down,
        m_downb,
    )


def solution(mesh):
    rows, whole = P(("rep", "shard"), None), P("shard")
    matrix = P("shard", None)
    in_specs = (
        rows,
        rows,
        P(None, ("rep", "shard")),
        whole,
        whole,
        matrix,
        whole,
        matrix,
        whole,
        whole,
        whole,
        matrix,
        whole,
        matrix,
        whole,
        rows,
    )
    out_specs = (
        rows,
        rows,
        whole,
        whole,
        matrix,
        whole,
        matrix,
        whole,
        whole,
        whole,
        matrix,
        whole,
        matrix,
        whole,
    )
    body = partial(per_device, n_rep=mesh.shape["rep"], n_shard=mesh.shape["shard"])
    return jax.shard_map(
        body, mesh=mesh, in_specs=in_specs, out_specs=out_specs, check_vma=False
    )
```

```python
from functools import partial

import jax
import jax.numpy as jnp
from jax import lax
from jax.experimental import pallas as pl
from jax.experimental.pallas import tpu as pltpu
from jax.sharding import PartitionSpec as P

HEADS = 16


norm_eps = 1e-06
quick_slope = 1.702


def apply_layer_norm(matrix):
    center = matrix - jnp.mean(matrix, axis=-1, keepdims=True)
    spread = jnp.mean(center * center, axis=-1, keepdims=True)
    inverse_spread = lax.rsqrt(spread + norm_eps)
    return (center * inverse_spread, inverse_spread)


def norm_gradient_step(normalized_gradient, centered_standard, inverse_spread, norm_gain):
    scaled_rows = normalized_gradient * norm_gain
    return inverse_spread * (
        scaled_rows
        - jnp.mean(scaled_rows, axis=-1, keepdims=True)
        - centered_standard * jnp.mean(scaled_rows * centered_standard, axis=-1, keepdims=True)
    )


def rotary_tables(positions, head_size):
    quarter = head_size // 4
    counter = jnp.arange(quarter, dtype=jnp.float32)
    inverse = jnp.power(jnp.float32(10000.0), -2.0 * counter / (head_size // 2))
    row_angle = positions[0].astype(jnp.float32)[:, None] * inverse[None, :]
    col_angle = positions[1].astype(jnp.float32)[:, None] * inverse[None, :]
    angle = jnp.concatenate([row_angle, col_angle], axis=1)
    angle = jnp.concatenate([angle, angle], axis=1)
    return (jnp.cos(angle), jnp.sin(angle))


def apply_rotary(matrix, cosine, sine):
    half_size = matrix.shape[-1] // 2
    turned = jnp.concatenate([-matrix[..., half_size:], matrix[..., :half_size]], axis=-1)
    return matrix * cosine[:, None, :] + turned * sine[:, None, :]


def rotary_back(grad_rows, cosine, sine):
    half_size = grad_rows.shape[-1] // 2
    sined = grad_rows * sine[:, None, :]
    turned = jnp.concatenate([sined[..., half_size:], -sined[..., :half_size]], axis=-1)
    return grad_rows * cosine[:, None, :] + turned


def masked_scores(queries, keys_rot, ident, score_scale):
    scores = (
        jnp.einsum("qhd,khd->hqk", queries, keys_rot, preferred_element_type=jnp.float32)
        * score_scale
    )
    same_pic = ident[:, None] == ident[None, :]
    return jnp.where(same_pic[None], scores, -1000000000.0)


def attend(pieces, score_scale):
    queries, keys_rot, values_all, ident = pieces
    scores = masked_scores(queries, keys_rot, ident, score_scale)
    top_score = jnp.max(scores, axis=2, keepdims=True)
    exp_scores = jnp.exp(scores - top_score)
    total = jnp.sum(exp_scores, axis=2, keepdims=True)
    probs = (exp_scores / total).astype(jnp.bfloat16)
    attended = jnp.einsum("hqk,khd->qhd", probs, values_all, preferred_element_type=jnp.float32)
    return (attended, (top_score + jnp.log(total))[:, :, 0])


def attend_back(pieces, score_scale):
    queries, keys_rot, values_all, ident, grad_heads, log_total = pieces
    scores = masked_scores(queries, keys_rot, ident, score_scale)
    probs = jnp.exp(scores - log_total[:, :, None])
    grad_probs = jnp.einsum(
        "qhd,khd->hqk", grad_heads, values_all, preferred_element_type=jnp.float32
    )
    inner = jnp.sum(probs * grad_probs, axis=2, keepdims=True)
    grad_scores = (probs * (grad_probs - inner)).astype(jnp.bfloat16)
    grad_query = (
        jnp.einsum("hqk,khd->qhd", grad_scores, keys_rot, preferred_element_type=jnp.float32)
        * score_scale
    )
    grad_key = (
        jnp.einsum("hqk,qhd->khd", grad_scores, queries, preferred_element_type=jnp.float32)
        * score_scale
    )
    grad_value = jnp.einsum(
        "hqk,qhd->khd", probs.astype(jnp.bfloat16), grad_heads, preferred_element_type=jnp.float32
    )
    return (grad_query, grad_key, grad_value)


def row_product(left, right):
    return jnp.einsum("ti,tj->ij", left, right, preferred_element_type=jnp.float32)


def back_product(grad_rows, weight_full):
    return jnp.einsum("tj,ij->ti", grad_rows, weight_full, preferred_element_type=jnp.float32)


MESH = pl.DeviceIdType.MESH


class Place:
    def __init__(self, n_rep):
        rep = lax.axis_index("rep")
        self.nz = n_rep // 4
        self.half = self.nz // 2
        self.y = lax.axis_index("shard")
        self.z, self.x, self.c = rep // 4, (rep // 2) % 2, rep % 2
        self.low = self.z < self.half
        self.depth = jnp.where(self.low, self.z, self.nz - 1 - self.z)
        side = jnp.where(self.low, 1, -1)
        self.to_core = {"rep": self.z * 4 + self.x * 2 + (1 - self.c)}
        self.to_x = {"rep": self.z * 4 + (1 - self.x) * 2 + self.c}
        self.to_y = {"shard": 1 - self.y}
        self.to_in = {"rep": (self.z + side) * 4 + self.x * 2 + self.c}
        self.to_out = {"rep": (self.z - side) * 4 + self.x * 2 + self.c}

    def at_depth(self, depth):
        return pl.when(self.depth == depth)

    def meet(self, with_y):
        barrier = pltpu.get_barrier_semaphore()
        near = [self.to_core, self.to_x, self.to_in] + ([self.to_y] if with_y else [])
        for device in near:
            pl.semaphore_signal(barrier, inc=1, device_id=device, device_id_type=MESH)

        @pl.when(self.depth > 0)
        def _():
            pl.semaphore_signal(barrier, inc=1, device_id=self.to_out, device_id_type=MESH)

        pl.semaphore_wait(barrier, jnp.where(self.depth > 0, len(near) + 1, len(near)))


def remote(src, dst, sems, k, device):
    return pltpu.make_async_remote_copy(
        src_ref=src,
        dst_ref=dst,
        send_sem=sems.at[0, k],
        recv_sem=sems.at[1, k],
        device_id=device,
        device_id_type=MESH,
    )


def add_into(dst, one, two):
    rows = dst.shape[0]
    step = 32 if rows % 32 == 0 else rows

    @pl.loop(0, rows // step)
    def _(i):
        spot = pl.ds(pl.multiple_of(i * step, step), step)
        total = one[spot, :].astype(jnp.float32) + two[spot, :].astype(jnp.float32)
        dst[spot, :] = total.astype(dst.dtype)


def skewed(count, stages):
    last = max(offset for offset, _ in stages)
    for tick in range(count + last):
        for offset, stage in sorted(stages, key=lambda item: -item[0]):
            if 0 <= tick - offset < count:
                stage(tick - offset)


def gather_kernel(n_rep, chunks, shard_rows, rows, wide, *refs):
    count, n_w = len(chunks), len(shard_rows)
    shards, fulls = refs[:n_w], refs[n_w : 2 * n_w]
    hold, own_in, own_out, y_sem, d_sem, in_sem, mid_sem, back_sem, x_sem, c_sem, cd_sem = refs[
        2 * n_w :
    ]
    at = Place(n_rep)
    nz, half = at.nz, at.half
    plane = rows * 4 // 5
    unit = plane // n_rep
    straight = (rows - plane) // 2
    mine, yours = at.y, 1 - at.y

    def shard(k, first, size):
        w, row0, col0 = chunks[k]
        return shards[w].at[pl.ds(pl.multiple_of(row0 + first, 8), size), pl.ds(col0, wide)]

    def full(k, owner, first, size):
        w, row0, col0 = chunks[k]
        start = pl.multiple_of(owner * shard_rows[w] + row0 + first, 8)
        return fulls[w].at[pl.ds(start, size), pl.ds(col0, wide)]

    def place(c, x, z):
        return ((c * 2 + x) * nz + z) * unit

    def y_copy(k, owner):
        first = place(at.c, at.x, at.z)
        return remote(shard(k, first, unit), full(k, owner, first, unit), y_sem, k, at.to_y)

    def d_copy(k, owner):
        first = plane + at.c * straight
        return remote(
            shard(k, first, straight), full(k, owner, first, straight), d_sem, k, at.to_y
        )

    def along(k, begin, size, sems, device):
        view = full(k, yours, place(at.c, at.x, begin), size * unit)
        return remote(view, view, sems, k, device)

    def in_send(k, depth):
        return along(k, jnp.where(at.low, 0, nz - 1 - depth), depth + 1, in_sem, at.to_in)

    def in_take(k, depth):
        return along(k, jnp.where(at.low, 0, nz - depth), depth, in_sem, at.to_in)

    def mid_send(k):
        return along(k, jnp.where(at.low, 0, half), half, mid_sem, at.to_in)

    def mid_take(k):
        return along(k, jnp.where(at.low, half, 0), half, mid_sem, at.to_in)

    def back_send(k, depth):
        return along(k, jnp.where(at.low, depth, 0), nz - depth, back_sem, at.to_out)

    def back_take(k, depth):
        return along(k, jnp.where(at.low, depth + 1, 0), nz - depth - 1, back_sem, at.to_out)

    def x_copy(k, x):
        view = full(k, yours, place(at.c, x, 0), nz * unit)
        return remote(view, view, x_sem, k, at.to_x)

    def c_copy(k, c):
        view = full(k, yours, place(c, 0, 0), 2 * nz * unit)
        return remote(view, view, c_sem, k, at.to_core)

    def cd_copy(k, c):
        view = full(k, yours, plane + c * straight, straight)
        return remote(view, view, cd_sem, k, at.to_core)

    def own_load(k):
        return pltpu.make_async_copy(shard(k, 0, rows), hold.at[k % 3], own_in.at[k])

    def own_store(k):
        return pltpu.make_async_copy(hold.at[k % 3], full(k, mine, 0, rows), own_out.at[k])

    def inner_send(k, depth):
        (mid_send(k) if depth == half - 1 else in_send(k, depth)).start()

    def take_own(k):
        if k >= 3:
            own_store(k - 3).wait()
        own_load(k).start()

    def crossed(k):
        own_load(k).wait()
        own_store(k).start()
        y_copy(k, yours).wait_recv()

        @at.at_depth(0)
        def _():
            inner_send(k, 0)

        d_copy(k, yours).wait_recv()
        cd_copy(k, at.c).start()

    def pass_in(depth):
        def stage(k):
            @at.at_depth(depth)
            def _():
                in_take(k, depth).wait_recv()
                inner_send(k, depth)

        return stage

    def middle(k):
        @at.at_depth(half - 1)
        def _():
            mid_take(k).wait_recv()
            if half > 1:
                back_send(k, half - 1).start()
            x_copy(k, at.x).start()

    def pass_out(depth):
        def stage(k):
            @at.at_depth(depth)
            def _():
                back_take(k, depth).wait_recv()
                if depth > 0:
                    back_send(k, depth).start()
                x_copy(k, at.x).start()

        return stage

    def crossed_x(k):
        x_copy(k, 1 - at.x).wait_recv()
        c_copy(k, at.c).start()

    at.meet(True)
    for k in range(count):
        y_copy(k, mine).start()
        d_copy(k, mine).start()
    stages = [(0, take_own), (1, crossed)]
    stages += [(1 + depth, pass_in(depth)) for depth in range(1, half)]
    stages += [(1 + half, middle)]
    stages += [(1 + half + (half - 1 - depth), pass_out(depth)) for depth in range(half - 1)]
    stages += [(2 * half + 1, crossed_x)]
    skewed(count, stages)
    for k in range(count):
        if k >= count - 3:
            own_store(k).wait()
        y_copy(k, mine).wait_send()
        d_copy(k, mine).wait_send()
        x_copy(k, at.x).wait_send()
        c_copy(k, at.c).wait_send()
        cd_copy(k, at.c).wait_send()
        for depth in range(half):

            @at.at_depth(depth)
            def _():
                (mid_send(k) if depth == half - 1 else in_send(k, depth)).wait_send()
                if depth > 0:
                    back_send(k, depth).wait_send()

        c_copy(k, 1 - at.c).wait_recv()
        cd_copy(k, 1 - at.c).wait_recv()


def gather_weights(shards, n_rep, n_shard):
    if n_shard != 2:
        return [lax.all_gather(shard, "shard", axis=0, tiled=True) for shard in shards]
    rows, wide, chunks = cut_chunks(shards)
    count = len(chunks)
    shapes = [(shard.shape[0] * n_shard, shard.shape[1]) for shard in shards]
    kernel = partial(
        gather_kernel, n_rep, chunks, [shard.shape[0] for shard in shards], rows, wide
    )
    pair = pltpu.SemaphoreType.DMA((2, count))
    return pl.pallas_call(
        kernel,
        out_shape=[jax.ShapeDtypeStruct(shape, jnp.bfloat16) for shape in shapes],
        in_specs=[pl.BlockSpec(memory_space=pl.ANY)] * len(shards),
        out_specs=[pl.BlockSpec(memory_space=pl.ANY)] * len(shards),
        scratch_shapes=[pltpu.VMEM((3, rows, wide), jnp.bfloat16)]
        + [pltpu.SemaphoreType.DMA((count,))] * 2
        + [pair] * 8,
        compiler_params=pltpu.CompilerParams(
            collective_id=0, has_side_effects=True, vmem_limit_bytes=60 << 20
        ),
        name="gather_weights",
    )(*shards)


def cut_chunks(shards):
    rows = min(shard.shape[0] for shard in shards)
    wide = min(shard.shape[1] for shard in shards)
    chunks = []
    for w, shard in enumerate(shards):
        for row0 in range(0, shard.shape[0], rows):
            for col0 in range(0, shard.shape[1], wide):
                chunks.append((w, row0, col0))
    return rows, wide, chunks


def reduce_kernel(n_rep, parts, chunks, shard_rows, rows, wide, *refs):
    count, n_w = len(chunks), len(shard_rows)
    sources, outs, arrived = refs[:n_w], refs[n_w : 2 * n_w], refs[2 * n_w]
    (
        held, lent, got_y, got_x, got_in, got_mid, total,
        own_in, lent_in, put, c0_sem, c1_sem, y_sem, x_sem, in_sem, mid_sem, back_sem,
        ax_sem, ac_sem, af_sem,
    ) = refs[2 * n_w + 1 :]
    c_sems = [c0_sem, c1_sem]
    at = Place(n_rep)
    half = at.half
    block = rows // 4
    with_y = parts == 2
    mine = at.y if with_y else 0

    def source(k, owner, c):
        w, row0, col0 = chunks[k]
        start = pl.multiple_of(owner * shard_rows[w] + row0 + c * 2 * block, 8)
        return sources[w].at[pl.ds(start, 2 * block), pl.ds(col0, wide)]

    def out(k, c, x):
        w, row0, col0 = chunks[k]
        start = pl.multiple_of(row0 + (c * 2 + x) * block, 8)
        return outs[w].at[pl.ds(start, block), pl.ds(col0, wide)]

    def rows_of(x):
        return pl.ds(pl.multiple_of(x * block, 8), block)

    def c_send(k, owner):
        return remote(
            source(k, owner, 1 - at.c), arrived.at[k, owner], c_sems[owner], k, at.to_core
        )

    def own_load(k, owner):
        return pltpu.make_async_copy(
            source(k, owner, at.c), held.at[k, owner], own_in.at[owner, k]
        )

    def lent_load(k, owner):
        return pltpu.make_async_copy(
            arrived.at[k, owner], lent.at[k % 2, owner], lent_in.at[owner, k]
        )

    def y_send(k):
        return remote(held.at[k, 1 - mine], got_y.at[k], y_sem, k, at.to_y)

    def x_send(k):
        return remote(
            held.at[k, mine, rows_of(1 - at.x)], got_x.at[k], x_sem, k, at.to_x
        )

    def part(k):
        return held.at[k, mine, rows_of(at.x)]

    def in_send(k):
        return remote(part(k), got_in.at[k], in_sem, k, at.to_in)

    def mid_send(k):
        return remote(part(k), got_mid.at[k], mid_sem, k, at.to_in)

    def back_send(k):
        return remote(total.at[k], total.at[k], back_sem, k, at.to_out)

    def ax_send(k, x):
        return remote(total.at[k], out(k, at.c, x), ax_sem, k, at.to_x)

    def ac_send(k, c):
        return remote(total.at[k], out(k, c, at.x), ac_sem, k, at.to_core)

    def af_send(k, c):
        view = out(k, c, 1 - at.x)
        return remote(view, view, af_sem, k, at.to_core)

    def own_put(k):
        return pltpu.make_async_copy(total.at[k], out(k, at.c, at.x), put.at[k])

    def start_core(k):
        for owner in range(parts):
            c_send(k, owner).start()
            own_load(k, owner).start()

    def load_core(k):
        for owner in range(parts):
            c_send(k, owner).wait_recv()
            lent_load(k, owner).start()

    def start_y(k):
        for owner in range(parts):
            own_load(k, owner).wait()
            lent_load(k, owner).wait()
        if with_y:
            other = 1 - mine
            add_into(held.at[k, other], held.at[k, other], lent.at[k % 2, other])
            y_send(k).start()
        add_into(held.at[k, mine], held.at[k, mine], lent.at[k % 2, mine])

    def start_x(k):
        if with_y:
            y_send(k).wait_recv()
            spot = rows_of(1 - at.x)
            add_into(held.at[k, mine, spot], held.at[k, mine, spot], got_y.at[k, spot])
        x_send(k).start()
        if with_y:
            add_into(part(k), part(k), got_y.at[k, rows_of(at.x)])

    def inner_send(k, depth):
        (mid_send(k) if depth == half - 1 else in_send(k)).start()

    def start_z(k):
        x_send(k).wait_recv()
        add_into(part(k), part(k), got_x.at[k])

        @at.at_depth(0)
        def _():
            inner_send(k, 0)

    def pass_in(depth):
        def stage(k):
            @at.at_depth(depth)
            def _():
                in_send(k).wait_recv()
                add_into(part(k), part(k), got_in.at[k])
                inner_send(k, depth)

        return stage

    def spread(k, depth):
        if depth > 0:
            back_send(k).start()
        ax_send(k, at.x).start()
        ac_send(k, at.c).start()
        own_put(k).start()

    def middle(k):
        @at.at_depth(half - 1)
        def _():
            mid_send(k).wait_recv()
            add_into(total.at[k], part(k), got_mid.at[k])
            spread(k, half - 1)

    def pass_out(depth):
        def stage(k):
            @at.at_depth(depth)
            def _():
                back_send(k).wait_recv()
                spread(k, depth)

        return stage

    def forward(k):
        ax_send(k, 1 - at.x).wait_recv()
        af_send(k, at.c).start()

    at.meet(with_y)
    stages = [(0, start_core), (1, load_core), (2, start_y), (4, start_x), (5, start_z)]
    stages += [(6 + depth - 1, pass_in(depth)) for depth in range(1, half)]
    stages += [(6 + half - 1, middle)]
    stages += [(6 + half + (half - 2 - depth), pass_out(depth)) for depth in range(half - 1)]
    stages += [(5 + 2 * half, forward)]
    skewed(count, stages)
    for k in range(count):
        for owner in range(parts):
            c_send(k, owner).wait_send()
        if with_y:
            y_send(k).wait_send()
        x_send(k).wait_send()
        for depth in range(half):

            @at.at_depth(depth)
            def _():
                (mid_send(k) if depth == half - 1 else in_send(k)).wait_send()
                if depth > 0:
                    back_send(k).wait_send()

        ax_send(k, at.x).wait_send()
        ac_send(k, at.c).wait_send()
        af_send(k, at.c).wait_send()
        own_put(k).wait()
        ac_send(k, 1 - at.c).wait_recv()
        af_send(k, 1 - at.c).wait_recv()


def reduce_products(products, n_rep, n_shard):
    parts = n_shard
    if n_shard != 2:
        products = [
            lax.psum_scatter(item, "shard", scatter_dimension=0, tiled=True) for item in products
        ]
        parts = 1
    owned = [
        jax.ShapeDtypeStruct((item.shape[0] // parts, item.shape[1]), jnp.bfloat16)
        for item in products
    ]
    rows, wide, chunks = cut_chunks(owned)
    count, block = len(chunks), rows // 4
    kernel = partial(
        reduce_kernel, n_rep, parts, chunks, [item.shape[0] for item in owned], rows, wide
    )
    pair = pltpu.SemaphoreType.DMA((2, count))
    low = jnp.bfloat16
    anywhere = pl.BlockSpec(memory_space=pl.ANY)
    results = pl.pallas_call(
        kernel,
        out_shape=owned + [jax.ShapeDtypeStruct((count, parts, 2 * block, wide), low)],
        in_specs=[anywhere] * len(products),
        out_specs=[anywhere] * (len(products) + 1),
        scratch_shapes=[
            pltpu.VMEM((count, parts, 2 * block, wide), low),
            pltpu.VMEM((2, parts, 2 * block, wide), low),
            pltpu.VMEM((count, 2 * block, wide), low),
            pltpu.VMEM((count, block, wide), low),
            pltpu.VMEM((count, block, wide), low),
            pltpu.VMEM((count, block, wide), low),
            pltpu.VMEM((count, block, wide), low),
            pltpu.SemaphoreType.DMA((parts, count)),
            pltpu.SemaphoreType.DMA((parts, count)),
            pltpu.SemaphoreType.DMA((count,)),
        ]
        + [pair] * 10,
        compiler_params=pltpu.CompilerParams(
            collective_id=1, has_side_effects=True, vmem_limit_bytes=62 << 20
        ),
        name="reduce_products",
    )(*products)
    return results[:-1]


class Links:
    def __init__(self, n_rep, n_shard):
        self.nz, self.ny, self.n_rep = n_rep // 4, n_shard, n_rep
        self.y = lax.axis_index("shard")

    def gather_vector(self, vector):
        return lax.all_gather(vector, "shard", axis=0, tiled=False)

    def sum_all(self, vector):
        for flip in (1, 2):
            vector = vector + lax.ppermute(
                vector, "rep", [(i, i ^ flip) for i in range(self.n_rep)]
            )
        step = 1
        while step < self.nz:
            pairs = [(i, i ^ (4 * step)) for i in range(self.n_rep)]
            vector = vector + lax.ppermute(vector, "rep", pairs)
            step *= 2
        step = 1
        while step < self.ny:
            pairs = [(i, i ^ step) for i in range(self.ny)]
            vector = vector + lax.ppermute(vector, "shard", pairs)
            step *= 2
        return vector


def per_device(
    patches,
    lengths,
    positions,
    ln1_gain,
    ln1_bias,
    qkv_weight,
    qkv_bias,
    proj_weight,
    proj_bias,
    ln2_gain,
    ln2_bias,
    fc1_weight,
    fc1_bias,
    fc2_weight,
    fc2_bias,
    cotangent,
    n_rep,
    n_shard,
):
    links = Links(n_rep, n_shard)
    pack_count = lengths.shape[0]
    row_count = patches.shape[0]
    length = row_count // pack_count
    model_width = patches.shape[1]
    head_count = HEADS
    head_size = model_width // head_count
    score_scale = head_size ** (-0.5)
    pic_ends = jnp.cumsum(lengths[:, :-1], axis=1)
    slot_index = jnp.arange(length, dtype=jnp.int32)
    idents = jnp.sum((slot_index[None, :, None] >= pic_ends[:, None, :]).astype(jnp.int32), axis=2)
    cosine, sine = rotary_tables(positions, head_size)
    pack_shape = (pack_count, length, head_count, head_size)

    small = [ln1_gain, ln1_bias, qkv_bias, proj_bias, ln2_gain, ln2_bias, fc1_bias, fc2_bias]
    sizes = [item.shape[0] for item in small]
    gathered = links.gather_vector(jnp.concatenate(small))
    spots = [sum(sizes[:i]) for i in range(len(sizes) + 1)]
    (
        first_norm_gain, first_norm_bias, b_qkv, b_proj,
        second_norm_gain, second_norm_bias, b_up, b_down,
    ) = [
        gathered[:, spots[i] : spots[i + 1]].reshape(-1).astype(jnp.float32)
        for i in range(len(sizes))
    ]

    w_qkv, w_proj, w_up, w_down = gather_weights(
        [qkv_weight, proj_weight, fc1_weight, fc2_weight], n_rep, n_shard
    )

    input_rows = patches.astype(jnp.float32)
    first_centered_standard, first_inverse_spread = apply_layer_norm(input_rows)
    first_normalized = (first_centered_standard * first_norm_gain + first_norm_bias).astype(
        jnp.bfloat16
    )
    qkv_rows = jnp.dot(first_normalized, w_qkv, preferred_element_type=jnp.float32) + b_qkv
    qkv_rows = qkv_rows.reshape(row_count, 3, head_count, head_size)
    queries = apply_rotary(qkv_rows[:, 0], cosine, sine).astype(jnp.bfloat16).reshape(pack_shape)
    keys_rot = apply_rotary(qkv_rows[:, 1], cosine, sine).astype(jnp.bfloat16).reshape(pack_shape)
    values_all = qkv_rows[:, 2].astype(jnp.bfloat16).reshape(pack_shape)
    attended, log_total = lax.map(
        partial(attend, score_scale=score_scale), (queries, keys_rot, values_all, idents)
    )
    heads_out = attended.reshape(row_count, model_width).astype(jnp.bfloat16)
    hidden_rows = (
        input_rows + jnp.dot(heads_out, w_proj, preferred_element_type=jnp.float32) + b_proj
    )
    second_centered_standard, second_inverse_spread = apply_layer_norm(hidden_rows)
    second_normalized = (second_centered_standard * second_norm_gain + second_norm_bias).astype(
        jnp.bfloat16
    )
    up_pre = jnp.dot(second_normalized, w_up, preferred_element_type=jnp.float32) + b_up
    sigmoid_up = 1.0 / (1.0 + jnp.exp(-quick_slope * up_pre))
    activation = (up_pre * sigmoid_up).astype(jnp.bfloat16)

    d_w_down = row_product(activation, cotangent).astype(jnp.bfloat16)
    out_full = (
        hidden_rows + jnp.dot(activation, w_down, preferred_element_type=jnp.float32) + b_down
    )
    layer_out = out_full.astype(jnp.bfloat16)
    grad_out = cotangent.astype(jnp.float32)
    d_b_down = jnp.sum(grad_out, axis=0)
    grad_act = back_product(cotangent, w_down)
    slope_up = sigmoid_up + quick_slope * up_pre * sigmoid_up * (1.0 - sigmoid_up)
    grad_pre = (grad_act * slope_up).astype(jnp.bfloat16)
    d_w_up = row_product(second_normalized, grad_pre).astype(jnp.bfloat16)
    d_b_up = jnp.sum(grad_pre.astype(jnp.float32), axis=0)
    second_normalized_gradient = back_product(grad_pre, w_up)
    second_gain_gradient = jnp.sum(second_normalized_gradient * second_centered_standard, axis=0)
    d_bias_two = jnp.sum(second_normalized_gradient, axis=0)
    grad_hidden = grad_out + norm_gradient_step(
        second_normalized_gradient,
        second_centered_standard,
        second_inverse_spread,
        second_norm_gain,
    )
    grad_branch = grad_hidden.astype(jnp.bfloat16)
    d_w_proj = row_product(heads_out, grad_branch).astype(jnp.bfloat16)
    d_b_proj = jnp.sum(grad_branch.astype(jnp.float32), axis=0)
    grad_heads = back_product(grad_branch, w_proj).astype(jnp.bfloat16).reshape(pack_shape)
    grad_query, grad_key, grad_value = lax.map(
        partial(attend_back, score_scale=score_scale),
        (queries, keys_rot, values_all, idents, grad_heads, log_total),
    )
    rows_shape = (row_count, head_count, head_size)
    grad_query = rotary_back(grad_query.reshape(rows_shape), cosine, sine)
    grad_key = rotary_back(grad_key.reshape(rows_shape), cosine, sine)
    grad_qkv = (
        jnp.stack([grad_query, grad_key, grad_value.reshape(rows_shape)], axis=1)
        .reshape(row_count, 3 * model_width)
        .astype(jnp.bfloat16)
    )
    d_w_qkv = row_product(first_normalized, grad_qkv).astype(jnp.bfloat16)
    d_b_qkv = jnp.sum(grad_qkv.astype(jnp.float32), axis=0)
    first_normalized_gradient = back_product(grad_qkv, w_qkv)
    first_gain_gradient = jnp.sum(first_normalized_gradient * first_centered_standard, axis=0)
    d_bias_one = jnp.sum(first_normalized_gradient, axis=0)
    d_patches = grad_hidden + norm_gradient_step(
        first_normalized_gradient,
        first_centered_standard,
        first_inverse_spread,
        first_norm_gain,
    )

    d_w_down, d_w_up, d_w_proj, d_w_qkv = [
        item.astype(jnp.float32)
        for item in reduce_products([d_w_down, d_w_up, d_w_proj, d_w_qkv], n_rep, n_shard)
    ]

    def own_parts(vectors):
        lens = [item.shape[0] for item in vectors]
        total = links.sum_all(jnp.concatenate(vectors))
        result, start = [], 0
        for size in lens:
            own = size // n_shard
            result.append(lax.dynamic_slice_in_dim(total, start + links.y * own, own, 0))
            start += size
        return result

    m_gain, m_bias, m_upb, m_downb = own_parts(
        [second_gain_gradient, d_bias_two, d_b_up, d_b_down]
    )
    a_gain, a_bias, a_qkvb, a_projb = own_parts(
        [first_gain_gradient, d_bias_one, d_b_qkv, d_b_proj]
    )
    return (
        layer_out,
        d_patches,
        a_gain,
        a_bias,
        d_w_qkv,
        a_qkvb,
        d_w_proj,
        a_projb,
        m_gain,
        m_bias,
        d_w_up,
        m_upb,
        d_w_down,
        m_downb,
    )


def solution(mesh):
    rows, whole = P(("rep", "shard"), None), P("shard")
    matrix = P("shard", None)
    in_specs = (
        rows,
        rows,
        P(None, ("rep", "shard")),
        whole,
        whole,
        matrix,
        whole,
        matrix,
        whole,
        whole,
        whole,
        matrix,
        whole,
        matrix,
        whole,
        rows,
    )
    out_specs = (
        rows,
        rows,
        whole,
        whole,
        matrix,
        whole,
        matrix,
        whole,
        whole,
        whole,
        matrix,
        whole,
        matrix,
        whole,
    )
    body = partial(per_device, n_rep=mesh.shape["rep"], n_shard=mesh.shape["shard"])
    return jax.shard_map(
        body, mesh=mesh, in_specs=in_specs, out_specs=out_specs, check_vma=False
    )
```

```python
from functools import partial

import jax
import jax.numpy as jnp
from jax import lax
from jax.experimental import pallas as pl
from jax.experimental.pallas import tpu as pltpu
from jax.sharding import PartitionSpec as P

HEADS = 16


norm_eps = 1e-06
quick_slope = 1.702


def apply_layer_norm(matrix):
    center = matrix - jnp.mean(matrix, axis=-1, keepdims=True)
    spread = jnp.mean(center * center, axis=-1, keepdims=True)
    inverse_spread = lax.rsqrt(spread + norm_eps)
    return (center * inverse_spread, inverse_spread)


def norm_gradient_step(normalized_gradient, centered_standard, inverse_spread, norm_gain):
    scaled_rows = normalized_gradient * norm_gain
    return inverse_spread * (
        scaled_rows
        - jnp.mean(scaled_rows, axis=-1, keepdims=True)
        - centered_standard * jnp.mean(scaled_rows * centered_standard, axis=-1, keepdims=True)
    )


def rotary_tables(positions, head_size):
    quarter = head_size // 4
    counter = jnp.arange(quarter, dtype=jnp.float32)
    inverse = jnp.power(jnp.float32(10000.0), -2.0 * counter / (head_size // 2))
    row_angle = inverse[:, None] * positions[0].astype(jnp.float32)[None, :]
    col_angle = inverse[:, None] * positions[1].astype(jnp.float32)[None, :]
    angle = jnp.concatenate([row_angle, col_angle], axis=0)
    angle = jnp.concatenate([angle, angle], axis=0)
    return (jnp.cos(angle), jnp.sin(angle))


def apply_rotary(matrix, cosine, sine):
    half_size = matrix.shape[-2] // 2
    turned = jnp.concatenate([-matrix[..., half_size:, :], matrix[..., :half_size, :]], axis=-2)
    return matrix * cosine + turned * sine


def rotary_back(grad, cosine, sine):
    half_size = grad.shape[-2] // 2
    sined = grad * sine
    turned = jnp.concatenate([sined[..., half_size:, :], -sined[..., :half_size, :]], axis=-2)
    return grad * cosine + turned


def contract(left, right, left_dim, right_dim):
    return lax.dot_general(
        left, right, (((left_dim,), (right_dim,)), ((), ())), preferred_element_type=jnp.float32
    )


def masked_scores(queries, keys_rot, ident, score_scale):
    scores = (
        jnp.einsum("hdk,hdq->hkq", keys_rot, queries, preferred_element_type=jnp.float32)
        * score_scale
    )
    same_pic = ident[:, None] == ident[None, :]
    return jnp.where(same_pic[None], scores, -1000000000.0)


def attend(queries, keys_rot, values_all, ident, score_scale):
    scores = masked_scores(queries, keys_rot, ident, score_scale)
    top_score = jnp.max(scores, axis=1, keepdims=True)
    exp_scores = jnp.exp(scores - top_score)
    total = jnp.sum(exp_scores, axis=1, keepdims=True)
    probs = (exp_scores / total).astype(jnp.bfloat16)
    attended = jnp.einsum("hdk,hkq->hdq", values_all, probs, preferred_element_type=jnp.float32)
    return (attended, (top_score + jnp.log(total))[:, 0, :])


def head_back(query, key, value, grad_head, same_pic, log_total, score_scale):
    scores = jnp.where(same_pic, contract(key, query, 0, 0) * score_scale, -1000000000.0)
    probs = jnp.exp(scores - log_total)
    grad_probs = contract(value, grad_head, 0, 0)
    inner = jnp.sum(probs * grad_probs, axis=0, keepdims=True)
    grad_scores = (probs * (grad_probs - inner)).astype(jnp.bfloat16)
    grad_query = contract(key, grad_scores, 1, 0) * score_scale
    grad_key = contract(query, grad_scores, 1, 1) * score_scale
    grad_value = contract(grad_head, probs.astype(jnp.bfloat16), 1, 1)
    return (grad_query, grad_key, grad_value)


MESH = pl.DeviceIdType.MESH


class Place:
    def __init__(self, n_rep):
        rep = lax.axis_index("rep")
        self.nz = n_rep // 4
        self.half = self.nz // 2
        self.y = lax.axis_index("shard")
        self.z, self.x, self.c = rep // 4, (rep // 2) % 2, rep % 2
        self.low = self.z < self.half
        self.depth = jnp.where(self.low, self.z, self.nz - 1 - self.z)
        side = jnp.where(self.low, 1, -1)
        self.to_core = {"rep": self.z * 4 + self.x * 2 + (1 - self.c)}
        self.to_x = {"rep": self.z * 4 + (1 - self.x) * 2 + self.c}
        self.to_y = {"shard": 1 - self.y}
        self.to_in = {"rep": (self.z + side) * 4 + self.x * 2 + self.c}
        self.to_out = {"rep": (self.z - side) * 4 + self.x * 2 + self.c}

    def at_depth(self, depth):
        return pl.when(self.depth == depth)

    def meet(self, with_y):
        barrier = pltpu.get_barrier_semaphore()
        near = [self.to_core, self.to_x, self.to_in] + ([self.to_y] if with_y else [])
        for device in near:
            pl.semaphore_signal(barrier, inc=1, device_id=device, device_id_type=MESH)

        @pl.when(self.depth > 0)
        def _():
            pl.semaphore_signal(barrier, inc=1, device_id=self.to_out, device_id_type=MESH)

        pl.semaphore_wait(barrier, jnp.where(self.depth > 0, len(near) + 1, len(near)))


def remote(src, dst, sems, k, device):
    return pltpu.make_async_remote_copy(
        src_ref=src,
        dst_ref=dst,
        send_sem=sems.at[0, k],
        recv_sem=sems.at[1, k],
        device_id=device,
        device_id_type=MESH,
    )


def add_into(dst, one, two):
    rows = dst.shape[0]
    step = 32 if rows % 32 == 0 else rows

    @pl.loop(0, rows // step)
    def _(i):
        spot = pl.ds(pl.multiple_of(i * step, step), step)
        total = one[spot, :].astype(jnp.float32) + two[spot, :].astype(jnp.float32)
        dst[spot, :] = total.astype(dst.dtype)


def skewed(count, stages):
    last = max(offset for offset, _ in stages)
    for tick in range(count + last):
        for offset, stage in sorted(stages, key=lambda item: -item[0]):
            if 0 <= tick - offset < count:
                stage(tick - offset)


def gather_kernel(n_rep, chunks, shard_rows, rows, wide, *refs):
    count, n_w = len(chunks), len(shard_rows)
    shards, fulls = refs[:n_w], refs[n_w : 2 * n_w]
    hold, own_in, own_out, y_sem, d_sem, in_sem, mid_sem, back_sem, x_sem, c_sem, cd_sem = refs[
        2 * n_w :
    ]
    at = Place(n_rep)
    nz, half = at.nz, at.half
    plane = rows * 4 // 5
    unit = plane // n_rep
    straight = (rows - plane) // 2
    mine, yours = at.y, 1 - at.y

    def shard(k, first, size):
        w, row0, col0 = chunks[k]
        return shards[w].at[pl.ds(pl.multiple_of(row0 + first, 8), size), pl.ds(col0, wide)]

    def full(k, owner, first, size):
        w, row0, col0 = chunks[k]
        start = pl.multiple_of(owner * shard_rows[w] + row0 + first, 8)
        return fulls[w].at[pl.ds(start, size), pl.ds(col0, wide)]

    def place(c, x, z):
        return ((c * 2 + x) * nz + z) * unit

    def y_copy(k, owner):
        first = place(at.c, at.x, at.z)
        return remote(shard(k, first, unit), full(k, owner, first, unit), y_sem, k, at.to_y)

    def d_copy(k, owner):
        first = plane + at.c * straight
        return remote(
            shard(k, first, straight), full(k, owner, first, straight), d_sem, k, at.to_y
        )

    def along(k, begin, size, sems, device):
        view = full(k, yours, place(at.c, at.x, begin), size * unit)
        return remote(view, view, sems, k, device)

    def in_send(k, depth):
        return along(k, jnp.where(at.low, 0, nz - 1 - depth), depth + 1, in_sem, at.to_in)

    def in_take(k, depth):
        return along(k, jnp.where(at.low, 0, nz - depth), depth, in_sem, at.to_in)

    def mid_send(k):
        return along(k, jnp.where(at.low, 0, half), half, mid_sem, at.to_in)

    def mid_take(k):
        return along(k, jnp.where(at.low, half, 0), half, mid_sem, at.to_in)

    def back_send(k, depth):
        return along(k, jnp.where(at.low, depth, 0), nz - depth, back_sem, at.to_out)

    def back_take(k, depth):
        return along(k, jnp.where(at.low, depth + 1, 0), nz - depth - 1, back_sem, at.to_out)

    def x_copy(k, x):
        view = full(k, yours, place(at.c, x, 0), nz * unit)
        return remote(view, view, x_sem, k, at.to_x)

    def c_copy(k, c):
        view = full(k, yours, place(c, 0, 0), 2 * nz * unit)
        return remote(view, view, c_sem, k, at.to_core)

    def cd_copy(k, c):
        view = full(k, yours, plane + c * straight, straight)
        return remote(view, view, cd_sem, k, at.to_core)

    def own_load(k):
        return pltpu.make_async_copy(shard(k, 0, rows), hold.at[k % 3], own_in.at[k])

    def own_store(k):
        return pltpu.make_async_copy(hold.at[k % 3], full(k, mine, 0, rows), own_out.at[k])

    def inner_send(k, depth):
        (mid_send(k) if depth == half - 1 else in_send(k, depth)).start()

    def take_own(k):
        if k >= 3:
            own_store(k - 3).wait()
        own_load(k).start()

    def crossed(k):
        own_load(k).wait()
        own_store(k).start()
        y_copy(k, yours).wait_recv()

        @at.at_depth(0)
        def _():
            inner_send(k, 0)

        d_copy(k, yours).wait_recv()
        cd_copy(k, at.c).start()

    def pass_in(depth):
        def stage(k):
            @at.at_depth(depth)
            def _():
                in_take(k, depth).wait_recv()
                inner_send(k, depth)

        return stage

    def middle(k):
        @at.at_depth(half - 1)
        def _():
            mid_take(k).wait_recv()
            if half > 1:
                back_send(k, half - 1).start()
            x_copy(k, at.x).start()

    def pass_out(depth):
        def stage(k):
            @at.at_depth(depth)
            def _():
                back_take(k, depth).wait_recv()
                if depth > 0:
                    back_send(k, depth).start()
                x_copy(k, at.x).start()

        return stage

    def crossed_x(k):
        x_copy(k, 1 - at.x).wait_recv()
        c_copy(k, at.c).start()

    at.meet(True)
    for k in range(count):
        y_copy(k, mine).start()
        d_copy(k, mine).start()
    stages = [(0, take_own), (1, crossed)]
    stages += [(1 + depth, pass_in(depth)) for depth in range(1, half)]
    stages += [(1 + half, middle)]
    stages += [(1 + half + (half - 1 - depth), pass_out(depth)) for depth in range(half - 1)]
    stages += [(2 * half + 1, crossed_x)]
    skewed(count, stages)
    for k in range(count):
        if k >= count - 3:
            own_store(k).wait()
        y_copy(k, mine).wait_send()
        d_copy(k, mine).wait_send()
        x_copy(k, at.x).wait_send()
        c_copy(k, at.c).wait_send()
        cd_copy(k, at.c).wait_send()
        for depth in range(half):

            @at.at_depth(depth)
            def _():
                (mid_send(k) if depth == half - 1 else in_send(k, depth)).wait_send()
                if depth > 0:
                    back_send(k, depth).wait_send()

        c_copy(k, 1 - at.c).wait_recv()
        cd_copy(k, 1 - at.c).wait_recv()


def gather_weights(shards, n_rep, n_shard):
    if n_shard != 2:
        return [lax.all_gather(shard, "shard", axis=0, tiled=True) for shard in shards]
    rows, wide, chunks = cut_chunks(shards)
    count = len(chunks)
    shapes = [(shard.shape[0] * n_shard, shard.shape[1]) for shard in shards]
    kernel = partial(
        gather_kernel, n_rep, chunks, [shard.shape[0] for shard in shards], rows, wide
    )
    pair = pltpu.SemaphoreType.DMA((2, count))
    return pl.pallas_call(
        kernel,
        out_shape=[jax.ShapeDtypeStruct(shape, jnp.bfloat16) for shape in shapes],
        in_specs=[pl.BlockSpec(memory_space=pl.ANY)] * len(shards),
        out_specs=[pl.BlockSpec(memory_space=pl.ANY)] * len(shards),
        scratch_shapes=[pltpu.VMEM((3, rows, wide), jnp.bfloat16)]
        + [pltpu.SemaphoreType.DMA((count,))] * 2
        + [pair] * 8,
        compiler_params=pltpu.CompilerParams(
            collective_id=0, has_side_effects=True, vmem_limit_bytes=60 << 20
        ),
        name="gather_weights",
    )(*shards)


def cut_chunks(shards):
    rows = min(shard.shape[0] for shard in shards)
    wide = min(shard.shape[1] for shard in shards)
    chunks = []
    for w, shard in enumerate(shards):
        for row0 in range(0, shard.shape[0], rows):
            for col0 in range(0, shard.shape[1], wide):
                chunks.append((w, row0, col0))
    return rows, wide, chunks


def reduce_kernel(n_rep, parts, chunks, shard_rows, rows, wide, *refs):
    count, n_w = len(chunks), len(shard_rows)
    sources, outs, arrived = refs[:n_w], refs[n_w : 2 * n_w], refs[2 * n_w]
    (
        held, lent, got_y, got_x, got_in, got_mid, total,
        own_in, lent_in, put, c0_sem, c1_sem, y_sem, x_sem, in_sem, mid_sem, back_sem,
        ax_sem, ac_sem, af_sem,
    ) = refs[2 * n_w + 1 :]
    c_sems = [c0_sem, c1_sem]
    at = Place(n_rep)
    half = at.half
    block = rows // 4
    with_y = parts == 2
    mine = at.y if with_y else 0

    def source(k, owner, c):
        w, row0, col0 = chunks[k]
        start = pl.multiple_of(owner * shard_rows[w] + row0 + c * 2 * block, 8)
        return sources[w].at[pl.ds(start, 2 * block), pl.ds(col0, wide)]

    def out(k, c, x):
        w, row0, col0 = chunks[k]
        start = pl.multiple_of(row0 + (c * 2 + x) * block, 8)
        return outs[w].at[pl.ds(start, block), pl.ds(col0, wide)]

    def rows_of(x):
        return pl.ds(pl.multiple_of(x * block, 8), block)

    def c_send(k, owner):
        return remote(
            source(k, owner, 1 - at.c), arrived.at[k, owner], c_sems[owner], k, at.to_core
        )

    def own_load(k, owner):
        return pltpu.make_async_copy(
            source(k, owner, at.c), held.at[k, owner], own_in.at[owner, k]
        )

    def lent_load(k, owner):
        return pltpu.make_async_copy(
            arrived.at[k, owner], lent.at[k % 2, owner], lent_in.at[owner, k]
        )

    def y_send(k):
        return remote(held.at[k, 1 - mine], got_y.at[k], y_sem, k, at.to_y)

    def x_send(k):
        return remote(
            held.at[k, mine, rows_of(1 - at.x)], got_x.at[k], x_sem, k, at.to_x
        )

    def part(k):
        return held.at[k, mine, rows_of(at.x)]

    def in_send(k):
        return remote(part(k), got_in.at[k], in_sem, k, at.to_in)

    def mid_send(k):
        return remote(part(k), got_mid.at[k], mid_sem, k, at.to_in)

    def back_send(k):
        return remote(total.at[k], total.at[k], back_sem, k, at.to_out)

    def ax_send(k, x):
        return remote(total.at[k], out(k, at.c, x), ax_sem, k, at.to_x)

    def ac_send(k, c):
        return remote(total.at[k], out(k, c, at.x), ac_sem, k, at.to_core)

    def af_send(k, c):
        view = out(k, c, 1 - at.x)
        return remote(view, view, af_sem, k, at.to_core)

    def own_put(k):
        return pltpu.make_async_copy(total.at[k], out(k, at.c, at.x), put.at[k])

    def start_core(k):
        for owner in range(parts):
            c_send(k, owner).start()
            own_load(k, owner).start()

    def load_core(k):
        for owner in range(parts):
            c_send(k, owner).wait_recv()
            lent_load(k, owner).start()

    def start_y(k):
        for owner in range(parts):
            own_load(k, owner).wait()
            lent_load(k, owner).wait()
        if with_y:
            other = 1 - mine
            add_into(held.at[k, other], held.at[k, other], lent.at[k % 2, other])
            y_send(k).start()
        add_into(held.at[k, mine], held.at[k, mine], lent.at[k % 2, mine])

    def start_x(k):
        if with_y:
            y_send(k).wait_recv()
            spot = rows_of(1 - at.x)
            add_into(held.at[k, mine, spot], held.at[k, mine, spot], got_y.at[k, spot])
        x_send(k).start()
        if with_y:
            add_into(part(k), part(k), got_y.at[k, rows_of(at.x)])

    def inner_send(k, depth):
        (mid_send(k) if depth == half - 1 else in_send(k)).start()

    def start_z(k):
        x_send(k).wait_recv()
        add_into(part(k), part(k), got_x.at[k])

        @at.at_depth(0)
        def _():
            inner_send(k, 0)

    def pass_in(depth):
        def stage(k):
            @at.at_depth(depth)
            def _():
                in_send(k).wait_recv()
                add_into(part(k), part(k), got_in.at[k])
                inner_send(k, depth)

        return stage

    def spread(k, depth):
        if depth > 0:
            back_send(k).start()
        ax_send(k, at.x).start()
        ac_send(k, at.c).start()
        own_put(k).start()

    def middle(k):
        @at.at_depth(half - 1)
        def _():
            mid_send(k).wait_recv()
            add_into(total.at[k], part(k), got_mid.at[k])
            spread(k, half - 1)

    def pass_out(depth):
        def stage(k):
            @at.at_depth(depth)
            def _():
                back_send(k).wait_recv()
                spread(k, depth)

        return stage

    def forward(k):
        ax_send(k, 1 - at.x).wait_recv()
        af_send(k, at.c).start()

    at.meet(with_y)
    stages = [(0, start_core), (1, load_core), (2, start_y), (4, start_x), (5, start_z)]
    stages += [(6 + depth - 1, pass_in(depth)) for depth in range(1, half)]
    stages += [(6 + half - 1, middle)]
    stages += [(6 + half + (half - 2 - depth), pass_out(depth)) for depth in range(half - 1)]
    stages += [(5 + 2 * half, forward)]
    skewed(count, stages)
    for k in range(count):
        for owner in range(parts):
            c_send(k, owner).wait_send()
        if with_y:
            y_send(k).wait_send()
        x_send(k).wait_send()
        for depth in range(half):

            @at.at_depth(depth)
            def _():
                (mid_send(k) if depth == half - 1 else in_send(k)).wait_send()
                if depth > 0:
                    back_send(k).wait_send()

        ax_send(k, at.x).wait_send()
        ac_send(k, at.c).wait_send()
        af_send(k, at.c).wait_send()
        own_put(k).wait()
        ac_send(k, 1 - at.c).wait_recv()
        af_send(k, 1 - at.c).wait_recv()


def reduce_products(products, n_rep, n_shard):
    parts = n_shard
    if n_shard != 2:
        products = [
            lax.psum_scatter(item, "shard", scatter_dimension=0, tiled=True) for item in products
        ]
        parts = 1
    owned = [
        jax.ShapeDtypeStruct((item.shape[0] // parts, item.shape[1]), jnp.bfloat16)
        for item in products
    ]
    rows, wide, chunks = cut_chunks(owned)
    count, block = len(chunks), rows // 4
    kernel = partial(
        reduce_kernel, n_rep, parts, chunks, [item.shape[0] for item in owned], rows, wide
    )
    pair = pltpu.SemaphoreType.DMA((2, count))
    low = jnp.bfloat16
    anywhere = pl.BlockSpec(memory_space=pl.ANY)
    results = pl.pallas_call(
        kernel,
        out_shape=owned + [jax.ShapeDtypeStruct((count, parts, 2 * block, wide), low)],
        in_specs=[anywhere] * len(products),
        out_specs=[anywhere] * (len(products) + 1),
        scratch_shapes=[
            pltpu.VMEM((count, parts, 2 * block, wide), low),
            pltpu.VMEM((2, parts, 2 * block, wide), low),
            pltpu.VMEM((count, 2 * block, wide), low),
            pltpu.VMEM((count, block, wide), low),
            pltpu.VMEM((count, block, wide), low),
            pltpu.VMEM((count, block, wide), low),
            pltpu.VMEM((count, block, wide), low),
            pltpu.SemaphoreType.DMA((parts, count)),
            pltpu.SemaphoreType.DMA((parts, count)),
            pltpu.SemaphoreType.DMA((count,)),
        ]
        + [pair] * 10,
        compiler_params=pltpu.CompilerParams(
            collective_id=1, has_side_effects=True, vmem_limit_bytes=62 << 20
        ),
        name="reduce_products",
    )(*products)
    return results[:-1]


class Cuts:
    def __init__(self, sizes, n_shard):
        self.shard_rows = [left // n_shard for left, _ in sizes]
        self.rows = min(self.shard_rows) // 2
        self.wide = min(right for _, right in sizes)
        self.down = [rows // self.rows for rows in self.shard_rows]
        self.across = [right // self.wide for _, right in sizes]
        self.first = [0]
        for down, across in zip(self.down, self.across):
            self.first.append(self.first[-1] + down * across)
        self.count = self.first[-1]

    def weight_of(self, k, act):
        for w, down in enumerate(self.down):

            @pl.when((k >= self.first[w]) & (k < self.first[w + 1]))
            def _():
                inside = k - self.first[w]
                act(w, inside % down, inside // down)

    def whole(self, chunks, w):
        first, down, rows, wide = self.first[w], self.down[w], self.rows, self.wide

        def widen(part, dst):
            dst[...] = part[0].astype(jnp.float32)

        return pl.pallas_call(
            widen,
            grid=(down, self.across[w]),
            in_specs=[pl.BlockSpec((1, rows, wide), lambda i, j: (first + j * down + i, 0, 0))],
            out_specs=pl.BlockSpec((rows, wide), lambda i, j: (i, j)),
            out_shape=jax.ShapeDtypeStruct(
                (self.shard_rows[w], self.across[w] * wide), jnp.float32
            ),
            compiler_params=pltpu.CompilerParams(vmem_limit_bytes=24 << 20),
            name="widen",
        )(chunks)


def backward_kernel(n_rep, cuts, n_heads, slots, score_scale, *refs):
    (
        left_0, left_1, left_2, left_3, right_0, right_1, right_2, qkv, w_qkv,
        grad_heads, log_total, pic_key, pic_query, cosine, sine,
        out, grad_qkv, grad_first, lent_left, lent_right,
        op_left, op_right, held, got_y, got_x, got_in, got_mid, total, swap, w_block,
        load_l, load_r, put, qkv_sem, block_sem,
        l0_sem, l1_sem, r_sem, y_sem, x_sem, in_sem, mid_sem, back_sem, ax_sem, ac_sem, af_sem,
    ) = refs
    lefts = [left_0, left_1, left_2, left_3]
    rights = [right_0, right_1, right_2, grad_qkv]
    l_sems = [l0_sem, l1_sem]
    at = Place(n_rep)
    half = at.half
    count, rows, wide = cuts.count, cuts.rows, cuts.wide
    block, width = rows // 2, wide // 2
    mine = at.y
    head = qkv.shape[0] // (3 * n_heads)
    model = n_heads * head

    def left_rows(w, row, owner):
        start = owner * cuts.shard_rows[w] + row * rows
        return lefts[w].at[pl.ds(pl.multiple_of(start, 16), rows), :]

    def right_rows(w, col, c):
        start = col * wide + c * width
        return rights[w].at[pl.ds(pl.multiple_of(start, 16), width), :]

    def left_push(k, owner, src):
        return remote(src, lent_left.at[k, owner], l_sems[owner], k, at.to_core)

    def right_push(k, src):
        return remote(src, lent_right.at[k], r_sem, k, at.to_core)

    def left_load(k, whose, owner, src):
        slot = k % 2
        return pltpu.make_async_copy(
            src, op_left.at[slot, whose, owner], load_l.at[whose, owner, k]
        )

    def right_load(k, whose, src):
        return pltpu.make_async_copy(src, op_right.at[k % 2, whose], load_r.at[whose, k])

    def rows_of(x):
        return pl.ds(pl.multiple_of(x * block, 16), block)

    def mine_of(k, x):
        return held.at[k % slots, mine, rows_of(x)]

    def y_send(k):
        return remote(held.at[k % slots, 1 - mine], got_y.at[k], y_sem, k, at.to_y)

    def x_send(k):
        return remote(mine_of(k, 1 - at.x), got_x.at[k], x_sem, k, at.to_x)

    def in_send(k):
        return remote(mine_of(k, at.x), got_in.at[k], in_sem, k, at.to_in)

    def mid_send(k):
        return remote(mine_of(k, at.x), got_mid.at[k], mid_sem, k, at.to_in)

    def back_send(k):
        return remote(total.at[k], total.at[k], back_sem, k, at.to_out)

    def out_of(k, c, x):
        cols = pl.ds(pl.multiple_of(c * width, 128), width)
        return out.at[k, rows_of(x), cols]

    def ax_send(k, x):
        return remote(total.at[k], out_of(k, at.c, x), ax_sem, k, at.to_x)

    def ac_send(k, c):
        return remote(total.at[k], out_of(k, c, at.x), ac_sem, k, at.to_core)

    def af_send(k, c):
        view = out_of(k, c, 1 - at.x)
        return remote(view, view, af_sem, k, at.to_core)

    def own_put(k):
        return pltpu.make_async_copy(total.at[k], out_of(k, at.c, at.x), put.at[k])

    def push(k):
        def act(w, row, col):
            for owner in range(2):
                left_push(k, owner, left_rows(w, row, owner)).start()
            right_push(k, right_rows(w, col, 1 - at.c)).start()

        cuts.weight_of(k, act)

    def load(k):
        def act(w, row, col):
            for owner in range(2):
                left_load(k, 0, owner, left_rows(w, row, owner)).start()
            right_load(k, 0, right_rows(w, col, at.c)).start()

        cuts.weight_of(k, act)
        for owner in range(2):
            left_push(k, owner, lent_left.at[k, owner]).wait_recv()
            left_load(k, 1, owner, lent_left.at[k, owner]).start()
        right_push(k, lent_right.at[k]).wait_recv()
        right_load(k, 1, lent_right.at[k]).start()

    def product(k):
        slot = k % 2
        for whose in range(2):
            for owner in range(2):
                left_load(k, whose, owner, lent_left.at[k, owner]).wait()
            right_load(k, whose, lent_right.at[k]).wait()
        for owner in range(2):
            left_push(k, owner, lent_left.at[k, owner]).wait_send()
        right_push(k, lent_right.at[k]).wait_send()
        for owner in (1 - mine, mine):
            result = contract(op_left[slot, 0, owner], op_right[slot, 0], 1, 1)
            result += contract(op_left[slot, 1, owner], op_right[slot, 1], 1, 1)
            held[k % slots, owner] = result.astype(jnp.bfloat16)
            if owner is not mine:
                y_send(k).start()

    def start_x(k):
        y_send(k).wait_recv()
        other = mine_of(k, 1 - at.x)
        add_into(other, other, got_y.at[k, rows_of(1 - at.x)])
        x_send(k).start()
        own = mine_of(k, at.x)
        add_into(own, own, got_y.at[k, rows_of(at.x)])
        y_send(k).wait_send()

    def inner_send(k, depth):
        return mid_send(k) if depth == half - 1 else in_send(k)

    def start_z(k):
        x_send(k).wait_recv()
        own = mine_of(k, at.x)
        add_into(own, own, got_x.at[k])

        @at.at_depth(0)
        def _():
            inner_send(k, 0).start()

        x_send(k).wait_send()

    def pass_in(depth):
        def stage(k):
            @at.at_depth(depth)
            def _():
                in_send(k).wait_recv()
                own = mine_of(k, at.x)
                add_into(own, own, got_in.at[k])
                inner_send(k, depth).start()

        return stage

    def spread(k, depth):
        if depth > 0:
            back_send(k).start()
        ax_send(k, at.x).start()
        ac_send(k, at.c).start()
        own_put(k).start()

    def middle(k):
        @at.at_depth(half - 1)
        def _():
            mid_send(k).wait_recv()
            add_into(total.at[k], mine_of(k, at.x), got_mid.at[k])
            spread(k, half - 1)

    def pass_out(depth):
        def stage(k):
            @at.at_depth(depth)
            def _():
                back_send(k).wait_recv()
                spread(k, depth)

        return stage

    def sent(k):
        for depth in range(half):

            @at.at_depth(depth)
            def _():
                inner_send(k, depth).wait_send()

    def forward(k):
        ax_send(k, 1 - at.x).wait_recv()
        af_send(k, at.c).start()

    def finish(k):
        @pl.when(at.depth > 0)
        def _():
            back_send(k).wait_send()

        ax_send(k, at.x).wait_send()
        ac_send(k, at.c).wait_send()
        af_send(k, at.c).wait_send()
        own_put(k).wait()
        ac_send(k, 1 - at.c).wait_recv()
        af_send(k, 1 - at.c).wait_recv()

    def head_step(h):
        def part(i):
            return pl.ds(pl.multiple_of(i * model + h * head, 16), head)

        query, key, value = swap[part(0), :], swap[part(1), :], swap[part(2), :]
        grads = head_back(
            query,
            key,
            value,
            grad_heads[part(0), :],
            pic_key[...] == pic_query[...],
            log_total[pl.ds(h, 1), :],
            score_scale,
        )
        grad_query, grad_key, grad_value = grads
        turn_c, turn_s = cosine[...], sine[...]
        swap[part(0), :] = rotary_back(grad_query, turn_c, turn_s).astype(jnp.bfloat16)
        swap[part(1), :] = rotary_back(grad_key, turn_c, turn_s).astype(jnp.bfloat16)
        swap[part(2), :] = grad_value.astype(jnp.bfloat16)

    def block_load(j):
        cols = pl.ds(pl.multiple_of(j * width, 128), width)
        return pltpu.make_async_copy(w_qkv.at[:, cols], w_block.at[j % 2], block_sem.at[j])

    def first_step(j):
        block_load(j).wait()
        inside = pl.ds(pl.multiple_of(j * width, 16), width)
        step = 256

        @pl.loop(0, model // step)
        def _(i):
            spot = pl.ds(pl.multiple_of(i * step, 16), step)
            grad_first[spot, :] += contract(w_block[j % 2, spot, :], swap[inside, :], 1, 0)

    n_blocks = qkv.shape[0] // width
    take_qkv = pltpu.make_async_copy(qkv, swap, qkv_sem.at[0])
    give_qkv = pltpu.make_async_copy(swap, grad_qkv, qkv_sem.at[1])
    take_qkv.start()
    at.meet(True)
    grad_first[...] = jnp.zeros_like(grad_first)
    take_qkv.wait()
    stages = [(0, push), (1, load), (2, product), (4, start_x), (6, start_z)]
    stages += [(6 + depth, pass_in(depth)) for depth in range(1, half)]
    stages += [(6 + half, middle)]
    stages += [(6 + half + (half - 1 - depth), pass_out(depth)) for depth in range(half - 1)]
    stages += [(slots + 2, sent), (7 + 2 * half, forward), (9 + 2 * half, finish)]
    stages.sort(key=lambda item: -item[0])
    per_tick = -(-n_heads // (cuts.first[3] - 2))
    done = -(-n_heads // per_tick)

    def tick_body(tick, carry):
        for offset, stage in stages:

            @pl.when((tick >= offset) & (tick < count + offset))
            def _():
                stage(tick - offset)

        @pl.when(tick < done)
        def _():
            @pl.loop(0, per_tick)
            def _(i):
                head_step(tick * per_tick + i)

        @pl.when(tick == done)
        def _():
            give_qkv.start()
            give_qkv.wait()

        @pl.when((tick > done) & (tick <= done + n_blocks))
        def _():
            first_step(tick - done - 1)

        @pl.when((tick >= done) & (tick < done + n_blocks))
        def _():
            block_load(tick - done).start()

        return carry

    lax.fori_loop(0, count + 9 + 2 * half, tick_body, 0)


def reduce_backward(lefts, rights, qkv, w_qkv, small, n_rep, n_heads, score_scale):
    tokens = qkv.shape[1]
    sizes = [(left.shape[0], right.shape[0]) for left, right in zip(lefts, rights + [qkv])]
    cuts = Cuts(sizes, 2)
    half = n_rep // 8
    slots = 3 + 2 * half
    count, rows, wide = cuts.count, cuts.rows, cuts.wide
    block, width = rows // 2, wide // 2
    low, dma = jnp.bfloat16, pltpu.SemaphoreType.DMA
    anywhere, local = pl.BlockSpec(memory_space=pl.ANY), pl.BlockSpec(memory_space=pltpu.VMEM)
    model = w_qkv.shape[0]
    chunks, grad_qkv, grad_first, _, _ = pl.pallas_call(
        partial(backward_kernel, n_rep, cuts, n_heads, slots, score_scale),
        out_shape=[
            jax.ShapeDtypeStruct((count, rows, wide), low),
            jax.ShapeDtypeStruct(qkv.shape, low),
            jax.ShapeDtypeStruct((model, tokens), jnp.float32),
            jax.ShapeDtypeStruct((count, 2, rows, tokens), low),
            jax.ShapeDtypeStruct((count, width, tokens), low),
        ],
        in_specs=[anywhere] * 9 + [local] * len(small),
        out_specs=[anywhere, anywhere, local, anywhere, anywhere],
        scratch_shapes=[
            pltpu.VMEM((2, 2, 2, rows, tokens), low),
            pltpu.VMEM((2, 2, width, tokens), low),
            pltpu.VMEM((slots, 2, rows, width), low),
            pltpu.VMEM((count, rows, width), low),
            pltpu.VMEM((count, block, width), low),
            pltpu.VMEM((count, block, width), low),
            pltpu.VMEM((count, block, width), low),
            pltpu.VMEM((count, block, width), low),
            pltpu.VMEM(qkv.shape, low),
            pltpu.VMEM((2, model, width), low),
            dma((2, 2, count)),
            dma((2, count)),
            dma((count,)),
            dma((2,)),
            dma((qkv.shape[0] // width,)),
        ]
        + [dma((2, count))] * 11,
        compiler_params=pltpu.CompilerParams(
            collective_id=1, has_side_effects=True, vmem_limit_bytes=63 << 20
        ),
        name="reduce_backward",
    )(*lefts, *rights, qkv, w_qkv, *small)
    return [cuts.whole(chunks, w) for w in range(len(sizes))], grad_qkv, grad_first


class Links:
    def __init__(self, n_rep, n_shard):
        self.nz, self.ny, self.n_rep = n_rep // 4, n_shard, n_rep
        self.y = lax.axis_index("shard")

    def gather_vector(self, vector):
        return lax.all_gather(vector, "shard", axis=0, tiled=False)

    def sum_all(self, vector):
        for flip in (1, 2):
            vector = vector + lax.ppermute(
                vector, "rep", [(i, i ^ flip) for i in range(self.n_rep)]
            )
        step = 1
        while step < self.nz:
            pairs = [(i, i ^ (4 * step)) for i in range(self.n_rep)]
            vector = vector + lax.ppermute(vector, "rep", pairs)
            step *= 2
        step = 1
        while step < self.ny:
            pairs = [(i, i ^ step) for i in range(self.ny)]
            vector = vector + lax.ppermute(vector, "shard", pairs)
            step *= 2
        return vector


def per_device(
    patches,
    lengths,
    positions,
    ln1_gain,
    ln1_bias,
    qkv_weight,
    qkv_bias,
    proj_weight,
    proj_bias,
    ln2_gain,
    ln2_bias,
    fc1_weight,
    fc1_bias,
    fc2_weight,
    fc2_bias,
    cotangent,
    n_rep,
    n_shard,
):
    links = Links(n_rep, n_shard)
    pack_count = lengths.shape[0]
    row_count = patches.shape[0]
    length = row_count // pack_count
    model_width = patches.shape[1]
    head_count = HEADS
    head_size = model_width // head_count
    score_scale = head_size ** (-0.5)
    pic_ends = jnp.cumsum(lengths[:, :-1], axis=1)
    slot_index = jnp.arange(length, dtype=jnp.int32)
    idents = jnp.sum((slot_index[None, :, None] >= pic_ends[:, None, :]).astype(jnp.int32), axis=2)
    pack_index = jnp.arange(pack_count, dtype=jnp.int32)
    idents = (idents + pack_index[:, None] * lengths.shape[1]).reshape(-1)
    cosine, sine = rotary_tables(positions, head_size)

    small = [ln1_gain, ln1_bias, qkv_bias, proj_bias, ln2_gain, ln2_bias, fc1_bias, fc2_bias]
    sizes = [item.shape[0] for item in small]
    gathered = links.gather_vector(jnp.concatenate(small))
    spots = [sum(sizes[:i]) for i in range(len(sizes) + 1)]
    (
        first_norm_gain, first_norm_bias, b_qkv, b_proj,
        second_norm_gain, second_norm_bias, b_up, b_down,
    ) = [
        gathered[:, spots[i] : spots[i + 1]].reshape(-1).astype(jnp.float32)
        for i in range(len(sizes))
    ]

    w_qkv, w_proj, w_up, w_down = gather_weights(
        [qkv_weight, proj_weight, fc1_weight, fc2_weight], n_rep, n_shard
    )

    input_rows = patches.astype(jnp.float32)
    first_centered_standard, first_inverse_spread = apply_layer_norm(input_rows)
    first_normalized = (first_centered_standard * first_norm_gain + first_norm_bias).astype(
        jnp.bfloat16
    )
    qkv_rows = contract(w_qkv, first_normalized, 0, 1) + b_qkv[:, None]
    qkv_rows = qkv_rows.reshape(3, head_count, head_size, row_count)
    queries = apply_rotary(qkv_rows[0], cosine, sine).astype(jnp.bfloat16)
    keys_rot = apply_rotary(qkv_rows[1], cosine, sine).astype(jnp.bfloat16)
    values_all = qkv_rows[2].astype(jnp.bfloat16)
    attended, log_total = attend(queries, keys_rot, values_all, idents, score_scale)
    heads_out = attended.reshape(model_width, row_count).astype(jnp.bfloat16)
    hidden_rows = input_rows + contract(heads_out, w_proj, 0, 0) + b_proj
    second_centered_standard, second_inverse_spread = apply_layer_norm(hidden_rows)
    second_normalized = (second_centered_standard * second_norm_gain + second_norm_bias).astype(
        jnp.bfloat16
    )
    up_pre = contract(w_up, second_normalized, 0, 1) + b_up[:, None]
    sigmoid_up = 1.0 / (1.0 + jnp.exp(-quick_slope * up_pre))
    activation = (up_pre * sigmoid_up).astype(jnp.bfloat16)

    out_full = hidden_rows + contract(activation, w_down, 0, 0) + b_down
    layer_out = out_full.astype(jnp.bfloat16)
    grad_out = cotangent.astype(jnp.float32)
    d_b_down = jnp.sum(grad_out, axis=0)
    grad_act = contract(w_down, cotangent, 1, 1)
    slope_up = sigmoid_up + quick_slope * up_pre * sigmoid_up * (1.0 - sigmoid_up)
    grad_pre = (grad_act * slope_up).astype(jnp.bfloat16)
    d_b_up = jnp.sum(grad_pre.astype(jnp.float32), axis=1)
    second_normalized_gradient = contract(grad_pre, w_up, 0, 1)
    second_gain_gradient = jnp.sum(second_normalized_gradient * second_centered_standard, axis=0)
    d_bias_two = jnp.sum(second_normalized_gradient, axis=0)
    grad_hidden = grad_out + norm_gradient_step(
        second_normalized_gradient,
        second_centered_standard,
        second_inverse_spread,
        second_norm_gain,
    )
    grad_branch = grad_hidden.astype(jnp.bfloat16)
    d_b_proj = jnp.sum(grad_branch.astype(jnp.float32), axis=0)
    grad_heads = contract(w_proj, grad_branch, 1, 1).astype(jnp.bfloat16)
    lefts = [activation, second_normalized.T, heads_out, first_normalized.T]
    rights = [cotangent.T, grad_pre, grad_branch.T]
    qkv_shape = (3 * model_width, row_count)
    if n_shard == 2:
        qkv = jnp.stack([queries, keys_rot, values_all]).reshape(qkv_shape)
        small_args = [
            grad_heads, log_total, idents[:, None], idents[None, :], cosine, sine,
        ]
        products, grad_qkv, first_gradient = reduce_backward(
            lefts, rights, qkv, w_qkv, small_args, n_rep, head_count, score_scale
        )
    else:
        back = partial(head_back, score_scale=score_scale)
        grad_query, grad_key, grad_value = jax.vmap(back, in_axes=(0, 0, 0, 0, None, 0))(
            queries,
            keys_rot,
            values_all,
            grad_heads.reshape(head_count, head_size, row_count),
            idents[:, None] == idents[None, :],
            log_total[:, None, :],
        )
        grad_query = rotary_back(grad_query, cosine, sine)
        grad_key = rotary_back(grad_key, cosine, sine)
        grad_qkv = jnp.stack([grad_query, grad_key, grad_value]).reshape(qkv_shape)
        grad_qkv = grad_qkv.astype(jnp.bfloat16)
        first_gradient = contract(w_qkv, grad_qkv, 1, 0)
        products = [
            contract(left, right, 1, 1).astype(jnp.bfloat16)
            for left, right in zip(lefts, rights + [grad_qkv])
        ]
        products = [
            item.astype(jnp.float32) for item in reduce_products(products, n_rep, n_shard)
        ]
    d_w_down, d_w_up, d_w_proj, d_w_qkv = products
    d_b_qkv = jnp.sum(grad_qkv.astype(jnp.float32), axis=1)
    first_normalized_gradient = first_gradient.T
    first_gain_gradient = jnp.sum(first_normalized_gradient * first_centered_standard, axis=0)
    d_bias_one = jnp.sum(first_normalized_gradient, axis=0)
    d_patches = grad_hidden + norm_gradient_step(
        first_normalized_gradient,
        first_centered_standard,
        first_inverse_spread,
        first_norm_gain,
    )

    def own_parts(vectors):
        lens = [item.shape[0] for item in vectors]
        total = links.sum_all(jnp.concatenate(vectors))
        result, start = [], 0
        for size in lens:
            own = size // n_shard
            result.append(lax.dynamic_slice_in_dim(total, start + links.y * own, own, 0))
            start += size
        return result

    m_gain, m_bias, m_upb, m_downb = own_parts(
        [second_gain_gradient, d_bias_two, d_b_up, d_b_down]
    )
    a_gain, a_bias, a_qkvb, a_projb = own_parts(
        [first_gain_gradient, d_bias_one, d_b_qkv, d_b_proj]
    )
    return (
        layer_out,
        d_patches,
        a_gain,
        a_bias,
        d_w_qkv,
        a_qkvb,
        d_w_proj,
        a_projb,
        m_gain,
        m_bias,
        d_w_up,
        m_upb,
        d_w_down,
        m_downb,
    )


def solution(mesh):
    rows, whole = P(("rep", "shard"), None), P("shard")
    matrix = P("shard", None)
    in_specs = (
        rows,
        rows,
        P(None, ("rep", "shard")),
        whole,
        whole,
        matrix,
        whole,
        matrix,
        whole,
        whole,
        whole,
        matrix,
        whole,
        matrix,
        whole,
        rows,
    )
    out_specs = (
        rows,
        rows,
        whole,
        whole,
        matrix,
        whole,
        matrix,
        whole,
        whole,
        whole,
        matrix,
        whole,
        matrix,
        whole,
    )
    body = partial(per_device, n_rep=mesh.shape["rep"], n_shard=mesh.shape["shard"])
    return jax.shard_map(
        body, mesh=mesh, in_specs=in_specs, out_specs=out_specs, check_vma=False
    )
```

```python
from functools import partial

import jax
import jax.numpy as jnp
from jax import lax
from jax.experimental import pallas as pl
from jax.experimental.pallas import tpu as pltpu
from jax.sharding import PartitionSpec as P

HEADS = 16


norm_eps = 1e-06
quick_slope = 1.702


def apply_layer_norm(matrix):
    center = matrix - jnp.mean(matrix, axis=-1, keepdims=True)
    spread = jnp.mean(center * center, axis=-1, keepdims=True)
    inverse_spread = lax.rsqrt(spread + norm_eps)
    return (center * inverse_spread, inverse_spread)


def norm_gradient_step(normalized_gradient, centered_standard, inverse_spread, norm_gain):
    scaled_rows = normalized_gradient * norm_gain
    return inverse_spread * (
        scaled_rows
        - jnp.mean(scaled_rows, axis=-1, keepdims=True)
        - centered_standard * jnp.mean(scaled_rows * centered_standard, axis=-1, keepdims=True)
    )


def rotary_tables(positions, head_size):
    quarter = head_size // 4
    counter = jnp.arange(quarter, dtype=jnp.float32)
    inverse = jnp.power(jnp.float32(10000.0), -2.0 * counter / (head_size // 2))
    row_angle = inverse[:, None] * positions[0].astype(jnp.float32)[None, :]
    col_angle = inverse[:, None] * positions[1].astype(jnp.float32)[None, :]
    angle = jnp.concatenate([row_angle, col_angle], axis=0)
    angle = jnp.concatenate([angle, angle], axis=0)
    return (jnp.cos(angle), jnp.sin(angle))


def apply_rotary(matrix, cosine, sine):
    half_size = matrix.shape[-2] // 2
    turned = jnp.concatenate([-matrix[..., half_size:, :], matrix[..., :half_size, :]], axis=-2)
    return matrix * cosine + turned * sine


def rotary_back(grad, cosine, sine):
    half_size = grad.shape[-2] // 2
    sined = grad * sine
    turned = jnp.concatenate([sined[..., half_size:, :], -sined[..., :half_size, :]], axis=-2)
    return grad * cosine + turned


def contract(left, right, left_dim, right_dim):
    return lax.dot_general(
        left, right, (((left_dim,), (right_dim,)), ((), ())), preferred_element_type=jnp.float32
    )


def masked_scores(queries, keys_rot, ident, score_scale):
    scores = (
        jnp.einsum("hdk,hdq->hkq", keys_rot, queries, preferred_element_type=jnp.float32)
        * score_scale
    )
    same_pic = ident[:, None] == ident[None, :]
    return jnp.where(same_pic[None], scores, -1000000000.0)


def attend(queries, keys_rot, values_all, ident, score_scale):
    scores = masked_scores(queries, keys_rot, ident, score_scale)
    top_score = jnp.max(scores, axis=1, keepdims=True)
    exp_scores = jnp.exp(scores - top_score)
    total = jnp.sum(exp_scores, axis=1, keepdims=True)
    probs = (exp_scores / total).astype(jnp.bfloat16)
    attended = jnp.einsum("hdk,hkq->hdq", values_all, probs, preferred_element_type=jnp.float32)
    return (attended, (top_score + jnp.log(total))[:, 0, :])


def head_back(query, key, value, grad_head, same_pic, log_total, score_scale):
    scores = jnp.where(same_pic, contract(key, query, 0, 0) * score_scale, -1000000000.0)
    probs = jnp.exp(scores - log_total)
    grad_probs = contract(value, grad_head, 0, 0)
    inner = jnp.sum(probs * grad_probs, axis=0, keepdims=True)
    grad_scores = (probs * (grad_probs - inner)).astype(jnp.bfloat16)
    grad_query = contract(key, grad_scores, 1, 0) * score_scale
    grad_key = contract(query, grad_scores, 1, 1) * score_scale
    grad_value = contract(grad_head, probs.astype(jnp.bfloat16), 1, 1)
    return (grad_query, grad_key, grad_value)


MESH = pl.DeviceIdType.MESH


class Place:
    def __init__(self, n_rep):
        rep = lax.axis_index("rep")
        self.nz = n_rep // 4
        self.half = self.nz // 2
        self.y = lax.axis_index("shard")
        self.z, self.x, self.c = rep // 4, (rep // 2) % 2, rep % 2
        self.low = self.z < self.half
        self.depth = jnp.where(self.low, self.z, self.nz - 1 - self.z)
        side = jnp.where(self.low, 1, -1)
        self.to_core = {"rep": self.z * 4 + self.x * 2 + (1 - self.c)}
        self.to_x = {"rep": self.z * 4 + (1 - self.x) * 2 + self.c}
        self.to_y = {"shard": 1 - self.y}
        self.to_in = {"rep": (self.z + side) * 4 + self.x * 2 + self.c}
        self.to_out = {"rep": (self.z - side) * 4 + self.x * 2 + self.c}

    def at_depth(self, depth):
        return pl.when(self.depth == depth)

    def meet(self, with_y):
        barrier = pltpu.get_barrier_semaphore()
        near = [self.to_core, self.to_x, self.to_in] + ([self.to_y] if with_y else [])
        for device in near:
            pl.semaphore_signal(barrier, inc=1, device_id=device, device_id_type=MESH)

        @pl.when(self.depth > 0)
        def _():
            pl.semaphore_signal(barrier, inc=1, device_id=self.to_out, device_id_type=MESH)

        pl.semaphore_wait(barrier, jnp.where(self.depth > 0, len(near) + 1, len(near)))


def remote(src, dst, sems, k, device):
    return pltpu.make_async_remote_copy(
        src_ref=src,
        dst_ref=dst,
        send_sem=sems.at[0, k],
        recv_sem=sems.at[1, k],
        device_id=device,
        device_id_type=MESH,
    )


def add_into(dst, one, two):
    rows = dst.shape[0]
    step = 32 if rows % 32 == 0 else rows

    @pl.loop(0, rows // step)
    def _(i):
        spot = pl.ds(pl.multiple_of(i * step, step), step)
        total = one[spot, :].astype(jnp.float32) + two[spot, :].astype(jnp.float32)
        dst[spot, :] = total.astype(dst.dtype)


def skewed(count, stages):
    last = max(offset for offset, _ in stages)
    for tick in range(count + last):
        for offset, stage in sorted(stages, key=lambda item: -item[0]):
            if 0 <= tick - offset < count:
                stage(tick - offset)


def cut_chunks(shards):
    rows = min(shard.shape[0] for shard in shards)
    wide = min(shard.shape[1] for shard in shards)
    chunks = []
    for w, shard in enumerate(shards):
        for row0 in range(0, shard.shape[0], rows):
            for col0 in range(0, shard.shape[1], wide):
                chunks.append((w, row0, col0))
    return rows, wide, chunks


def reduce_kernel(n_rep, parts, chunks, shard_rows, rows, wide, *refs):
    count, n_w = len(chunks), len(shard_rows)
    sources, outs, arrived = refs[:n_w], refs[n_w : 2 * n_w], refs[2 * n_w]
    (
        held, lent, got_y, got_x, got_in, got_mid, total,
        own_in, lent_in, put, c0_sem, c1_sem, y_sem, x_sem, in_sem, mid_sem, back_sem,
        ax_sem, ac_sem, af_sem,
    ) = refs[2 * n_w + 1 :]
    c_sems = [c0_sem, c1_sem]
    at = Place(n_rep)
    half = at.half
    block = rows // 4
    with_y = parts == 2
    mine = at.y if with_y else 0

    def source(k, owner, c):
        w, row0, col0 = chunks[k]
        start = pl.multiple_of(owner * shard_rows[w] + row0 + c * 2 * block, 8)
        return sources[w].at[pl.ds(start, 2 * block), pl.ds(col0, wide)]

    def out(k, c, x):
        w, row0, col0 = chunks[k]
        start = pl.multiple_of(row0 + (c * 2 + x) * block, 8)
        return outs[w].at[pl.ds(start, block), pl.ds(col0, wide)]

    def rows_of(x):
        return pl.ds(pl.multiple_of(x * block, 8), block)

    def c_send(k, owner):
        return remote(
            source(k, owner, 1 - at.c), arrived.at[k, owner], c_sems[owner], k, at.to_core
        )

    def own_load(k, owner):
        return pltpu.make_async_copy(
            source(k, owner, at.c), held.at[k, owner], own_in.at[owner, k]
        )

    def lent_load(k, owner):
        return pltpu.make_async_copy(
            arrived.at[k, owner], lent.at[k % 2, owner], lent_in.at[owner, k]
        )

    def y_send(k):
        return remote(held.at[k, 1 - mine], got_y.at[k], y_sem, k, at.to_y)

    def x_send(k):
        return remote(
            held.at[k, mine, rows_of(1 - at.x)], got_x.at[k], x_sem, k, at.to_x
        )

    def part(k):
        return held.at[k, mine, rows_of(at.x)]

    def in_send(k):
        return remote(part(k), got_in.at[k], in_sem, k, at.to_in)

    def mid_send(k):
        return remote(part(k), got_mid.at[k], mid_sem, k, at.to_in)

    def back_send(k):
        return remote(total.at[k], total.at[k], back_sem, k, at.to_out)

    def ax_send(k, x):
        return remote(total.at[k], out(k, at.c, x), ax_sem, k, at.to_x)

    def ac_send(k, c):
        return remote(total.at[k], out(k, c, at.x), ac_sem, k, at.to_core)

    def af_send(k, c):
        view = out(k, c, 1 - at.x)
        return remote(view, view, af_sem, k, at.to_core)

    def own_put(k):
        return pltpu.make_async_copy(total.at[k], out(k, at.c, at.x), put.at[k])

    def start_core(k):
        for owner in range(parts):
            c_send(k, owner).start()
            own_load(k, owner).start()

    def load_core(k):
        for owner in range(parts):
            c_send(k, owner).wait_recv()
            lent_load(k, owner).start()

    def start_y(k):
        for owner in range(parts):
            own_load(k, owner).wait()
            lent_load(k, owner).wait()
        if with_y:
            other = 1 - mine
            add_into(held.at[k, other], held.at[k, other], lent.at[k % 2, other])
            y_send(k).start()
        add_into(held.at[k, mine], held.at[k, mine], lent.at[k % 2, mine])

    def start_x(k):
        if with_y:
            y_send(k).wait_recv()
            spot = rows_of(1 - at.x)
            add_into(held.at[k, mine, spot], held.at[k, mine, spot], got_y.at[k, spot])
        x_send(k).start()
        if with_y:
            add_into(part(k), part(k), got_y.at[k, rows_of(at.x)])

    def inner_send(k, depth):
        (mid_send(k) if depth == half - 1 else in_send(k)).start()

    def start_z(k):
        x_send(k).wait_recv()
        add_into(part(k), part(k), got_x.at[k])

        @at.at_depth(0)
        def _():
            inner_send(k, 0)

    def pass_in(depth):
        def stage(k):
            @at.at_depth(depth)
            def _():
                in_send(k).wait_recv()
                add_into(part(k), part(k), got_in.at[k])
                inner_send(k, depth)

        return stage

    def spread(k, depth):
        if depth > 0:
            back_send(k).start()
        ax_send(k, at.x).start()
        ac_send(k, at.c).start()
        own_put(k).start()

    def middle(k):
        @at.at_depth(half - 1)
        def _():
            mid_send(k).wait_recv()
            add_into(total.at[k], part(k), got_mid.at[k])
            spread(k, half - 1)

    def pass_out(depth):
        def stage(k):
            @at.at_depth(depth)
            def _():
                back_send(k).wait_recv()
                spread(k, depth)

        return stage

    def forward(k):
        ax_send(k, 1 - at.x).wait_recv()
        af_send(k, at.c).start()

    at.meet(with_y)
    stages = [(0, start_core), (1, load_core), (2, start_y), (4, start_x), (5, start_z)]
    stages += [(6 + depth - 1, pass_in(depth)) for depth in range(1, half)]
    stages += [(6 + half - 1, middle)]
    stages += [(6 + half + (half - 2 - depth), pass_out(depth)) for depth in range(half - 1)]
    stages += [(5 + 2 * half, forward)]
    skewed(count, stages)
    for k in range(count):
        for owner in range(parts):
            c_send(k, owner).wait_send()
        if with_y:
            y_send(k).wait_send()
        x_send(k).wait_send()
        for depth in range(half):

            @at.at_depth(depth)
            def _():
                (mid_send(k) if depth == half - 1 else in_send(k)).wait_send()
                if depth > 0:
                    back_send(k).wait_send()

        ax_send(k, at.x).wait_send()
        ac_send(k, at.c).wait_send()
        af_send(k, at.c).wait_send()
        own_put(k).wait()
        ac_send(k, 1 - at.c).wait_recv()
        af_send(k, 1 - at.c).wait_recv()


def reduce_products(products, n_rep, n_shard):
    parts = n_shard
    if n_shard != 2:
        products = [
            lax.psum_scatter(item, "shard", scatter_dimension=0, tiled=True) for item in products
        ]
        parts = 1
    owned = [
        jax.ShapeDtypeStruct((item.shape[0] // parts, item.shape[1]), jnp.bfloat16)
        for item in products
    ]
    rows, wide, chunks = cut_chunks(owned)
    count, block = len(chunks), rows // 4
    kernel = partial(
        reduce_kernel, n_rep, parts, chunks, [item.shape[0] for item in owned], rows, wide
    )
    pair = pltpu.SemaphoreType.DMA((2, count))
    low = jnp.bfloat16
    anywhere = pl.BlockSpec(memory_space=pl.ANY)
    results = pl.pallas_call(
        kernel,
        out_shape=owned + [jax.ShapeDtypeStruct((count, parts, 2 * block, wide), low)],
        in_specs=[anywhere] * len(products),
        out_specs=[anywhere] * (len(products) + 1),
        scratch_shapes=[
            pltpu.VMEM((count, parts, 2 * block, wide), low),
            pltpu.VMEM((2, parts, 2 * block, wide), low),
            pltpu.VMEM((count, 2 * block, wide), low),
            pltpu.VMEM((count, block, wide), low),
            pltpu.VMEM((count, block, wide), low),
            pltpu.VMEM((count, block, wide), low),
            pltpu.VMEM((count, block, wide), low),
            pltpu.SemaphoreType.DMA((parts, count)),
            pltpu.SemaphoreType.DMA((parts, count)),
            pltpu.SemaphoreType.DMA((count,)),
        ]
        + [pair] * 10,
        compiler_params=pltpu.CompilerParams(
            collective_id=1, has_side_effects=True, vmem_limit_bytes=62 << 20
        ),
        name="reduce_products",
    )(*products)
    return results[:-1]


class Cuts:
    def __init__(self, sizes, n_shard):
        self.shard_rows = [left // n_shard for left, _ in sizes]
        self.rows = min(self.shard_rows) // 2
        self.wide = min(right for _, right in sizes)
        self.down = [rows // self.rows for rows in self.shard_rows]
        self.across = [right // self.wide for _, right in sizes]
        self.first = [0]
        for down, across in zip(self.down, self.across):
            self.first.append(self.first[-1] + down * across)
        self.count = self.first[-1]

    def weight_of(self, k, act):
        for w, down in enumerate(self.down):

            @pl.when((k >= self.first[w]) & (k < self.first[w + 1]))
            def _():
                inside = k - self.first[w]
                act(w, inside % down, inside // down)

    def whole(self, chunks, w):
        first, down, rows, wide = self.first[w], self.down[w], self.rows, self.wide

        def widen(part, dst):
            dst[...] = part[0].astype(jnp.float32)

        return pl.pallas_call(
            widen,
            grid=(down, self.across[w]),
            in_specs=[pl.BlockSpec((1, rows, wide), lambda i, j: (first + j * down + i, 0, 0))],
            out_specs=pl.BlockSpec((rows, wide), lambda i, j: (i, j)),
            out_shape=jax.ShapeDtypeStruct(
                (self.shard_rows[w], self.across[w] * wide), jnp.float32
            ),
            compiler_params=pltpu.CompilerParams(vmem_limit_bytes=24 << 20),
            cost_estimate=pl.CostEstimate(
                flops=0,
                transcendentals=0,
                bytes_accessed=6 * down * self.across[w] * rows * wide,
            ),
            name="widen",
        )(chunks)


def backward_kernel(n_rep, cuts, n_heads, slots, score_scale, *refs):
    (
        left_0, left_1, left_2, left_3, right_0, right_1, right_2, qkv, w_qkv,
        grad_heads, log_total, pic_key, pic_query, cosine, sine,
        out, grad_qkv, grad_first, lent_left, lent_right,
        op_left, op_right, held, got_y, got_x, got_in, got_mid, total, swap, w_block,
        load_l, load_r, put, qkv_sem, block_sem,
        l0_sem, l1_sem, r_sem, y_sem, x_sem, in_sem, mid_sem, back_sem, ax_sem, ac_sem, af_sem,
    ) = refs
    lefts = [left_0, left_1, left_2, left_3]
    rights = [right_0, right_1, right_2, grad_qkv]
    l_sems = [l0_sem, l1_sem]
    at = Place(n_rep)
    half = at.half
    count, rows, wide = cuts.count, cuts.rows, cuts.wide
    block, width = rows // 2, wide // 2
    mine = at.y
    head = qkv.shape[0] // (3 * n_heads)
    model = n_heads * head

    def left_rows(w, row, owner):
        start = owner * cuts.shard_rows[w] + row * rows
        return lefts[w].at[pl.ds(pl.multiple_of(start, 16), rows), :]

    def right_rows(w, col, c):
        start = col * wide + c * width
        return rights[w].at[pl.ds(pl.multiple_of(start, 16), width), :]

    def left_push(k, owner, src):
        return remote(src, lent_left.at[k, owner], l_sems[owner], k, at.to_core)

    def right_push(k, src):
        return remote(src, lent_right.at[k], r_sem, k, at.to_core)

    def left_load(k, whose, owner, src):
        slot = k % 2
        return pltpu.make_async_copy(
            src, op_left.at[slot, whose, owner], load_l.at[whose, owner, k]
        )

    def right_load(k, whose, src):
        return pltpu.make_async_copy(src, op_right.at[k % 2, whose], load_r.at[whose, k])

    def rows_of(x):
        return pl.ds(pl.multiple_of(x * block, 16), block)

    def mine_of(k, x):
        return held.at[k % slots, mine, rows_of(x)]

    def y_send(k):
        return remote(held.at[k % slots, 1 - mine], got_y.at[k], y_sem, k, at.to_y)

    def x_send(k):
        return remote(mine_of(k, 1 - at.x), got_x.at[k], x_sem, k, at.to_x)

    def in_send(k):
        return remote(mine_of(k, at.x), got_in.at[k], in_sem, k, at.to_in)

    def mid_send(k):
        return remote(mine_of(k, at.x), got_mid.at[k], mid_sem, k, at.to_in)

    def back_send(k):
        return remote(total.at[k], total.at[k], back_sem, k, at.to_out)

    def out_of(k, c, x):
        cols = pl.ds(pl.multiple_of(c * width, 128), width)
        return out.at[k, rows_of(x), cols]

    def ax_send(k, x):
        return remote(total.at[k], out_of(k, at.c, x), ax_sem, k, at.to_x)

    def ac_send(k, c):
        return remote(total.at[k], out_of(k, c, at.x), ac_sem, k, at.to_core)

    def af_send(k, c):
        view = out_of(k, c, 1 - at.x)
        return remote(view, view, af_sem, k, at.to_core)

    def own_put(k):
        return pltpu.make_async_copy(total.at[k], out_of(k, at.c, at.x), put.at[k])

    def push(k):
        def act(w, row, col):
            for owner in range(2):
                left_push(k, owner, left_rows(w, row, owner)).start()
            right_push(k, right_rows(w, col, 1 - at.c)).start()

        cuts.weight_of(k, act)

    def load(k):
        def act(w, row, col):
            for owner in range(2):
                left_load(k, 0, owner, left_rows(w, row, owner)).start()
            right_load(k, 0, right_rows(w, col, at.c)).start()

        cuts.weight_of(k, act)
        for owner in range(2):
            left_push(k, owner, lent_left.at[k, owner]).wait_recv()
            left_load(k, 1, owner, lent_left.at[k, owner]).start()
        right_push(k, lent_right.at[k]).wait_recv()
        right_load(k, 1, lent_right.at[k]).start()

    def product(k):
        slot = k % 2
        for whose in range(2):
            for owner in range(2):
                left_load(k, whose, owner, lent_left.at[k, owner]).wait()
            right_load(k, whose, lent_right.at[k]).wait()
        for owner in range(2):
            left_push(k, owner, lent_left.at[k, owner]).wait_send()
        right_push(k, lent_right.at[k]).wait_send()
        for owner in (1 - mine, mine):
            result = contract(op_left[slot, 0, owner], op_right[slot, 0], 1, 1)
            result += contract(op_left[slot, 1, owner], op_right[slot, 1], 1, 1)
            held[k % slots, owner] = result.astype(jnp.bfloat16)
            if owner is not mine:
                y_send(k).start()

    def start_x(k):
        y_send(k).wait_recv()
        other = mine_of(k, 1 - at.x)
        add_into(other, other, got_y.at[k, rows_of(1 - at.x)])
        x_send(k).start()
        own = mine_of(k, at.x)
        add_into(own, own, got_y.at[k, rows_of(at.x)])
        y_send(k).wait_send()

    def inner_send(k, depth):
        return mid_send(k) if depth == half - 1 else in_send(k)

    def start_z(k):
        x_send(k).wait_recv()
        own = mine_of(k, at.x)
        add_into(own, own, got_x.at[k])

        @at.at_depth(0)
        def _():
            inner_send(k, 0).start()

        x_send(k).wait_send()

    def pass_in(depth):
        def stage(k):
            @at.at_depth(depth)
            def _():
                in_send(k).wait_recv()
                own = mine_of(k, at.x)
                add_into(own, own, got_in.at[k])
                inner_send(k, depth).start()

        return stage

    def spread(k, depth):
        if depth > 0:
            back_send(k).start()
        ax_send(k, at.x).start()
        ac_send(k, at.c).start()
        own_put(k).start()

    def middle(k):
        @at.at_depth(half - 1)
        def _():
            mid_send(k).wait_recv()
            add_into(total.at[k], mine_of(k, at.x), got_mid.at[k])
            spread(k, half - 1)

    def pass_out(depth):
        def stage(k):
            @at.at_depth(depth)
            def _():
                back_send(k).wait_recv()
                spread(k, depth)

        return stage

    def sent(k):
        for depth in range(half):

            @at.at_depth(depth)
            def _():
                inner_send(k, depth).wait_send()

    def forward(k):
        ax_send(k, 1 - at.x).wait_recv()
        af_send(k, at.c).start()

    def finish(k):
        @pl.when(at.depth > 0)
        def _():
            back_send(k).wait_send()

        ax_send(k, at.x).wait_send()
        ac_send(k, at.c).wait_send()
        af_send(k, at.c).wait_send()
        own_put(k).wait()
        ac_send(k, 1 - at.c).wait_recv()
        af_send(k, 1 - at.c).wait_recv()

    def head_step(h):
        def part(i):
            return pl.ds(pl.multiple_of(i * model + h * head, 16), head)

        query, key, value = swap[part(0), :], swap[part(1), :], swap[part(2), :]
        grads = head_back(
            query,
            key,
            value,
            grad_heads[part(0), :],
            pic_key[...] == pic_query[...],
            log_total[pl.ds(h, 1), :],
            score_scale,
        )
        grad_query, grad_key, grad_value = grads
        turn_c, turn_s = cosine[...], sine[...]
        swap[part(0), :] = rotary_back(grad_query, turn_c, turn_s).astype(jnp.bfloat16)
        swap[part(1), :] = rotary_back(grad_key, turn_c, turn_s).astype(jnp.bfloat16)
        swap[part(2), :] = grad_value.astype(jnp.bfloat16)

    def block_load(j):
        cols = pl.ds(pl.multiple_of(j * width, 128), width)
        return pltpu.make_async_copy(w_qkv.at[:, cols], w_block.at[j % 2], block_sem.at[j])

    def first_step(j):
        block_load(j).wait()
        inside = pl.ds(pl.multiple_of(j * width, 16), width)
        step = 256

        @pl.loop(0, model // step)
        def _(i):
            spot = pl.ds(pl.multiple_of(i * step, 16), step)
            grad_first[spot, :] += contract(w_block[j % 2, spot, :], swap[inside, :], 1, 0)

    n_blocks = qkv.shape[0] // width
    take_qkv = pltpu.make_async_copy(qkv, swap, qkv_sem.at[0])
    give_qkv = pltpu.make_async_copy(swap, grad_qkv, qkv_sem.at[1])
    take_qkv.start()
    at.meet(True)
    grad_first[...] = jnp.zeros_like(grad_first)
    take_qkv.wait()
    stages = [(0, push), (1, load), (2, product), (4, start_x), (6, start_z)]
    stages += [(6 + depth, pass_in(depth)) for depth in range(1, half)]
    stages += [(6 + half, middle)]
    stages += [(6 + half + (half - 1 - depth), pass_out(depth)) for depth in range(half - 1)]
    stages += [(slots + 2, sent), (7 + 2 * half, forward), (9 + 2 * half, finish)]
    stages.sort(key=lambda item: -item[0])
    per_tick = -(-n_heads // (cuts.first[3] - 2))
    done = -(-n_heads // per_tick)

    def tick_body(tick, carry):
        for offset, stage in stages:

            @pl.when((tick >= offset) & (tick < count + offset))
            def _():
                stage(tick - offset)

        @pl.when(tick < done)
        def _():
            @pl.loop(0, per_tick)
            def _(i):
                head_step(tick * per_tick + i)

        @pl.when(tick == done)
        def _():
            give_qkv.start()
            give_qkv.wait()

        @pl.when((tick > done) & (tick <= done + n_blocks))
        def _():
            first_step(tick - done - 1)

        @pl.when((tick >= done) & (tick < done + n_blocks))
        def _():
            block_load(tick - done).start()

        return carry

    lax.fori_loop(0, count + 9 + 2 * half, tick_body, 0)


def reduce_backward(lefts, rights, qkv, w_qkv, small, n_rep, n_heads, score_scale):
    tokens = qkv.shape[1]
    sizes = [(left.shape[0], right.shape[0]) for left, right in zip(lefts, rights + [qkv])]
    cuts = Cuts(sizes, 2)
    half = n_rep // 8
    slots = 3 + 2 * half
    count, rows, wide = cuts.count, cuts.rows, cuts.wide
    block, width = rows // 2, wide // 2
    low, dma = jnp.bfloat16, pltpu.SemaphoreType.DMA
    anywhere, local = pl.BlockSpec(memory_space=pl.ANY), pl.BlockSpec(memory_space=pltpu.VMEM)
    model = w_qkv.shape[0]
    chunks, grad_qkv, grad_first, _, _ = pl.pallas_call(
        partial(backward_kernel, n_rep, cuts, n_heads, slots, score_scale),
        out_shape=[
            jax.ShapeDtypeStruct((count, rows, wide), low),
            jax.ShapeDtypeStruct(qkv.shape, low),
            jax.ShapeDtypeStruct((model, tokens), jnp.float32),
            jax.ShapeDtypeStruct((count, 2, rows, tokens), low),
            jax.ShapeDtypeStruct((count, width, tokens), low),
        ],
        in_specs=[anywhere] * 9 + [local] * len(small),
        out_specs=[anywhere, anywhere, local, anywhere, anywhere],
        scratch_shapes=[
            pltpu.VMEM((2, 2, 2, rows, tokens), low),
            pltpu.VMEM((2, 2, width, tokens), low),
            pltpu.VMEM((slots, 2, rows, width), low),
            pltpu.VMEM((count, rows, width), low),
            pltpu.VMEM((count, block, width), low),
            pltpu.VMEM((count, block, width), low),
            pltpu.VMEM((count, block, width), low),
            pltpu.VMEM((count, block, width), low),
            pltpu.VMEM(qkv.shape, low),
            pltpu.VMEM((2, model, width), low),
            dma((2, 2, count)),
            dma((2, count)),
            dma((count,)),
            dma((2,)),
            dma((qkv.shape[0] // width,)),
        ]
        + [dma((2, count))] * 11,
        compiler_params=pltpu.CompilerParams(
            collective_id=1, has_side_effects=True, vmem_limit_bytes=63 << 20
        ),
        name="reduce_backward",
    )(*lefts, *rights, qkv, w_qkv, *small)
    return [cuts.whole(chunks, w) for w in range(len(sizes))], grad_qkv, grad_first


def forward_kernel(n_rep, cuts, n_heads, score_scale, *refs):
    n_w = len(cuts.down)
    shards, refs = refs[:n_w], refs[n_w:]
    (
        normed, patches, cotangent, qkv_bias, proj_bias, gain, bias, up_bias, down_bias,
        pic_key, pic_query, cosine, sine,
    ) = refs[:13]
    fulls, refs = refs[13 : 13 + n_w], refs[13 + n_w :]
    (
        swap, heads_out, log_total, hidden, normed_two, act_turned, pre_turned, layer_out,
        hold, w_block, turned, up_pre, act, out_sum,
        own_in, own_out, w_sem, y_sem, d_sem, in_sem, mid_sem, back_sem, x_sem, c_sem, cd_sem,
    ) = refs
    at = Place(n_rep)
    nz, half = at.nz, at.half
    count, rows, wide = cuts.count, cuts.rows, cuts.wide
    plane = rows * 4 // 5
    unit = plane // n_rep
    straight = (rows - plane) // 2
    mine, yours = at.y, 1 - at.y
    model = normed.shape[1]
    tokens = normed.shape[0]
    head = model // n_heads

    def shard(w, row, col, first, size):
        start = pl.multiple_of(row * rows + first, 16)
        cols = pl.ds(pl.multiple_of(col * wide, 128), wide)
        return shards[w].at[pl.ds(start, size), cols]

    def full(w, row, col, owner, first, size):
        start = pl.multiple_of(owner * cuts.shard_rows[w] + row * rows + first, 16)
        cols = pl.ds(pl.multiple_of(col * wide, 128), wide)
        return fulls[w].at[pl.ds(start, size), cols]

    def alike(size):
        return fulls[0].at[pl.ds(0, size), pl.ds(0, wide)]

    def place(c, x, z):
        return ((c * 2 + x) * nz + z) * unit

    def spread_copy(k, first, size, sems, device):
        def act_on(w, row, col):
            view = full(w, row, col, yours, first, size)
            remote(view, view, sems, k, device).start()

        cuts.weight_of(k, act_on)

    def settle(k, size, sems, device, received):
        view = alike(size)
        copy = remote(view, view, sems, k, device)
        if received:
            copy.wait_recv()
        else:
            copy.wait_send()

    def along(k, begin, size, sems, device):
        spread_copy(k, place(at.c, at.x, begin), size * unit, sems, device)

    def start_y(k):
        def act_on(w, row, col):
            first = place(at.c, at.x, at.z)
            remote(
                shard(w, row, col, first, unit),
                full(w, row, col, mine, first, unit),
                y_sem, k, at.to_y,
            ).start()
            first = plane + at.c * straight
            remote(
                shard(w, row, col, first, straight),
                full(w, row, col, mine, first, straight),
                d_sem, k, at.to_y,
            ).start()

        cuts.weight_of(k, act_on)

    def inner_send(k, depth):
        if depth == half - 1:
            along(k, jnp.where(at.low, 0, half), half, mid_sem, at.to_in)
        else:
            along(k, jnp.where(at.low, 0, nz - 1 - depth), depth + 1, in_sem, at.to_in)

    def back_start(k, depth):
        along(k, jnp.where(at.low, depth, 0), nz - depth, back_sem, at.to_out)

    def x_start(k):
        along(k, 0, nz, x_sem, at.to_x)

    def crossed(k):
        settle(k, unit, y_sem, at.to_y, True)

        @at.at_depth(0)
        def _():
            inner_send(k, 0)

        settle(k, straight, d_sem, at.to_y, True)
        spread_copy(k, plane + at.c * straight, straight, cd_sem, at.to_core)

    def pass_in(depth):
        def stage(k):
            @at.at_depth(depth)
            def _():
                settle(k, depth * unit, in_sem, at.to_in, True)
                inner_send(k, depth)

        return stage

    def middle(k):
        @at.at_depth(half - 1)
        def _():
            settle(k, half * unit, mid_sem, at.to_in, True)
            if half > 1:
                back_start(k, half - 1)
            x_start(k)

    def pass_out(depth):
        def stage(k):
            @at.at_depth(depth)
            def _():
                settle(k, (nz - depth - 1) * unit, back_sem, at.to_out, True)
                if depth > 0:
                    back_start(k, depth)
                x_start(k)

        return stage

    def crossed_x(k):
        settle(k, nz * unit, x_sem, at.to_x, True)
        spread_copy(k, place(at.c, 0, 0), 2 * nz * unit, c_sem, at.to_core)

    def own_load(k, view):
        return pltpu.make_async_copy(view, hold.at[k % 3], own_in.at[k])

    def own_store(k, view):
        return pltpu.make_async_copy(hold.at[k % 3], view, own_out.at[k])

    def take_own(k):
        cuts.weight_of(k, lambda w, row, col: own_load(k, shard(w, row, col, 0, rows)).start())

    def give_own(k):
        own_load(k, alike(rows)).wait()
        cuts.weight_of(
            k, lambda w, row, col: own_store(k, full(w, row, col, mine, 0, rows)).start()
        )

    def arrived(k):
        own_store(k, alike(rows)).wait()
        settle(k, 2 * nz * unit, c_sem, at.to_core, True)
        settle(k, straight, cd_sem, at.to_core, True)
        settle(k, unit, y_sem, at.to_y, False)
        settle(k, straight, d_sem, at.to_y, False)
        settle(k, nz * unit, x_sem, at.to_x, False)
        settle(k, 2 * nz * unit, c_sem, at.to_core, False)
        settle(k, straight, cd_sem, at.to_core, False)
        for depth in range(half):

            @at.at_depth(depth)
            def _():
                if depth == half - 1:
                    settle(k, half * unit, mid_sem, at.to_in, False)
                else:
                    settle(k, (depth + 1) * unit, in_sem, at.to_in, False)
                if depth > 0:
                    settle(k, (nz - depth) * unit, back_sem, at.to_out, False)

    def block_of(u, view):
        return pltpu.make_async_copy(view, w_block.at[u % 2], w_sem.at[0, u])

    def half_block(u, owner, view):
        spot = pl.ds(owner * (wide // 2), wide // 2)
        return pltpu.make_async_copy(view, w_block.at[u % 2, spot, :], w_sem.at[owner, u])

    def columns(w, col):
        return fulls[w].at[:, pl.ds(pl.multiple_of(col * wide, 128), wide)]

    def down_rows(i, owner):
        start = owner * cuts.shard_rows[3] + i * (wide // 2)
        return fulls[3].at[pl.ds(pl.multiple_of(start, 16), wide // 2), :]

    step = 256

    def qkv_step(b, u):
        block_of(u, columns(0, 0)).wait()

        @pl.loop(0, wide // step)
        def _(i):
            spot = pl.ds(pl.multiple_of(i * step, 128), step)
            col = pl.ds(pl.multiple_of(b * wide + i * step, 128), step)
            part = contract(normed[...], w_block[u % 2, :, spot], 1, 0) + qkv_bias[:, col]
            turned[pl.ds(pl.multiple_of(i * step, 16), step), :] = part.T

        @pl.loop(0, n_heads)
        def _(h):
            part = turned[pl.ds(pl.multiple_of(h * head, 8), head), :]
            spot = pl.ds(pl.multiple_of(b * model + h * head, 16), head)

            @pl.when(b < 2)
            def _():
                swap[spot, :] = apply_rotary(part, cosine[...], sine[...]).astype(jnp.bfloat16)

            @pl.when(b == 2)
            def _():
                swap[spot, :] = part.astype(jnp.bfloat16)

    def head_step(h):
        def part(i):
            return swap[pl.ds(pl.multiple_of(i * model + h * head, 16), head), :]

        scores = contract(part(1), part(0), 0, 0) * score_scale
        scores = jnp.where(pic_key[...] == pic_query[...], scores, -1000000000.0)
        top = jnp.max(scores, axis=0, keepdims=True)
        exp_scores = jnp.exp(scores - top)
        total = jnp.sum(exp_scores, axis=0, keepdims=True)
        probs = (exp_scores / total).astype(jnp.bfloat16)
        attended = contract(part(2), probs, 1, 0)
        heads_out[pl.ds(pl.multiple_of(h * head, 16), head), :] = attended.astype(jnp.bfloat16)
        log_total[pl.ds(h, 1), :] = top + jnp.log(total)

    def proj_step(u):
        block_of(u, columns(0, 0)).wait()

        @pl.loop(0, tokens // step)
        def _(i):
            spot = pl.ds(pl.multiple_of(i * step, 16), step)
            lanes = pl.ds(pl.multiple_of(i * step, 128), step)
            branch = contract(heads_out[:, lanes], w_block[u % 2], 0, 0)
            rows_in = patches[spot, :].astype(jnp.float32) + branch + proj_bias[...]
            hidden[spot, :] = rows_in
            out_sum[spot, :] = rows_in + down_bias[...]
            standard, _ = apply_layer_norm(rows_in)
            normed_two[spot, :] = (standard * gain[...] + bias[...]).astype(jnp.bfloat16)

    def up_step(c, u):
        block_of(u, columns(0, 0)).wait()

        @pl.loop(0, wide // step)
        def _(i):
            spot = pl.ds(pl.multiple_of(i * step, 128), step)
            col = pl.multiple_of(c * wide + i * step, 128)
            cols = pl.ds(col, step)
            pre = contract(normed_two[...], w_block[u % 2, :, spot], 1, 0) + up_bias[:, cols]
            up_pre[:, cols] = pre
            result = (pre / (1.0 + jnp.exp(-quick_slope * pre))).astype(jnp.bfloat16)
            act[:, cols] = result
            act_turned[pl.ds(col, step), :] = result.T

    def down_step(i, u):
        for owner in range(2):
            half_block(u, owner, down_rows(0, 0)).wait()
            size = wide // 2
            col = pl.multiple_of(owner * cuts.shard_rows[3] + i * size, 128)

            @pl.loop(0, tokens // step)
            def _(j):
                spot = pl.ds(pl.multiple_of(j * step, 16), step)
                lanes = pl.ds(pl.multiple_of(j * step, 128), step)
                weight = w_block[u % 2, pl.ds(owner * size, size), :]
                pre = up_pre[spot, pl.ds(col, size)]
                sigmoid = 1.0 / (1.0 + jnp.exp(-quick_slope * pre))
                slope = sigmoid + quick_slope * pre * sigmoid * (1.0 - sigmoid)
                grad = contract(cotangent[spot, :], weight, 1, 1) * slope
                pre_turned[pl.ds(col, size), lanes] = grad.astype(jnp.bfloat16).T
                out_sum[spot, :] += contract(act[spot, pl.ds(col, size)], weight, 1, 0)

    offset = 2 * half + 2
    stages = [(1, crossed)]
    stages += [(1 + depth, pass_in(depth)) for depth in range(1, half)]
    stages += [(1 + half, middle)]
    stages += [(1 + half + (half - 1 - depth), pass_out(depth)) for depth in range(half - 1)]
    stages += [(2 * half + 1, crossed_x)]
    stages += [(offset - 2, take_own), (offset - 1, give_own), (offset, arrived)]
    stages.sort(key=lambda item: -item[0])
    n_up, n_down = cuts.across[2], cuts.down[3] // 2
    per_tick = 3
    first_head = cuts.first[1] + 1
    at_proj = first_head + -(-n_heads // per_tick)
    at_up = at_proj + 1
    at_down = max(at_up + n_up, cuts.first[3] + 2)
    n_steps = 4 + n_up + n_down

    at.meet(True)

    @pl.loop(0, count)
    def _(k):
        start_y(k)

    def tick_body(tick, carry):
        for lag, stage in stages:

            @pl.when((tick >= lag) & (tick < count + lag))
            def _():
                stage(tick - lag)

        now = tick - offset

        @pl.when((now >= 2) & (now < first_head) & (now % 2 == 0))
        def _():
            qkv_step(now // 2 - 1, now // 2 - 1)

        @pl.when((now >= first_head) & (now < at_proj))
        def _():
            @pl.loop(0, per_tick)
            def _(i):
                h = (now - first_head) * per_tick + i

                @pl.when(h < n_heads)
                def _():
                    head_step(h)

        @pl.when(now == at_proj)
        def _():
            proj_step(3)

        @pl.when((now >= at_up) & (now < at_up + n_up))
        def _():
            up_step(now - at_up, now - at_up + 4)

        down_i = (now - at_down) // 2

        @pl.when((now >= at_down) & (down_i < n_down) & ((now - at_down) % 2 == 0))
        def _():
            down_step(down_i, down_i + 4 + n_up)

        soon = now + 1

        @pl.when((soon >= 2) & (soon < first_head) & (soon % 2 == 0))
        def _():
            block_of(soon // 2 - 1, columns(0, soon // 2 - 1)).start()

        @pl.when(soon == at_proj)
        def _():
            block_of(3, columns(1, 0)).start()

        @pl.when((soon >= at_up) & (soon < at_up + n_up))
        def _():
            block_of(soon - at_up + 4, columns(2, soon - at_up)).start()

        next_i = (soon - at_down) // 2

        @pl.when((soon >= at_down) & (next_i < n_down) & ((soon - at_down) % 2 == 0))
        def _():
            for owner in range(2):
                half_block(next_i + 4 + n_up, owner, down_rows(next_i, owner)).start()

        return carry

    lax.fori_loop(0, offset + at_down + 2 * n_down - 1, tick_body, 0)
    layer_out[...] = out_sum[...].astype(jnp.bfloat16)


def gather_forward(shards, inputs, n_rep, n_heads, score_scale):
    cuts = Cuts([(shard.shape[0] * 2, shard.shape[1]) for shard in shards], 2)
    tokens, model = inputs[0].shape
    wide_two = shards[2].shape[1]
    count, rows, wide = cuts.count, cuts.rows, cuts.wide
    low, dma = jnp.bfloat16, pltpu.SemaphoreType.DMA
    anywhere, local = pl.BlockSpec(memory_space=pl.ANY), pl.BlockSpec(memory_space=pltpu.VMEM)
    n_steps = 4 + cuts.across[2] + cuts.down[3] // 2

    def shape(*sizes, kind=low):
        return jax.ShapeDtypeStruct(sizes, kind)

    results = pl.pallas_call(
        partial(forward_kernel, n_rep, cuts, n_heads, score_scale),
        out_shape=[shape(item.shape[0] * 2, item.shape[1]) for item in shards]
        + [
            shape(3 * model, tokens),
            shape(model, tokens),
            shape(n_heads, tokens, kind=jnp.float32),
            shape(tokens, model, kind=jnp.float32),
            shape(tokens, model),
            shape(wide_two, tokens),
            shape(wide_two, tokens),
            shape(tokens, model),
        ],
        in_specs=[anywhere] * len(shards) + [local] * len(inputs),
        out_specs=[anywhere] * len(shards) + [local] * 8,
        scratch_shapes=[
            pltpu.VMEM((3, rows, wide), low),
            pltpu.VMEM((2, model, wide), low),
            pltpu.VMEM((model, tokens), jnp.float32),
            pltpu.VMEM((tokens, wide_two), jnp.float32),
            pltpu.VMEM((tokens, wide_two), low),
            pltpu.VMEM((tokens, model), jnp.float32),
            dma((count,)),
            dma((count,)),
            dma((2, n_steps)),
        ]
        + [dma((2, count))] * 8,
        compiler_params=pltpu.CompilerParams(
            collective_id=0, has_side_effects=True, vmem_limit_bytes=63 << 20
        ),
        name="gather_forward",
    )(*shards, *inputs)
    return results[: len(shards)], results[len(shards) :]


class Links:
    def __init__(self, n_rep, n_shard):
        self.nz, self.ny, self.n_rep = n_rep // 4, n_shard, n_rep
        self.y = lax.axis_index("shard")

    def gather_vector(self, vector):
        if self.ny != 2:
            return lax.all_gather(vector, "shard", axis=0, tiled=False)
        other = lax.ppermute(vector, "shard", [(0, 1), (1, 0)])
        low, high = jnp.where(self.y == 0, vector, other), jnp.where(self.y == 0, other, vector)
        return jnp.stack([low, high])

    def sum_all(self, vector):
        for flip in (1, 2):
            vector = vector + lax.ppermute(
                vector, "rep", [(i, i ^ flip) for i in range(self.n_rep)]
            )
        step = 1
        while step < self.nz:
            pairs = [(i, i ^ (4 * step)) for i in range(self.n_rep)]
            vector = vector + lax.ppermute(vector, "rep", pairs)
            step *= 2
        step = 1
        while step < self.ny:
            pairs = [(i, i ^ step) for i in range(self.ny)]
            vector = vector + lax.ppermute(vector, "shard", pairs)
            step *= 2
        return vector


def per_device(
    patches,
    lengths,
    positions,
    ln1_gain,
    ln1_bias,
    qkv_weight,
    qkv_bias,
    proj_weight,
    proj_bias,
    ln2_gain,
    ln2_bias,
    fc1_weight,
    fc1_bias,
    fc2_weight,
    fc2_bias,
    cotangent,
    n_rep,
    n_shard,
):
    links = Links(n_rep, n_shard)
    pack_count = lengths.shape[0]
    row_count = patches.shape[0]
    length = row_count // pack_count
    model_width = patches.shape[1]
    head_count = HEADS
    head_size = model_width // head_count
    score_scale = head_size ** (-0.5)
    pic_ends = jnp.cumsum(lengths[:, :-1], axis=1)
    slot_index = jnp.arange(length, dtype=jnp.int32)
    idents = jnp.sum((slot_index[None, :, None] >= pic_ends[:, None, :]).astype(jnp.int32), axis=2)
    pack_index = jnp.arange(pack_count, dtype=jnp.int32)
    idents = (idents + pack_index[:, None] * lengths.shape[1]).reshape(-1)
    cosine, sine = rotary_tables(positions, head_size)

    small = [ln1_gain, ln1_bias, qkv_bias, proj_bias, ln2_gain, ln2_bias, fc1_bias, fc2_bias]
    sizes = [item.shape[0] for item in small]
    spots = [sum(sizes[:i]) for i in range(len(sizes) + 1)]
    packed = sum(
        jnp.pad(item, (spots[i], spots[-1] - spots[i + 1])) for i, item in enumerate(small)
    )
    gathered = links.gather_vector(packed)
    (
        first_norm_gain, first_norm_bias, b_qkv, b_proj,
        second_norm_gain, second_norm_bias, b_up, b_down,
    ) = [
        gathered[:, spots[i] : spots[i + 1]].reshape(-1).astype(jnp.float32)
        for i in range(len(sizes))
    ]

    input_rows = patches.astype(jnp.float32)
    first_centered_standard, first_inverse_spread = apply_layer_norm(input_rows)
    first_normalized = (first_centered_standard * first_norm_gain + first_norm_bias).astype(
        jnp.bfloat16
    )
    shards = [qkv_weight, proj_weight, fc1_weight, fc2_weight]
    qkv_shape = (3 * model_width, row_count)
    grad_out = cotangent.astype(jnp.float32)
    d_b_down = jnp.sum(grad_out, axis=0)
    if n_shard == 2:
        rows_in = [
            item[None, :]
            for item in (b_qkv, b_proj, second_norm_gain, second_norm_bias, b_up, b_down)
        ]
        inputs = [first_normalized, patches, cotangent] + rows_in
        inputs += [idents[:, None], idents[None, :], cosine, sine]
        weights, results = gather_forward(shards, inputs, n_rep, head_count, score_scale)
        w_qkv, w_proj, w_up, w_down = weights
        qkv, heads_out, log_total, hidden_rows, second_normalized = results[:5]
        activation, grad_pre, layer_out = results[5:]
        second_centered_standard, second_inverse_spread = apply_layer_norm(hidden_rows)
    else:
        w_qkv, w_proj, w_up, w_down = [
            lax.all_gather(shard, "shard", axis=0, tiled=True) for shard in shards
        ]
        qkv_rows = contract(w_qkv, first_normalized, 0, 1) + b_qkv[:, None]
        qkv_rows = qkv_rows.reshape(3, head_count, head_size, row_count)
        queries = apply_rotary(qkv_rows[0], cosine, sine).astype(jnp.bfloat16)
        keys_rot = apply_rotary(qkv_rows[1], cosine, sine).astype(jnp.bfloat16)
        values_all = qkv_rows[2].astype(jnp.bfloat16)
        attended, log_total = attend(queries, keys_rot, values_all, idents, score_scale)
        heads_out = attended.reshape(model_width, row_count).astype(jnp.bfloat16)
        hidden_rows = input_rows + contract(heads_out, w_proj, 0, 0) + b_proj
        second_centered_standard, second_inverse_spread = apply_layer_norm(hidden_rows)
        second_normalized = (
            second_centered_standard * second_norm_gain + second_norm_bias
        ).astype(jnp.bfloat16)
        up_pre = contract(w_up, second_normalized, 0, 1) + b_up[:, None]
        sigmoid_up = 1.0 / (1.0 + jnp.exp(-quick_slope * up_pre))
        activation = (up_pre * sigmoid_up).astype(jnp.bfloat16)
        out_full = hidden_rows + contract(activation, w_down, 0, 0) + b_down
        layer_out = out_full.astype(jnp.bfloat16)
        grad_act = contract(w_down, cotangent, 1, 1)
        slope_up = sigmoid_up + quick_slope * up_pre * sigmoid_up * (1.0 - sigmoid_up)
        grad_pre = (grad_act * slope_up).astype(jnp.bfloat16)
    d_b_up = jnp.sum(grad_pre.astype(jnp.float32), axis=1)
    second_normalized_gradient = contract(grad_pre, w_up, 0, 1)
    second_gain_gradient = jnp.sum(second_normalized_gradient * second_centered_standard, axis=0)
    d_bias_two = jnp.sum(second_normalized_gradient, axis=0)
    grad_hidden = grad_out + norm_gradient_step(
        second_normalized_gradient,
        second_centered_standard,
        second_inverse_spread,
        second_norm_gain,
    )
    grad_branch = grad_hidden.astype(jnp.bfloat16)
    d_b_proj = jnp.sum(grad_branch.astype(jnp.float32), axis=0)
    grad_heads = contract(w_proj, grad_branch, 1, 1).astype(jnp.bfloat16)
    lefts = [activation, second_normalized.T, heads_out, first_normalized.T]
    rights = [cotangent.T, grad_pre, grad_branch.T]
    if n_shard == 2:
        small_args = [
            grad_heads, log_total, idents[:, None], idents[None, :], cosine, sine,
        ]
        products, grad_qkv, first_gradient = reduce_backward(
            lefts, rights, qkv, w_qkv, small_args, n_rep, head_count, score_scale
        )
    else:
        back = partial(head_back, score_scale=score_scale)
        grad_query, grad_key, grad_value = jax.vmap(back, in_axes=(0, 0, 0, 0, None, 0))(
            queries,
            keys_rot,
            values_all,
            grad_heads.reshape(head_count, head_size, row_count),
            idents[:, None] == idents[None, :],
            log_total[:, None, :],
        )
        grad_query = rotary_back(grad_query, cosine, sine)
        grad_key = rotary_back(grad_key, cosine, sine)
        grad_qkv = jnp.stack([grad_query, grad_key, grad_value]).reshape(qkv_shape)
        grad_qkv = grad_qkv.astype(jnp.bfloat16)
        first_gradient = contract(w_qkv, grad_qkv, 1, 0)
        products = [
            contract(left, right, 1, 1).astype(jnp.bfloat16)
            for left, right in zip(lefts, rights + [grad_qkv])
        ]
        products = [
            item.astype(jnp.float32) for item in reduce_products(products, n_rep, n_shard)
        ]
    d_w_down, d_w_up, d_w_proj, d_w_qkv = products
    d_b_qkv = jnp.sum(grad_qkv.astype(jnp.float32), axis=1)
    first_normalized_gradient = first_gradient.T
    first_gain_gradient = jnp.sum(first_normalized_gradient * first_centered_standard, axis=0)
    d_bias_one = jnp.sum(first_normalized_gradient, axis=0)
    d_patches = grad_hidden + norm_gradient_step(
        first_normalized_gradient,
        first_centered_standard,
        first_inverse_spread,
        first_norm_gain,
    )

    def own_parts(vectors):
        lens = [item.shape[0] for item in vectors]
        total = links.sum_all(jnp.concatenate(vectors))
        result, start = [], 0
        for size in lens:
            own = size // n_shard
            result.append(lax.dynamic_slice_in_dim(total, start + links.y * own, own, 0))
            start += size
        return result

    m_gain, m_bias, m_upb, m_downb = own_parts(
        [second_gain_gradient, d_bias_two, d_b_up, d_b_down]
    )
    a_gain, a_bias, a_qkvb, a_projb = own_parts(
        [first_gain_gradient, d_bias_one, d_b_qkv, d_b_proj]
    )
    return (
        layer_out,
        d_patches,
        a_gain,
        a_bias,
        d_w_qkv,
        a_qkvb,
        d_w_proj,
        a_projb,
        m_gain,
        m_bias,
        d_w_up,
        m_upb,
        d_w_down,
        m_downb,
    )


def solution(mesh):
    rows, whole = P(("rep", "shard"), None), P("shard")
    matrix = P("shard", None)
    in_specs = (
        rows,
        rows,
        P(None, ("rep", "shard")),
        whole,
        whole,
        matrix,
        whole,
        matrix,
        whole,
        whole,
        whole,
        matrix,
        whole,
        matrix,
        whole,
        rows,
    )
    out_specs = (
        rows,
        rows,
        whole,
        whole,
        matrix,
        whole,
        matrix,
        whole,
        whole,
        whole,
        matrix,
        whole,
        matrix,
        whole,
    )
    body = partial(per_device, n_rep=mesh.shape["rep"], n_shard=mesh.shape["shard"])
    return jax.shard_map(
        body, mesh=mesh, in_specs=in_specs, out_specs=out_specs, check_vma=False
    )
```

```python
from functools import partial

import jax
import jax.numpy as jnp
from jax import lax
from jax.experimental import pallas as pl
from jax.experimental.pallas import tpu as pltpu
from jax.sharding import PartitionSpec as P

HEADS = 16


norm_eps = 1e-06
quick_slope = 1.702


def apply_layer_norm(matrix):
    center = matrix - jnp.mean(matrix, axis=-1, keepdims=True)
    spread = jnp.mean(center * center, axis=-1, keepdims=True)
    inverse_spread = lax.rsqrt(spread + norm_eps)
    return (center * inverse_spread, inverse_spread)


def norm_gradient_step(normalized_gradient, centered_standard, inverse_spread, norm_gain):
    scaled_rows = normalized_gradient * norm_gain
    return inverse_spread * (
        scaled_rows
        - jnp.mean(scaled_rows, axis=-1, keepdims=True)
        - centered_standard * jnp.mean(scaled_rows * centered_standard, axis=-1, keepdims=True)
    )


def rotary_tables(positions, head_size):
    quarter = head_size // 4
    counter = jnp.arange(quarter, dtype=jnp.float32)
    inverse = jnp.power(jnp.float32(10000.0), -2.0 * counter / (head_size // 2))
    row_angle = inverse[:, None] * positions[0].astype(jnp.float32)[None, :]
    col_angle = inverse[:, None] * positions[1].astype(jnp.float32)[None, :]
    angle = jnp.concatenate([row_angle, col_angle], axis=0)
    angle = jnp.concatenate([angle, angle], axis=0)
    return (jnp.cos(angle), jnp.sin(angle))


def apply_rotary(matrix, cosine, sine):
    half_size = matrix.shape[-2] // 2
    turned = jnp.concatenate([-matrix[..., half_size:, :], matrix[..., :half_size, :]], axis=-2)
    return matrix * cosine + turned * sine


def rotary_back(grad, cosine, sine):
    half_size = grad.shape[-2] // 2
    sined = grad * sine
    turned = jnp.concatenate([sined[..., half_size:, :], -sined[..., :half_size, :]], axis=-2)
    return grad * cosine + turned


def contract(left, right, left_dim, right_dim):
    return lax.dot_general(
        left, right, (((left_dim,), (right_dim,)), ((), ())), preferred_element_type=jnp.float32
    )


def masked_scores(queries, keys_rot, ident, score_scale):
    scores = (
        jnp.einsum("hdk,hdq->hkq", keys_rot, queries, preferred_element_type=jnp.float32)
        * score_scale
    )
    same_pic = ident[:, None] == ident[None, :]
    return jnp.where(same_pic[None], scores, -1000000000.0)


def attend(queries, keys_rot, values_all, ident, score_scale):
    scores = masked_scores(queries, keys_rot, ident, score_scale)
    top_score = jnp.max(scores, axis=1, keepdims=True)
    exp_scores = jnp.exp(scores - top_score)
    total = jnp.sum(exp_scores, axis=1, keepdims=True)
    probs = (exp_scores / total).astype(jnp.bfloat16)
    attended = jnp.einsum("hdk,hkq->hdq", values_all, probs, preferred_element_type=jnp.float32)
    return (attended, (top_score + jnp.log(total))[:, 0, :])


def head_back(query, key, value, grad_head, same_pic, log_total, score_scale):
    scores = jnp.where(same_pic, contract(key, query, 0, 0) * score_scale, -1000000000.0)
    probs = jnp.exp(scores - log_total)
    grad_probs = contract(value, grad_head, 0, 0)
    inner = jnp.sum(probs * grad_probs, axis=0, keepdims=True)
    grad_scores = (probs * (grad_probs - inner)).astype(jnp.bfloat16)
    grad_query = contract(key, grad_scores, 1, 0) * score_scale
    grad_key = contract(query, grad_scores, 1, 1) * score_scale
    grad_value = contract(grad_head, probs.astype(jnp.bfloat16), 1, 1)
    return (grad_query, grad_key, grad_value)


MESH = pl.DeviceIdType.MESH


class Place:
    def __init__(self, n_rep):
        rep = lax.axis_index("rep")
        self.nz = n_rep // 4
        self.half = self.nz // 2
        self.y = lax.axis_index("shard")
        self.z, self.x, self.c = rep // 4, (rep // 2) % 2, rep % 2
        self.low = self.z < self.half
        self.depth = jnp.where(self.low, self.z, self.nz - 1 - self.z)
        side = jnp.where(self.low, 1, -1)
        self.to_core = {"rep": self.z * 4 + self.x * 2 + (1 - self.c)}
        self.to_x = {"rep": self.z * 4 + (1 - self.x) * 2 + self.c}
        self.to_y = {"shard": 1 - self.y}
        self.to_in = {"rep": (self.z + side) * 4 + self.x * 2 + self.c}
        self.to_out = {"rep": (self.z - side) * 4 + self.x * 2 + self.c}

    def at_depth(self, depth):
        return pl.when(self.depth == depth)

    def meet(self, with_y):
        barrier = pltpu.get_barrier_semaphore()
        near = [self.to_core, self.to_x, self.to_in] + ([self.to_y] if with_y else [])
        for device in near:
            pl.semaphore_signal(barrier, inc=1, device_id=device, device_id_type=MESH)

        @pl.when(self.depth > 0)
        def _():
            pl.semaphore_signal(barrier, inc=1, device_id=self.to_out, device_id_type=MESH)

        pl.semaphore_wait(barrier, jnp.where(self.depth > 0, len(near) + 1, len(near)))


def remote(src, dst, sems, k, device):
    return pltpu.make_async_remote_copy(
        src_ref=src,
        dst_ref=dst,
        send_sem=sems.at[0, k],
        recv_sem=sems.at[1, k],
        device_id=device,
        device_id_type=MESH,
    )


def add_into(dst, one, two):
    rows = dst.shape[0]
    step = 32 if rows % 32 == 0 else rows

    @pl.loop(0, rows // step)
    def _(i):
        spot = pl.ds(pl.multiple_of(i * step, step), step)
        total = one[spot, :].astype(jnp.float32) + two[spot, :].astype(jnp.float32)
        dst[spot, :] = total.astype(dst.dtype)


def skewed(count, stages):
    last = max(offset for offset, _ in stages)
    for tick in range(count + last):
        for offset, stage in sorted(stages, key=lambda item: -item[0]):
            if 0 <= tick - offset < count:
                stage(tick - offset)


def cut_chunks(shards):
    rows = min(shard.shape[0] for shard in shards)
    wide = min(shard.shape[1] for shard in shards)
    chunks = []
    for w, shard in enumerate(shards):
        for row0 in range(0, shard.shape[0], rows):
            for col0 in range(0, shard.shape[1], wide):
                chunks.append((w, row0, col0))
    return rows, wide, chunks


def reduce_kernel(n_rep, parts, chunks, shard_rows, rows, wide, *refs):
    count, n_w = len(chunks), len(shard_rows)
    sources, outs, arrived = refs[:n_w], refs[n_w : 2 * n_w], refs[2 * n_w]
    (
        held, lent, got_y, got_x, got_in, got_mid, total,
        own_in, lent_in, put, c0_sem, c1_sem, y_sem, x_sem, in_sem, mid_sem, back_sem,
        ax_sem, ac_sem, af_sem,
    ) = refs[2 * n_w + 1 :]
    c_sems = [c0_sem, c1_sem]
    at = Place(n_rep)
    half = at.half
    block = rows // 4
    with_y = parts == 2
    mine = at.y if with_y else 0

    def source(k, owner, c):
        w, row0, col0 = chunks[k]
        start = pl.multiple_of(owner * shard_rows[w] + row0 + c * 2 * block, 8)
        return sources[w].at[pl.ds(start, 2 * block), pl.ds(col0, wide)]

    def out(k, c, x):
        w, row0, col0 = chunks[k]
        start = pl.multiple_of(row0 + (c * 2 + x) * block, 8)
        return outs[w].at[pl.ds(start, block), pl.ds(col0, wide)]

    def rows_of(x):
        return pl.ds(pl.multiple_of(x * block, 8), block)

    def c_send(k, owner):
        return remote(
            source(k, owner, 1 - at.c), arrived.at[k, owner], c_sems[owner], k, at.to_core
        )

    def own_load(k, owner):
        return pltpu.make_async_copy(
            source(k, owner, at.c), held.at[k, owner], own_in.at[owner, k]
        )

    def lent_load(k, owner):
        return pltpu.make_async_copy(
            arrived.at[k, owner], lent.at[k % 2, owner], lent_in.at[owner, k]
        )

    def y_send(k):
        return remote(held.at[k, 1 - mine], got_y.at[k], y_sem, k, at.to_y)

    def x_send(k):
        return remote(
            held.at[k, mine, rows_of(1 - at.x)], got_x.at[k], x_sem, k, at.to_x
        )

    def part(k):
        return held.at[k, mine, rows_of(at.x)]

    def in_send(k):
        return remote(part(k), got_in.at[k], in_sem, k, at.to_in)

    def mid_send(k):
        return remote(part(k), got_mid.at[k], mid_sem, k, at.to_in)

    def back_send(k):
        return remote(total.at[k], total.at[k], back_sem, k, at.to_out)

    def ax_send(k, x):
        return remote(total.at[k], out(k, at.c, x), ax_sem, k, at.to_x)

    def ac_send(k, c):
        return remote(total.at[k], out(k, c, at.x), ac_sem, k, at.to_core)

    def af_send(k, c):
        view = out(k, c, 1 - at.x)
        return remote(view, view, af_sem, k, at.to_core)

    def own_put(k):
        return pltpu.make_async_copy(total.at[k], out(k, at.c, at.x), put.at[k])

    def start_core(k):
        for owner in range(parts):
            c_send(k, owner).start()
            own_load(k, owner).start()

    def load_core(k):
        for owner in range(parts):
            c_send(k, owner).wait_recv()
            lent_load(k, owner).start()

    def start_y(k):
        for owner in range(parts):
            own_load(k, owner).wait()
            lent_load(k, owner).wait()
        if with_y:
            other = 1 - mine
            add_into(held.at[k, other], held.at[k, other], lent.at[k % 2, other])
            y_send(k).start()
        add_into(held.at[k, mine], held.at[k, mine], lent.at[k % 2, mine])

    def start_x(k):
        if with_y:
            y_send(k).wait_recv()
            spot = rows_of(1 - at.x)
            add_into(held.at[k, mine, spot], held.at[k, mine, spot], got_y.at[k, spot])
        x_send(k).start()
        if with_y:
            add_into(part(k), part(k), got_y.at[k, rows_of(at.x)])

    def inner_send(k, depth):
        (mid_send(k) if depth == half - 1 else in_send(k)).start()

    def start_z(k):
        x_send(k).wait_recv()
        add_into(part(k), part(k), got_x.at[k])

        @at.at_depth(0)
        def _():
            inner_send(k, 0)

    def pass_in(depth):
        def stage(k):
            @at.at_depth(depth)
            def _():
                in_send(k).wait_recv()
                add_into(part(k), part(k), got_in.at[k])
                inner_send(k, depth)

        return stage

    def spread(k, depth):
        if depth > 0:
            back_send(k).start()
        ax_send(k, at.x).start()
        ac_send(k, at.c).start()
        own_put(k).start()

    def middle(k):
        @at.at_depth(half - 1)
        def _():
            mid_send(k).wait_recv()
            add_into(total.at[k], part(k), got_mid.at[k])
            spread(k, half - 1)

    def pass_out(depth):
        def stage(k):
            @at.at_depth(depth)
            def _():
                back_send(k).wait_recv()
                spread(k, depth)

        return stage

    def forward(k):
        ax_send(k, 1 - at.x).wait_recv()
        af_send(k, at.c).start()

    at.meet(with_y)
    stages = [(0, start_core), (1, load_core), (2, start_y), (4, start_x), (5, start_z)]
    stages += [(6 + depth - 1, pass_in(depth)) for depth in range(1, half)]
    stages += [(6 + half - 1, middle)]
    stages += [(6 + half + (half - 2 - depth), pass_out(depth)) for depth in range(half - 1)]
    stages += [(5 + 2 * half, forward)]
    skewed(count, stages)
    for k in range(count):
        for owner in range(parts):
            c_send(k, owner).wait_send()
        if with_y:
            y_send(k).wait_send()
        x_send(k).wait_send()
        for depth in range(half):

            @at.at_depth(depth)
            def _():
                (mid_send(k) if depth == half - 1 else in_send(k)).wait_send()
                if depth > 0:
                    back_send(k).wait_send()

        ax_send(k, at.x).wait_send()
        ac_send(k, at.c).wait_send()
        af_send(k, at.c).wait_send()
        own_put(k).wait()
        ac_send(k, 1 - at.c).wait_recv()
        af_send(k, 1 - at.c).wait_recv()


def reduce_products(products, n_rep, n_shard):
    parts = n_shard
    if n_shard != 2:
        products = [
            lax.psum_scatter(item, "shard", scatter_dimension=0, tiled=True) for item in products
        ]
        parts = 1
    owned = [
        jax.ShapeDtypeStruct((item.shape[0] // parts, item.shape[1]), jnp.bfloat16)
        for item in products
    ]
    rows, wide, chunks = cut_chunks(owned)
    count, block = len(chunks), rows // 4
    kernel = partial(
        reduce_kernel, n_rep, parts, chunks, [item.shape[0] for item in owned], rows, wide
    )
    pair = pltpu.SemaphoreType.DMA((2, count))
    low = jnp.bfloat16
    anywhere = pl.BlockSpec(memory_space=pl.ANY)
    results = pl.pallas_call(
        kernel,
        out_shape=owned + [jax.ShapeDtypeStruct((count, parts, 2 * block, wide), low)],
        in_specs=[anywhere] * len(products),
        out_specs=[anywhere] * (len(products) + 1),
        scratch_shapes=[
            pltpu.VMEM((count, parts, 2 * block, wide), low),
            pltpu.VMEM((2, parts, 2 * block, wide), low),
            pltpu.VMEM((count, 2 * block, wide), low),
            pltpu.VMEM((count, block, wide), low),
            pltpu.VMEM((count, block, wide), low),
            pltpu.VMEM((count, block, wide), low),
            pltpu.VMEM((count, block, wide), low),
            pltpu.SemaphoreType.DMA((parts, count)),
            pltpu.SemaphoreType.DMA((parts, count)),
            pltpu.SemaphoreType.DMA((count,)),
        ]
        + [pair] * 10,
        compiler_params=pltpu.CompilerParams(
            collective_id=1, has_side_effects=True, vmem_limit_bytes=62 << 20
        ),
        name="reduce_products",
    )(*products)
    return results[:-1]


class Cuts:
    def __init__(self, sizes, n_shard):
        self.shard_rows = [left // n_shard for left, _ in sizes]
        self.rows = min(self.shard_rows) // 2
        self.wide = min(right for _, right in sizes)
        self.down = [rows // self.rows for rows in self.shard_rows]
        self.across = [right // self.wide for _, right in sizes]
        self.first = [0]
        for down, across in zip(self.down, self.across):
            self.first.append(self.first[-1] + down * across)
        self.count = self.first[-1]

    def weight_of(self, k, act):
        for w, down in enumerate(self.down):

            @pl.when((k >= self.first[w]) & (k < self.first[w + 1]))
            def _():
                inside = k - self.first[w]
                act(w, inside % down, inside // down)

    def whole(self, chunks, w):
        first, down, rows, wide = self.first[w], self.down[w], self.rows, self.wide

        def widen(part, dst):
            dst[...] = part[0].astype(jnp.float32)

        return pl.pallas_call(
            widen,
            grid=(down, self.across[w]),
            in_specs=[pl.BlockSpec((1, rows, wide), lambda i, j: (first + j * down + i, 0, 0))],
            out_specs=pl.BlockSpec((rows, wide), lambda i, j: (i, j)),
            out_shape=jax.ShapeDtypeStruct(
                (self.shard_rows[w], self.across[w] * wide), jnp.float32
            ),
            compiler_params=pltpu.CompilerParams(vmem_limit_bytes=24 << 20),
            cost_estimate=pl.CostEstimate(
                flops=0,
                transcendentals=0,
                bytes_accessed=6 * down * self.across[w] * rows * wide,
            ),
            name="widen",
        )(chunks)


def backward_kernel(n_rep, cuts, n_heads, slots, score_scale, *refs):
    (
        left_0, left_1, left_2, left_3, right_0, right_1, qkv, w_qkv, w_up, w_proj,
        hidden, cotangent, patches,
        log_total, pic_key, pic_query, cosine, sine, gain_one, gain_two, down_sum,
        out, right_2, grad_qkv, d_rows, sums, lent_left, lent_right,
        op_left, op_right, held, got_y, got_x, got_in, got_mid, total, swap, w_block,
        pre_block, turned, branch, grad_heads, rows_in, got_sums,
        load_l, load_r, put, once_sem, block_sem, sum_sem,
        l0_sem, l1_sem, r_sem, y_sem, x_sem, in_sem, mid_sem, back_sem, ax_sem, ac_sem, af_sem,
    ) = refs
    lefts = [left_0, left_1, left_2, left_3]
    rights = [right_0, right_1, right_2, grad_qkv]
    l_sems = [l0_sem, l1_sem]
    at = Place(n_rep)
    half = at.half
    count, rows, wide = cuts.count, cuts.rows, cuts.wide
    block, width = rows // 2, wide // 2
    mine = at.y
    head = qkv.shape[0] // (3 * n_heads)
    model = n_heads * head

    def left_rows(w, row, owner):
        start = owner * cuts.shard_rows[w] + row * rows
        return lefts[w].at[pl.ds(pl.multiple_of(start, 16), rows), :]

    def right_rows(w, col, c):
        start = col * wide + c * width
        return rights[w].at[pl.ds(pl.multiple_of(start, 16), width), :]

    def left_push(k, owner, src):
        return remote(src, lent_left.at[k, owner], l_sems[owner], k, at.to_core)

    def right_push(k, src):
        return remote(src, lent_right.at[k], r_sem, k, at.to_core)

    def left_load(k, whose, owner, src):
        slot = k % 2
        return pltpu.make_async_copy(
            src, op_left.at[slot, whose, owner], load_l.at[whose, owner, k]
        )

    def right_load(k, whose, src):
        return pltpu.make_async_copy(src, op_right.at[k % 2, whose], load_r.at[whose, k])

    def rows_of(x):
        return pl.ds(pl.multiple_of(x * block, 16), block)

    def mine_of(k, x):
        return held.at[k % slots, mine, rows_of(x)]

    def y_send(k):
        return remote(held.at[k % slots, 1 - mine], got_y.at[k], y_sem, k, at.to_y)

    def x_send(k):
        return remote(mine_of(k, 1 - at.x), got_x.at[k], x_sem, k, at.to_x)

    def in_send(k):
        return remote(mine_of(k, at.x), got_in.at[k], in_sem, k, at.to_in)

    def mid_send(k):
        return remote(mine_of(k, at.x), got_mid.at[k], mid_sem, k, at.to_in)

    def back_send(k):
        return remote(total.at[k], total.at[k], back_sem, k, at.to_out)

    def out_of(k, c, x):
        cols = pl.ds(pl.multiple_of(c * width, 128), width)
        return out.at[k, rows_of(x), cols]

    def ax_send(k, x):
        return remote(total.at[k], out_of(k, at.c, x), ax_sem, k, at.to_x)

    def ac_send(k, c):
        return remote(total.at[k], out_of(k, c, at.x), ac_sem, k, at.to_core)

    def af_send(k, c):
        view = out_of(k, c, 1 - at.x)
        return remote(view, view, af_sem, k, at.to_core)

    def own_put(k):
        return pltpu.make_async_copy(total.at[k], out_of(k, at.c, at.x), put.at[k])

    def push(k):
        def act(w, row, col):
            for owner in range(2):
                left_push(k, owner, left_rows(w, row, owner)).start()
            right_push(k, right_rows(w, col, 1 - at.c)).start()

        cuts.weight_of(k, act)

    def load(k):
        def act(w, row, col):
            for owner in range(2):
                left_load(k, 0, owner, left_rows(w, row, owner)).start()
            right_load(k, 0, right_rows(w, col, at.c)).start()

        cuts.weight_of(k, act)
        for owner in range(2):
            left_push(k, owner, lent_left.at[k, owner]).wait_recv()
            left_load(k, 1, owner, lent_left.at[k, owner]).start()
        right_push(k, lent_right.at[k]).wait_recv()
        right_load(k, 1, lent_right.at[k]).start()

    def product(k):
        slot = k % 2
        for whose in range(2):
            for owner in range(2):
                left_load(k, whose, owner, lent_left.at[k, owner]).wait()
            right_load(k, whose, lent_right.at[k]).wait()
        for owner in range(2):
            left_push(k, owner, lent_left.at[k, owner]).wait_send()
        right_push(k, lent_right.at[k]).wait_send()
        for owner in (1 - mine, mine):
            result = contract(op_left[slot, 0, owner], op_right[slot, 0], 1, 1)
            result += contract(op_left[slot, 1, owner], op_right[slot, 1], 1, 1)
            held[k % slots, owner] = result.astype(jnp.bfloat16)
            if owner is not mine:
                y_send(k).start()

    def start_x(k):
        y_send(k).wait_recv()
        other = mine_of(k, 1 - at.x)
        add_into(other, other, got_y.at[k, rows_of(1 - at.x)])
        x_send(k).start()
        own = mine_of(k, at.x)
        add_into(own, own, got_y.at[k, rows_of(at.x)])
        y_send(k).wait_send()

    def inner_send(k, depth):
        return mid_send(k) if depth == half - 1 else in_send(k)

    def start_z(k):
        x_send(k).wait_recv()
        own = mine_of(k, at.x)
        add_into(own, own, got_x.at[k])

        @at.at_depth(0)
        def _():
            inner_send(k, 0).start()

        x_send(k).wait_send()

    def pass_in(depth):
        def stage(k):
            @at.at_depth(depth)
            def _():
                in_send(k).wait_recv()
                own = mine_of(k, at.x)
                add_into(own, own, got_in.at[k])
                inner_send(k, depth).start()

        return stage

    def spread(k, depth):
        if depth > 0:
            back_send(k).start()
        ax_send(k, at.x).start()
        ac_send(k, at.c).start()
        own_put(k).start()

    def middle(k):
        @at.at_depth(half - 1)
        def _():
            mid_send(k).wait_recv()
            add_into(total.at[k], mine_of(k, at.x), got_mid.at[k])
            spread(k, half - 1)

    def pass_out(depth):
        def stage(k):
            @at.at_depth(depth)
            def _():
                back_send(k).wait_recv()
                spread(k, depth)

        return stage

    def sent(k):
        for depth in range(half):

            @at.at_depth(depth)
            def _():
                inner_send(k, depth).wait_send()

    def forward(k):
        ax_send(k, 1 - at.x).wait_recv()
        af_send(k, at.c).start()

    def finish(k):
        @pl.when(at.depth > 0)
        def _():
            back_send(k).wait_send()

        ax_send(k, at.x).wait_send()
        ac_send(k, at.c).wait_send()
        af_send(k, at.c).wait_send()
        own_put(k).wait()
        ac_send(k, 1 - at.c).wait_recv()
        af_send(k, 1 - at.c).wait_recv()

    def head_step(h):
        def part(i):
            return pl.ds(pl.multiple_of(i * model + h * head, 16), head)

        query, key, value = swap[part(0), :], swap[part(1), :], swap[part(2), :]
        grads = head_back(
            query,
            key,
            value,
            grad_heads[part(0), :],
            pic_key[...] == pic_query[...],
            log_total[pl.ds(h, 1), :],
            score_scale,
        )
        grad_query, grad_key, grad_value = grads
        turn_c, turn_s = cosine[...], sine[...]
        swap[part(0), :] = rotary_back(grad_query, turn_c, turn_s).astype(jnp.bfloat16)
        swap[part(1), :] = rotary_back(grad_key, turn_c, turn_s).astype(jnp.bfloat16)
        swap[part(2), :] = grad_value.astype(jnp.bfloat16)

    tokens = qkv.shape[1]
    wide_two = right_1.shape[0]
    n_up, n_qkv = wide_two // width, qkv.shape[0] // width
    ends = [0]
    for size in (model, model, wide_two, model, model, model, qkv.shape[0], model):
        ends.append(ends[-1] + size)

    def sums_of(i, start=0, size=model):
        return pl.ds(pl.multiple_of(ends[i] + start, 128), size)

    def column_sums(block):
        ones = jnp.ones((8, tokens), jnp.bfloat16)
        return contract(ones, block, 1, 1)[0:1, :]

    def w_load(src, j, slot):
        cols = pl.ds(pl.multiple_of(j * width, 128), width)
        return lambda k: pltpu.make_async_copy(src.at[:, cols], w_block.at[slot], block_sem.at[0, k])

    def pre_load(j, slot):
        spot = pl.ds(pl.multiple_of(j * width, 16), width)
        return pltpu.make_async_copy(right_1.at[spot, :], pre_block.at[slot], block_sem.at[1, j])

    def once(i, src, dst):
        return pltpu.make_async_copy(src, dst, once_sem.at[i])

    def add_turned(slot, right):
        step = 256

        @pl.loop(0, model // step)
        def _(i):
            spot = pl.ds(pl.multiple_of(i * step, 16), step)
            turned[spot, :] += contract(w_block[slot, spot, :], right, 1, 0)

    def clear_turned():
        turned[...] = jnp.zeros_like(turned)

    def load_up(pair):
        for slot in range(2):
            j = pair * 2 + slot
            w_load(w_up, j, slot)(j).start()
            pre_load(j, slot).start()

    def up_step(pair):
        for slot in range(2):
            j = pair * 2 + slot
            w_load(w_up, j, slot)(j).wait()
            pre_load(j, slot).wait()
            block = pre_block[slot]
            add_turned(slot, block)
            sums[:, sums_of(2, j * width, width)] = column_sums(block)

    def load_proj():
        for slot in range(2):
            w_load(w_proj, slot, slot)(n_up + slot).start()

    def load_qkv(pair):
        for slot in range(2):
            j = pair * 2 + slot
            w_load(w_qkv, j, slot)(n_up + 2 + j).start()

    def qkv_step(pair):
        for slot in range(2):
            j = pair * 2 + slot
            w_load(w_qkv, j, slot)(n_up + 2 + j).wait()
            block = swap[pl.ds(pl.multiple_of(j * width, 16), width), :]
            add_turned(slot, block)
            sums[:, sums_of(6, j * width, width)] = column_sums(block)

    step = 128

    def norm_two():
        once(2, hidden, d_rows).wait()
        once(3, cotangent, rows_in).wait()

        @pl.loop(0, tokens // step)
        def _(i):
            spot = pl.ds(pl.multiple_of(i * step, 16), step)
            lanes = pl.ds(pl.multiple_of(i * step, 128), step)
            standard, inverse = apply_layer_norm(d_rows[spot, :])
            grad = turned[:, lanes].T
            sums[:, sums_of(0)] += jnp.sum(grad * standard, axis=0, keepdims=True)
            sums[:, sums_of(1)] += jnp.sum(grad, axis=0, keepdims=True)
            back = norm_gradient_step(grad, standard, inverse, gain_two[...])
            back = back + rows_in[spot, :].astype(jnp.float32)
            d_rows[spot, :] = back
            low = back.astype(jnp.bfloat16)
            branch[:, lanes] = low.T

        sums[:, sums_of(7)] = column_sums(branch[...])
        once(4, patches, rows_in).start()
        once(5, branch, right_2).start()
        for slot in range(2):
            w_load(w_proj, slot, slot)(n_up + slot).wait()

        @pl.loop(0, model // step)
        def _(i):
            spot = pl.ds(pl.multiple_of(i * step, 16), step)
            result = contract(w_block[0, spot, :], branch[pl.ds(0, width), :], 1, 0)
            result += contract(w_block[1, spot, :], branch[pl.ds(width, width), :], 1, 0)
            grad_heads[spot, :] = result.astype(jnp.bfloat16)

        once(5, branch, right_2).wait()
        clear_turned()

    def norm_one():
        once(4, patches, rows_in).wait()

        @pl.loop(0, tokens // step)
        def _(i):
            spot = pl.ds(pl.multiple_of(i * step, 16), step)
            lanes = pl.ds(pl.multiple_of(i * step, 128), step)
            standard, inverse = apply_layer_norm(rows_in[spot, :].astype(jnp.float32))
            grad = turned[:, lanes].T
            sums[:, sums_of(4)] += jnp.sum(grad * standard, axis=0, keepdims=True)
            sums[:, sums_of(5)] += jnp.sum(grad, axis=0, keepdims=True)
            d_rows[spot, :] += norm_gradient_step(grad, standard, inverse, gain_one[...])

    def sums_to(i, device):
        return remote(sums, got_sums.at[i], sum_sem, i, device)

    def swap_sums(i, device):
        def begin():
            sums_to(i, device).start()

        def end():
            sums_to(i, device).wait()
            sums[...] += got_sums[i]

        return begin, end

    def sums_in(depth):
        def act():
            @at.at_depth(depth)
            def _():
                if depth > 0:
                    sums_to(3, at.to_in).wait_recv()
                    sums[...] += got_sums[3]
                sums_to(4 if depth == half - 1 else 3, at.to_in).start()

            @at.at_depth(depth - 1)
            def _():
                if depth > 0:
                    sums_to(3, at.to_in).wait_send()

        return act

    def sums_middle():
        @at.at_depth(half - 1)
        def _():
            sums_to(4, at.to_in).wait()
            sums[...] += got_sums[4]
            if half > 1:
                sums_to(5, at.to_out).start()

    def sums_out(depth):
        def act():
            @at.at_depth(depth)
            def _():
                sums_to(5, at.to_out).wait_recv()
                sums[...] = got_sums[5]
                if depth > 0:
                    sums_to(5, at.to_out).start()

            @at.at_depth(depth + 1)
            def _():
                sums_to(5, at.to_out).wait_send()

        return act

    take_qkv = once(0, qkv, swap)
    give_qkv = once(1, swap, grad_qkv)
    take_qkv.start()
    once(2, hidden, d_rows).start()
    once(3, cotangent, rows_in).start()
    at.meet(True)
    load_up(0)
    clear_turned()
    sums[...] = jnp.zeros_like(sums)
    sums[:, sums_of(3)] = down_sum[...]
    take_qkv.wait()
    stages = [(0, push), (1, load), (2, product), (4, start_x), (6, start_z)]
    stages += [(6 + depth, pass_in(depth)) for depth in range(1, half)]
    stages += [(6 + half, middle)]
    stages += [(6 + half + (half - 1 - depth), pass_out(depth)) for depth in range(half - 1)]
    stages += [(slots + 2, sent), (7 + 2 * half, forward), (9 + 2 * half, finish)]
    stages.sort(key=lambda item: -item[0])
    per_tick = 2
    at_norm = n_up // 2
    at_heads = at_norm + 1
    at_qkv = at_heads + -(-n_heads // per_tick)
    at_one = at_qkv + n_qkv // 2
    begins, ends_of = zip(
        swap_sums(0, at.to_core), swap_sums(1, at.to_x), swap_sums(2, at.to_y)
    )
    events = {at_norm: [norm_two], at_one: [norm_one, begins[0]]}
    now = at_one
    for i in range(3):
        now += 1
        events[now] = [ends_of[i]] + ([begins[i + 1]] if i < 2 else [sums_in(0)])
    for act in (
        [sums_in(depth) for depth in range(1, half)]
        + [sums_middle]
        + [sums_out(depth) for depth in reversed(range(half - 1))]
    ):
        now += 1
        events[now] = [act]
    last = count + 9 + 2 * half
    assert now < last and at_norm < cuts.first[2] and at_qkv < cuts.first[3]

    def tick_body(tick, carry):
        for offset, stage in stages:

            @pl.when((tick >= offset) & (tick < count + offset))
            def _():
                stage(tick - offset)

        @pl.when(tick < at_norm)
        def _():
            up_step(tick)

        @pl.when(tick < at_norm - 1)
        def _():
            load_up(tick + 1)

        @pl.when(tick == at_norm - 1)
        def _():
            load_proj()

        for when, acts in events.items():

            @pl.when(tick == when)
            def _():
                for act in acts:
                    act()

        @pl.when((tick >= at_heads) & (tick < at_qkv))
        def _():
            @pl.loop(0, per_tick)
            def _(i):
                h = (tick - at_heads) * per_tick + i

                @pl.when(h < n_heads)
                def _():
                    head_step(h)

        @pl.when(tick == at_qkv)
        def _():
            give_qkv.start()
            give_qkv.wait()

        @pl.when((tick >= at_qkv) & (tick < at_one))
        def _():
            qkv_step(tick - at_qkv)

        @pl.when((tick >= at_qkv - 1) & (tick < at_one - 1))
        def _():
            load_qkv(tick - at_qkv + 1)

        return carry

    lax.fori_loop(0, last, tick_body, 0)


def reduce_backward(lefts, rights, others, small, n_rep, n_heads, score_scale):
    qkv, _, w_up, w_proj, hidden = others[:5]
    tokens, model = hidden.shape
    sizes = [(left.shape[0], right) for left, right in zip(lefts, (model, w_up.shape[1], model))]
    sizes.append((model, qkv.shape[0]))
    cuts = Cuts(sizes, 2)
    half = n_rep // 8
    slots = 3 + 2 * half
    count, rows, wide = cuts.count, cuts.rows, cuts.wide
    block, width = rows // 2, wide // 2
    n_sums = 6 * model + w_up.shape[1] + qkv.shape[0]
    low, full, dma = jnp.bfloat16, jnp.float32, pltpu.SemaphoreType.DMA
    anywhere, local = pl.BlockSpec(memory_space=pl.ANY), pl.BlockSpec(memory_space=pltpu.VMEM)
    n_blocks = (w_up.shape[1] + qkv.shape[0]) // width + 2
    chunks, _, _, d_rows, sums, _, _ = pl.pallas_call(
        partial(backward_kernel, n_rep, cuts, n_heads, slots, score_scale),
        out_shape=[
            jax.ShapeDtypeStruct((count, rows, wide), low),
            jax.ShapeDtypeStruct((model, tokens), low),
            jax.ShapeDtypeStruct(qkv.shape, low),
            jax.ShapeDtypeStruct((tokens, model), full),
            jax.ShapeDtypeStruct((1, n_sums), full),
            jax.ShapeDtypeStruct((count, 2, rows, tokens), low),
            jax.ShapeDtypeStruct((count, width, tokens), low),
        ],
        in_specs=[anywhere] * (len(lefts) + len(rights) + len(others)) + [local] * len(small),
        out_specs=[anywhere] * 3 + [local] * 2 + [anywhere] * 2,
        scratch_shapes=[
            pltpu.VMEM((2, 2, 2, rows, tokens), low),
            pltpu.VMEM((2, 2, width, tokens), low),
            pltpu.VMEM((slots, 2, rows, width), low),
            pltpu.VMEM((count, rows, width), low),
            pltpu.VMEM((count, block, width), low),
            pltpu.VMEM((count, block, width), low),
            pltpu.VMEM((count, block, width), low),
            pltpu.VMEM((count, block, width), low),
            pltpu.VMEM(qkv.shape, low),
            pltpu.VMEM((2, model, width), low),
            pltpu.VMEM((2, width, tokens), low),
            pltpu.VMEM((model, tokens), full),
            pltpu.VMEM((model, tokens), low),
            pltpu.VMEM((model, tokens), low),
            pltpu.VMEM((tokens, model), low),
            pltpu.VMEM((6, 1, n_sums), full),
            dma((2, 2, count)),
            dma((2, count)),
            dma((count,)),
            dma((6,)),
            dma((2, n_blocks)),
            dma((2, 6)),
        ]
        + [dma((2, count))] * 11,
        compiler_params=pltpu.CompilerParams(
            collective_id=1, has_side_effects=True, vmem_limit_bytes=63 << 20
        ),
        name="reduce_backward",
    )(*lefts, *rights, *others, *small)
    return [cuts.whole(chunks, w) for w in range(len(sizes))], d_rows, sums[0]


def forward_kernel(n_rep, cuts, n_heads, score_scale, *refs):
    n_w = len(cuts.down)
    shards, refs = refs[:n_w], refs[n_w:]
    (
        normed, patches, cotangent, qkv_bias, proj_bias, gain, bias, up_bias, down_bias,
        pic_key, pic_query, cosine, sine,
    ) = refs[:13]
    fulls, refs = refs[13 : 13 + n_w], refs[13 + n_w :]
    (
        swap, heads_out, log_total, hidden, two_turned, act_turned, pre_turned, layer_out,
        hold, w_block, turned, up_pre, act, out_sum, normed_two,
        own_in, own_out, w_sem, y_sem, d_sem, in_sem, mid_sem, back_sem, x_sem, c_sem, cd_sem,
    ) = refs
    at = Place(n_rep)
    nz, half = at.nz, at.half
    count, rows, wide = cuts.count, cuts.rows, cuts.wide
    plane = rows * 4 // 5
    unit = plane // n_rep
    straight = (rows - plane) // 2
    mine, yours = at.y, 1 - at.y
    model = normed.shape[1]
    tokens = normed.shape[0]
    head = model // n_heads

    def shard(w, row, col, first, size):
        start = pl.multiple_of(row * rows + first, 16)
        cols = pl.ds(pl.multiple_of(col * wide, 128), wide)
        return shards[w].at[pl.ds(start, size), cols]

    def full(w, row, col, owner, first, size):
        start = pl.multiple_of(owner * cuts.shard_rows[w] + row * rows + first, 16)
        cols = pl.ds(pl.multiple_of(col * wide, 128), wide)
        return fulls[w].at[pl.ds(start, size), cols]

    def alike(size):
        return fulls[0].at[pl.ds(0, size), pl.ds(0, wide)]

    def place(c, x, z):
        return ((c * 2 + x) * nz + z) * unit

    def spread_copy(k, first, size, sems, device):
        def act_on(w, row, col):
            view = full(w, row, col, yours, first, size)
            remote(view, view, sems, k, device).start()

        cuts.weight_of(k, act_on)

    def settle(k, size, sems, device, received):
        view = alike(size)
        copy = remote(view, view, sems, k, device)
        if received:
            copy.wait_recv()
        else:
            copy.wait_send()

    def along(k, begin, size, sems, device):
        spread_copy(k, place(at.c, at.x, begin), size * unit, sems, device)

    def start_y(k):
        def act_on(w, row, col):
            first = place(at.c, at.x, at.z)
            remote(
                shard(w, row, col, first, unit),
                full(w, row, col, mine, first, unit),
                y_sem, k, at.to_y,
            ).start()
            first = plane + at.c * straight
            remote(
                shard(w, row, col, first, straight),
                full(w, row, col, mine, first, straight),
                d_sem, k, at.to_y,
            ).start()

        cuts.weight_of(k, act_on)

    def inner_send(k, depth):
        if depth == half - 1:
            along(k, jnp.where(at.low, 0, half), half, mid_sem, at.to_in)
        else:
            along(k, jnp.where(at.low, 0, nz - 1 - depth), depth + 1, in_sem, at.to_in)

    def back_start(k, depth):
        along(k, jnp.where(at.low, depth, 0), nz - depth, back_sem, at.to_out)

    def x_start(k):
        along(k, 0, nz, x_sem, at.to_x)

    def crossed(k):
        settle(k, unit, y_sem, at.to_y, True)

        @at.at_depth(0)
        def _():
            inner_send(k, 0)

        settle(k, straight, d_sem, at.to_y, True)
        spread_copy(k, plane + at.c * straight, straight, cd_sem, at.to_core)

    def pass_in(depth):
        def stage(k):
            @at.at_depth(depth)
            def _():
                settle(k, depth * unit, in_sem, at.to_in, True)
                inner_send(k, depth)

        return stage

    def middle(k):
        @at.at_depth(half - 1)
        def _():
            settle(k, half * unit, mid_sem, at.to_in, True)
            if half > 1:
                back_start(k, half - 1)
            x_start(k)

    def pass_out(depth):
        def stage(k):
            @at.at_depth(depth)
            def _():
                settle(k, (nz - depth - 1) * unit, back_sem, at.to_out, True)
                if depth > 0:
                    back_start(k, depth)
                x_start(k)

        return stage

    def crossed_x(k):
        settle(k, nz * unit, x_sem, at.to_x, True)
        spread_copy(k, place(at.c, 0, 0), 2 * nz * unit, c_sem, at.to_core)

    def own_load(k, view):
        return pltpu.make_async_copy(view, hold.at[k % 3], own_in.at[k])

    def own_store(k, view):
        return pltpu.make_async_copy(hold.at[k % 3], view, own_out.at[k])

    def take_own(k):
        cuts.weight_of(k, lambda w, row, col: own_load(k, shard(w, row, col, 0, rows)).start())

    def give_own(k):
        own_load(k, alike(rows)).wait()
        cuts.weight_of(
            k, lambda w, row, col: own_store(k, full(w, row, col, mine, 0, rows)).start()
        )

    def arrived(k):
        own_store(k, alike(rows)).wait()
        settle(k, 2 * nz * unit, c_sem, at.to_core, True)
        settle(k, straight, cd_sem, at.to_core, True)
        settle(k, unit, y_sem, at.to_y, False)
        settle(k, straight, d_sem, at.to_y, False)
        settle(k, nz * unit, x_sem, at.to_x, False)
        settle(k, 2 * nz * unit, c_sem, at.to_core, False)
        settle(k, straight, cd_sem, at.to_core, False)
        for depth in range(half):

            @at.at_depth(depth)
            def _():
                if depth == half - 1:
                    settle(k, half * unit, mid_sem, at.to_in, False)
                else:
                    settle(k, (depth + 1) * unit, in_sem, at.to_in, False)
                if depth > 0:
                    settle(k, (nz - depth) * unit, back_sem, at.to_out, False)

    def block_of(u, view):
        return pltpu.make_async_copy(view, w_block.at[u % 2], w_sem.at[0, u])

    def half_block(u, owner, view):
        spot = pl.ds(owner * (wide // 2), wide // 2)
        return pltpu.make_async_copy(view, w_block.at[u % 2, spot, :], w_sem.at[owner, u])

    def columns(w, col):
        return fulls[w].at[:, pl.ds(pl.multiple_of(col * wide, 128), wide)]

    def down_rows(i, owner):
        start = owner * cuts.shard_rows[3] + i * (wide // 2)
        return fulls[3].at[pl.ds(pl.multiple_of(start, 16), wide // 2), :]

    step = 256

    def qkv_step(b, u):
        block_of(u, columns(0, 0)).wait()

        @pl.loop(0, wide // step)
        def _(i):
            spot = pl.ds(pl.multiple_of(i * step, 128), step)
            col = pl.ds(pl.multiple_of(b * wide + i * step, 128), step)
            part = contract(normed[...], w_block[u % 2, :, spot], 1, 0) + qkv_bias[:, col]
            turned[pl.ds(pl.multiple_of(i * step, 16), step), :] = part.T

        @pl.loop(0, n_heads)
        def _(h):
            part = turned[pl.ds(pl.multiple_of(h * head, 8), head), :]
            spot = pl.ds(pl.multiple_of(b * model + h * head, 16), head)

            @pl.when(b < 2)
            def _():
                swap[spot, :] = apply_rotary(part, cosine[...], sine[...]).astype(jnp.bfloat16)

            @pl.when(b == 2)
            def _():
                swap[spot, :] = part.astype(jnp.bfloat16)

    def head_step(h):
        def part(i):
            return swap[pl.ds(pl.multiple_of(i * model + h * head, 16), head), :]

        scores = contract(part(1), part(0), 0, 0) * score_scale
        scores = jnp.where(pic_key[...] == pic_query[...], scores, -1000000000.0)
        top = jnp.max(scores, axis=0, keepdims=True)
        exp_scores = jnp.exp(scores - top)
        total = jnp.sum(exp_scores, axis=0, keepdims=True)
        probs = (exp_scores / total).astype(jnp.bfloat16)
        attended = contract(part(2), probs, 1, 0)
        heads_out[pl.ds(pl.multiple_of(h * head, 16), head), :] = attended.astype(jnp.bfloat16)
        log_total[pl.ds(h, 1), :] = top + jnp.log(total)

    def proj_step(u):
        block_of(u, columns(0, 0)).wait()

        @pl.loop(0, tokens // step)
        def _(i):
            spot = pl.ds(pl.multiple_of(i * step, 16), step)
            lanes = pl.ds(pl.multiple_of(i * step, 128), step)
            branch = contract(heads_out[:, lanes], w_block[u % 2], 0, 0)
            rows_in = patches[spot, :].astype(jnp.float32) + branch + proj_bias[...]
            hidden[spot, :] = rows_in
            out_sum[spot, :] = rows_in + down_bias[...]
            standard, _ = apply_layer_norm(rows_in)
            result = (standard * gain[...] + bias[...]).astype(jnp.bfloat16)
            normed_two[spot, :] = result
            two_turned[:, lanes] = result.T

    def up_step(c, u):
        block_of(u, columns(0, 0)).wait()

        @pl.loop(0, wide // step)
        def _(i):
            spot = pl.ds(pl.multiple_of(i * step, 128), step)
            col = pl.multiple_of(c * wide + i * step, 128)
            cols = pl.ds(col, step)
            pre = contract(normed_two[...], w_block[u % 2, :, spot], 1, 0) + up_bias[:, cols]
            up_pre[:, cols] = pre
            result = (pre / (1.0 + jnp.exp(-quick_slope * pre))).astype(jnp.bfloat16)
            act[:, cols] = result
            act_turned[pl.ds(col, step), :] = result.T

    def down_step(i, u):
        for owner in range(2):
            half_block(u, owner, down_rows(0, 0)).wait()
            size = wide // 2
            col = pl.multiple_of(owner * cuts.shard_rows[3] + i * size, 128)

            @pl.loop(0, tokens // step)
            def _(j):
                spot = pl.ds(pl.multiple_of(j * step, 16), step)
                lanes = pl.ds(pl.multiple_of(j * step, 128), step)
                weight = w_block[u % 2, pl.ds(owner * size, size), :]
                pre = up_pre[spot, pl.ds(col, size)]
                sigmoid = 1.0 / (1.0 + jnp.exp(-quick_slope * pre))
                slope = sigmoid + quick_slope * pre * sigmoid * (1.0 - sigmoid)
                grad = contract(cotangent[spot, :], weight, 1, 1) * slope
                pre_turned[pl.ds(col, size), lanes] = grad.astype(jnp.bfloat16).T
                out_sum[spot, :] += contract(act[spot, pl.ds(col, size)], weight, 1, 0)

    offset = 2 * half + 2
    stages = [(1, crossed)]
    stages += [(1 + depth, pass_in(depth)) for depth in range(1, half)]
    stages += [(1 + half, middle)]
    stages += [(1 + half + (half - 1 - depth), pass_out(depth)) for depth in range(half - 1)]
    stages += [(2 * half + 1, crossed_x)]
    stages += [(offset - 2, take_own), (offset - 1, give_own), (offset, arrived)]
    stages.sort(key=lambda item: -item[0])
    n_up, n_down = cuts.across[2], cuts.down[3] // 2
    per_tick = 3
    first_head = cuts.first[1] + 1
    at_proj = first_head + -(-n_heads // per_tick)
    at_up = at_proj + 1
    at_down = max(at_up + n_up, cuts.first[3] + 2)
    n_steps = 4 + n_up + n_down

    at.meet(True)

    @pl.loop(0, count)
    def _(k):
        start_y(k)

    def tick_body(tick, carry):
        for lag, stage in stages:

            @pl.when((tick >= lag) & (tick < count + lag))
            def _():
                stage(tick - lag)

        now = tick - offset

        @pl.when((now >= 2) & (now < first_head) & (now % 2 == 0))
        def _():
            qkv_step(now // 2 - 1, now // 2 - 1)

        @pl.when((now >= first_head) & (now < at_proj))
        def _():
            @pl.loop(0, per_tick)
            def _(i):
                h = (now - first_head) * per_tick + i

                @pl.when(h < n_heads)
                def _():
                    head_step(h)

        @pl.when(now == at_proj)
        def _():
            proj_step(3)

        @pl.when((now >= at_up) & (now < at_up + n_up))
        def _():
            up_step(now - at_up, now - at_up + 4)

        down_i = (now - at_down) // 2

        @pl.when((now >= at_down) & (down_i < n_down) & ((now - at_down) % 2 == 0))
        def _():
            down_step(down_i, down_i + 4 + n_up)

        soon = now + 1

        @pl.when((soon >= 2) & (soon < first_head) & (soon % 2 == 0))
        def _():
            block_of(soon // 2 - 1, columns(0, soon // 2 - 1)).start()

        @pl.when(soon == at_proj)
        def _():
            block_of(3, columns(1, 0)).start()

        @pl.when((soon >= at_up) & (soon < at_up + n_up))
        def _():
            block_of(soon - at_up + 4, columns(2, soon - at_up)).start()

        next_i = (soon - at_down) // 2

        @pl.when((soon >= at_down) & (next_i < n_down) & ((soon - at_down) % 2 == 0))
        def _():
            for owner in range(2):
                half_block(next_i + 4 + n_up, owner, down_rows(next_i, owner)).start()

        return carry

    lax.fori_loop(0, offset + at_down + 2 * n_down - 1, tick_body, 0)
    layer_out[...] = out_sum[...].astype(jnp.bfloat16)


def gather_forward(shards, inputs, n_rep, n_heads, score_scale):
    cuts = Cuts([(shard.shape[0] * 2, shard.shape[1]) for shard in shards], 2)
    tokens, model = inputs[0].shape
    wide_two = shards[2].shape[1]
    count, rows, wide = cuts.count, cuts.rows, cuts.wide
    low, dma = jnp.bfloat16, pltpu.SemaphoreType.DMA
    anywhere, local = pl.BlockSpec(memory_space=pl.ANY), pl.BlockSpec(memory_space=pltpu.VMEM)
    n_steps = 4 + cuts.across[2] + cuts.down[3] // 2

    def shape(*sizes, kind=low):
        return jax.ShapeDtypeStruct(sizes, kind)

    results = pl.pallas_call(
        partial(forward_kernel, n_rep, cuts, n_heads, score_scale),
        out_shape=[shape(item.shape[0] * 2, item.shape[1]) for item in shards]
        + [
            shape(3 * model, tokens),
            shape(model, tokens),
            shape(n_heads, tokens, kind=jnp.float32),
            shape(tokens, model, kind=jnp.float32),
            shape(model, tokens),
            shape(wide_two, tokens),
            shape(wide_two, tokens),
            shape(tokens, model),
        ],
        in_specs=[anywhere] * len(shards) + [local] * len(inputs),
        out_specs=[anywhere] * len(shards) + [local] * 8,
        scratch_shapes=[
            pltpu.VMEM((3, rows, wide), low),
            pltpu.VMEM((2, model, wide), low),
            pltpu.VMEM((model, tokens), jnp.float32),
            pltpu.VMEM((tokens, wide_two), jnp.float32),
            pltpu.VMEM((tokens, wide_two), low),
            pltpu.VMEM((tokens, model), jnp.float32),
            pltpu.VMEM((tokens, model), low),
            dma((count,)),
            dma((count,)),
            dma((2, n_steps)),
        ]
        + [dma((2, count))] * 8,
        compiler_params=pltpu.CompilerParams(
            collective_id=0, has_side_effects=True, vmem_limit_bytes=63 << 20
        ),
        name="gather_forward",
    )(*shards, *inputs)
    return results[: len(shards)], results[len(shards) :]


class Links:
    def __init__(self, n_rep, n_shard):
        self.nz, self.ny, self.n_rep = n_rep // 4, n_shard, n_rep
        self.y = lax.axis_index("shard")

    def gather_vector(self, vector):
        if self.ny != 2:
            return lax.all_gather(vector, "shard", axis=0, tiled=False)
        other = lax.ppermute(vector, "shard", [(0, 1), (1, 0)])
        low, high = jnp.where(self.y == 0, vector, other), jnp.where(self.y == 0, other, vector)
        return jnp.stack([low, high])

    def sum_all(self, vector):
        for flip in (1, 2):
            vector = vector + lax.ppermute(
                vector, "rep", [(i, i ^ flip) for i in range(self.n_rep)]
            )
        step = 1
        while step < self.nz:
            pairs = [(i, i ^ (4 * step)) for i in range(self.n_rep)]
            vector = vector + lax.ppermute(vector, "rep", pairs)
            step *= 2
        step = 1
        while step < self.ny:
            pairs = [(i, i ^ step) for i in range(self.ny)]
            vector = vector + lax.ppermute(vector, "shard", pairs)
            step *= 2
        return vector


def per_device(
    patches,
    lengths,
    positions,
    ln1_gain,
    ln1_bias,
    qkv_weight,
    qkv_bias,
    proj_weight,
    proj_bias,
    ln2_gain,
    ln2_bias,
    fc1_weight,
    fc1_bias,
    fc2_weight,
    fc2_bias,
    cotangent,
    n_rep,
    n_shard,
):
    links = Links(n_rep, n_shard)
    pack_count = lengths.shape[0]
    row_count = patches.shape[0]
    length = row_count // pack_count
    model_width = patches.shape[1]
    head_count = HEADS
    head_size = model_width // head_count
    score_scale = head_size ** (-0.5)
    pic_ends = jnp.cumsum(lengths[:, :-1], axis=1)
    slot_index = jnp.arange(length, dtype=jnp.int32)
    idents = jnp.sum((slot_index[None, :, None] >= pic_ends[:, None, :]).astype(jnp.int32), axis=2)
    pack_index = jnp.arange(pack_count, dtype=jnp.int32)
    idents = (idents + pack_index[:, None] * lengths.shape[1]).reshape(-1)
    cosine, sine = rotary_tables(positions, head_size)

    small = [ln1_gain, ln1_bias, qkv_bias, proj_bias, ln2_gain, ln2_bias, fc1_bias, fc2_bias]
    sizes = [item.shape[0] for item in small]
    spots = [sum(sizes[:i]) for i in range(len(sizes) + 1)]
    packed = sum(
        jnp.pad(item, (spots[i], spots[-1] - spots[i + 1])) for i, item in enumerate(small)
    )
    gathered = links.gather_vector(packed)
    (
        first_norm_gain, first_norm_bias, b_qkv, b_proj,
        second_norm_gain, second_norm_bias, b_up, b_down,
    ) = [
        gathered[:, spots[i] : spots[i + 1]].reshape(-1).astype(jnp.float32)
        for i in range(len(sizes))
    ]

    input_rows = patches.astype(jnp.float32)
    first_centered_standard, first_inverse_spread = apply_layer_norm(input_rows)
    first_normalized = (first_centered_standard * first_norm_gain + first_norm_bias).astype(
        jnp.bfloat16
    )
    shards = [qkv_weight, proj_weight, fc1_weight, fc2_weight]
    qkv_shape = (3 * model_width, row_count)
    grad_out = cotangent.astype(jnp.float32)
    d_b_down = jnp.sum(grad_out, axis=0)
    if n_shard == 2:
        rows_in = [
            item[None, :]
            for item in (b_qkv, b_proj, second_norm_gain, second_norm_bias, b_up, b_down)
        ]
        inputs = [first_normalized, patches, cotangent] + rows_in
        inputs += [idents[:, None], idents[None, :], cosine, sine]
        weights, results = gather_forward(shards, inputs, n_rep, head_count, score_scale)
        w_qkv, w_proj, w_up, w_down = weights
        qkv, heads_out, log_total, hidden_rows, second_turned = results[:5]
        activation, grad_pre, layer_out = results[5:]
        others = [qkv, w_qkv, w_up, w_proj, hidden_rows, cotangent, patches]
        row_args = [first_norm_gain[None, :], second_norm_gain[None, :], d_b_down[None, :]]
        small_args = [log_total, idents[:, None], idents[None, :], cosine, sine] + row_args
        lefts = [activation, second_turned, heads_out, first_normalized.T]
        rights = [cotangent.T, grad_pre]
        products, d_patches, total = reduce_backward(
            lefts, rights, others, small_args, n_rep, head_count, score_scale
        )
    else:
        w_qkv, w_proj, w_up, w_down = [
            lax.all_gather(shard, "shard", axis=0, tiled=True) for shard in shards
        ]
        qkv_rows = contract(w_qkv, first_normalized, 0, 1) + b_qkv[:, None]
        qkv_rows = qkv_rows.reshape(3, head_count, head_size, row_count)
        queries = apply_rotary(qkv_rows[0], cosine, sine).astype(jnp.bfloat16)
        keys_rot = apply_rotary(qkv_rows[1], cosine, sine).astype(jnp.bfloat16)
        values_all = qkv_rows[2].astype(jnp.bfloat16)
        attended, log_total = attend(queries, keys_rot, values_all, idents, score_scale)
        heads_out = attended.reshape(model_width, row_count).astype(jnp.bfloat16)
        hidden_rows = input_rows + contract(heads_out, w_proj, 0, 0) + b_proj
        second_centered_standard, second_inverse_spread = apply_layer_norm(hidden_rows)
        second_normalized = (
            second_centered_standard * second_norm_gain + second_norm_bias
        ).astype(jnp.bfloat16)
        up_pre = contract(w_up, second_normalized, 0, 1) + b_up[:, None]
        sigmoid_up = 1.0 / (1.0 + jnp.exp(-quick_slope * up_pre))
        activation = (up_pre * sigmoid_up).astype(jnp.bfloat16)
        out_full = hidden_rows + contract(activation, w_down, 0, 0) + b_down
        layer_out = out_full.astype(jnp.bfloat16)
        grad_act = contract(w_down, cotangent, 1, 1)
        slope_up = sigmoid_up + quick_slope * up_pre * sigmoid_up * (1.0 - sigmoid_up)
        grad_pre = (grad_act * slope_up).astype(jnp.bfloat16)
        d_b_up = jnp.sum(grad_pre.astype(jnp.float32), axis=1)
        second_normalized_gradient = contract(grad_pre, w_up, 0, 1)
        second_gain_gradient = jnp.sum(
            second_normalized_gradient * second_centered_standard, axis=0
        )
        d_bias_two = jnp.sum(second_normalized_gradient, axis=0)
        grad_hidden = grad_out + norm_gradient_step(
            second_normalized_gradient,
            second_centered_standard,
            second_inverse_spread,
            second_norm_gain,
        )
        grad_branch = grad_hidden.astype(jnp.bfloat16)
        d_b_proj = jnp.sum(grad_branch.astype(jnp.float32), axis=0)
        grad_heads = contract(w_proj, grad_branch, 1, 1).astype(jnp.bfloat16)
        back = partial(head_back, score_scale=score_scale)
        grad_query, grad_key, grad_value = jax.vmap(back, in_axes=(0, 0, 0, 0, None, 0))(
            queries,
            keys_rot,
            values_all,
            grad_heads.reshape(head_count, head_size, row_count),
            idents[:, None] == idents[None, :],
            log_total[:, None, :],
        )
        grad_query = rotary_back(grad_query, cosine, sine)
        grad_key = rotary_back(grad_key, cosine, sine)
        grad_qkv = jnp.stack([grad_query, grad_key, grad_value]).reshape(qkv_shape)
        grad_qkv = grad_qkv.astype(jnp.bfloat16)
        first_normalized_gradient = contract(grad_qkv, w_qkv, 0, 1)
        lefts = [activation, second_normalized.T, heads_out, first_normalized.T]
        rights = [cotangent.T, grad_pre, grad_branch.T, grad_qkv]
        products = [
            contract(left, right, 1, 1).astype(jnp.bfloat16) for left, right in zip(lefts, rights)
        ]
        products = [
            item.astype(jnp.float32) for item in reduce_products(products, n_rep, n_shard)
        ]
        d_b_qkv = jnp.sum(grad_qkv.astype(jnp.float32), axis=1)
        first_gain_gradient = jnp.sum(first_normalized_gradient * first_centered_standard, axis=0)
        d_bias_one = jnp.sum(first_normalized_gradient, axis=0)
        d_patches = grad_hidden + norm_gradient_step(
            first_normalized_gradient,
            first_centered_standard,
            first_inverse_spread,
            first_norm_gain,
        )
        total = jnp.concatenate(
            [
                second_gain_gradient, d_bias_two, d_b_up, d_b_down,
                first_gain_gradient, d_bias_one, d_b_qkv, d_b_proj,
            ]
        )
        total = links.sum_all(total)
    d_w_down, d_w_up, d_w_proj, d_w_qkv = products

    ff = fc1_weight.shape[1]
    own_parts, start = [], 0
    for size in (
        model_width, model_width, ff, model_width,
        model_width, model_width, 3 * model_width, model_width,
    ):
        own = size // n_shard
        own_parts.append(lax.dynamic_slice_in_dim(total, start + links.y * own, own, 0))
        start += size
    m_gain, m_bias, m_upb, m_downb, a_gain, a_bias, a_qkvb, a_projb = own_parts
    return (
        layer_out,
        d_patches,
        a_gain,
        a_bias,
        d_w_qkv,
        a_qkvb,
        d_w_proj,
        a_projb,
        m_gain,
        m_bias,
        d_w_up,
        m_upb,
        d_w_down,
        m_downb,
    )


def solution(mesh):
    rows, whole = P(("rep", "shard"), None), P("shard")
    matrix = P("shard", None)
    in_specs = (
        rows,
        rows,
        P(None, ("rep", "shard")),
        whole,
        whole,
        matrix,
        whole,
        matrix,
        whole,
        whole,
        whole,
        matrix,
        whole,
        matrix,
        whole,
        rows,
    )
    out_specs = (
        rows,
        rows,
        whole,
        whole,
        matrix,
        whole,
        matrix,
        whole,
        whole,
        whole,
        matrix,
        whole,
        matrix,
        whole,
    )
    body = partial(per_device, n_rep=mesh.shape["rep"], n_shard=mesh.shape["shard"])
    return jax.shard_map(
        body, mesh=mesh, in_specs=in_specs, out_specs=out_specs, check_vma=False
    )
```

```python
from functools import partial

import jax
import jax.numpy as jnp
from jax import lax
from jax.experimental import pallas as pl
from jax.experimental.pallas import tpu as pltpu
from jax.sharding import PartitionSpec as P

HEADS = 16


norm_eps = 1e-06
quick_slope = 1.702


def apply_layer_norm(matrix):
    center = matrix - jnp.mean(matrix, axis=-1, keepdims=True)
    spread = jnp.mean(center * center, axis=-1, keepdims=True)
    inverse_spread = lax.rsqrt(spread + norm_eps)
    return (center * inverse_spread, inverse_spread)


def norm_gradient_step(normalized_gradient, centered_standard, inverse_spread, norm_gain):
    scaled_rows = normalized_gradient * norm_gain
    return inverse_spread * (
        scaled_rows
        - jnp.mean(scaled_rows, axis=-1, keepdims=True)
        - centered_standard * jnp.mean(scaled_rows * centered_standard, axis=-1, keepdims=True)
    )


def rotary_tables(positions, head_size):
    quarter = head_size // 4
    counter = jnp.arange(quarter, dtype=jnp.float32)
    inverse = jnp.power(jnp.float32(10000.0), -2.0 * counter / (head_size // 2))
    row_angle = inverse[:, None] * positions[0].astype(jnp.float32)[None, :]
    col_angle = inverse[:, None] * positions[1].astype(jnp.float32)[None, :]
    angle = jnp.concatenate([row_angle, col_angle], axis=0)
    angle = jnp.concatenate([angle, angle], axis=0)
    return (jnp.cos(angle), jnp.sin(angle))


def apply_rotary(matrix, cosine, sine):
    half_size = matrix.shape[-2] // 2
    turned = jnp.concatenate([-matrix[..., half_size:, :], matrix[..., :half_size, :]], axis=-2)
    return matrix * cosine + turned * sine


def rotary_back(grad, cosine, sine):
    half_size = grad.shape[-2] // 2
    sined = grad * sine
    turned = jnp.concatenate([sined[..., half_size:, :], -sined[..., :half_size, :]], axis=-2)
    return grad * cosine + turned


def contract(left, right, left_dim, right_dim):
    return lax.dot_general(
        left, right, (((left_dim,), (right_dim,)), ((), ())), preferred_element_type=jnp.float32
    )


def masked_scores(queries, keys_rot, ident, score_scale):
    scores = (
        jnp.einsum("hdk,hdq->hkq", keys_rot, queries, preferred_element_type=jnp.float32)
        * score_scale
    )
    same_pic = ident[:, None] == ident[None, :]
    return jnp.where(same_pic[None], scores, -1000000000.0)


def attend(queries, keys_rot, values_all, ident, score_scale):
    scores = masked_scores(queries, keys_rot, ident, score_scale)
    top_score = jnp.max(scores, axis=1, keepdims=True)
    exp_scores = jnp.exp(scores - top_score)
    total = jnp.sum(exp_scores, axis=1, keepdims=True)
    probs = (exp_scores / total).astype(jnp.bfloat16)
    attended = jnp.einsum("hdk,hkq->hdq", values_all, probs, preferred_element_type=jnp.float32)
    return (attended, (top_score + jnp.log(total))[:, 0, :])


def head_back(query, key, value, grad_head, same_pic, log_total, score_scale):
    scores = jnp.where(same_pic, contract(key, query, 0, 0) * score_scale, -1000000000.0)
    probs = jnp.exp(scores - log_total)
    grad_probs = contract(value, grad_head, 0, 0)
    inner = jnp.sum(probs * grad_probs, axis=0, keepdims=True)
    grad_scores = (probs * (grad_probs - inner)).astype(jnp.bfloat16)
    grad_query = contract(key, grad_scores, 1, 0) * score_scale
    grad_key = contract(query, grad_scores, 1, 1) * score_scale
    grad_value = contract(grad_head, probs.astype(jnp.bfloat16), 1, 1)
    return (grad_query, grad_key, grad_value)


MESH = pl.DeviceIdType.MESH


class Place:
    def __init__(self, n_rep):
        rep = lax.axis_index("rep")
        self.nz = n_rep // 4
        self.half = self.nz // 2
        self.y = lax.axis_index("shard")
        self.z, self.x, self.c = rep // 4, (rep // 2) % 2, rep % 2
        self.low = self.z < self.half
        self.depth = jnp.where(self.low, self.z, self.nz - 1 - self.z)
        side = jnp.where(self.low, 1, -1)
        self.to_core = {"rep": self.z * 4 + self.x * 2 + (1 - self.c)}
        self.to_x = {"rep": self.z * 4 + (1 - self.x) * 2 + self.c}
        self.to_y = {"shard": 1 - self.y}
        self.to_in = {"rep": (self.z + side) * 4 + self.x * 2 + self.c}
        self.to_out = {"rep": (self.z - side) * 4 + self.x * 2 + self.c}

    def at_depth(self, depth):
        return pl.when(self.depth == depth)

    def meet(self, with_y):
        barrier = pltpu.get_barrier_semaphore()
        near = [self.to_core, self.to_x, self.to_in] + ([self.to_y] if with_y else [])
        for device in near:
            pl.semaphore_signal(barrier, inc=1, device_id=device, device_id_type=MESH)

        @pl.when(self.depth > 0)
        def _():
            pl.semaphore_signal(barrier, inc=1, device_id=self.to_out, device_id_type=MESH)

        pl.semaphore_wait(barrier, jnp.where(self.depth > 0, len(near) + 1, len(near)))


def remote(src, dst, sems, k, device):
    return pltpu.make_async_remote_copy(
        src_ref=src,
        dst_ref=dst,
        send_sem=sems.at[0, k],
        recv_sem=sems.at[1, k],
        device_id=device,
        device_id_type=MESH,
    )


def add_into(dst, one, two):
    rows = dst.shape[0]
    step = 32 if rows % 32 == 0 else rows

    @pl.loop(0, rows // step)
    def _(i):
        spot = pl.ds(pl.multiple_of(i * step, step), step)
        total = one[spot, :].astype(jnp.float32) + two[spot, :].astype(jnp.float32)
        dst[spot, :] = total.astype(dst.dtype)


def skewed(count, stages):
    last = max(offset for offset, _ in stages)
    for tick in range(count + last):
        for offset, stage in sorted(stages, key=lambda item: -item[0]):
            if 0 <= tick - offset < count:
                stage(tick - offset)


def cut_chunks(shards):
    rows = min(shard.shape[0] for shard in shards)
    wide = min(shard.shape[1] for shard in shards)
    chunks = []
    for w, shard in enumerate(shards):
        for row0 in range(0, shard.shape[0], rows):
            for col0 in range(0, shard.shape[1], wide):
                chunks.append((w, row0, col0))
    return rows, wide, chunks


def reduce_kernel(n_rep, parts, chunks, shard_rows, rows, wide, *refs):
    count, n_w = len(chunks), len(shard_rows)
    sources, outs, arrived = refs[:n_w], refs[n_w : 2 * n_w], refs[2 * n_w]
    (
        held, lent, got_y, got_x, got_in, got_mid, total,
        own_in, lent_in, put, c0_sem, c1_sem, y_sem, x_sem, in_sem, mid_sem, back_sem,
        ax_sem, ac_sem, af_sem,
    ) = refs[2 * n_w + 1 :]
    c_sems = [c0_sem, c1_sem]
    at = Place(n_rep)
    half = at.half
    block = rows // 4
    with_y = parts == 2
    mine = at.y if with_y else 0

    def source(k, owner, c):
        w, row0, col0 = chunks[k]
        start = pl.multiple_of(owner * shard_rows[w] + row0 + c * 2 * block, 8)
        return sources[w].at[pl.ds(start, 2 * block), pl.ds(col0, wide)]

    def out(k, c, x):
        w, row0, col0 = chunks[k]
        start = pl.multiple_of(row0 + (c * 2 + x) * block, 8)
        return outs[w].at[pl.ds(start, block), pl.ds(col0, wide)]

    def rows_of(x):
        return pl.ds(pl.multiple_of(x * block, 8), block)

    def c_send(k, owner):
        return remote(
            source(k, owner, 1 - at.c), arrived.at[k, owner], c_sems[owner], k, at.to_core
        )

    def own_load(k, owner):
        return pltpu.make_async_copy(
            source(k, owner, at.c), held.at[k, owner], own_in.at[owner, k]
        )

    def lent_load(k, owner):
        return pltpu.make_async_copy(
            arrived.at[k, owner], lent.at[k % 2, owner], lent_in.at[owner, k]
        )

    def y_send(k):
        return remote(held.at[k, 1 - mine], got_y.at[k], y_sem, k, at.to_y)

    def x_send(k):
        return remote(
            held.at[k, mine, rows_of(1 - at.x)], got_x.at[k], x_sem, k, at.to_x
        )

    def part(k):
        return held.at[k, mine, rows_of(at.x)]

    def in_send(k):
        return remote(part(k), got_in.at[k], in_sem, k, at.to_in)

    def mid_send(k):
        return remote(part(k), got_mid.at[k], mid_sem, k, at.to_in)

    def back_send(k):
        return remote(total.at[k], total.at[k], back_sem, k, at.to_out)

    def ax_send(k, x):
        return remote(total.at[k], out(k, at.c, x), ax_sem, k, at.to_x)

    def ac_send(k, c):
        return remote(total.at[k], out(k, c, at.x), ac_sem, k, at.to_core)

    def af_send(k, c):
        view = out(k, c, 1 - at.x)
        return remote(view, view, af_sem, k, at.to_core)

    def own_put(k):
        return pltpu.make_async_copy(total.at[k], out(k, at.c, at.x), put.at[k])

    def start_core(k):
        for owner in range(parts):
            c_send(k, owner).start()
            own_load(k, owner).start()

    def load_core(k):
        for owner in range(parts):
            c_send(k, owner).wait_recv()
            lent_load(k, owner).start()

    def start_y(k):
        for owner in range(parts):
            own_load(k, owner).wait()
            lent_load(k, owner).wait()
        if with_y:
            other = 1 - mine
            add_into(held.at[k, other], held.at[k, other], lent.at[k % 2, other])
            y_send(k).start()
        add_into(held.at[k, mine], held.at[k, mine], lent.at[k % 2, mine])

    def start_x(k):
        if with_y:
            y_send(k).wait_recv()
            spot = rows_of(1 - at.x)
            add_into(held.at[k, mine, spot], held.at[k, mine, spot], got_y.at[k, spot])
        x_send(k).start()
        if with_y:
            add_into(part(k), part(k), got_y.at[k, rows_of(at.x)])

    def inner_send(k, depth):
        (mid_send(k) if depth == half - 1 else in_send(k)).start()

    def start_z(k):
        x_send(k).wait_recv()
        add_into(part(k), part(k), got_x.at[k])

        @at.at_depth(0)
        def _():
            inner_send(k, 0)

    def pass_in(depth):
        def stage(k):
            @at.at_depth(depth)
            def _():
                in_send(k).wait_recv()
                add_into(part(k), part(k), got_in.at[k])
                inner_send(k, depth)

        return stage

    def spread(k, depth):
        if depth > 0:
            back_send(k).start()
        ax_send(k, at.x).start()
        ac_send(k, at.c).start()
        own_put(k).start()

    def middle(k):
        @at.at_depth(half - 1)
        def _():
            mid_send(k).wait_recv()
            add_into(total.at[k], part(k), got_mid.at[k])
            spread(k, half - 1)

    def pass_out(depth):
        def stage(k):
            @at.at_depth(depth)
            def _():
                back_send(k).wait_recv()
                spread(k, depth)

        return stage

    def forward(k):
        ax_send(k, 1 - at.x).wait_recv()
        af_send(k, at.c).start()

    at.meet(with_y)
    stages = [(0, start_core), (1, load_core), (2, start_y), (4, start_x), (5, start_z)]
    stages += [(6 + depth - 1, pass_in(depth)) for depth in range(1, half)]
    stages += [(6 + half - 1, middle)]
    stages += [(6 + half + (half - 2 - depth), pass_out(depth)) for depth in range(half - 1)]
    stages += [(5 + 2 * half, forward)]
    skewed(count, stages)
    for k in range(count):
        for owner in range(parts):
            c_send(k, owner).wait_send()
        if with_y:
            y_send(k).wait_send()
        x_send(k).wait_send()
        for depth in range(half):

            @at.at_depth(depth)
            def _():
                (mid_send(k) if depth == half - 1 else in_send(k)).wait_send()
                if depth > 0:
                    back_send(k).wait_send()

        ax_send(k, at.x).wait_send()
        ac_send(k, at.c).wait_send()
        af_send(k, at.c).wait_send()
        own_put(k).wait()
        ac_send(k, 1 - at.c).wait_recv()
        af_send(k, 1 - at.c).wait_recv()


def reduce_products(products, n_rep, n_shard):
    parts = n_shard
    if n_shard != 2:
        products = [
            lax.psum_scatter(item, "shard", scatter_dimension=0, tiled=True) for item in products
        ]
        parts = 1
    owned = [
        jax.ShapeDtypeStruct((item.shape[0] // parts, item.shape[1]), jnp.bfloat16)
        for item in products
    ]
    rows, wide, chunks = cut_chunks(owned)
    count, block = len(chunks), rows // 4
    kernel = partial(
        reduce_kernel, n_rep, parts, chunks, [item.shape[0] for item in owned], rows, wide
    )
    pair = pltpu.SemaphoreType.DMA((2, count))
    low = jnp.bfloat16
    anywhere = pl.BlockSpec(memory_space=pl.ANY)
    results = pl.pallas_call(
        kernel,
        out_shape=owned + [jax.ShapeDtypeStruct((count, parts, 2 * block, wide), low)],
        in_specs=[anywhere] * len(products),
        out_specs=[anywhere] * (len(products) + 1),
        scratch_shapes=[
            pltpu.VMEM((count, parts, 2 * block, wide), low),
            pltpu.VMEM((2, parts, 2 * block, wide), low),
            pltpu.VMEM((count, 2 * block, wide), low),
            pltpu.VMEM((count, block, wide), low),
            pltpu.VMEM((count, block, wide), low),
            pltpu.VMEM((count, block, wide), low),
            pltpu.VMEM((count, block, wide), low),
            pltpu.SemaphoreType.DMA((parts, count)),
            pltpu.SemaphoreType.DMA((parts, count)),
            pltpu.SemaphoreType.DMA((count,)),
        ]
        + [pair] * 10,
        compiler_params=pltpu.CompilerParams(
            collective_id=1, has_side_effects=True, vmem_limit_bytes=62 << 20
        ),
        name="reduce_products",
    )(*products)
    return results[:-1]


class Cuts:
    def __init__(self, sizes, n_shard):
        self.shard_rows = [left // n_shard for left, _ in sizes]
        self.rows = min(self.shard_rows) // 2
        self.wide = min(right for _, right in sizes)
        self.down = [rows // self.rows for rows in self.shard_rows]
        self.across = [right // self.wide for _, right in sizes]
        self.first = [0]
        for down, across in zip(self.down, self.across):
            self.first.append(self.first[-1] + down * across)
        self.count = self.first[-1]

    def weight_of(self, k, act):
        for w, down in enumerate(self.down):

            @pl.when((k >= self.first[w]) & (k < self.first[w + 1]))
            def _():
                inside = k - self.first[w]
                act(w, inside % down, inside // down)

    def whole(self, chunks, w):
        first, down, rows, wide = self.first[w], self.down[w], self.rows, self.wide

        def widen(part, dst):
            dst[...] = part[0].astype(jnp.float32)

        return pl.pallas_call(
            widen,
            grid=(down, self.across[w]),
            in_specs=[pl.BlockSpec((1, rows, wide), lambda i, j: (first + j * down + i, 0, 0))],
            out_specs=pl.BlockSpec((rows, wide), lambda i, j: (i, j)),
            out_shape=jax.ShapeDtypeStruct(
                (self.shard_rows[w], self.across[w] * wide), jnp.float32
            ),
            compiler_params=pltpu.CompilerParams(vmem_limit_bytes=60 << 20),
            cost_estimate=pl.CostEstimate(
                flops=0,
                transcendentals=0,
                bytes_accessed=6 * down * self.across[w] * rows * wide,
            ),
            name="widen",
        )(chunks)


class LAGS:
    x, z, step, end = 4, 6, 1, 2


def backward_kernel(n_rep, cuts, n_heads, slots, score_scale, *refs):
    (
        left_0, left_1, left_2, left_3, right_0, right_1, qkv, w_qkv, w_up, w_proj,
        hidden, cotangent, patches,
        log_total, pic_key, pic_query, cosine, sine, gain_one, gain_two, down_sum,
        out, right_2, grad_qkv, d_rows, sums, lent_left, lent_right,
        op_left, op_right, held, got_y, got_x, got_in, got_mid, total, swap, w_block,
        pre_block, turned, branch, grad_heads, rows_in, got_sums,
        load_l, load_r, put, once_sem, block_sem, sum_sem,
        l0_sem, l1_sem, r_sem, y_sem, x_sem, in_sem, mid_sem, back_sem, ax_sem, ac_sem, af_sem,
    ) = refs
    lefts = [left_0, left_1, left_2, left_3]
    rights = [right_0, right_1, right_2, grad_qkv]
    l_sems = [l0_sem, l1_sem]
    at = Place(n_rep)
    half = at.half
    count, rows, wide = cuts.count, cuts.rows, cuts.wide
    block, width = rows // 2, wide // 2
    mine = at.y
    head = qkv.shape[0] // (3 * n_heads)
    model = n_heads * head

    def left_rows(w, row, owner):
        start = owner * cuts.shard_rows[w] + row * rows
        return lefts[w].at[pl.ds(pl.multiple_of(start, 16), rows), :]

    def right_rows(w, col, c):
        start = col * wide + c * width
        return rights[w].at[pl.ds(pl.multiple_of(start, 16), width), :]

    def left_push(k, owner, src):
        return remote(src, lent_left.at[k, owner], l_sems[owner], k, at.to_core)

    def right_push(k, src):
        return remote(src, lent_right.at[k], r_sem, k, at.to_core)

    def left_load(k, whose, owner, src):
        slot = k % 2
        return pltpu.make_async_copy(
            src, op_left.at[slot, whose, owner], load_l.at[whose, owner, k]
        )

    def right_load(k, whose, src):
        return pltpu.make_async_copy(src, op_right.at[k % 2, whose], load_r.at[whose, k])

    def rows_of(x):
        return pl.ds(pl.multiple_of(x * block, 16), block)

    def mine_of(k, x):
        return held.at[k % slots, mine, rows_of(x)]

    def y_send(k):
        return remote(held.at[k % slots, 1 - mine], got_y.at[k], y_sem, k, at.to_y)

    def x_send(k):
        return remote(mine_of(k, 1 - at.x), got_x.at[k], x_sem, k, at.to_x)

    def in_send(k):
        return remote(mine_of(k, at.x), got_in.at[k], in_sem, k, at.to_in)

    def mid_send(k):
        return remote(mine_of(k, at.x), got_mid.at[k], mid_sem, k, at.to_in)

    def back_send(k):
        return remote(total.at[k], total.at[k], back_sem, k, at.to_out)

    def out_of(k, c, x):
        cols = pl.ds(pl.multiple_of(c * width, 128), width)
        return out.at[k, rows_of(x), cols]

    def ax_send(k, x):
        return remote(total.at[k], out_of(k, at.c, x), ax_sem, k, at.to_x)

    def ac_send(k, c):
        return remote(total.at[k], out_of(k, c, at.x), ac_sem, k, at.to_core)

    def af_send(k, c):
        view = out_of(k, c, 1 - at.x)
        return remote(view, view, af_sem, k, at.to_core)

    def own_put(k):
        return pltpu.make_async_copy(total.at[k], out_of(k, at.c, at.x), put.at[k])

    def push(k):
        def act(w, row, col):
            for owner in range(2):
                left_push(k, owner, left_rows(w, row, owner)).start()
            right_push(k, right_rows(w, col, 1 - at.c)).start()

        cuts.weight_of(k, act)

    def load(k):
        def act(w, row, col):
            for owner in range(2):
                left_load(k, 0, owner, left_rows(w, row, owner)).start()
            right_load(k, 0, right_rows(w, col, at.c)).start()

        cuts.weight_of(k, act)
        for owner in range(2):
            left_push(k, owner, lent_left.at[k, owner]).wait_recv()
            left_load(k, 1, owner, lent_left.at[k, owner]).start()
        right_push(k, lent_right.at[k]).wait_recv()
        right_load(k, 1, lent_right.at[k]).start()

    def product(k):
        slot = k % 2
        for whose in range(2):
            for owner in range(2):
                left_load(k, whose, owner, lent_left.at[k, owner]).wait()
            right_load(k, whose, lent_right.at[k]).wait()
        for owner in range(2):
            left_push(k, owner, lent_left.at[k, owner]).wait_send()
        right_push(k, lent_right.at[k]).wait_send()
        for owner in (1 - mine, mine):
            result = contract(op_left[slot, 0, owner], op_right[slot, 0], 1, 1)
            result += contract(op_left[slot, 1, owner], op_right[slot, 1], 1, 1)
            held[k % slots, owner] = result.astype(jnp.bfloat16)
            if owner is not mine:
                y_send(k).start()

    def start_x(k):
        y_send(k).wait_recv()
        other = mine_of(k, 1 - at.x)
        add_into(other, other, got_y.at[k, rows_of(1 - at.x)])
        x_send(k).start()
        own = mine_of(k, at.x)
        add_into(own, own, got_y.at[k, rows_of(at.x)])
        y_send(k).wait_send()

    def inner_send(k, depth):
        return mid_send(k) if depth == half - 1 else in_send(k)

    def start_z(k):
        x_send(k).wait_recv()
        own = mine_of(k, at.x)
        add_into(own, own, got_x.at[k])

        @at.at_depth(0)
        def _():
            inner_send(k, 0).start()

        x_send(k).wait_send()

    def pass_in(depth):
        def stage(k):
            @at.at_depth(depth)
            def _():
                in_send(k).wait_recv()
                own = mine_of(k, at.x)
                add_into(own, own, got_in.at[k])
                inner_send(k, depth).start()

        return stage

    def spread(k, depth):
        if depth > 0:
            back_send(k).start()
        ax_send(k, at.x).start()
        ac_send(k, at.c).start()
        own_put(k).start()

    def middle(k):
        @at.at_depth(half - 1)
        def _():
            mid_send(k).wait_recv()
            add_into(total.at[k], mine_of(k, at.x), got_mid.at[k])
            spread(k, half - 1)

    def pass_out(depth):
        def stage(k):
            @at.at_depth(depth)
            def _():
                back_send(k).wait_recv()
                spread(k, depth)

        return stage

    def sent(k):
        for depth in range(half):

            @at.at_depth(depth)
            def _():
                inner_send(k, depth).wait_send()

    def forward(k):
        ax_send(k, 1 - at.x).wait_recv()
        af_send(k, at.c).start()

    def finish(k):
        @pl.when(at.depth > 0)
        def _():
            back_send(k).wait_send()

        ax_send(k, at.x).wait_send()
        ac_send(k, at.c).wait_send()
        af_send(k, at.c).wait_send()
        own_put(k).wait()
        ac_send(k, 1 - at.c).wait_recv()
        af_send(k, 1 - at.c).wait_recv()

    def head_step(h):
        def part(i):
            return pl.ds(pl.multiple_of(i * model + h * head, 16), head)

        query, key, value = swap[part(0), :], swap[part(1), :], swap[part(2), :]
        grads = head_back(
            query,
            key,
            value,
            grad_heads[part(0), :],
            pic_key[...] == pic_query[...],
            log_total[pl.ds(h, 1), :],
            score_scale,
        )
        grad_query, grad_key, grad_value = grads
        turn_c, turn_s = cosine[...], sine[...]
        swap[part(0), :] = rotary_back(grad_query, turn_c, turn_s).astype(jnp.bfloat16)
        swap[part(1), :] = rotary_back(grad_key, turn_c, turn_s).astype(jnp.bfloat16)
        swap[part(2), :] = grad_value.astype(jnp.bfloat16)

    tokens = qkv.shape[1]
    wide_two = right_1.shape[0]
    n_up, n_qkv = wide_two // width, qkv.shape[0] // width
    ends = [0]
    for size in (model, model, wide_two, model, model, model, qkv.shape[0], model):
        ends.append(ends[-1] + size)

    def sums_of(i, start=0, size=model):
        return pl.ds(pl.multiple_of(ends[i] + start, 128), size)

    def column_sums(block):
        ones = jnp.ones((8, tokens), jnp.bfloat16)
        return contract(ones, block, 1, 1)[0:1, :]

    def w_load(src, j, slot):
        cols = pl.ds(pl.multiple_of(j * width, 128), width)
        return lambda k: pltpu.make_async_copy(src.at[:, cols], w_block.at[slot], block_sem.at[0, k])

    def pre_load(j, slot):
        spot = pl.ds(pl.multiple_of(j * width, 16), width)
        return pltpu.make_async_copy(right_1.at[spot, :], pre_block.at[slot], block_sem.at[1, j])

    def once(i, src, dst):
        return pltpu.make_async_copy(src, dst, once_sem.at[i])

    def add_turned(slot, right):
        step = 256

        @pl.loop(0, model // step)
        def _(i):
            spot = pl.ds(pl.multiple_of(i * step, 16), step)
            turned[spot, :] += contract(w_block[slot, spot, :], right, 1, 0)

    def clear_turned():
        turned[...] = jnp.zeros_like(turned)

    def load_up(pair):
        for slot in range(2):
            j = pair * 2 + slot
            w_load(w_up, j, slot)(j).start()
            pre_load(j, slot).start()

    def up_step(pair):
        for slot in range(2):
            j = pair * 2 + slot
            w_load(w_up, j, slot)(j).wait()
            pre_load(j, slot).wait()
            block = pre_block[slot]
            add_turned(slot, block)
            sums[:, sums_of(2, j * width, width)] = column_sums(block)

    def load_proj():
        for slot in range(2):
            w_load(w_proj, slot, slot)(n_up + slot).start()

    def load_qkv(pair):
        for slot in range(2):
            j = pair * 2 + slot
            w_load(w_qkv, j, slot)(n_up + 2 + j).start()

    def qkv_step(pair):
        for slot in range(2):
            j = pair * 2 + slot
            w_load(w_qkv, j, slot)(n_up + 2 + j).wait()
            block = swap[pl.ds(pl.multiple_of(j * width, 16), width), :]
            add_turned(slot, block)
            sums[:, sums_of(6, j * width, width)] = column_sums(block)

    step = 128

    def norm_two():
        once(2, hidden, d_rows).wait()
        once(3, cotangent, rows_in).wait()

        @pl.loop(0, tokens // step)
        def _(i):
            spot = pl.ds(pl.multiple_of(i * step, 16), step)
            lanes = pl.ds(pl.multiple_of(i * step, 128), step)
            standard, inverse = apply_layer_norm(d_rows[spot, :])
            grad = turned[:, lanes].T
            sums[:, sums_of(0)] += jnp.sum(grad * standard, axis=0, keepdims=True)
            sums[:, sums_of(1)] += jnp.sum(grad, axis=0, keepdims=True)
            back = norm_gradient_step(grad, standard, inverse, gain_two[...])
            back = back + rows_in[spot, :].astype(jnp.float32)
            d_rows[spot, :] = back
            low = back.astype(jnp.bfloat16)
            branch[:, lanes] = low.T

        sums[:, sums_of(7)] = column_sums(branch[...])
        once(4, patches, rows_in).start()
        once(5, branch, right_2).start()
        for slot in range(2):
            w_load(w_proj, slot, slot)(n_up + slot).wait()

        @pl.loop(0, model // step)
        def _(i):
            spot = pl.ds(pl.multiple_of(i * step, 16), step)
            result = contract(w_block[0, spot, :], branch[pl.ds(0, width), :], 1, 0)
            result += contract(w_block[1, spot, :], branch[pl.ds(width, width), :], 1, 0)
            grad_heads[spot, :] = result.astype(jnp.bfloat16)

        once(5, branch, right_2).wait()
        clear_turned()

    def norm_one():
        once(4, patches, rows_in).wait()

        @pl.loop(0, tokens // step)
        def _(i):
            spot = pl.ds(pl.multiple_of(i * step, 16), step)
            lanes = pl.ds(pl.multiple_of(i * step, 128), step)
            standard, inverse = apply_layer_norm(rows_in[spot, :].astype(jnp.float32))
            grad = turned[:, lanes].T
            sums[:, sums_of(4)] += jnp.sum(grad * standard, axis=0, keepdims=True)
            sums[:, sums_of(5)] += jnp.sum(grad, axis=0, keepdims=True)
            d_rows[spot, :] += norm_gradient_step(grad, standard, inverse, gain_one[...])

    def sums_to(i, device):
        return remote(sums, got_sums.at[i], sum_sem, i, device)

    def swap_sums(i, device):
        def begin():
            sums_to(i, device).start()

        def end():
            sums_to(i, device).wait()
            sums[...] += got_sums[i]

        return begin, end

    def sums_in(depth):
        def act():
            @at.at_depth(depth)
            def _():
                if depth > 0:
                    sums_to(3, at.to_in).wait_recv()
                    sums[...] += got_sums[3]
                sums_to(4 if depth == half - 1 else 3, at.to_in).start()

            @at.at_depth(depth - 1)
            def _():
                if depth > 0:
                    sums_to(3, at.to_in).wait_send()

        return act

    def sums_middle():
        @at.at_depth(half - 1)
        def _():
            sums_to(4, at.to_in).wait()
            sums[...] += got_sums[4]
            if half > 1:
                sums_to(5, at.to_out).start()

    def sums_out(depth):
        def act():
            @at.at_depth(depth)
            def _():
                sums_to(5, at.to_out).wait_recv()
                sums[...] = got_sums[5]
                if depth > 0:
                    sums_to(5, at.to_out).start()

            @at.at_depth(depth + 1)
            def _():
                sums_to(5, at.to_out).wait_send()

        return act

    take_qkv = once(0, qkv, swap)
    give_qkv = once(1, swap, grad_qkv)
    take_qkv.start()
    once(2, hidden, d_rows).start()
    once(3, cotangent, rows_in).start()
    at.meet(True)
    load_up(0)
    clear_turned()
    sums[...] = jnp.zeros_like(sums)
    sums[:, sums_of(3)] = down_sum[...]
    take_qkv.wait()
    stages = [(0, push), (1, load), (2, product), (LAGS.x, start_x), (LAGS.z, start_z)]
    stages += [(LAGS.z + LAGS.step * depth, pass_in(depth)) for depth in range(1, half)]
    middle_lag = LAGS.z + LAGS.step * half
    stages += [(middle_lag, middle)]
    stages += [
        (middle_lag + LAGS.step * (half - 1 - depth), pass_out(depth)) for depth in range(half - 1)
    ]
    forward_lag = middle_lag + LAGS.step * (half - 1) + 2
    stages += [(slots + 2, sent), (forward_lag, forward), (forward_lag + LAGS.end, finish)]
    stages.sort(key=lambda item: -item[0])
    per_tick = 2
    at_norm = n_up // 2
    at_heads = at_norm + 1
    at_qkv = at_heads + -(-n_heads // per_tick)
    at_one = at_qkv + n_qkv // 2
    begins, ends_of = zip(
        swap_sums(0, at.to_core), swap_sums(1, at.to_x), swap_sums(2, at.to_y)
    )
    events = {at_norm: [norm_two], at_one: [norm_one, begins[0]]}
    now = at_one
    for i in range(3):
        now += 1
        events[now] = [ends_of[i]] + ([begins[i + 1]] if i < 2 else [sums_in(0)])
    for act in (
        [sums_in(depth) for depth in range(1, half)]
        + [sums_middle]
        + [sums_out(depth) for depth in reversed(range(half - 1))]
    ):
        now += 1
        events[now] = [act]
    last = count + forward_lag + LAGS.end
    assert now < last and at_norm < cuts.first[2] and at_qkv < cuts.first[3]

    def tick_body(tick, carry):
        for offset, stage in stages:

            @pl.when((tick >= offset) & (tick < count + offset))
            def _():
                stage(tick - offset)

        @pl.when(tick < at_norm)
        def _():
            up_step(tick)

        @pl.when(tick < at_norm - 1)
        def _():
            load_up(tick + 1)

        @pl.when(tick == at_norm - 1)
        def _():
            load_proj()

        for when, acts in events.items():

            @pl.when(tick == when)
            def _():
                for act in acts:
                    act()

        @pl.when((tick >= at_heads) & (tick < at_qkv))
        def _():
            @pl.loop(0, per_tick)
            def _(i):
                h = (tick - at_heads) * per_tick + i

                @pl.when(h < n_heads)
                def _():
                    head_step(h)

        @pl.when(tick == at_qkv)
        def _():
            give_qkv.start()
            give_qkv.wait()

        @pl.when((tick >= at_qkv) & (tick < at_one))
        def _():
            qkv_step(tick - at_qkv)

        @pl.when((tick >= at_qkv - 1) & (tick < at_one - 1))
        def _():
            load_qkv(tick - at_qkv + 1)

        return carry

    lax.fori_loop(0, last, tick_body, 0)


def reduce_backward(lefts, rights, others, small, n_rep, n_heads, score_scale):
    qkv, _, w_up, w_proj, hidden = others[:5]
    tokens, model = hidden.shape
    sizes = [(left.shape[0], right) for left, right in zip(lefts, (model, w_up.shape[1], model))]
    sizes.append((model, qkv.shape[0]))
    cuts = Cuts(sizes, 2)
    half = n_rep // 8
    slots = LAGS.z + LAGS.step * half + 1 - 2
    count, rows, wide = cuts.count, cuts.rows, cuts.wide
    block, width = rows // 2, wide // 2
    n_sums = 6 * model + w_up.shape[1] + qkv.shape[0]
    low, full, dma = jnp.bfloat16, jnp.float32, pltpu.SemaphoreType.DMA
    anywhere, local = pl.BlockSpec(memory_space=pl.ANY), pl.BlockSpec(memory_space=pltpu.VMEM)
    n_blocks = (w_up.shape[1] + qkv.shape[0]) // width + 2
    chunks, _, _, d_rows, sums, _, _ = pl.pallas_call(
        partial(backward_kernel, n_rep, cuts, n_heads, slots, score_scale),
        out_shape=[
            jax.ShapeDtypeStruct((count, rows, wide), low),
            jax.ShapeDtypeStruct((model, tokens), low),
            jax.ShapeDtypeStruct(qkv.shape, low),
            jax.ShapeDtypeStruct((tokens, model), full),
            jax.ShapeDtypeStruct((1, n_sums), full),
            jax.ShapeDtypeStruct((count, 2, rows, tokens), low),
            jax.ShapeDtypeStruct((count, width, tokens), low),
        ],
        in_specs=[anywhere] * (len(lefts) + len(rights) + len(others)) + [local] * len(small),
        out_specs=[anywhere] * 3 + [local] * 2 + [anywhere] * 2,
        scratch_shapes=[
            pltpu.VMEM((2, 2, 2, rows, tokens), low),
            pltpu.VMEM((2, 2, width, tokens), low),
            pltpu.VMEM((slots, 2, rows, width), low),
            pltpu.VMEM((count, rows, width), low),
            pltpu.VMEM((count, block, width), low),
            pltpu.VMEM((count, block, width), low),
            pltpu.VMEM((count, block, width), low),
            pltpu.VMEM((count, block, width), low),
            pltpu.VMEM(qkv.shape, low),
            pltpu.VMEM((2, model, width), low),
            pltpu.VMEM((2, width, tokens), low),
            pltpu.VMEM((model, tokens), full),
            pltpu.VMEM((model, tokens), low),
            pltpu.VMEM((model, tokens), low),
            pltpu.VMEM((tokens, model), low),
            pltpu.VMEM((6, 1, n_sums), full),
            dma((2, 2, count)),
            dma((2, count)),
            dma((count,)),
            dma((6,)),
            dma((2, n_blocks)),
            dma((2, 6)),
        ]
        + [dma((2, count))] * 11,
        compiler_params=pltpu.CompilerParams(
            collective_id=1, has_side_effects=True, vmem_limit_bytes=63 << 20
        ),
        name="reduce_backward",
    )(*lefts, *rights, *others, *small)
    return [cuts.whole(chunks, w) for w in range(len(sizes))], d_rows, sums[0]


def forward_kernel(n_rep, cuts, n_heads, score_scale, *refs):
    n_w = len(cuts.down)
    shards, refs = refs[:n_w], refs[n_w:]
    (
        normed, patches, cotangent, qkv_bias, proj_bias, gain, bias, up_bias, down_bias,
        pic_key, pic_query, cosine, sine,
    ) = refs[:13]
    fulls, refs = refs[13 : 13 + n_w], refs[13 + n_w :]
    (
        swap, heads_out, log_total, hidden, two_turned, act_turned, pre_turned, layer_out,
        hold, w_block, turned, up_pre, act, out_sum, normed_two,
        own_in, own_out, w_sem, y_sem, d_sem, in_sem, mid_sem, back_sem, x_sem, c_sem, cd_sem,
    ) = refs
    at = Place(n_rep)
    nz, half = at.nz, at.half
    count, rows, wide = cuts.count, cuts.rows, cuts.wide
    plane = rows * 4 // 5
    unit = plane // n_rep
    straight = (rows - plane) // 2
    mine, yours = at.y, 1 - at.y
    model = normed.shape[1]
    tokens = normed.shape[0]
    head = model // n_heads

    def shard(w, row, col, first, size):
        start = pl.multiple_of(row * rows + first, 16)
        cols = pl.ds(pl.multiple_of(col * wide, 128), wide)
        return shards[w].at[pl.ds(start, size), cols]

    def full(w, row, col, owner, first, size):
        start = pl.multiple_of(owner * cuts.shard_rows[w] + row * rows + first, 16)
        cols = pl.ds(pl.multiple_of(col * wide, 128), wide)
        return fulls[w].at[pl.ds(start, size), cols]

    def alike(size):
        return fulls[0].at[pl.ds(0, size), pl.ds(0, wide)]

    def place(c, x, z):
        return ((c * 2 + x) * nz + z) * unit

    def spread_copy(k, first, size, sems, device):
        def act_on(w, row, col):
            view = full(w, row, col, yours, first, size)
            remote(view, view, sems, k, device).start()

        cuts.weight_of(k, act_on)

    def settle(k, size, sems, device, received):
        view = alike(size)
        copy = remote(view, view, sems, k, device)
        if received:
            copy.wait_recv()
        else:
            copy.wait_send()

    def along(k, begin, size, sems, device):
        spread_copy(k, place(at.c, at.x, begin), size * unit, sems, device)

    def start_y(k):
        def act_on(w, row, col):
            first = place(at.c, at.x, at.z)
            remote(
                shard(w, row, col, first, unit),
                full(w, row, col, mine, first, unit),
                y_sem, k, at.to_y,
            ).start()
            first = plane + at.c * straight
            remote(
                shard(w, row, col, first, straight),
                full(w, row, col, mine, first, straight),
                d_sem, k, at.to_y,
            ).start()

        cuts.weight_of(k, act_on)

    def inner_send(k, depth):
        if depth == half - 1:
            along(k, jnp.where(at.low, 0, half), half, mid_sem, at.to_in)
        else:
            along(k, jnp.where(at.low, 0, nz - 1 - depth), depth + 1, in_sem, at.to_in)

    def back_start(k, depth):
        along(k, jnp.where(at.low, depth, 0), nz - depth, back_sem, at.to_out)

    def x_start(k):
        along(k, 0, nz, x_sem, at.to_x)

    def crossed(k):
        settle(k, unit, y_sem, at.to_y, True)

        @at.at_depth(0)
        def _():
            inner_send(k, 0)

        settle(k, straight, d_sem, at.to_y, True)
        spread_copy(k, plane + at.c * straight, straight, cd_sem, at.to_core)

    def pass_in(depth):
        def stage(k):
            @at.at_depth(depth)
            def _():
                settle(k, depth * unit, in_sem, at.to_in, True)
                inner_send(k, depth)

        return stage

    def middle(k):
        @at.at_depth(half - 1)
        def _():
            settle(k, half * unit, mid_sem, at.to_in, True)
            if half > 1:
                back_start(k, half - 1)
            x_start(k)

    def pass_out(depth):
        def stage(k):
            @at.at_depth(depth)
            def _():
                settle(k, (nz - depth - 1) * unit, back_sem, at.to_out, True)
                if depth > 0:
                    back_start(k, depth)
                x_start(k)

        return stage

    def crossed_x(k):
        settle(k, nz * unit, x_sem, at.to_x, True)
        spread_copy(k, place(at.c, 0, 0), 2 * nz * unit, c_sem, at.to_core)

    def own_load(k, view):
        return pltpu.make_async_copy(view, hold.at[k % 3], own_in.at[k])

    def own_store(k, view):
        return pltpu.make_async_copy(hold.at[k % 3], view, own_out.at[k])

    def take_own(k):
        cuts.weight_of(k, lambda w, row, col: own_load(k, shard(w, row, col, 0, rows)).start())

    def give_own(k):
        own_load(k, alike(rows)).wait()
        cuts.weight_of(
            k, lambda w, row, col: own_store(k, full(w, row, col, mine, 0, rows)).start()
        )

    def arrived(k):
        own_store(k, alike(rows)).wait()
        settle(k, 2 * nz * unit, c_sem, at.to_core, True)
        settle(k, straight, cd_sem, at.to_core, True)
        settle(k, unit, y_sem, at.to_y, False)
        settle(k, straight, d_sem, at.to_y, False)
        settle(k, nz * unit, x_sem, at.to_x, False)
        settle(k, 2 * nz * unit, c_sem, at.to_core, False)
        settle(k, straight, cd_sem, at.to_core, False)
        for depth in range(half):

            @at.at_depth(depth)
            def _():
                if depth == half - 1:
                    settle(k, half * unit, mid_sem, at.to_in, False)
                else:
                    settle(k, (depth + 1) * unit, in_sem, at.to_in, False)
                if depth > 0:
                    settle(k, (nz - depth) * unit, back_sem, at.to_out, False)

    def block_of(u, view):
        return pltpu.make_async_copy(view, w_block.at[u % 2], w_sem.at[0, u])

    def half_block(u, owner, view):
        spot = pl.ds(owner * (wide // 2), wide // 2)
        return pltpu.make_async_copy(view, w_block.at[u % 2, spot, :], w_sem.at[owner, u])

    def columns(w, col):
        return fulls[w].at[:, pl.ds(pl.multiple_of(col * wide, 128), wide)]

    def down_rows(i, owner):
        start = owner * cuts.shard_rows[3] + i * (wide // 2)
        return fulls[3].at[pl.ds(pl.multiple_of(start, 16), wide // 2), :]

    step = 256

    def qkv_step(b, u):
        block_of(u, columns(0, 0)).wait()

        @pl.loop(0, wide // step)
        def _(i):
            spot = pl.ds(pl.multiple_of(i * step, 128), step)
            col = pl.ds(pl.multiple_of(b * wide + i * step, 128), step)
            part = contract(normed[...], w_block[u % 2, :, spot], 1, 0) + qkv_bias[:, col]
            turned[pl.ds(pl.multiple_of(i * step, 16), step), :] = part.T

        @pl.loop(0, n_heads)
        def _(h):
            part = turned[pl.ds(pl.multiple_of(h * head, 8), head), :]
            spot = pl.ds(pl.multiple_of(b * model + h * head, 16), head)

            @pl.when(b < 2)
            def _():
                swap[spot, :] = apply_rotary(part, cosine[...], sine[...]).astype(jnp.bfloat16)

            @pl.when(b == 2)
            def _():
                swap[spot, :] = part.astype(jnp.bfloat16)

    def head_step(h):
        def part(i):
            return swap[pl.ds(pl.multiple_of(i * model + h * head, 16), head), :]

        scores = contract(part(1), part(0), 0, 0) * score_scale
        scores = jnp.where(pic_key[...] == pic_query[...], scores, -1000000000.0)
        top = jnp.max(scores, axis=0, keepdims=True)
        exp_scores = jnp.exp(scores - top)
        total = jnp.sum(exp_scores, axis=0, keepdims=True)
        probs = (exp_scores / total).astype(jnp.bfloat16)
        attended = contract(part(2), probs, 1, 0)
        heads_out[pl.ds(pl.multiple_of(h * head, 16), head), :] = attended.astype(jnp.bfloat16)
        log_total[pl.ds(h, 1), :] = top + jnp.log(total)

    def proj_step(u):
        block_of(u, columns(0, 0)).wait()

        @pl.loop(0, tokens // step)
        def _(i):
            spot = pl.ds(pl.multiple_of(i * step, 16), step)
            lanes = pl.ds(pl.multiple_of(i * step, 128), step)
            branch = contract(heads_out[:, lanes], w_block[u % 2], 0, 0)
            rows_in = patches[spot, :].astype(jnp.float32) + branch + proj_bias[...]
            hidden[spot, :] = rows_in
            out_sum[spot, :] = rows_in + down_bias[...]
            standard, _ = apply_layer_norm(rows_in)
            result = (standard * gain[...] + bias[...]).astype(jnp.bfloat16)
            normed_two[spot, :] = result
            two_turned[:, lanes] = result.T

    def up_step(c, u):
        block_of(u, columns(0, 0)).wait()

        @pl.loop(0, wide // step)
        def _(i):
            spot = pl.ds(pl.multiple_of(i * step, 128), step)
            col = pl.multiple_of(c * wide + i * step, 128)
            cols = pl.ds(col, step)
            pre = contract(normed_two[...], w_block[u % 2, :, spot], 1, 0) + up_bias[:, cols]
            up_pre[:, cols] = pre
            result = (pre / (1.0 + jnp.exp(-quick_slope * pre))).astype(jnp.bfloat16)
            act[:, cols] = result
            act_turned[pl.ds(col, step), :] = result.T

    def down_step(i, u):
        for owner in range(2):
            half_block(u, owner, down_rows(0, 0)).wait()
            size = wide // 2
            col = pl.multiple_of(owner * cuts.shard_rows[3] + i * size, 128)

            @pl.loop(0, tokens // step)
            def _(j):
                spot = pl.ds(pl.multiple_of(j * step, 16), step)
                lanes = pl.ds(pl.multiple_of(j * step, 128), step)
                weight = w_block[u % 2, pl.ds(owner * size, size), :]
                pre = up_pre[spot, pl.ds(col, size)]
                sigmoid = 1.0 / (1.0 + jnp.exp(-quick_slope * pre))
                slope = sigmoid + quick_slope * pre * sigmoid * (1.0 - sigmoid)
                grad = contract(cotangent[spot, :], weight, 1, 1) * slope
                pre_turned[pl.ds(col, size), lanes] = grad.astype(jnp.bfloat16).T
                out_sum[spot, :] += contract(act[spot, pl.ds(col, size)], weight, 1, 0)

    gap = 2
    across = 1 + gap * 2 * half
    offset = across + 1
    stages = [(1, crossed)]
    stages += [(1 + gap * depth, pass_in(depth)) for depth in range(1, half)]
    stages += [(1 + gap * half, middle)]
    stages += [
        (1 + gap * (2 * half - 1 - depth), pass_out(depth)) for depth in range(half - 1)
    ]
    stages += [(across, crossed_x)]
    stages += [(offset - 2, take_own), (offset - 1, give_own), (offset, arrived)]
    stages.sort(key=lambda item: -item[0])
    n_up, n_down = cuts.across[2], cuts.down[3] // 2
    per_tick = 3
    first_head = cuts.first[1] + 1
    at_proj = first_head + -(-n_heads // per_tick)
    at_up = at_proj + 1
    at_down = max(at_up + n_up, cuts.first[3] + 2)
    n_steps = 4 + n_up + n_down

    at.meet(True)

    @pl.loop(0, count)
    def _(k):
        start_y(k)

    def tick_body(tick, carry):
        for lag, stage in stages:

            @pl.when((tick >= lag) & (tick < count + lag))
            def _():
                stage(tick - lag)

        now = tick - offset

        @pl.when((now >= 2) & (now < first_head) & (now % 2 == 0))
        def _():
            qkv_step(now // 2 - 1, now // 2 - 1)

        @pl.when((now >= first_head) & (now < at_proj))
        def _():
            @pl.loop(0, per_tick)
            def _(i):
                h = (now - first_head) * per_tick + i

                @pl.when(h < n_heads)
                def _():
                    head_step(h)

        @pl.when(now == at_proj)
        def _():
            proj_step(3)

        @pl.when((now >= at_up) & (now < at_up + n_up))
        def _():
            up_step(now - at_up, now - at_up + 4)

        down_i = (now - at_down) // 2

        @pl.when((now >= at_down) & (down_i < n_down) & ((now - at_down) % 2 == 0))
        def _():
            down_step(down_i, down_i + 4 + n_up)

        soon = now + 1

        @pl.when((soon >= 2) & (soon < first_head) & (soon % 2 == 0))
        def _():
            block_of(soon // 2 - 1, columns(0, soon // 2 - 1)).start()

        @pl.when(soon == at_proj)
        def _():
            block_of(3, columns(1, 0)).start()

        @pl.when((soon >= at_up) & (soon < at_up + n_up))
        def _():
            block_of(soon - at_up + 4, columns(2, soon - at_up)).start()

        next_i = (soon - at_down) // 2

        @pl.when((soon >= at_down) & (next_i < n_down) & ((soon - at_down) % 2 == 0))
        def _():
            for owner in range(2):
                half_block(next_i + 4 + n_up, owner, down_rows(next_i, owner)).start()

        return carry

    lax.fori_loop(0, offset + at_down + 2 * n_down - 1, tick_body, 0)
    layer_out[...] = out_sum[...].astype(jnp.bfloat16)


def gather_forward(shards, inputs, n_rep, n_heads, score_scale):
    cuts = Cuts([(shard.shape[0] * 2, shard.shape[1]) for shard in shards], 2)
    tokens, model = inputs[0].shape
    wide_two = shards[2].shape[1]
    count, rows, wide = cuts.count, cuts.rows, cuts.wide
    low, dma = jnp.bfloat16, pltpu.SemaphoreType.DMA
    anywhere, local = pl.BlockSpec(memory_space=pl.ANY), pl.BlockSpec(memory_space=pltpu.VMEM)
    n_steps = 4 + cuts.across[2] + cuts.down[3] // 2

    def shape(*sizes, kind=low):
        return jax.ShapeDtypeStruct(sizes, kind)

    results = pl.pallas_call(
        partial(forward_kernel, n_rep, cuts, n_heads, score_scale),
        out_shape=[shape(item.shape[0] * 2, item.shape[1]) for item in shards]
        + [
            shape(3 * model, tokens),
            shape(model, tokens),
            shape(n_heads, tokens, kind=jnp.float32),
            shape(tokens, model, kind=jnp.float32),
            shape(model, tokens),
            shape(wide_two, tokens),
            shape(wide_two, tokens),
            shape(tokens, model),
        ],
        in_specs=[anywhere] * len(shards) + [local] * len(inputs),
        out_specs=[anywhere] * len(shards) + [local] * 8,
        scratch_shapes=[
            pltpu.VMEM((3, rows, wide), low),
            pltpu.VMEM((2, model, wide), low),
            pltpu.VMEM((model, tokens), jnp.float32),
            pltpu.VMEM((tokens, wide_two), jnp.float32),
            pltpu.VMEM((tokens, wide_two), low),
            pltpu.VMEM((tokens, model), jnp.float32),
            pltpu.VMEM((tokens, model), low),
            dma((count,)),
            dma((count,)),
            dma((2, n_steps)),
        ]
        + [dma((2, count))] * 8,
        compiler_params=pltpu.CompilerParams(
            collective_id=0, has_side_effects=True, vmem_limit_bytes=63 << 20
        ),
        name="gather_forward",
    )(*shards, *inputs)
    return results[: len(shards)], results[len(shards) :]


class Links:
    def __init__(self, n_rep, n_shard):
        self.nz, self.ny, self.n_rep = n_rep // 4, n_shard, n_rep
        self.y = lax.axis_index("shard")

    def gather_vector(self, vector):
        if self.ny != 2:
            return lax.all_gather(vector, "shard", axis=0, tiled=False)
        other = lax.ppermute(vector, "shard", [(0, 1), (1, 0)])
        low, high = jnp.where(self.y == 0, vector, other), jnp.where(self.y == 0, other, vector)
        return jnp.stack([low, high])

    def sum_all(self, vector):
        for flip in (1, 2):
            vector = vector + lax.ppermute(
                vector, "rep", [(i, i ^ flip) for i in range(self.n_rep)]
            )
        step = 1
        while step < self.nz:
            pairs = [(i, i ^ (4 * step)) for i in range(self.n_rep)]
            vector = vector + lax.ppermute(vector, "rep", pairs)
            step *= 2
        step = 1
        while step < self.ny:
            pairs = [(i, i ^ step) for i in range(self.ny)]
            vector = vector + lax.ppermute(vector, "shard", pairs)
            step *= 2
        return vector


def per_device(
    patches,
    lengths,
    positions,
    ln1_gain,
    ln1_bias,
    qkv_weight,
    qkv_bias,
    proj_weight,
    proj_bias,
    ln2_gain,
    ln2_bias,
    fc1_weight,
    fc1_bias,
    fc2_weight,
    fc2_bias,
    cotangent,
    n_rep,
    n_shard,
):
    links = Links(n_rep, n_shard)
    pack_count = lengths.shape[0]
    row_count = patches.shape[0]
    length = row_count // pack_count
    model_width = patches.shape[1]
    head_count = HEADS
    head_size = model_width // head_count
    score_scale = head_size ** (-0.5)
    pic_ends = jnp.cumsum(lengths[:, :-1], axis=1)
    slot_index = jnp.arange(length, dtype=jnp.int32)
    idents = jnp.sum((slot_index[None, :, None] >= pic_ends[:, None, :]).astype(jnp.int32), axis=2)
    pack_index = jnp.arange(pack_count, dtype=jnp.int32)
    idents = (idents + pack_index[:, None] * lengths.shape[1]).reshape(-1)
    cosine, sine = rotary_tables(positions, head_size)

    small = [ln1_gain, ln1_bias, qkv_bias, proj_bias, ln2_gain, ln2_bias, fc1_bias, fc2_bias]
    sizes = [item.shape[0] for item in small]
    spots = [sum(sizes[:i]) for i in range(len(sizes) + 1)]
    packed = sum(
        jnp.pad(item, (spots[i], spots[-1] - spots[i + 1])) for i, item in enumerate(small)
    )
    gathered = links.gather_vector(packed)
    (
        first_norm_gain, first_norm_bias, b_qkv, b_proj,
        second_norm_gain, second_norm_bias, b_up, b_down,
    ) = [
        gathered[:, spots[i] : spots[i + 1]].reshape(-1).astype(jnp.float32)
        for i in range(len(sizes))
    ]

    input_rows = patches.astype(jnp.float32)
    first_centered_standard, first_inverse_spread = apply_layer_norm(input_rows)
    first_normalized = (first_centered_standard * first_norm_gain + first_norm_bias).astype(
        jnp.bfloat16
    )
    shards = [qkv_weight, proj_weight, fc1_weight, fc2_weight]
    qkv_shape = (3 * model_width, row_count)
    grad_out = cotangent.astype(jnp.float32)
    d_b_down = jnp.sum(grad_out, axis=0)
    if n_shard == 2:
        rows_in = [
            item[None, :]
            for item in (b_qkv, b_proj, second_norm_gain, second_norm_bias, b_up, b_down)
        ]
        inputs = [first_normalized, patches, cotangent] + rows_in
        inputs += [idents[:, None], idents[None, :], cosine, sine]
        weights, results = gather_forward(shards, inputs, n_rep, head_count, score_scale)
        w_qkv, w_proj, w_up, w_down = weights
        qkv, heads_out, log_total, hidden_rows, second_turned = results[:5]
        activation, grad_pre, layer_out = results[5:]
        others = [qkv, w_qkv, w_up, w_proj, hidden_rows, cotangent, patches]
        row_args = [first_norm_gain[None, :], second_norm_gain[None, :], d_b_down[None, :]]
        small_args = [log_total, idents[:, None], idents[None, :], cosine, sine] + row_args
        lefts = [activation, second_turned, heads_out, first_normalized.T]
        rights = [cotangent.T, grad_pre]
        products, d_patches, total = reduce_backward(
            lefts, rights, others, small_args, n_rep, head_count, score_scale
        )
    else:
        w_qkv, w_proj, w_up, w_down = [
            lax.all_gather(shard, "shard", axis=0, tiled=True) for shard in shards
        ]
        qkv_rows = contract(w_qkv, first_normalized, 0, 1) + b_qkv[:, None]
        qkv_rows = qkv_rows.reshape(3, head_count, head_size, row_count)
        queries = apply_rotary(qkv_rows[0], cosine, sine).astype(jnp.bfloat16)
        keys_rot = apply_rotary(qkv_rows[1], cosine, sine).astype(jnp.bfloat16)
        values_all = qkv_rows[2].astype(jnp.bfloat16)
        attended, log_total = attend(queries, keys_rot, values_all, idents, score_scale)
        heads_out = attended.reshape(model_width, row_count).astype(jnp.bfloat16)
        hidden_rows = input_rows + contract(heads_out, w_proj, 0, 0) + b_proj
        second_centered_standard, second_inverse_spread = apply_layer_norm(hidden_rows)
        second_normalized = (
            second_centered_standard * second_norm_gain + second_norm_bias
        ).astype(jnp.bfloat16)
        up_pre = contract(w_up, second_normalized, 0, 1) + b_up[:, None]
        sigmoid_up = 1.0 / (1.0 + jnp.exp(-quick_slope * up_pre))
        activation = (up_pre * sigmoid_up).astype(jnp.bfloat16)
        out_full = hidden_rows + contract(activation, w_down, 0, 0) + b_down
        layer_out = out_full.astype(jnp.bfloat16)
        grad_act = contract(w_down, cotangent, 1, 1)
        slope_up = sigmoid_up + quick_slope * up_pre * sigmoid_up * (1.0 - sigmoid_up)
        grad_pre = (grad_act * slope_up).astype(jnp.bfloat16)
        d_b_up = jnp.sum(grad_pre.astype(jnp.float32), axis=1)
        second_normalized_gradient = contract(grad_pre, w_up, 0, 1)
        second_gain_gradient = jnp.sum(
            second_normalized_gradient * second_centered_standard, axis=0
        )
        d_bias_two = jnp.sum(second_normalized_gradient, axis=0)
        grad_hidden = grad_out + norm_gradient_step(
            second_normalized_gradient,
            second_centered_standard,
            second_inverse_spread,
            second_norm_gain,
        )
        grad_branch = grad_hidden.astype(jnp.bfloat16)
        d_b_proj = jnp.sum(grad_branch.astype(jnp.float32), axis=0)
        grad_heads = contract(w_proj, grad_branch, 1, 1).astype(jnp.bfloat16)
        back = partial(head_back, score_scale=score_scale)
        grad_query, grad_key, grad_value = jax.vmap(back, in_axes=(0, 0, 0, 0, None, 0))(
            queries,
            keys_rot,
            values_all,
            grad_heads.reshape(head_count, head_size, row_count),
            idents[:, None] == idents[None, :],
            log_total[:, None, :],
        )
        grad_query = rotary_back(grad_query, cosine, sine)
        grad_key = rotary_back(grad_key, cosine, sine)
        grad_qkv = jnp.stack([grad_query, grad_key, grad_value]).reshape(qkv_shape)
        grad_qkv = grad_qkv.astype(jnp.bfloat16)
        first_normalized_gradient = contract(grad_qkv, w_qkv, 0, 1)
        lefts = [activation, second_normalized.T, heads_out, first_normalized.T]
        rights = [cotangent.T, grad_pre, grad_branch.T, grad_qkv]
        products = [
            contract(left, right, 1, 1).astype(jnp.bfloat16) for left, right in zip(lefts, rights)
        ]
        products = [
            item.astype(jnp.float32) for item in reduce_products(products, n_rep, n_shard)
        ]
        d_b_qkv = jnp.sum(grad_qkv.astype(jnp.float32), axis=1)
        first_gain_gradient = jnp.sum(first_normalized_gradient * first_centered_standard, axis=0)
        d_bias_one = jnp.sum(first_normalized_gradient, axis=0)
        d_patches = grad_hidden + norm_gradient_step(
            first_normalized_gradient,
            first_centered_standard,
            first_inverse_spread,
            first_norm_gain,
        )
        total = jnp.concatenate(
            [
                second_gain_gradient, d_bias_two, d_b_up, d_b_down,
                first_gain_gradient, d_bias_one, d_b_qkv, d_b_proj,
            ]
        )
        total = links.sum_all(total)
    d_w_down, d_w_up, d_w_proj, d_w_qkv = products

    ff = fc1_weight.shape[1]
    own_parts, start = [], 0
    for size in (
        model_width, model_width, ff, model_width,
        model_width, model_width, 3 * model_width, model_width,
    ):
        own = size // n_shard
        own_parts.append(lax.dynamic_slice_in_dim(total, start + links.y * own, own, 0))
        start += size
    m_gain, m_bias, m_upb, m_downb, a_gain, a_bias, a_qkvb, a_projb = own_parts
    return (
        layer_out,
        d_patches,
        a_gain,
        a_bias,
        d_w_qkv,
        a_qkvb,
        d_w_proj,
        a_projb,
        m_gain,
        m_bias,
        d_w_up,
        m_upb,
        d_w_down,
        m_downb,
    )


def solution(mesh):
    rows, whole = P(("rep", "shard"), None), P("shard")
    matrix = P("shard", None)
    in_specs = (
        rows,
        rows,
        P(None, ("rep", "shard")),
        whole,
        whole,
        matrix,
        whole,
        matrix,
        whole,
        whole,
        whole,
        matrix,
        whole,
        matrix,
        whole,
        rows,
    )
    out_specs = (
        rows,
        rows,
        whole,
        whole,
        matrix,
        whole,
        matrix,
        whole,
        whole,
        whole,
        matrix,
        whole,
        matrix,
        whole,
    )
    body = partial(per_device, n_rep=mesh.shape["rep"], n_shard=mesh.shape["shard"])
    return jax.shard_map(
        body, mesh=mesh, in_specs=in_specs, out_specs=out_specs, check_vma=False
    )
```

```python
from functools import partial

import jax
import jax.numpy as jnp
from jax import lax
from jax.experimental import pallas as pl
from jax.experimental.pallas import tpu as pltpu
from jax.sharding import PartitionSpec as P

HEADS = 16


norm_eps = 1e-06
quick_slope = 1.702


def apply_layer_norm(matrix):
    center = matrix - jnp.mean(matrix, axis=-1, keepdims=True)
    spread = jnp.mean(center * center, axis=-1, keepdims=True)
    inverse_spread = lax.rsqrt(spread + norm_eps)
    return (center * inverse_spread, inverse_spread)


def norm_gradient_step(normalized_gradient, centered_standard, inverse_spread, norm_gain):
    scaled_rows = normalized_gradient * norm_gain
    return inverse_spread * (
        scaled_rows
        - jnp.mean(scaled_rows, axis=-1, keepdims=True)
        - centered_standard * jnp.mean(scaled_rows * centered_standard, axis=-1, keepdims=True)
    )


def rotary_tables(positions, head_size):
    quarter = head_size // 4
    counter = jnp.arange(quarter, dtype=jnp.float32)
    inverse = jnp.power(jnp.float32(10000.0), -2.0 * counter / (head_size // 2))
    row_angle = inverse[:, None] * positions[0].astype(jnp.float32)[None, :]
    col_angle = inverse[:, None] * positions[1].astype(jnp.float32)[None, :]
    angle = jnp.concatenate([row_angle, col_angle], axis=0)
    angle = jnp.concatenate([angle, angle], axis=0)
    return (jnp.cos(angle), jnp.sin(angle))


def apply_rotary(matrix, cosine, sine):
    half_size = matrix.shape[-2] // 2
    turned = jnp.concatenate([-matrix[..., half_size:, :], matrix[..., :half_size, :]], axis=-2)
    return matrix * cosine + turned * sine


def rotary_back(grad, cosine, sine):
    half_size = grad.shape[-2] // 2
    sined = grad * sine
    turned = jnp.concatenate([sined[..., half_size:, :], -sined[..., :half_size, :]], axis=-2)
    return grad * cosine + turned


def contract(left, right, left_dim, right_dim):
    return lax.dot_general(
        left, right, (((left_dim,), (right_dim,)), ((), ())), preferred_element_type=jnp.float32
    )


def masked_scores(queries, keys_rot, ident, score_scale):
    scores = (
        jnp.einsum("hdk,hdq->hkq", keys_rot, queries, preferred_element_type=jnp.float32)
        * score_scale
    )
    same_pic = ident[:, None] == ident[None, :]
    return jnp.where(same_pic[None], scores, -1000000000.0)


def attend(queries, keys_rot, values_all, ident, score_scale):
    scores = masked_scores(queries, keys_rot, ident, score_scale)
    top_score = jnp.max(scores, axis=1, keepdims=True)
    exp_scores = jnp.exp(scores - top_score)
    total = jnp.sum(exp_scores, axis=1, keepdims=True)
    probs = (exp_scores / total).astype(jnp.bfloat16)
    attended = jnp.einsum("hdk,hkq->hdq", values_all, probs, preferred_element_type=jnp.float32)
    return (attended, (top_score + jnp.log(total))[:, 0, :])


def head_back(query, key, value, grad_head, same_pic, log_total, score_scale):
    scores = jnp.where(same_pic, contract(key, query, 0, 0) * score_scale, -1000000000.0)
    probs = jnp.exp(scores - log_total)
    grad_probs = contract(value, grad_head, 0, 0)
    inner = jnp.sum(probs * grad_probs, axis=0, keepdims=True)
    grad_scores = (probs * (grad_probs - inner)).astype(jnp.bfloat16)
    grad_query = contract(key, grad_scores, 1, 0) * score_scale
    grad_key = contract(query, grad_scores, 1, 1) * score_scale
    grad_value = contract(grad_head, probs.astype(jnp.bfloat16), 1, 1)
    return (grad_query, grad_key, grad_value)


MESH = pl.DeviceIdType.MESH


class Place:
    def __init__(self, n_rep):
        rep = lax.axis_index("rep")
        self.nz = n_rep // 4
        self.half = self.nz // 2
        self.y = lax.axis_index("shard")
        self.z, self.x, self.c = rep // 4, (rep // 2) % 2, rep % 2
        self.low = self.z < self.half
        self.depth = jnp.where(self.low, self.z, self.nz - 1 - self.z)
        side = jnp.where(self.low, 1, -1)
        self.to_core = {"rep": self.z * 4 + self.x * 2 + (1 - self.c)}
        self.to_x = {"rep": self.z * 4 + (1 - self.x) * 2 + self.c}
        self.to_y = {"shard": 1 - self.y}
        self.to_in = {"rep": (self.z + side) * 4 + self.x * 2 + self.c}
        self.to_out = {"rep": (self.z - side) * 4 + self.x * 2 + self.c}

    def at_depth(self, depth):
        return pl.when(self.depth == depth)

    def meet(self, with_y):
        barrier = pltpu.get_barrier_semaphore()
        near = [self.to_core, self.to_x, self.to_in] + ([self.to_y] if with_y else [])
        for device in near:
            pl.semaphore_signal(barrier, inc=1, device_id=device, device_id_type=MESH)

        @pl.when(self.depth > 0)
        def _():
            pl.semaphore_signal(barrier, inc=1, device_id=self.to_out, device_id_type=MESH)

        pl.semaphore_wait(barrier, jnp.where(self.depth > 0, len(near) + 1, len(near)))


def remote(src, dst, sems, k, device):
    return pltpu.make_async_remote_copy(
        src_ref=src,
        dst_ref=dst,
        send_sem=sems.at[0, k],
        recv_sem=sems.at[1, k],
        device_id=device,
        device_id_type=MESH,
    )


def add_into(dst, one, two):
    rows = dst.shape[0]
    step = 32 if rows % 32 == 0 else rows

    @pl.loop(0, rows // step)
    def _(i):
        spot = pl.ds(pl.multiple_of(i * step, step), step)
        total = one[spot, :].astype(jnp.float32) + two[spot, :].astype(jnp.float32)
        dst[spot, :] = total.astype(dst.dtype)


def skewed(count, stages):
    last = max(offset for offset, _ in stages)
    for tick in range(count + last):
        for offset, stage in sorted(stages, key=lambda item: -item[0]):
            if 0 <= tick - offset < count:
                stage(tick - offset)


def cut_chunks(shards):
    rows = min(shard.shape[0] for shard in shards)
    wide = min(shard.shape[1] for shard in shards)
    chunks = []
    for w, shard in enumerate(shards):
        for row0 in range(0, shard.shape[0], rows):
            for col0 in range(0, shard.shape[1], wide):
                chunks.append((w, row0, col0))
    return rows, wide, chunks


def reduce_kernel(n_rep, parts, chunks, shard_rows, rows, wide, *refs):
    count, n_w = len(chunks), len(shard_rows)
    sources, outs, arrived = refs[:n_w], refs[n_w : 2 * n_w], refs[2 * n_w]
    (
        held, lent, got_y, got_x, got_in, got_mid, total,
        own_in, lent_in, put, c0_sem, c1_sem, y_sem, x_sem, in_sem, mid_sem, back_sem,
        ax_sem, ac_sem, af_sem,
    ) = refs[2 * n_w + 1 :]
    c_sems = [c0_sem, c1_sem]
    at = Place(n_rep)
    half = at.half
    block = rows // 4
    with_y = parts == 2
    mine = at.y if with_y else 0

    def source(k, owner, c):
        w, row0, col0 = chunks[k]
        start = pl.multiple_of(owner * shard_rows[w] + row0 + c * 2 * block, 8)
        return sources[w].at[pl.ds(start, 2 * block), pl.ds(col0, wide)]

    def out(k, c, x):
        w, row0, col0 = chunks[k]
        start = pl.multiple_of(row0 + (c * 2 + x) * block, 8)
        return outs[w].at[pl.ds(start, block), pl.ds(col0, wide)]

    def rows_of(x):
        return pl.ds(pl.multiple_of(x * block, 8), block)

    def c_send(k, owner):
        return remote(
            source(k, owner, 1 - at.c), arrived.at[k, owner], c_sems[owner], k, at.to_core
        )

    def own_load(k, owner):
        return pltpu.make_async_copy(
            source(k, owner, at.c), held.at[k, owner], own_in.at[owner, k]
        )

    def lent_load(k, owner):
        return pltpu.make_async_copy(
            arrived.at[k, owner], lent.at[k % 2, owner], lent_in.at[owner, k]
        )

    def y_send(k):
        return remote(held.at[k, 1 - mine], got_y.at[k], y_sem, k, at.to_y)

    def x_send(k):
        return remote(
            held.at[k, mine, rows_of(1 - at.x)], got_x.at[k], x_sem, k, at.to_x
        )

    def part(k):
        return held.at[k, mine, rows_of(at.x)]

    def in_send(k):
        return remote(part(k), got_in.at[k], in_sem, k, at.to_in)

    def mid_send(k):
        return remote(part(k), got_mid.at[k], mid_sem, k, at.to_in)

    def back_send(k):
        return remote(total.at[k], total.at[k], back_sem, k, at.to_out)

    def ax_send(k, x):
        return remote(total.at[k], out(k, at.c, x), ax_sem, k, at.to_x)

    def ac_send(k, c):
        return remote(total.at[k], out(k, c, at.x), ac_sem, k, at.to_core)

    def af_send(k, c):
        view = out(k, c, 1 - at.x)
        return remote(view, view, af_sem, k, at.to_core)

    def own_put(k):
        return pltpu.make_async_copy(total.at[k], out(k, at.c, at.x), put.at[k])

    def start_core(k):
        for owner in range(parts):
            c_send(k, owner).start()
            own_load(k, owner).start()

    def load_core(k):
        for owner in range(parts):
            c_send(k, owner).wait_recv()
            lent_load(k, owner).start()

    def start_y(k):
        for owner in range(parts):
            own_load(k, owner).wait()
            lent_load(k, owner).wait()
        if with_y:
            other = 1 - mine
            add_into(held.at[k, other], held.at[k, other], lent.at[k % 2, other])
            y_send(k).start()
        add_into(held.at[k, mine], held.at[k, mine], lent.at[k % 2, mine])

    def start_x(k):
        if with_y:
            y_send(k).wait_recv()
            spot = rows_of(1 - at.x)
            add_into(held.at[k, mine, spot], held.at[k, mine, spot], got_y.at[k, spot])
        x_send(k).start()
        if with_y:
            add_into(part(k), part(k), got_y.at[k, rows_of(at.x)])

    def inner_send(k, depth):
        (mid_send(k) if depth == half - 1 else in_send(k)).start()

    def start_z(k):
        x_send(k).wait_recv()
        add_into(part(k), part(k), got_x.at[k])

        @at.at_depth(0)
        def _():
            inner_send(k, 0)

    def pass_in(depth):
        def stage(k):
            @at.at_depth(depth)
            def _():
                in_send(k).wait_recv()
                add_into(part(k), part(k), got_in.at[k])
                inner_send(k, depth)

        return stage

    def spread(k, depth):
        if depth > 0:
            back_send(k).start()
        ax_send(k, at.x).start()
        ac_send(k, at.c).start()
        own_put(k).start()

    def middle(k):
        @at.at_depth(half - 1)
        def _():
            mid_send(k).wait_recv()
            add_into(total.at[k], part(k), got_mid.at[k])
            spread(k, half - 1)

    def pass_out(depth):
        def stage(k):
            @at.at_depth(depth)
            def _():
                back_send(k).wait_recv()
                spread(k, depth)

        return stage

    def forward(k):
        ax_send(k, 1 - at.x).wait_recv()
        af_send(k, at.c).start()

    at.meet(with_y)
    stages = [(0, start_core), (1, load_core), (2, start_y), (4, start_x), (5, start_z)]
    stages += [(6 + depth - 1, pass_in(depth)) for depth in range(1, half)]
    stages += [(6 + half - 1, middle)]
    stages += [(6 + half + (half - 2 - depth), pass_out(depth)) for depth in range(half - 1)]
    stages += [(5 + 2 * half, forward)]
    skewed(count, stages)
    for k in range(count):
        for owner in range(parts):
            c_send(k, owner).wait_send()
        if with_y:
            y_send(k).wait_send()
        x_send(k).wait_send()
        for depth in range(half):

            @at.at_depth(depth)
            def _():
                (mid_send(k) if depth == half - 1 else in_send(k)).wait_send()
                if depth > 0:
                    back_send(k).wait_send()

        ax_send(k, at.x).wait_send()
        ac_send(k, at.c).wait_send()
        af_send(k, at.c).wait_send()
        own_put(k).wait()
        ac_send(k, 1 - at.c).wait_recv()
        af_send(k, 1 - at.c).wait_recv()


def reduce_products(products, n_rep, n_shard):
    parts = n_shard
    if n_shard != 2:
        products = [
            lax.psum_scatter(item, "shard", scatter_dimension=0, tiled=True) for item in products
        ]
        parts = 1
    owned = [
        jax.ShapeDtypeStruct((item.shape[0] // parts, item.shape[1]), jnp.bfloat16)
        for item in products
    ]
    rows, wide, chunks = cut_chunks(owned)
    count, block = len(chunks), rows // 4
    kernel = partial(
        reduce_kernel, n_rep, parts, chunks, [item.shape[0] for item in owned], rows, wide
    )
    pair = pltpu.SemaphoreType.DMA((2, count))
    low = jnp.bfloat16
    anywhere = pl.BlockSpec(memory_space=pl.ANY)
    results = pl.pallas_call(
        kernel,
        out_shape=owned + [jax.ShapeDtypeStruct((count, parts, 2 * block, wide), low)],
        in_specs=[anywhere] * len(products),
        out_specs=[anywhere] * (len(products) + 1),
        scratch_shapes=[
            pltpu.VMEM((count, parts, 2 * block, wide), low),
            pltpu.VMEM((2, parts, 2 * block, wide), low),
            pltpu.VMEM((count, 2 * block, wide), low),
            pltpu.VMEM((count, block, wide), low),
            pltpu.VMEM((count, block, wide), low),
            pltpu.VMEM((count, block, wide), low),
            pltpu.VMEM((count, block, wide), low),
            pltpu.SemaphoreType.DMA((parts, count)),
            pltpu.SemaphoreType.DMA((parts, count)),
            pltpu.SemaphoreType.DMA((count,)),
        ]
        + [pair] * 10,
        compiler_params=pltpu.CompilerParams(
            collective_id=1, has_side_effects=True, vmem_limit_bytes=62 << 20
        ),
        name="reduce_products",
    )(*products)
    return results[:-1]


class Cuts:
    def __init__(self, sizes, n_shard):
        self.shard_rows = [left // n_shard for left, _ in sizes]
        self.rows = min(self.shard_rows) // 2
        self.wide = min(right for _, right in sizes)
        self.down = [rows // self.rows for rows in self.shard_rows]
        self.across = [right // self.wide for _, right in sizes]
        self.first = [0]
        for down, across in zip(self.down, self.across):
            self.first.append(self.first[-1] + down * across)
        self.count = self.first[-1]

    def weight_of(self, k, act):
        for w, down in enumerate(self.down):

            @pl.when((k >= self.first[w]) & (k < self.first[w + 1]))
            def _():
                inside = k - self.first[w]
                act(w, inside % down, inside // down)

    def whole(self, chunks, w):
        first, down, rows, wide = self.first[w], self.down[w], self.rows, self.wide

        pair = 2

        def widen(part, dst):
            for i in range(pair):
                dst[pl.ds(i * rows, rows), :] = part[i].astype(jnp.float32)

        return pl.pallas_call(
            widen,
            grid=(down // pair, self.across[w]),
            in_specs=[
                pl.BlockSpec((pair, rows, wide), lambda i, j: ((first + j * down) // pair + i, 0, 0))
            ],
            out_specs=pl.BlockSpec((pair * rows, wide), lambda i, j: (i, j)),
            out_shape=jax.ShapeDtypeStruct(
                (self.shard_rows[w], self.across[w] * wide), jnp.float32
            ),
            compiler_params=pltpu.CompilerParams(vmem_limit_bytes=60 << 20),
            cost_estimate=pl.CostEstimate(
                flops=0,
                transcendentals=0,
                bytes_accessed=6 * down * self.across[w] * rows * wide,
            ),
            name="widen",
        )(chunks)


class LAGS:
    x, z, step, end = 4, 6, 1, 2


def backward_kernel(n_rep, cuts, n_heads, slots, score_scale, *refs):
    (
        left_0, left_1, left_2, left_3, right_0, right_1, qkv, w_qkv, w_up, w_proj,
        hidden, cotangent, patches,
        log_total, pic_key, pic_query, cosine, sine, vectors,
        out, right_2, grad_qkv, d_rows, sums, lent_left, lent_right,
        op_left, op_right, held, got_y, got_x, got_in, got_mid, total, swap, w_block,
        pre_block, turned, branch, grad_heads, rows_in, got_sums,
        load_l, load_r, put, once_sem, block_sem, sum_sem,
        l0_sem, l1_sem, r_sem, y_sem, x_sem, in_sem, mid_sem, back_sem, ax_sem, ac_sem, af_sem,
    ) = refs
    lefts = [left_0, left_1, left_2, left_3]
    rights = [right_0, right_1, right_2, grad_qkv]
    l_sems = [l0_sem, l1_sem]
    at = Place(n_rep)
    half = at.half
    count, rows, wide = cuts.count, cuts.rows, cuts.wide
    block, width = rows // 2, wide // 2
    mine = at.y
    head = qkv.shape[0] // (3 * n_heads)
    model = n_heads * head

    def left_rows(w, row, owner):
        start = owner * cuts.shard_rows[w] + row * rows
        return lefts[w].at[pl.ds(pl.multiple_of(start, 16), rows), :]

    def right_rows(w, col, c):
        start = col * wide + c * width
        return rights[w].at[pl.ds(pl.multiple_of(start, 16), width), :]

    def left_push(k, owner, src):
        return remote(src, lent_left.at[k, owner], l_sems[owner], k, at.to_core)

    def right_push(k, src):
        return remote(src, lent_right.at[k], r_sem, k, at.to_core)

    def left_load(k, whose, owner, src):
        slot = k % 2
        return pltpu.make_async_copy(
            src, op_left.at[slot, whose, owner], load_l.at[whose, owner, k]
        )

    def right_load(k, whose, src):
        return pltpu.make_async_copy(src, op_right.at[k % 2, whose], load_r.at[whose, k])

    def rows_of(x):
        return pl.ds(pl.multiple_of(x * block, 16), block)

    def mine_of(k, x):
        return held.at[k % slots, mine, rows_of(x)]

    def y_send(k):
        return remote(held.at[k % slots, 1 - mine], got_y.at[k], y_sem, k, at.to_y)

    def x_send(k):
        return remote(mine_of(k, 1 - at.x), got_x.at[k], x_sem, k, at.to_x)

    def in_send(k):
        return remote(mine_of(k, at.x), got_in.at[k], in_sem, k, at.to_in)

    def mid_send(k):
        return remote(mine_of(k, at.x), got_mid.at[k], mid_sem, k, at.to_in)

    def back_send(k):
        return remote(total.at[k], total.at[k], back_sem, k, at.to_out)

    def out_of(k, c, x):
        cols = pl.ds(pl.multiple_of(c * width, 128), width)
        return out.at[k, rows_of(x), cols]

    def ax_send(k, x):
        return remote(total.at[k], out_of(k, at.c, x), ax_sem, k, at.to_x)

    def ac_send(k, c):
        return remote(total.at[k], out_of(k, c, at.x), ac_sem, k, at.to_core)

    def af_send(k, c):
        view = out_of(k, c, 1 - at.x)
        return remote(view, view, af_sem, k, at.to_core)

    def own_put(k):
        return pltpu.make_async_copy(total.at[k], out_of(k, at.c, at.x), put.at[k])

    def push(k):
        def act(w, row, col):
            for owner in range(2):
                left_push(k, owner, left_rows(w, row, owner)).start()
            right_push(k, right_rows(w, col, 1 - at.c)).start()

        cuts.weight_of(k, act)

    def load(k):
        def act(w, row, col):
            for owner in range(2):
                left_load(k, 0, owner, left_rows(w, row, owner)).start()
            right_load(k, 0, right_rows(w, col, at.c)).start()

        cuts.weight_of(k, act)
        for owner in range(2):
            left_push(k, owner, lent_left.at[k, owner]).wait_recv()
            left_load(k, 1, owner, lent_left.at[k, owner]).start()
        right_push(k, lent_right.at[k]).wait_recv()
        right_load(k, 1, lent_right.at[k]).start()

    def product(k):
        slot = k % 2
        for whose in range(2):
            for owner in range(2):
                left_load(k, whose, owner, lent_left.at[k, owner]).wait()
            right_load(k, whose, lent_right.at[k]).wait()
        for owner in range(2):
            left_push(k, owner, lent_left.at[k, owner]).wait_send()
        right_push(k, lent_right.at[k]).wait_send()
        for owner in (1 - mine, mine):
            result = contract(op_left[slot, 0, owner], op_right[slot, 0], 1, 1)
            result += contract(op_left[slot, 1, owner], op_right[slot, 1], 1, 1)
            held[k % slots, owner] = result.astype(jnp.bfloat16)
            if owner is not mine:
                y_send(k).start()

    def start_x(k):
        y_send(k).wait_recv()
        other = mine_of(k, 1 - at.x)
        add_into(other, other, got_y.at[k, rows_of(1 - at.x)])
        x_send(k).start()
        own = mine_of(k, at.x)
        add_into(own, own, got_y.at[k, rows_of(at.x)])
        y_send(k).wait_send()

    def inner_send(k, depth):
        return mid_send(k) if depth == half - 1 else in_send(k)

    def start_z(k):
        x_send(k).wait_recv()
        own = mine_of(k, at.x)
        add_into(own, own, got_x.at[k])

        @at.at_depth(0)
        def _():
            inner_send(k, 0).start()

        x_send(k).wait_send()

    def pass_in(depth):
        def stage(k):
            @at.at_depth(depth)
            def _():
                in_send(k).wait_recv()
                own = mine_of(k, at.x)
                add_into(own, own, got_in.at[k])
                inner_send(k, depth).start()

        return stage

    def spread(k, depth):
        if depth > 0:
            back_send(k).start()
        ax_send(k, at.x).start()
        ac_send(k, at.c).start()
        own_put(k).start()

    def middle(k):
        @at.at_depth(half - 1)
        def _():
            mid_send(k).wait_recv()
            add_into(total.at[k], mine_of(k, at.x), got_mid.at[k])
            spread(k, half - 1)

    def pass_out(depth):
        def stage(k):
            @at.at_depth(depth)
            def _():
                back_send(k).wait_recv()
                spread(k, depth)

        return stage

    def sent(k):
        for depth in range(half):

            @at.at_depth(depth)
            def _():
                inner_send(k, depth).wait_send()

    def forward(k):
        ax_send(k, 1 - at.x).wait_recv()
        af_send(k, at.c).start()

    def finish(k):
        @pl.when(at.depth > 0)
        def _():
            back_send(k).wait_send()

        ax_send(k, at.x).wait_send()
        ac_send(k, at.c).wait_send()
        af_send(k, at.c).wait_send()
        own_put(k).wait()
        ac_send(k, 1 - at.c).wait_recv()
        af_send(k, 1 - at.c).wait_recv()

    def head_step(h):
        def part(i):
            return pl.ds(pl.multiple_of(i * model + h * head, 16), head)

        query, key, value = swap[part(0), :], swap[part(1), :], swap[part(2), :]
        grads = head_back(
            query,
            key,
            value,
            grad_heads[part(0), :],
            pic_key[...] == pic_query[...],
            log_total[pl.ds(h, 1), :],
            score_scale,
        )
        grad_query, grad_key, grad_value = grads
        turn_c, turn_s = cosine[...], sine[...]
        swap[part(0), :] = rotary_back(grad_query, turn_c, turn_s).astype(jnp.bfloat16)
        swap[part(1), :] = rotary_back(grad_key, turn_c, turn_s).astype(jnp.bfloat16)
        swap[part(2), :] = grad_value.astype(jnp.bfloat16)

    tokens = qkv.shape[1]
    wide_two = right_1.shape[0]
    n_up, n_qkv = wide_two // width, qkv.shape[0] // width
    starts = [0]
    for size in vector_sizes(model, wide_two):
        starts.append(starts[-1] + size)
    ends = [0]
    for size in (model, model, wide_two, model, model, model, qkv.shape[0], model):
        ends.append(ends[-1] + size)

    def sums_of(i, start=0, size=model):
        return pl.ds(pl.multiple_of(ends[i] + start, 128), size)

    def column_sums(block):
        ones = jnp.ones((8, tokens), jnp.bfloat16)
        return contract(ones, block, 1, 1)[0:1, :]

    def w_load(src, j, slot):
        cols = pl.ds(pl.multiple_of(j * width, 128), width)
        return lambda k: pltpu.make_async_copy(src.at[:, cols], w_block.at[slot], block_sem.at[0, k])

    def pre_load(j, slot):
        spot = pl.ds(pl.multiple_of(j * width, 16), width)
        return pltpu.make_async_copy(right_1.at[spot, :], pre_block.at[slot], block_sem.at[1, j])

    def once(i, src, dst):
        return pltpu.make_async_copy(src, dst, once_sem.at[i])

    def add_turned(slot, right):
        step = 256

        @pl.loop(0, model // step)
        def _(i):
            spot = pl.ds(pl.multiple_of(i * step, 16), step)
            turned[spot, :] += contract(w_block[slot, spot, :], right, 1, 0)

    def clear_turned():
        turned[...] = jnp.zeros_like(turned)

    def load_up(pair):
        for slot in range(2):
            j = pair * 2 + slot
            w_load(w_up, j, slot)(j).start()
            pre_load(j, slot).start()

    def up_step(pair):
        for slot in range(2):
            j = pair * 2 + slot
            w_load(w_up, j, slot)(j).wait()
            pre_load(j, slot).wait()
            block = pre_block[slot]
            add_turned(slot, block)
            sums[:, sums_of(2, j * width, width)] = column_sums(block)

    def load_proj():
        for slot in range(2):
            w_load(w_proj, slot, slot)(n_up + slot).start()

    def load_qkv(pair):
        for slot in range(2):
            j = pair * 2 + slot
            w_load(w_qkv, j, slot)(n_up + 2 + j).start()

    def qkv_step(pair):
        for slot in range(2):
            j = pair * 2 + slot
            w_load(w_qkv, j, slot)(n_up + 2 + j).wait()
            block = swap[pl.ds(pl.multiple_of(j * width, 16), width), :]
            add_turned(slot, block)
            sums[:, sums_of(6, j * width, width)] = column_sums(block)

    step = 128

    def norm_two():
        once(2, hidden, d_rows).wait()
        once(3, cotangent, rows_in).wait()

        @pl.loop(0, tokens // step)
        def _(i):
            spot = pl.ds(pl.multiple_of(i * step, 16), step)
            lanes = pl.ds(pl.multiple_of(i * step, 128), step)
            standard, inverse = apply_layer_norm(d_rows[spot, :])
            grad = turned[:, lanes].T
            sums[:, sums_of(0)] += jnp.sum(grad * standard, axis=0, keepdims=True)
            sums[:, sums_of(1)] += jnp.sum(grad, axis=0, keepdims=True)
            back = norm_gradient_step(grad, standard, inverse, vectors[:, pl.ds(starts[4], model)])
            back = back + rows_in[spot, :].astype(jnp.float32)
            d_rows[spot, :] = back
            low = back.astype(jnp.bfloat16)
            branch[:, lanes] = low.T

        sums[:, sums_of(7)] = column_sums(branch[...])
        once(4, patches, rows_in).start()
        once(5, branch, right_2).start()
        for slot in range(2):
            w_load(w_proj, slot, slot)(n_up + slot).wait()

        @pl.loop(0, model // step)
        def _(i):
            spot = pl.ds(pl.multiple_of(i * step, 16), step)
            result = contract(w_block[0, spot, :], branch[pl.ds(0, width), :], 1, 0)
            result += contract(w_block[1, spot, :], branch[pl.ds(width, width), :], 1, 0)
            grad_heads[spot, :] = result.astype(jnp.bfloat16)

        once(5, branch, right_2).wait()
        clear_turned()

    def norm_one():
        once(4, patches, rows_in).wait()

        @pl.loop(0, tokens // step)
        def _(i):
            spot = pl.ds(pl.multiple_of(i * step, 16), step)
            lanes = pl.ds(pl.multiple_of(i * step, 128), step)
            standard, inverse = apply_layer_norm(rows_in[spot, :].astype(jnp.float32))
            grad = turned[:, lanes].T
            sums[:, sums_of(4)] += jnp.sum(grad * standard, axis=0, keepdims=True)
            sums[:, sums_of(5)] += jnp.sum(grad, axis=0, keepdims=True)
            d_rows[spot, :] += norm_gradient_step(grad, standard, inverse, vectors[:, pl.ds(starts[0], model)])

    def sums_to(i, device):
        return remote(sums, got_sums.at[i], sum_sem, i, device)

    def swap_sums(i, device):
        def begin():
            sums_to(i, device).start()

        def end():
            sums_to(i, device).wait()
            sums[...] += got_sums[i]

        return begin, end

    def sums_in(depth):
        def act():
            @at.at_depth(depth)
            def _():
                if depth > 0:
                    sums_to(3, at.to_in).wait_recv()
                    sums[...] += got_sums[3]
                sums_to(4 if depth == half - 1 else 3, at.to_in).start()

            @at.at_depth(depth - 1)
            def _():
                if depth > 0:
                    sums_to(3, at.to_in).wait_send()

        return act

    def sums_middle():
        @at.at_depth(half - 1)
        def _():
            sums_to(4, at.to_in).wait()
            sums[...] += got_sums[4]
            if half > 1:
                sums_to(5, at.to_out).start()

    def sums_out(depth):
        def act():
            @at.at_depth(depth)
            def _():
                sums_to(5, at.to_out).wait_recv()
                sums[...] = got_sums[5]
                if depth > 0:
                    sums_to(5, at.to_out).start()

            @at.at_depth(depth + 1)
            def _():
                sums_to(5, at.to_out).wait_send()

        return act

    take_qkv = once(0, qkv, swap)
    give_qkv = once(1, swap, grad_qkv)
    take_qkv.start()
    once(2, hidden, d_rows).start()
    once(3, cotangent, rows_in).start()
    at.meet(True)
    load_up(0)
    clear_turned()
    sums[...] = jnp.zeros_like(sums)
    sums[:, sums_of(3)] = vectors[:, pl.ds(starts[-1], model)]
    take_qkv.wait()
    stages = [(0, push), (1, load), (2, product), (LAGS.x, start_x), (LAGS.z, start_z)]
    stages += [(LAGS.z + LAGS.step * depth, pass_in(depth)) for depth in range(1, half)]
    middle_lag = LAGS.z + LAGS.step * half
    stages += [(middle_lag, middle)]
    stages += [
        (middle_lag + LAGS.step * (half - 1 - depth), pass_out(depth)) for depth in range(half - 1)
    ]
    forward_lag = middle_lag + LAGS.step * (half - 1) + 2
    stages += [(slots + 2, sent), (forward_lag, forward), (forward_lag + LAGS.end, finish)]
    stages.sort(key=lambda item: -item[0])
    per_tick = 2
    at_second = 2
    at_norm = at_second + n_up // 2
    at_heads = at_norm + 1
    at_qkv = at_heads + -(-n_heads // per_tick)
    at_one = at_qkv + n_qkv // 2
    begins, ends_of = zip(
        swap_sums(0, at.to_core), swap_sums(1, at.to_x), swap_sums(2, at.to_y)
    )
    events = {at_norm: [norm_two], at_one: [norm_one, begins[0]]}
    now = at_one
    for i in range(3):
        now += 1
        events[now] = [ends_of[i]] + ([begins[i + 1]] if i < 2 else [sums_in(0)])
    for act in (
        [sums_in(depth) for depth in range(1, half)]
        + [sums_middle]
        + [sums_out(depth) for depth in reversed(range(half - 1))]
    ):
        now += 1
        events[now] = [act]
    last = count + forward_lag + LAGS.end
    assert now < last and at_norm < cuts.first[2] and at_qkv < cuts.first[3]

    def tick_body(tick, carry):
        for offset, stage in stages:

            @pl.when((tick >= offset) & (tick < count + offset))
            def _():
                stage(tick - offset)

        @pl.when((tick >= at_second) & (tick < at_norm))
        def _():
            up_step(tick - at_second)

        @pl.when((tick >= at_second) & (tick < at_norm - 1))
        def _():
            load_up(tick - at_second + 1)

        @pl.when(tick == at_norm - 1)
        def _():
            load_proj()

        for when, acts in events.items():

            @pl.when(tick == when)
            def _():
                for act in acts:
                    act()

        @pl.when((tick >= at_heads) & (tick < at_qkv))
        def _():
            @pl.loop(0, per_tick)
            def _(i):
                h = (tick - at_heads) * per_tick + i

                @pl.when(h < n_heads)
                def _():
                    head_step(h)

        @pl.when(tick == at_qkv)
        def _():
            give_qkv.start()
            give_qkv.wait()

        @pl.when((tick >= at_qkv) & (tick < at_one))
        def _():
            qkv_step(tick - at_qkv)

        @pl.when((tick >= at_qkv - 1) & (tick < at_one - 1))
        def _():
            load_qkv(tick - at_qkv + 1)

        return carry

    lax.fori_loop(0, last, tick_body, 0)


def reduce_backward(lefts, rights, others, small, n_rep, n_heads, score_scale):
    qkv, _, w_up, w_proj, hidden = others[:5]
    tokens, model = hidden.shape
    sizes = [(left.shape[0], right) for left, right in zip(lefts, (model, w_up.shape[1], model))]
    sizes.append((model, qkv.shape[0]))
    cuts = Cuts(sizes, 2)
    half = n_rep // 8
    slots = LAGS.z + LAGS.step * half + 1 - 2
    count, rows, wide = cuts.count, cuts.rows, cuts.wide
    block, width = rows // 2, wide // 2
    n_sums = 6 * model + w_up.shape[1] + qkv.shape[0]
    low, full, dma = jnp.bfloat16, jnp.float32, pltpu.SemaphoreType.DMA
    anywhere, local = pl.BlockSpec(memory_space=pl.ANY), pl.BlockSpec(memory_space=pltpu.VMEM)
    n_blocks = (w_up.shape[1] + qkv.shape[0]) // width + 2
    chunks, _, _, d_rows, sums, _, _ = pl.pallas_call(
        partial(backward_kernel, n_rep, cuts, n_heads, slots, score_scale),
        out_shape=[
            jax.ShapeDtypeStruct((count, rows, wide), low),
            jax.ShapeDtypeStruct((model, tokens), low),
            jax.ShapeDtypeStruct(qkv.shape, low),
            jax.ShapeDtypeStruct((tokens, model), full),
            jax.ShapeDtypeStruct((1, n_sums), full),
            jax.ShapeDtypeStruct((count, 2, rows, tokens), low),
            jax.ShapeDtypeStruct((count, width, tokens), low),
        ],
        in_specs=[anywhere] * (len(lefts) + len(rights) + len(others)) + [local] * len(small),
        out_specs=[anywhere] * 3 + [local] * 2 + [anywhere] * 2,
        scratch_shapes=[
            pltpu.VMEM((2, 2, 2, rows, tokens), low),
            pltpu.VMEM((2, 2, width, tokens), low),
            pltpu.VMEM((slots, 2, rows, width), low),
            pltpu.VMEM((count, rows, width), low),
            pltpu.VMEM((count, block, width), low),
            pltpu.VMEM((count, block, width), low),
            pltpu.VMEM((count, block, width), low),
            pltpu.VMEM((count, block, width), low),
            pltpu.VMEM(qkv.shape, low),
            pltpu.VMEM((2, model, width), low),
            pltpu.VMEM((2, width, tokens), low),
            pltpu.VMEM((model, tokens), full),
            pltpu.VMEM((model, tokens), low),
            pltpu.VMEM((model, tokens), low),
            pltpu.VMEM((tokens, model), low),
            pltpu.VMEM((6, 1, n_sums), full),
            dma((2, 2, count)),
            dma((2, count)),
            dma((count,)),
            dma((6,)),
            dma((2, n_blocks)),
            dma((2, 6)),
        ]
        + [dma((2, count))] * 11,
        compiler_params=pltpu.CompilerParams(
            collective_id=1, has_side_effects=True, vmem_limit_bytes=63 << 20
        ),
        name="reduce_backward",
    )(*lefts, *rights, *others, *small)
    return [cuts.whole(chunks, w) for w in range(len(sizes))], d_rows, sums[0]


def forward_kernel(n_rep, cuts, n_heads, score_scale, *refs):
    n_w = len(cuts.down)
    shards, refs = refs[:n_w], refs[n_w:]
    (
        patches, cotangent, own_vectors, pic_key, pic_query, cosine, sine,
    ) = refs[:7]
    fulls, refs = refs[7 : 7 + n_w], refs[7 + n_w :]
    (
        swap_out, heads_to, log_total, hidden_out, two_out, act_out, pre_out, layer_out,
        one_out, cot_out, vectors,
        swap, heads_out, hidden, two_turned, act_turned, pre_turned, one_turned, cot_turned,
        hold, w_block, turned, up_pre, act, out_sum, normed_two, normed, got_vectors,
        vec_sem, give_sem, pre_sem, own_in, own_out, w_sem, y_sem, d_sem, in_sem, mid_sem, back_sem, x_sem, c_sem, cd_sem,
    ) = refs
    at = Place(n_rep)
    nz, half = at.nz, at.half
    count, rows, wide = cuts.count, cuts.rows, cuts.wide
    plane = rows * 4 // 5
    unit = plane // n_rep
    straight = (rows - plane) // 2
    mine, yours = at.y, 1 - at.y
    tokens, model = patches.shape
    head = model // n_heads
    sizes = vector_sizes(model, up_pre.shape[1])
    starts = [sum(sizes[:i]) for i in range(len(sizes) + 1)]

    def vector(i, start=0, size=model):
        return vectors[:, pl.ds(pl.multiple_of(starts[i] + start, 128), size)]

    def shard(w, row, col, first, size):
        start = pl.multiple_of(row * rows + first, 16)
        cols = pl.ds(pl.multiple_of(col * wide, 128), wide)
        return shards[w].at[pl.ds(start, size), cols]

    def full(w, row, col, owner, first, size):
        start = pl.multiple_of(owner * cuts.shard_rows[w] + row * rows + first, 16)
        cols = pl.ds(pl.multiple_of(col * wide, 128), wide)
        return fulls[w].at[pl.ds(start, size), cols]

    def alike(size):
        return fulls[0].at[pl.ds(0, size), pl.ds(0, wide)]

    def place(c, x, z):
        return ((c * 2 + x) * nz + z) * unit

    def spread_copy(k, first, size, sems, device):
        def act_on(w, row, col):
            view = full(w, row, col, yours, first, size)
            remote(view, view, sems, k, device).start()

        cuts.weight_of(k, act_on)

    def settle(k, size, sems, device, received):
        view = alike(size)
        copy = remote(view, view, sems, k, device)
        if received:
            copy.wait_recv()
        else:
            copy.wait_send()

    def along(k, begin, size, sems, device):
        spread_copy(k, place(at.c, at.x, begin), size * unit, sems, device)

    def start_y(k):
        def act_on(w, row, col):
            first = place(at.c, at.x, at.z)
            remote(
                shard(w, row, col, first, unit),
                full(w, row, col, mine, first, unit),
                y_sem, k, at.to_y,
            ).start()
            first = plane + at.c * straight
            remote(
                shard(w, row, col, first, straight),
                full(w, row, col, mine, first, straight),
                d_sem, k, at.to_y,
            ).start()

        cuts.weight_of(k, act_on)

    def inner_send(k, depth):
        if depth == half - 1:
            along(k, jnp.where(at.low, 0, half), half, mid_sem, at.to_in)
        else:
            along(k, jnp.where(at.low, 0, nz - 1 - depth), depth + 1, in_sem, at.to_in)

    def back_start(k, depth):
        along(k, jnp.where(at.low, depth, 0), nz - depth, back_sem, at.to_out)

    def x_start(k):
        along(k, 0, nz, x_sem, at.to_x)

    def crossed(k):
        settle(k, unit, y_sem, at.to_y, True)

        @at.at_depth(0)
        def _():
            inner_send(k, 0)

        settle(k, straight, d_sem, at.to_y, True)
        spread_copy(k, plane + at.c * straight, straight, cd_sem, at.to_core)

    def pass_in(depth):
        def stage(k):
            @at.at_depth(depth)
            def _():
                settle(k, depth * unit, in_sem, at.to_in, True)
                inner_send(k, depth)

        return stage

    def middle(k):
        @at.at_depth(half - 1)
        def _():
            settle(k, half * unit, mid_sem, at.to_in, True)
            if half > 1:
                back_start(k, half - 1)
            x_start(k)

    def pass_out(depth):
        def stage(k):
            @at.at_depth(depth)
            def _():
                settle(k, (nz - depth - 1) * unit, back_sem, at.to_out, True)
                if depth > 0:
                    back_start(k, depth)
                x_start(k)

        return stage

    def crossed_x(k):
        settle(k, nz * unit, x_sem, at.to_x, True)
        spread_copy(k, place(at.c, 0, 0), 2 * nz * unit, c_sem, at.to_core)

    def own_load(k, view):
        return pltpu.make_async_copy(view, hold.at[k % 3], own_in.at[k])

    def own_store(k, view):
        return pltpu.make_async_copy(hold.at[k % 3], view, own_out.at[k])

    def take_own(k):
        cuts.weight_of(k, lambda w, row, col: own_load(k, shard(w, row, col, 0, rows)).start())

    def give_own(k):
        own_load(k, alike(rows)).wait()
        cuts.weight_of(
            k, lambda w, row, col: own_store(k, full(w, row, col, mine, 0, rows)).start()
        )

    def arrived(k):
        own_store(k, alike(rows)).wait()
        settle(k, 2 * nz * unit, c_sem, at.to_core, True)
        settle(k, straight, cd_sem, at.to_core, True)
        settle(k, unit, y_sem, at.to_y, False)
        settle(k, straight, d_sem, at.to_y, False)
        settle(k, nz * unit, x_sem, at.to_x, False)
        settle(k, 2 * nz * unit, c_sem, at.to_core, False)
        settle(k, straight, cd_sem, at.to_core, False)
        for depth in range(half):

            @at.at_depth(depth)
            def _():
                if depth == half - 1:
                    settle(k, half * unit, mid_sem, at.to_in, False)
                else:
                    settle(k, (depth + 1) * unit, in_sem, at.to_in, False)
                if depth > 0:
                    settle(k, (nz - depth) * unit, back_sem, at.to_out, False)

    def block_of(u, view):
        return pltpu.make_async_copy(view, w_block.at[u % 2], w_sem.at[0, u])

    def half_block(u, owner, view):
        spot = pl.ds(owner * (wide // 2), wide // 2)
        return pltpu.make_async_copy(view, w_block.at[u % 2, spot, :], w_sem.at[owner, u])

    def columns(w, col):
        return fulls[w].at[:, pl.ds(pl.multiple_of(col * wide, 128), wide)]

    def down_rows(i, owner):
        start = owner * cuts.shard_rows[3] + i * (wide // 2)
        return fulls[3].at[pl.ds(pl.multiple_of(start, 16), wide // 2), :]

    step = 256

    def qkv_step(b, u):
        block_of(u, columns(0, 0)).wait()

        @pl.loop(0, wide // step)
        def _(i):
            spot = pl.ds(pl.multiple_of(i * step, 128), step)
            part = contract(normed[...], w_block[u % 2, :, spot], 1, 0)
            part = part + vector(2, b * wide + i * step, step)
            turned[pl.ds(pl.multiple_of(i * step, 16), step), :] = part.T

        @pl.loop(0, n_heads)
        def _(h):
            part = turned[pl.ds(pl.multiple_of(h * head, 8), head), :]
            spot = pl.ds(pl.multiple_of(b * model + h * head, 16), head)

            @pl.when(b < 2)
            def _():
                swap[spot, :] = apply_rotary(part, cosine[...], sine[...]).astype(jnp.bfloat16)

            @pl.when(b == 2)
            def _():
                swap[spot, :] = part.astype(jnp.bfloat16)

    def head_step(h):
        def part(i):
            return swap[pl.ds(pl.multiple_of(i * model + h * head, 16), head), :]

        scores = contract(part(1), part(0), 0, 0) * score_scale
        scores = jnp.where(pic_key[...] == pic_query[...], scores, -1000000000.0)
        top = jnp.max(scores, axis=0, keepdims=True)
        exp_scores = jnp.exp(scores - top)
        total = jnp.sum(exp_scores, axis=0, keepdims=True)
        probs = (exp_scores / total).astype(jnp.bfloat16)
        attended = contract(part(2), probs, 1, 0)
        heads_out[pl.ds(pl.multiple_of(h * head, 16), head), :] = attended.astype(jnp.bfloat16)
        log_total[pl.ds(h, 1), :] = top + jnp.log(total)

    def proj_step(u):
        block_of(u, columns(0, 0)).wait()

        @pl.loop(0, tokens // step)
        def _(i):
            spot = pl.ds(pl.multiple_of(i * step, 16), step)
            lanes = pl.ds(pl.multiple_of(i * step, 128), step)
            branch = contract(heads_out[:, lanes], w_block[u % 2], 0, 0)
            rows_in = patches[spot, :].astype(jnp.float32) + branch + vector(3)
            hidden[spot, :] = rows_in
            out_sum[spot, :] = rows_in + vector(7)
            standard, _ = apply_layer_norm(rows_in)
            result = (standard * vector(4) + vector(5)).astype(jnp.bfloat16)
            normed_two[spot, :] = result
            two_turned[:, lanes] = result.T

    def up_step(c, u):
        block_of(u, columns(0, 0)).wait()

        @pl.loop(0, wide // step)
        def _(i):
            spot = pl.ds(pl.multiple_of(i * step, 128), step)
            col = pl.multiple_of(c * wide + i * step, 128)
            cols = pl.ds(col, step)
            pre = contract(normed_two[...], w_block[u % 2, :, spot], 1, 0)
            pre = pre + vector(6, c * wide + i * step, step)
            up_pre[:, cols] = pre
            result = (pre / (1.0 + jnp.exp(-quick_slope * pre))).astype(jnp.bfloat16)
            act[:, cols] = result
            act_turned[pl.ds(col, step), :] = result.T

    def down_step(i, u):
        for owner in range(2):
            half_block(u, owner, down_rows(0, 0)).wait()
            size = wide // 2
            col = pl.multiple_of(owner * cuts.shard_rows[3] + i * size, 128)

            @pl.loop(0, tokens // step)
            def _(j):
                spot = pl.ds(pl.multiple_of(j * step, 16), step)
                lanes = pl.ds(pl.multiple_of(j * step, 128), step)
                weight = w_block[u % 2, pl.ds(owner * size, size), :]
                pre = up_pre[spot, pl.ds(col, size)]
                sigmoid = 1.0 / (1.0 + jnp.exp(-quick_slope * pre))
                slope = sigmoid + quick_slope * pre * sigmoid * (1.0 - sigmoid)
                grad = contract(cotangent[spot, :], weight, 1, 1) * slope
                pre_turned[pl.ds(col, size), lanes] = grad.astype(jnp.bfloat16).T
                out_sum[spot, :] += contract(act[spot, pl.ds(col, size)], weight, 1, 0)

            pre_give(i, owner).start()

    pairs = [
        (one_turned, one_out), (cot_turned, cot_out), (swap, swap_out),
        (heads_out, heads_to), (hidden, hidden_out), (two_turned, two_out),
        (act_turned, act_out),
    ]
    gives = [pltpu.make_async_copy(a, b, give_sem.at[i]) for i, (a, b) in enumerate(pairs)]

    def pre_give(i, owner):
        start = owner * cuts.shard_rows[3] + i * (wide // 2)
        spot = pl.ds(pl.multiple_of(start, 16), wide // 2)
        return pltpu.make_async_copy(
            pre_turned.at[spot, :], pre_out.at[spot, :], pre_sem.at[owner, i]
        )

    vector_copy = remote(own_vectors, got_vectors, vec_sem, 0, at.to_y)
    slab = 128

    def join_vectors():
        vector_copy.wait()
        for i, size in enumerate(sizes):
            own, spot = size // 2, pl.ds(starts[i] // 2, size // 2)
            for y, part in ((mine, own_vectors), (yours, got_vectors)):
                start = pl.multiple_of(starts[i] + y * own, 128)
                vectors[:, pl.ds(start, own)] = part[:, spot]

    def norm_step(i):
        spot = pl.ds(pl.multiple_of(i * slab, 16), slab)
        lanes = pl.ds(pl.multiple_of(i * slab, 128), slab)
        standard, _ = apply_layer_norm(patches[spot, :].astype(jnp.float32))
        result = (standard * vector(0) + vector(1)).astype(jnp.bfloat16)
        normed[spot, :] = result
        one_turned[:, lanes] = result.T
        cot_turned[:, lanes] = cotangent[spot, :].T

    def cotangent_sums():
        ones = jnp.ones((8, tokens), jnp.bfloat16)
        sums = contract(ones, cot_turned[...], 1, 1)[0:1, :]
        vectors[:, pl.ds(starts[-1], model)] = sums

    gap = 2
    across = 1 + gap * 2 * half
    offset = across + 1
    stages = [(1, crossed)]
    stages += [(1 + gap * depth, pass_in(depth)) for depth in range(1, half)]
    stages += [(1 + gap * half, middle)]
    stages += [
        (1 + gap * (2 * half - 1 - depth), pass_out(depth)) for depth in range(half - 1)
    ]
    stages += [(across, crossed_x)]
    stages += [(offset - 2, take_own), (offset - 1, give_own), (offset, arrived)]
    stages.sort(key=lambda item: -item[0])
    n_up, n_down = cuts.across[2], cuts.down[3] // 2
    per_tick = 3
    first_head = cuts.first[1] + 1
    at_proj = first_head + -(-n_heads // per_tick)
    at_up = at_proj + 1
    at_down = max(at_up + n_up, cuts.first[3] + 2)
    n_steps = 4 + n_up + n_down

    at.meet(True)
    vector_copy.start()

    @pl.loop(0, count)
    def _(k):
        start_y(k)

    def tick_body(tick, carry):
        for lag, stage in stages:

            @pl.when((tick >= lag) & (tick < count + lag))
            def _():
                stage(tick - lag)

        @pl.when(tick == 0)
        def _():
            join_vectors()

        @pl.when((tick >= 2) & (tick % 2 == 0) & (tick <= tokens // slab * 2))
        def _():
            norm_step(tick // 2 - 1)

        @pl.when(tick == offset)
        def _():
            cotangent_sums()

        now = tick - offset

        @pl.when((now >= 2) & (now < first_head) & (now % 2 == 0))
        def _():
            qkv_step(now // 2 - 1, now // 2 - 1)

        @pl.when((now >= first_head) & (now < at_proj))
        def _():
            @pl.loop(0, per_tick)
            def _(i):
                h = (now - first_head) * per_tick + i

                @pl.when(h < n_heads)
                def _():
                    head_step(h)

        @pl.when(now == at_proj)
        def _():
            proj_step(3)

        @pl.when((now >= at_up) & (now < at_up + n_up))
        def _():
            up_step(now - at_up, now - at_up + 4)

        down_i = (now - at_down) // 2

        @pl.when((now >= at_down) & (down_i < n_down) & ((now - at_down) % 2 == 0))
        def _():
            down_step(down_i, down_i + 4 + n_up)

        for when, group in ((first_head, gives[:3]), (at_up, gives[3:6]), (at_down, gives[6:])):

            @pl.when(now == when)
            def _():
                for copy in group:
                    copy.start()

        soon = now + 1

        @pl.when((soon >= 2) & (soon < first_head) & (soon % 2 == 0))
        def _():
            block_of(soon // 2 - 1, columns(0, soon // 2 - 1)).start()

        @pl.when(soon == at_proj)
        def _():
            block_of(3, columns(1, 0)).start()

        @pl.when((soon >= at_up) & (soon < at_up + n_up))
        def _():
            block_of(soon - at_up + 4, columns(2, soon - at_up)).start()

        next_i = (soon - at_down) // 2

        @pl.when((soon >= at_down) & (next_i < n_down) & ((soon - at_down) % 2 == 0))
        def _():
            for owner in range(2):
                half_block(next_i + 4 + n_up, owner, down_rows(next_i, owner)).start()

        return carry

    lax.fori_loop(0, offset + at_down + 2 * n_down - 1, tick_body, 0)
    layer_out[...] = out_sum[...].astype(jnp.bfloat16)
    for copy in gives:
        copy.wait()
    for i in range(n_down):
        for owner in range(2):
            pre_give(i, owner).wait()


def vector_sizes(model, wide_two):
    return [model, model, 3 * model, model, model, model, wide_two, model]


def gather_forward(shards, inputs, n_rep, n_heads, score_scale):
    cuts = Cuts([(shard.shape[0] * 2, shard.shape[1]) for shard in shards], 2)
    tokens, model = inputs[0].shape
    wide_two = shards[2].shape[1]
    count, rows, wide = cuts.count, cuts.rows, cuts.wide
    low, dma = jnp.bfloat16, pltpu.SemaphoreType.DMA
    anywhere, local = pl.BlockSpec(memory_space=pl.ANY), pl.BlockSpec(memory_space=pltpu.VMEM)
    n_steps = 4 + cuts.across[2] + cuts.down[3] // 2
    n_vectors = sum(vector_sizes(model, wide_two))

    def shape(*sizes, kind=low):
        return jax.ShapeDtypeStruct(sizes, kind)

    results = pl.pallas_call(
        partial(forward_kernel, n_rep, cuts, n_heads, score_scale),
        out_shape=[shape(item.shape[0] * 2, item.shape[1]) for item in shards]
        + [
            shape(3 * model, tokens),
            shape(model, tokens),
            shape(n_heads, tokens, kind=jnp.float32),
            shape(tokens, model, kind=jnp.float32),
            shape(model, tokens),
            shape(wide_two, tokens),
            shape(wide_two, tokens),
            shape(tokens, model),
            shape(model, tokens),
            shape(model, tokens),
            shape(1, n_vectors + model, kind=jnp.float32),
        ],
        in_specs=[anywhere] * len(shards) + [local] * len(inputs),
        out_specs=[anywhere] * len(shards)
        + [anywhere] * 2 + [local] + [anywhere] * 4 + [local] + [anywhere] * 2 + [local],
        scratch_shapes=[
            pltpu.VMEM((3 * model, tokens), low),
            pltpu.VMEM((model, tokens), low),
            pltpu.VMEM((tokens, model), jnp.float32),
            pltpu.VMEM((model, tokens), low),
            pltpu.VMEM((wide_two, tokens), low),
            pltpu.VMEM((wide_two, tokens), low),
            pltpu.VMEM((model, tokens), low),
            pltpu.VMEM((model, tokens), low),
            pltpu.VMEM((3, rows, wide), low),
            pltpu.VMEM((2, model, wide), low),
            pltpu.VMEM((model, tokens), jnp.float32),
            pltpu.VMEM((tokens, wide_two), jnp.float32),
            pltpu.VMEM((tokens, wide_two), low),
            pltpu.VMEM((tokens, model), jnp.float32),
            pltpu.VMEM((tokens, model), low),
            pltpu.VMEM((tokens, model), low),
            pltpu.VMEM((1, n_vectors // 2), jnp.float32),
            dma((2, 1)),
            dma((7,)),
            dma((2, cuts.down[3] // 2)),
            dma((count,)),
            dma((count,)),
            dma((2, n_steps)),
        ]
        + [dma((2, count))] * 8,
        compiler_params=pltpu.CompilerParams(
            collective_id=0, has_side_effects=True, vmem_limit_bytes=63 << 20
        ),
        name="gather_forward",
    )(*shards, *inputs)
    return results[: len(shards)], results[len(shards) :]


class Links:
    def __init__(self, n_rep, n_shard):
        self.nz, self.ny, self.n_rep = n_rep // 4, n_shard, n_rep
        self.y = lax.axis_index("shard")

    def gather_vector(self, vector):
        return lax.all_gather(vector, "shard", axis=0, tiled=False)

    def sum_all(self, vector):
        for flip in (1, 2):
            vector = vector + lax.ppermute(
                vector, "rep", [(i, i ^ flip) for i in range(self.n_rep)]
            )
        step = 1
        while step < self.nz:
            pairs = [(i, i ^ (4 * step)) for i in range(self.n_rep)]
            vector = vector + lax.ppermute(vector, "rep", pairs)
            step *= 2
        step = 1
        while step < self.ny:
            pairs = [(i, i ^ step) for i in range(self.ny)]
            vector = vector + lax.ppermute(vector, "shard", pairs)
            step *= 2
        return vector


def per_device(
    patches,
    lengths,
    positions,
    ln1_gain,
    ln1_bias,
    qkv_weight,
    qkv_bias,
    proj_weight,
    proj_bias,
    ln2_gain,
    ln2_bias,
    fc1_weight,
    fc1_bias,
    fc2_weight,
    fc2_bias,
    cotangent,
    n_rep,
    n_shard,
):
    links = Links(n_rep, n_shard)
    pack_count = lengths.shape[0]
    row_count = patches.shape[0]
    length = row_count // pack_count
    model_width = patches.shape[1]
    head_count = HEADS
    head_size = model_width // head_count
    score_scale = head_size ** (-0.5)
    pic_ends = jnp.cumsum(lengths[:, :-1], axis=1)
    slot_index = jnp.arange(length, dtype=jnp.int32)
    idents = jnp.sum((slot_index[None, :, None] >= pic_ends[:, None, :]).astype(jnp.int32), axis=2)
    pack_index = jnp.arange(pack_count, dtype=jnp.int32)
    idents = (idents + pack_index[:, None] * lengths.shape[1]).reshape(-1)
    cosine, sine = rotary_tables(positions, head_size)

    shards = [qkv_weight, proj_weight, fc1_weight, fc2_weight]
    qkv_shape = (3 * model_width, row_count)
    small = [ln1_gain, ln1_bias, qkv_bias, proj_bias, ln2_gain, ln2_bias, fc1_bias, fc2_bias]
    spots = [0]
    for item in small:
        spots.append(spots[-1] + item.shape[0])
    packed = sum(
        jnp.pad(item, (spots[i], spots[-1] - spots[i + 1])) for i, item in enumerate(small)
    )
    if n_shard == 2:
        pictures = [idents[:, None], idents[None, :]]
        inputs = [patches, cotangent, packed.astype(jnp.float32)[None, :]]
        inputs += pictures + [cosine, sine]
        weights, results = gather_forward(shards, inputs, n_rep, head_count, score_scale)
        w_qkv, w_proj, w_up, w_down = weights
        qkv, heads_out, log_total, hidden_rows, second_turned = results[:5]
        activation, grad_pre, layer_out, first_turned, cotangent_turned, vectors = results[5:]
        others = [qkv, w_qkv, w_up, w_proj, hidden_rows, cotangent, patches]
        small_args = [log_total] + pictures + [cosine, sine, vectors]
        lefts = [activation, second_turned, heads_out, first_turned]
        rights = [cotangent_turned, grad_pre]
        products, d_patches, total = reduce_backward(
            lefts, rights, others, small_args, n_rep, head_count, score_scale
        )
    else:
        gathered = links.gather_vector(packed)
        (
            first_norm_gain, first_norm_bias, b_qkv, b_proj,
            second_norm_gain, second_norm_bias, b_up, b_down,
        ) = [
            gathered[:, spots[i] : spots[i + 1]].reshape(-1).astype(jnp.float32)
            for i in range(len(small))
        ]
        grad_out = cotangent.astype(jnp.float32)
        d_b_down = jnp.sum(grad_out, axis=0)
        input_rows = patches.astype(jnp.float32)
        first_centered_standard, first_inverse_spread = apply_layer_norm(input_rows)
        first_normalized = (first_centered_standard * first_norm_gain + first_norm_bias).astype(
            jnp.bfloat16
        )
        w_qkv, w_proj, w_up, w_down = [
            lax.all_gather(shard, "shard", axis=0, tiled=True) for shard in shards
        ]
        qkv_rows = contract(w_qkv, first_normalized, 0, 1) + b_qkv[:, None]
        qkv_rows = qkv_rows.reshape(3, head_count, head_size, row_count)
        queries = apply_rotary(qkv_rows[0], cosine, sine).astype(jnp.bfloat16)
        keys_rot = apply_rotary(qkv_rows[1], cosine, sine).astype(jnp.bfloat16)
        values_all = qkv_rows[2].astype(jnp.bfloat16)
        attended, log_total = attend(queries, keys_rot, values_all, idents, score_scale)
        heads_out = attended.reshape(model_width, row_count).astype(jnp.bfloat16)
        hidden_rows = input_rows + contract(heads_out, w_proj, 0, 0) + b_proj
        second_centered_standard, second_inverse_spread = apply_layer_norm(hidden_rows)
        second_normalized = (
            second_centered_standard * second_norm_gain + second_norm_bias
        ).astype(jnp.bfloat16)
        up_pre = contract(w_up, second_normalized, 0, 1) + b_up[:, None]
        sigmoid_up = 1.0 / (1.0 + jnp.exp(-quick_slope * up_pre))
        activation = (up_pre * sigmoid_up).astype(jnp.bfloat16)
        out_full = hidden_rows + contract(activation, w_down, 0, 0) + b_down
        layer_out = out_full.astype(jnp.bfloat16)
        grad_act = contract(w_down, cotangent, 1, 1)
        slope_up = sigmoid_up + quick_slope * up_pre * sigmoid_up * (1.0 - sigmoid_up)
        grad_pre = (grad_act * slope_up).astype(jnp.bfloat16)
        d_b_up = jnp.sum(grad_pre.astype(jnp.float32), axis=1)
        second_normalized_gradient = contract(grad_pre, w_up, 0, 1)
        second_gain_gradient = jnp.sum(
            second_normalized_gradient * second_centered_standard, axis=0
        )
        d_bias_two = jnp.sum(second_normalized_gradient, axis=0)
        grad_hidden = grad_out + norm_gradient_step(
            second_normalized_gradient,
            second_centered_standard,
            second_inverse_spread,
            second_norm_gain,
        )
        grad_branch = grad_hidden.astype(jnp.bfloat16)
        d_b_proj = jnp.sum(grad_branch.astype(jnp.float32), axis=0)
        grad_heads = contract(w_proj, grad_branch, 1, 1).astype(jnp.bfloat16)
        back = partial(head_back, score_scale=score_scale)
        grad_query, grad_key, grad_value = jax.vmap(back, in_axes=(0, 0, 0, 0, None, 0))(
            queries,
            keys_rot,
            values_all,
            grad_heads.reshape(head_count, head_size, row_count),
            idents[:, None] == idents[None, :],
            log_total[:, None, :],
        )
        grad_query = rotary_back(grad_query, cosine, sine)
        grad_key = rotary_back(grad_key, cosine, sine)
        grad_qkv = jnp.stack([grad_query, grad_key, grad_value]).reshape(qkv_shape)
        grad_qkv = grad_qkv.astype(jnp.bfloat16)
        first_normalized_gradient = contract(grad_qkv, w_qkv, 0, 1)
        lefts = [activation, second_normalized.T, heads_out, first_normalized.T]
        rights = [cotangent.T, grad_pre, grad_branch.T, grad_qkv]
        products = [
            contract(left, right, 1, 1).astype(jnp.bfloat16) for left, right in zip(lefts, rights)
        ]
        products = [
            item.astype(jnp.float32) for item in reduce_products(products, n_rep, n_shard)
        ]
        d_b_qkv = jnp.sum(grad_qkv.astype(jnp.float32), axis=1)
        first_gain_gradient = jnp.sum(first_normalized_gradient * first_centered_standard, axis=0)
        d_bias_one = jnp.sum(first_normalized_gradient, axis=0)
        d_patches = grad_hidden + norm_gradient_step(
            first_normalized_gradient,
            first_centered_standard,
            first_inverse_spread,
            first_norm_gain,
        )
        total = jnp.concatenate(
            [
                second_gain_gradient, d_bias_two, d_b_up, d_b_down,
                first_gain_gradient, d_bias_one, d_b_qkv, d_b_proj,
            ]
        )
        total = links.sum_all(total)
    d_w_down, d_w_up, d_w_proj, d_w_qkv = products

    ff = fc1_weight.shape[1]
    own_parts, start = [], 0
    for size in (
        model_width, model_width, ff, model_width,
        model_width, model_width, 3 * model_width, model_width,
    ):
        own = size // n_shard
        own_parts.append(lax.dynamic_slice_in_dim(total, start + links.y * own, own, 0))
        start += size
    m_gain, m_bias, m_upb, m_downb, a_gain, a_bias, a_qkvb, a_projb = own_parts
    return (
        layer_out,
        d_patches,
        a_gain,
        a_bias,
        d_w_qkv,
        a_qkvb,
        d_w_proj,
        a_projb,
        m_gain,
        m_bias,
        d_w_up,
        m_upb,
        d_w_down,
        m_downb,
    )


def solution(mesh):
    rows, whole = P(("rep", "shard"), None), P("shard")
    matrix = P("shard", None)
    in_specs = (
        rows,
        rows,
        P(None, ("rep", "shard")),
        whole,
        whole,
        matrix,
        whole,
        matrix,
        whole,
        whole,
        whole,
        matrix,
        whole,
        matrix,
        whole,
        rows,
    )
    out_specs = (
        rows,
        rows,
        whole,
        whole,
        matrix,
        whole,
        matrix,
        whole,
        whole,
        whole,
        matrix,
        whole,
        matrix,
        whole,
    )
    body = partial(per_device, n_rep=mesh.shape["rep"], n_shard=mesh.shape["shard"])
    return jax.shard_map(
        body, mesh=mesh, in_specs=in_specs, out_specs=out_specs, check_vma=False
    )
```

```python
from functools import partial

import jax
import jax.numpy as jnp
from jax import lax
from jax.experimental import pallas as pl
from jax.experimental.pallas import tpu as pltpu
from jax.sharding import PartitionSpec as P

HEADS = 16


norm_eps = 1e-06
quick_slope = 1.702


def apply_layer_norm(matrix):
    center = matrix - jnp.mean(matrix, axis=-1, keepdims=True)
    spread = jnp.mean(center * center, axis=-1, keepdims=True)
    inverse_spread = lax.rsqrt(spread + norm_eps)
    return (center * inverse_spread, inverse_spread)


def norm_gradient_step(normalized_gradient, centered_standard, inverse_spread, norm_gain):
    scaled_rows = normalized_gradient * norm_gain
    return inverse_spread * (
        scaled_rows
        - jnp.mean(scaled_rows, axis=-1, keepdims=True)
        - centered_standard * jnp.mean(scaled_rows * centered_standard, axis=-1, keepdims=True)
    )


def rotary_tables(positions, head_size):
    quarter = head_size // 4
    counter = jnp.arange(quarter, dtype=jnp.float32)
    inverse = jnp.power(jnp.float32(10000.0), -2.0 * counter / (head_size // 2))
    row_angle = inverse[:, None] * positions[0].astype(jnp.float32)[None, :]
    col_angle = inverse[:, None] * positions[1].astype(jnp.float32)[None, :]
    angle = jnp.concatenate([row_angle, col_angle], axis=0)
    angle = jnp.concatenate([angle, angle], axis=0)
    return (jnp.cos(angle), jnp.sin(angle))


def apply_rotary(matrix, cosine, sine):
    half_size = matrix.shape[-2] // 2
    turned = jnp.concatenate([-matrix[..., half_size:, :], matrix[..., :half_size, :]], axis=-2)
    return matrix * cosine + turned * sine


def rotary_back(grad, cosine, sine):
    half_size = grad.shape[-2] // 2
    sined = grad * sine
    turned = jnp.concatenate([sined[..., half_size:, :], -sined[..., :half_size, :]], axis=-2)
    return grad * cosine + turned


def contract(left, right, left_dim, right_dim):
    return lax.dot_general(
        left, right, (((left_dim,), (right_dim,)), ((), ())), preferred_element_type=jnp.float32
    )


def masked_scores(queries, keys_rot, ident, score_scale):
    scores = (
        jnp.einsum("hdk,hdq->hkq", keys_rot, queries, preferred_element_type=jnp.float32)
        * score_scale
    )
    same_pic = ident[:, None] == ident[None, :]
    return jnp.where(same_pic[None], scores, -1000000000.0)


def attend(queries, keys_rot, values_all, ident, score_scale):
    scores = masked_scores(queries, keys_rot, ident, score_scale)
    top_score = jnp.max(scores, axis=1, keepdims=True)
    exp_scores = jnp.exp(scores - top_score)
    total = jnp.sum(exp_scores, axis=1, keepdims=True)
    probs = (exp_scores / total).astype(jnp.bfloat16)
    attended = jnp.einsum("hdk,hkq->hdq", values_all, probs, preferred_element_type=jnp.float32)
    return (attended, (top_score + jnp.log(total))[:, 0, :])


def head_back(query, key, value, grad_head, same_pic, log_total, score_scale):
    scores = jnp.where(same_pic, contract(key, query, 0, 0) * score_scale, -1000000000.0)
    probs = jnp.exp(scores - log_total)
    grad_probs = contract(value, grad_head, 0, 0)
    inner = jnp.sum(probs * grad_probs, axis=0, keepdims=True)
    grad_scores = (probs * (grad_probs - inner)).astype(jnp.bfloat16)
    grad_query = contract(key, grad_scores, 1, 0) * score_scale
    grad_key = contract(query, grad_scores, 1, 1) * score_scale
    grad_value = contract(grad_head, probs.astype(jnp.bfloat16), 1, 1)
    return (grad_query, grad_key, grad_value)


MESH = pl.DeviceIdType.MESH


class Place:
    def __init__(self, n_rep):
        rep = lax.axis_index("rep")
        self.nz = n_rep // 4
        self.half = self.nz // 2
        self.y = lax.axis_index("shard")
        self.z, self.x, self.c = rep // 4, (rep // 2) % 2, rep % 2
        self.low = self.z < self.half
        self.depth = jnp.where(self.low, self.z, self.nz - 1 - self.z)
        side = jnp.where(self.low, 1, -1)
        self.to_core = {"rep": self.z * 4 + self.x * 2 + (1 - self.c)}
        self.to_x = {"rep": self.z * 4 + (1 - self.x) * 2 + self.c}
        self.to_y = {"shard": 1 - self.y}
        self.to_in = {"rep": (self.z + side) * 4 + self.x * 2 + self.c}
        self.to_out = {"rep": (self.z - side) * 4 + self.x * 2 + self.c}

    def at_depth(self, depth):
        return pl.when(self.depth == depth)

    def meet(self, with_y):
        barrier = pltpu.get_barrier_semaphore()
        near = [self.to_core, self.to_x, self.to_in] + ([self.to_y] if with_y else [])
        for device in near:
            pl.semaphore_signal(barrier, inc=1, device_id=device, device_id_type=MESH)

        @pl.when(self.depth > 0)
        def _():
            pl.semaphore_signal(barrier, inc=1, device_id=self.to_out, device_id_type=MESH)

        pl.semaphore_wait(barrier, jnp.where(self.depth > 0, len(near) + 1, len(near)))


def remote(src, dst, sems, k, device):
    return pltpu.make_async_remote_copy(
        src_ref=src,
        dst_ref=dst,
        send_sem=sems.at[0, k],
        recv_sem=sems.at[1, k],
        device_id=device,
        device_id_type=MESH,
    )


def add_into(dst, one, two):
    rows = dst.shape[0]
    step = 32 if rows % 32 == 0 else rows

    @pl.loop(0, rows // step)
    def _(i):
        spot = pl.ds(pl.multiple_of(i * step, step), step)
        total = one[spot, :].astype(jnp.float32) + two[spot, :].astype(jnp.float32)
        dst[spot, :] = total.astype(dst.dtype)


def skewed(count, stages):
    last = max(offset for offset, _ in stages)
    for tick in range(count + last):
        for offset, stage in sorted(stages, key=lambda item: -item[0]):
            if 0 <= tick - offset < count:
                stage(tick - offset)


def cut_chunks(shards):
    rows = min(shard.shape[0] for shard in shards)
    wide = min(shard.shape[1] for shard in shards)
    chunks = []
    for w, shard in enumerate(shards):
        for row0 in range(0, shard.shape[0], rows):
            for col0 in range(0, shard.shape[1], wide):
                chunks.append((w, row0, col0))
    return rows, wide, chunks


def reduce_kernel(n_rep, parts, chunks, shard_rows, rows, wide, *refs):
    count, n_w = len(chunks), len(shard_rows)
    sources, outs, arrived = refs[:n_w], refs[n_w : 2 * n_w], refs[2 * n_w]
    (
        held, lent, got_y, got_x, got_in, got_mid, total,
        own_in, lent_in, put, c0_sem, c1_sem, y_sem, x_sem, in_sem, mid_sem, back_sem,
        ax_sem, ac_sem, af_sem,
    ) = refs[2 * n_w + 1 :]
    c_sems = [c0_sem, c1_sem]
    at = Place(n_rep)
    half = at.half
    block = rows // 4
    with_y = parts == 2
    mine = at.y if with_y else 0

    def source(k, owner, c):
        w, row0, col0 = chunks[k]
        start = pl.multiple_of(owner * shard_rows[w] + row0 + c * 2 * block, 8)
        return sources[w].at[pl.ds(start, 2 * block), pl.ds(col0, wide)]

    def out(k, c, x):
        w, row0, col0 = chunks[k]
        start = pl.multiple_of(row0 + (c * 2 + x) * block, 8)
        return outs[w].at[pl.ds(start, block), pl.ds(col0, wide)]

    def rows_of(x):
        return pl.ds(pl.multiple_of(x * block, 8), block)

    def c_send(k, owner):
        return remote(
            source(k, owner, 1 - at.c), arrived.at[k, owner], c_sems[owner], k, at.to_core
        )

    def own_load(k, owner):
        return pltpu.make_async_copy(
            source(k, owner, at.c), held.at[k, owner], own_in.at[owner, k]
        )

    def lent_load(k, owner):
        return pltpu.make_async_copy(
            arrived.at[k, owner], lent.at[k % 2, owner], lent_in.at[owner, k]
        )

    def y_send(k):
        return remote(held.at[k, 1 - mine], got_y.at[k], y_sem, k, at.to_y)

    def x_send(k):
        return remote(
            held.at[k, mine, rows_of(1 - at.x)], got_x.at[k], x_sem, k, at.to_x
        )

    def part(k):
        return held.at[k, mine, rows_of(at.x)]

    def in_send(k):
        return remote(part(k), got_in.at[k], in_sem, k, at.to_in)

    def mid_send(k):
        return remote(part(k), got_mid.at[k], mid_sem, k, at.to_in)

    def back_send(k):
        return remote(total.at[k], total.at[k], back_sem, k, at.to_out)

    def ax_send(k, x):
        return remote(total.at[k], out(k, at.c, x), ax_sem, k, at.to_x)

    def ac_send(k, c):
        return remote(total.at[k], out(k, c, at.x), ac_sem, k, at.to_core)

    def af_send(k, c):
        view = out(k, c, 1 - at.x)
        return remote(view, view, af_sem, k, at.to_core)

    def own_put(k):
        return pltpu.make_async_copy(total.at[k], out(k, at.c, at.x), put.at[k])

    def start_core(k):
        for owner in range(parts):
            c_send(k, owner).start()
            own_load(k, owner).start()

    def load_core(k):
        for owner in range(parts):
            c_send(k, owner).wait_recv()
            lent_load(k, owner).start()

    def start_y(k):
        for owner in range(parts):
            own_load(k, owner).wait()
            lent_load(k, owner).wait()
        if with_y:
            other = 1 - mine
            add_into(held.at[k, other], held.at[k, other], lent.at[k % 2, other])
            y_send(k).start()
        add_into(held.at[k, mine], held.at[k, mine], lent.at[k % 2, mine])

    def start_x(k):
        if with_y:
            y_send(k).wait_recv()
            spot = rows_of(1 - at.x)
            add_into(held.at[k, mine, spot], held.at[k, mine, spot], got_y.at[k, spot])
        x_send(k).start()
        if with_y:
            add_into(part(k), part(k), got_y.at[k, rows_of(at.x)])

    def inner_send(k, depth):
        (mid_send(k) if depth == half - 1 else in_send(k)).start()

    def start_z(k):
        x_send(k).wait_recv()
        add_into(part(k), part(k), got_x.at[k])

        @at.at_depth(0)
        def _():
            inner_send(k, 0)

    def pass_in(depth):
        def stage(k):
            @at.at_depth(depth)
            def _():
                in_send(k).wait_recv()
                add_into(part(k), part(k), got_in.at[k])
                inner_send(k, depth)

        return stage

    def spread(k, depth):
        if depth > 0:
            back_send(k).start()
        ax_send(k, at.x).start()
        ac_send(k, at.c).start()
        own_put(k).start()

    def middle(k):
        @at.at_depth(half - 1)
        def _():
            mid_send(k).wait_recv()
            add_into(total.at[k], part(k), got_mid.at[k])
            spread(k, half - 1)

    def pass_out(depth):
        def stage(k):
            @at.at_depth(depth)
            def _():
                back_send(k).wait_recv()
                spread(k, depth)

        return stage

    def forward(k):
        ax_send(k, 1 - at.x).wait_recv()
        af_send(k, at.c).start()

    at.meet(with_y)
    stages = [(0, start_core), (1, load_core), (2, start_y), (4, start_x), (5, start_z)]
    stages += [(6 + depth - 1, pass_in(depth)) for depth in range(1, half)]
    stages += [(6 + half - 1, middle)]
    stages += [(6 + half + (half - 2 - depth), pass_out(depth)) for depth in range(half - 1)]
    stages += [(5 + 2 * half, forward)]
    skewed(count, stages)
    for k in range(count):
        for owner in range(parts):
            c_send(k, owner).wait_send()
        if with_y:
            y_send(k).wait_send()
        x_send(k).wait_send()
        for depth in range(half):

            @at.at_depth(depth)
            def _():
                (mid_send(k) if depth == half - 1 else in_send(k)).wait_send()
                if depth > 0:
                    back_send(k).wait_send()

        ax_send(k, at.x).wait_send()
        ac_send(k, at.c).wait_send()
        af_send(k, at.c).wait_send()
        own_put(k).wait()
        ac_send(k, 1 - at.c).wait_recv()
        af_send(k, 1 - at.c).wait_recv()


def reduce_products(products, n_rep, n_shard):
    parts = n_shard
    if n_shard != 2:
        products = [
            lax.psum_scatter(item, "shard", scatter_dimension=0, tiled=True) for item in products
        ]
        parts = 1
    owned = [
        jax.ShapeDtypeStruct((item.shape[0] // parts, item.shape[1]), jnp.bfloat16)
        for item in products
    ]
    rows, wide, chunks = cut_chunks(owned)
    count, block = len(chunks), rows // 4
    kernel = partial(
        reduce_kernel, n_rep, parts, chunks, [item.shape[0] for item in owned], rows, wide
    )
    pair = pltpu.SemaphoreType.DMA((2, count))
    low = jnp.bfloat16
    anywhere = pl.BlockSpec(memory_space=pl.ANY)
    results = pl.pallas_call(
        kernel,
        out_shape=owned + [jax.ShapeDtypeStruct((count, parts, 2 * block, wide), low)],
        in_specs=[anywhere] * len(products),
        out_specs=[anywhere] * (len(products) + 1),
        scratch_shapes=[
            pltpu.VMEM((count, parts, 2 * block, wide), low),
            pltpu.VMEM((2, parts, 2 * block, wide), low),
            pltpu.VMEM((count, 2 * block, wide), low),
            pltpu.VMEM((count, block, wide), low),
            pltpu.VMEM((count, block, wide), low),
            pltpu.VMEM((count, block, wide), low),
            pltpu.VMEM((count, block, wide), low),
            pltpu.SemaphoreType.DMA((parts, count)),
            pltpu.SemaphoreType.DMA((parts, count)),
            pltpu.SemaphoreType.DMA((count,)),
        ]
        + [pair] * 10,
        compiler_params=pltpu.CompilerParams(
            collective_id=1, has_side_effects=True, vmem_limit_bytes=62 << 20
        ),
        name="reduce_products",
    )(*products)
    return results[:-1]


class Cuts:
    def __init__(self, sizes, n_shard):
        self.shard_rows = [left // n_shard for left, _ in sizes]
        self.rows = min(self.shard_rows) // 2
        self.wide = min(right for _, right in sizes)
        self.down = [rows // self.rows for rows in self.shard_rows]
        self.across = [right // self.wide for _, right in sizes]
        self.first = [0]
        for down, across in zip(self.down, self.across):
            self.first.append(self.first[-1] + down * across)
        self.count = self.first[-1]

    def weight_of(self, k, act):
        for w, down in enumerate(self.down):

            @pl.when((k >= self.first[w]) & (k < self.first[w + 1]))
            def _():
                inside = k - self.first[w]
                act(w, inside % down, inside // down)

    def whole(self, chunks, w):
        first, down, rows, wide = self.first[w], self.down[w], self.rows, self.wide

        pair = min(down, 4)

        def widen(part, dst):
            for i in range(pair):
                dst[pl.ds(i * rows, rows), :] = part[i].astype(jnp.float32)

        return pl.pallas_call(
            widen,
            grid=(down // pair, self.across[w]),
            in_specs=[
                pl.BlockSpec((pair, rows, wide), lambda i, j: ((first + j * down) // pair + i, 0, 0))
            ],
            out_specs=pl.BlockSpec((pair * rows, wide), lambda i, j: (i, j)),
            out_shape=jax.ShapeDtypeStruct(
                (self.shard_rows[w], self.across[w] * wide), jnp.float32
            ),
            compiler_params=pltpu.CompilerParams(vmem_limit_bytes=60 << 20),
            cost_estimate=pl.CostEstimate(
                flops=0,
                transcendentals=0,
                bytes_accessed=6 * down * self.across[w] * rows * wide,
            ),
            name="widen",
        )(chunks)


class LAGS:
    x, z, step, end = 4, 6, 1, 1


def backward_kernel(n_rep, cuts, n_heads, slots, score_scale, *refs):
    (
        left_0, left_1, left_2, left_3, right_0, right_1, qkv, w_qkv, w_up, w_proj,
        hidden, cotangent, patches,
        log_total, pic_key, pic_query, cosine, sine, vectors,
        out, right_2, grad_qkv, d_rows, sums, lent_left, lent_right,
        op_left, op_right, held, got_y, got_x, got_in, got_mid, total, swap, w_block,
        pre_block, turned, branch, grad_heads, rows_in, got_sums,
        load_l, load_r, put, once_sem, block_sem, sum_sem,
        l0_sem, l1_sem, r_sem, y_sem, x_sem, in_sem, mid_sem, back_sem, ax_sem, ac_sem, af_sem,
    ) = refs
    lefts = [left_0, left_1, left_2, left_3]
    rights = [right_0, right_1, right_2, grad_qkv]
    l_sems = [l0_sem, l1_sem]
    at = Place(n_rep)
    half = at.half
    count, rows, wide = cuts.count, cuts.rows, cuts.wide
    block, width = rows // 2, wide // 2
    mine = at.y
    head = qkv.shape[0] // (3 * n_heads)
    model = n_heads * head

    def left_rows(w, row, owner):
        start = owner * cuts.shard_rows[w] + row * rows
        return lefts[w].at[pl.ds(pl.multiple_of(start, 16), rows), :]

    def right_rows(w, col, c):
        start = col * wide + c * width
        return rights[w].at[pl.ds(pl.multiple_of(start, 16), width), :]

    def left_push(k, owner, src):
        return remote(src, lent_left.at[k, owner], l_sems[owner], k, at.to_core)

    def right_push(k, src):
        return remote(src, lent_right.at[k], r_sem, k, at.to_core)

    def left_load(k, whose, owner, src):
        slot = k % 2
        return pltpu.make_async_copy(
            src, op_left.at[slot, whose, owner], load_l.at[whose, owner, k]
        )

    def right_load(k, whose, src):
        return pltpu.make_async_copy(src, op_right.at[k % 2, whose], load_r.at[whose, k])

    def rows_of(x):
        return pl.ds(pl.multiple_of(x * block, 16), block)

    def mine_of(k, x):
        return held.at[k % slots, mine, rows_of(x)]

    def y_send(k):
        return remote(held.at[k % slots, 1 - mine], got_y.at[k], y_sem, k, at.to_y)

    def x_send(k):
        return remote(mine_of(k, 1 - at.x), got_x.at[k], x_sem, k, at.to_x)

    def in_send(k):
        return remote(mine_of(k, at.x), got_in.at[k], in_sem, k, at.to_in)

    def mid_send(k):
        return remote(mine_of(k, at.x), got_mid.at[k], mid_sem, k, at.to_in)

    def back_send(k):
        return remote(total.at[k], total.at[k], back_sem, k, at.to_out)

    def out_of(k, c, x):
        cols = pl.ds(pl.multiple_of(c * width, 128), width)
        return out.at[k, rows_of(x), cols]

    def ax_send(k, x):
        return remote(total.at[k], out_of(k, at.c, x), ax_sem, k, at.to_x)

    def ac_send(k, c):
        return remote(total.at[k], out_of(k, c, at.x), ac_sem, k, at.to_core)

    def af_send(k, c):
        view = out_of(k, c, 1 - at.x)
        return remote(view, view, af_sem, k, at.to_core)

    def own_put(k):
        return pltpu.make_async_copy(total.at[k], out_of(k, at.c, at.x), put.at[k])

    def push(k):
        def act(w, row, col):
            for owner in range(2):
                left_push(k, owner, left_rows(w, row, owner)).start()
            right_push(k, right_rows(w, col, 1 - at.c)).start()

        cuts.weight_of(k, act)

    def load(k):
        def act(w, row, col):
            for owner in range(2):
                left_load(k, 0, owner, left_rows(w, row, owner)).start()
            right_load(k, 0, right_rows(w, col, at.c)).start()

        cuts.weight_of(k, act)
        for owner in range(2):
            left_push(k, owner, lent_left.at[k, owner]).wait_recv()
            left_load(k, 1, owner, lent_left.at[k, owner]).start()
        right_push(k, lent_right.at[k]).wait_recv()
        right_load(k, 1, lent_right.at[k]).start()

    def product(k):
        slot = k % 2
        for whose in range(2):
            for owner in range(2):
                left_load(k, whose, owner, lent_left.at[k, owner]).wait()
            right_load(k, whose, lent_right.at[k]).wait()
        for owner in range(2):
            left_push(k, owner, lent_left.at[k, owner]).wait_send()
        right_push(k, lent_right.at[k]).wait_send()
        for owner in (1 - mine, mine):
            result = contract(op_left[slot, 0, owner], op_right[slot, 0], 1, 1)
            result += contract(op_left[slot, 1, owner], op_right[slot, 1], 1, 1)
            held[k % slots, owner] = result.astype(jnp.bfloat16)
            if owner is not mine:
                y_send(k).start()

    def start_x(k):
        y_send(k).wait_recv()
        other = mine_of(k, 1 - at.x)
        add_into(other, other, got_y.at[k, rows_of(1 - at.x)])
        x_send(k).start()
        own = mine_of(k, at.x)
        add_into(own, own, got_y.at[k, rows_of(at.x)])
        y_send(k).wait_send()

    def inner_send(k, depth):
        return mid_send(k) if depth == half - 1 else in_send(k)

    def start_z(k):
        x_send(k).wait_recv()
        own = mine_of(k, at.x)
        add_into(own, own, got_x.at[k])

        @at.at_depth(0)
        def _():
            inner_send(k, 0).start()

        x_send(k).wait_send()

    def pass_in(depth):
        def stage(k):
            @at.at_depth(depth)
            def _():
                in_send(k).wait_recv()
                own = mine_of(k, at.x)
                add_into(own, own, got_in.at[k])
                inner_send(k, depth).start()

        return stage

    def spread(k, depth):
        if depth > 0:
            back_send(k).start()
        ax_send(k, at.x).start()
        ac_send(k, at.c).start()
        own_put(k).start()

    def middle(k):
        @at.at_depth(half - 1)
        def _():
            mid_send(k).wait_recv()
            add_into(total.at[k], mine_of(k, at.x), got_mid.at[k])
            spread(k, half - 1)

    def pass_out(depth):
        def stage(k):
            @at.at_depth(depth)
            def _():
                back_send(k).wait_recv()
                spread(k, depth)

        return stage

    def sent(k):
        for depth in range(half):

            @at.at_depth(depth)
            def _():
                inner_send(k, depth).wait_send()

    def forward(k):
        ax_send(k, 1 - at.x).wait_recv()
        af_send(k, at.c).start()

    def finish(k):
        @pl.when(at.depth > 0)
        def _():
            back_send(k).wait_send()

        ax_send(k, at.x).wait_send()
        ac_send(k, at.c).wait_send()
        af_send(k, at.c).wait_send()
        own_put(k).wait()
        ac_send(k, 1 - at.c).wait_recv()
        af_send(k, 1 - at.c).wait_recv()

    def head_step(h):
        def part(i):
            return pl.ds(pl.multiple_of(i * model + h * head, 16), head)

        query, key, value = swap[part(0), :], swap[part(1), :], swap[part(2), :]
        grads = head_back(
            query,
            key,
            value,
            grad_heads[part(0), :],
            pic_key[...] == pic_query[...],
            log_total[pl.ds(h, 1), :],
            score_scale,
        )
        grad_query, grad_key, grad_value = grads
        turn_c, turn_s = cosine[...], sine[...]
        swap[part(0), :] = rotary_back(grad_query, turn_c, turn_s).astype(jnp.bfloat16)
        swap[part(1), :] = rotary_back(grad_key, turn_c, turn_s).astype(jnp.bfloat16)
        swap[part(2), :] = grad_value.astype(jnp.bfloat16)

    tokens = qkv.shape[1]
    wide_two = right_1.shape[0]
    n_up, n_qkv = wide_two // width, qkv.shape[0] // width
    starts = [0]
    for size in vector_sizes(model, wide_two):
        starts.append(starts[-1] + size)
    ends = [0]
    for size in (model, model, wide_two, model, model, model, qkv.shape[0], model):
        ends.append(ends[-1] + size)

    def sums_of(i, start=0, size=model):
        return pl.ds(pl.multiple_of(ends[i] + start, 128), size)

    def column_sums(block):
        ones = jnp.ones((8, tokens), jnp.bfloat16)
        return contract(ones, block, 1, 1)[0:1, :]

    def w_load(src, j, slot):
        cols = pl.ds(pl.multiple_of(j * width, 128), width)
        return lambda k: pltpu.make_async_copy(src.at[:, cols], w_block.at[slot], block_sem.at[0, k])

    def pre_load(j, slot):
        spot = pl.ds(pl.multiple_of(j * width, 16), width)
        return pltpu.make_async_copy(right_1.at[spot, :], pre_block.at[slot], block_sem.at[1, j])

    def once(i, src, dst):
        return pltpu.make_async_copy(src, dst, once_sem.at[i])

    def add_turned(slot, right):
        step = 256

        @pl.loop(0, model // step)
        def _(i):
            spot = pl.ds(pl.multiple_of(i * step, 16), step)
            turned[spot, :] += contract(w_block[slot, spot, :], right, 1, 0)

    def clear_turned():
        turned[...] = jnp.zeros_like(turned)

    def load_up(pair):
        for slot in range(2):
            j = pair * 2 + slot
            w_load(w_up, j, slot)(j).start()
            pre_load(j, slot).start()

    def up_step(pair):
        for slot in range(2):
            j = pair * 2 + slot
            w_load(w_up, j, slot)(j).wait()
            pre_load(j, slot).wait()
            block = pre_block[slot]
            add_turned(slot, block)
            sums[:, sums_of(2, j * width, width)] = column_sums(block)

    def load_proj():
        for slot in range(2):
            w_load(w_proj, slot, slot)(n_up + slot).start()

    def load_qkv(pair):
        for slot in range(2):
            j = pair * 2 + slot
            w_load(w_qkv, j, slot)(n_up + 2 + j).start()

    def qkv_step(pair):
        for slot in range(2):
            j = pair * 2 + slot
            w_load(w_qkv, j, slot)(n_up + 2 + j).wait()
            block = swap[pl.ds(pl.multiple_of(j * width, 16), width), :]
            add_turned(slot, block)
            sums[:, sums_of(6, j * width, width)] = column_sums(block)

    step = 128

    def norm_two():
        once(2, hidden, d_rows).wait()
        once(3, cotangent, rows_in).wait()

        @pl.loop(0, tokens // step)
        def _(i):
            spot = pl.ds(pl.multiple_of(i * step, 16), step)
            lanes = pl.ds(pl.multiple_of(i * step, 128), step)
            standard, inverse = apply_layer_norm(d_rows[spot, :])
            grad = turned[:, lanes].T
            sums[:, sums_of(0)] += jnp.sum(grad * standard, axis=0, keepdims=True)
            sums[:, sums_of(1)] += jnp.sum(grad, axis=0, keepdims=True)
            back = norm_gradient_step(grad, standard, inverse, vectors[:, pl.ds(starts[4], model)])
            back = back + rows_in[spot, :].astype(jnp.float32)
            d_rows[spot, :] = back
            low = back.astype(jnp.bfloat16)
            branch[:, lanes] = low.T

        sums[:, sums_of(7)] = column_sums(branch[...])
        once(4, patches, rows_in).start()
        once(5, branch, right_2).start()
        for slot in range(2):
            w_load(w_proj, slot, slot)(n_up + slot).wait()

        @pl.loop(0, model // step)
        def _(i):
            spot = pl.ds(pl.multiple_of(i * step, 16), step)
            result = contract(w_block[0, spot, :], branch[pl.ds(0, width), :], 1, 0)
            result += contract(w_block[1, spot, :], branch[pl.ds(width, width), :], 1, 0)
            grad_heads[spot, :] = result.astype(jnp.bfloat16)

        once(5, branch, right_2).wait()
        clear_turned()

    def norm_one():
        once(4, patches, rows_in).wait()

        @pl.loop(0, tokens // step)
        def _(i):
            spot = pl.ds(pl.multiple_of(i * step, 16), step)
            lanes = pl.ds(pl.multiple_of(i * step, 128), step)
            standard, inverse = apply_layer_norm(rows_in[spot, :].astype(jnp.float32))
            grad = turned[:, lanes].T
            sums[:, sums_of(4)] += jnp.sum(grad * standard, axis=0, keepdims=True)
            sums[:, sums_of(5)] += jnp.sum(grad, axis=0, keepdims=True)
            d_rows[spot, :] += norm_gradient_step(grad, standard, inverse, vectors[:, pl.ds(starts[0], model)])

    def sums_to(i, device):
        return remote(sums, got_sums.at[i], sum_sem, i, device)

    def swap_sums(i, device):
        def begin():
            sums_to(i, device).start()

        def end():
            sums_to(i, device).wait()
            sums[...] += got_sums[i]

        return begin, end

    def sums_in(depth):
        def act():
            @at.at_depth(depth)
            def _():
                if depth > 0:
                    sums_to(3, at.to_in).wait_recv()
                    sums[...] += got_sums[3]
                sums_to(4 if depth == half - 1 else 3, at.to_in).start()

            @at.at_depth(depth - 1)
            def _():
                if depth > 0:
                    sums_to(3, at.to_in).wait_send()

        return act

    def sums_middle():
        @at.at_depth(half - 1)
        def _():
            sums_to(4, at.to_in).wait()
            sums[...] += got_sums[4]
            if half > 1:
                sums_to(5, at.to_out).start()

    def sums_out(depth):
        def act():
            @at.at_depth(depth)
            def _():
                sums_to(5, at.to_out).wait_recv()
                sums[...] = got_sums[5]
                if depth > 0:
                    sums_to(5, at.to_out).start()

            @at.at_depth(depth + 1)
            def _():
                sums_to(5, at.to_out).wait_send()

        return act

    take_qkv = once(0, qkv, swap)
    give_qkv = once(1, swap, grad_qkv)
    take_qkv.start()
    once(2, hidden, d_rows).start()
    once(3, cotangent, rows_in).start()
    at.meet(True)
    stages = [(0, push), (1, load), (2, product), (LAGS.x, start_x), (LAGS.z, start_z)]
    stages += [(LAGS.z + LAGS.step * depth, pass_in(depth)) for depth in range(1, half)]
    middle_lag = LAGS.z + LAGS.step * half
    stages += [(middle_lag, middle)]
    stages += [
        (middle_lag + LAGS.step * (half - 1 - depth), pass_out(depth)) for depth in range(half - 1)
    ]
    forward_lag = middle_lag + LAGS.step * (half - 1) + 2
    stages += [(slots + 2, sent), (forward_lag, forward), (forward_lag + LAGS.end, finish)]
    stages.sort(key=lambda item: -item[0])
    per_tick = 2
    at_second = 2
    at_norm = at_second + n_up // 2
    at_heads = at_norm + 1
    at_qkv = at_heads + -(-n_heads // per_tick)
    at_one = at_qkv + n_qkv // 2
    begins, ends_of = zip(
        swap_sums(0, at.to_core), swap_sums(1, at.to_x), swap_sums(2, at.to_y)
    )
    events = {at_norm: [norm_two], at_one: [norm_one, begins[0]]}
    now = at_one
    for i in range(3):
        now += 1
        events[now] = [ends_of[i]] + ([begins[i + 1]] if i < 2 else [sums_in(0)])
    for act in (
        [sums_in(depth) for depth in range(1, half)]
        + [sums_middle]
        + [sums_out(depth) for depth in reversed(range(half - 1))]
    ):
        now += 1
        events[now] = [act]
    last = count + forward_lag + LAGS.end
    assert now < last and at_norm < cuts.first[2] and at_qkv < cuts.first[3]

    def tick_body(tick, carry):
        for offset, stage in stages:

            @pl.when((tick >= offset) & (tick < count + offset))
            def _():
                stage(tick - offset)

        @pl.when(tick == at_second - 1)
        def _():
            load_up(0)
            clear_turned()
            sums[...] = jnp.zeros_like(sums)
            sums[:, sums_of(3)] = vectors[:, pl.ds(starts[-1], model)]
            take_qkv.wait()

        @pl.when((tick >= at_second) & (tick < at_norm))
        def _():
            up_step(tick - at_second)

        @pl.when((tick >= at_second) & (tick < at_norm - 1))
        def _():
            load_up(tick - at_second + 1)

        @pl.when(tick == at_norm - 1)
        def _():
            load_proj()

        for when, acts in events.items():

            @pl.when(tick == when)
            def _():
                for act in acts:
                    act()

        @pl.when((tick >= at_heads) & (tick < at_qkv))
        def _():
            @pl.loop(0, per_tick)
            def _(i):
                h = (tick - at_heads) * per_tick + i

                @pl.when(h < n_heads)
                def _():
                    head_step(h)

        @pl.when(tick == at_qkv)
        def _():
            give_qkv.start()
            give_qkv.wait()

        @pl.when((tick >= at_qkv) & (tick < at_one))
        def _():
            qkv_step(tick - at_qkv)

        @pl.when((tick >= at_qkv - 1) & (tick < at_one - 1))
        def _():
            load_qkv(tick - at_qkv + 1)

        return carry

    lax.fori_loop(0, last, tick_body, 0)


def reduce_backward(lefts, rights, others, small, n_rep, n_heads, score_scale):
    qkv, _, w_up, w_proj, hidden = others[:5]
    tokens, model = hidden.shape
    sizes = [(left.shape[0], right) for left, right in zip(lefts, (model, w_up.shape[1], model))]
    sizes.append((model, qkv.shape[0]))
    cuts = Cuts(sizes, 2)
    half = n_rep // 8
    slots = LAGS.z + LAGS.step * half + 1 - 2
    count, rows, wide = cuts.count, cuts.rows, cuts.wide
    block, width = rows // 2, wide // 2
    n_sums = 6 * model + w_up.shape[1] + qkv.shape[0]
    low, full, dma = jnp.bfloat16, jnp.float32, pltpu.SemaphoreType.DMA
    anywhere, local = pl.BlockSpec(memory_space=pl.ANY), pl.BlockSpec(memory_space=pltpu.VMEM)
    n_blocks = (w_up.shape[1] + qkv.shape[0]) // width + 2
    chunks, _, _, d_rows, sums, _, _ = pl.pallas_call(
        partial(backward_kernel, n_rep, cuts, n_heads, slots, score_scale),
        out_shape=[
            jax.ShapeDtypeStruct((count, rows, wide), low),
            jax.ShapeDtypeStruct((model, tokens), low),
            jax.ShapeDtypeStruct(qkv.shape, low),
            jax.ShapeDtypeStruct((tokens, model), full),
            jax.ShapeDtypeStruct((1, n_sums), full),
            jax.ShapeDtypeStruct((count, 2, rows, tokens), low),
            jax.ShapeDtypeStruct((count, width, tokens), low),
        ],
        in_specs=[anywhere] * (len(lefts) + len(rights) + len(others)) + [local] * len(small),
        out_specs=[anywhere] * 3 + [local] * 2 + [anywhere] * 2,
        scratch_shapes=[
            pltpu.VMEM((2, 2, 2, rows, tokens), low),
            pltpu.VMEM((2, 2, width, tokens), low),
            pltpu.VMEM((slots, 2, rows, width), low),
            pltpu.VMEM((count, rows, width), low),
            pltpu.VMEM((count, block, width), low),
            pltpu.VMEM((count, block, width), low),
            pltpu.VMEM((count, block, width), low),
            pltpu.VMEM((count, block, width), low),
            pltpu.VMEM(qkv.shape, low),
            pltpu.VMEM((2, model, width), low),
            pltpu.VMEM((2, width, tokens), low),
            pltpu.VMEM((model, tokens), full),
            pltpu.VMEM((model, tokens), low),
            pltpu.VMEM((model, tokens), low),
            pltpu.VMEM((tokens, model), low),
            pltpu.VMEM((6, 1, n_sums), full),
            dma((2, 2, count)),
            dma((2, count)),
            dma((count,)),
            dma((6,)),
            dma((2, n_blocks)),
            dma((2, 6)),
        ]
        + [dma((2, count))] * 11,
        compiler_params=pltpu.CompilerParams(
            collective_id=1, has_side_effects=True, vmem_limit_bytes=63 << 20
        ),
        name="reduce_backward",
    )(*lefts, *rights, *others, *small)
    return [cuts.whole(chunks, w) for w in range(len(sizes))], d_rows, sums[0]


def forward_kernel(n_rep, cuts, n_heads, score_scale, *refs):
    n_w = len(cuts.down)
    shards, refs = refs[:n_w], refs[n_w:]
    (
        patches, cotangent, own_vectors, pic_key, pic_query, cosine, sine,
    ) = refs[:7]
    fulls, refs = refs[7 : 7 + n_w], refs[7 + n_w :]
    (
        swap_out, heads_to, log_total, hidden_out, two_out, act_out, pre_out, layer_out,
        one_out, cot_out, vectors,
        swap, heads_out, hidden, two_turned, act_turned, pre_turned, one_turned, cot_turned,
        hold, w_block, turned, up_pre, act, out_sum, normed_two, normed, got_vectors,
        vec_sem, give_sem, pre_sem, own_in, own_out, w_sem, y_sem, d_sem, in_sem, mid_sem, back_sem, x_sem, c_sem, cd_sem,
    ) = refs
    at = Place(n_rep)
    nz, half = at.nz, at.half
    count, rows, wide = cuts.count, cuts.rows, cuts.wide
    plane = rows * 4 // 5
    unit = plane // n_rep
    straight = (rows - plane) // 2
    mine, yours = at.y, 1 - at.y
    tokens, model = patches.shape
    head = model // n_heads
    sizes = vector_sizes(model, up_pre.shape[1])
    starts = [sum(sizes[:i]) for i in range(len(sizes) + 1)]

    def vector(i, start=0, size=model):
        return vectors[:, pl.ds(pl.multiple_of(starts[i] + start, 128), size)]

    def shard(w, row, col, first, size):
        start = pl.multiple_of(row * rows + first, 16)
        cols = pl.ds(pl.multiple_of(col * wide, 128), wide)
        return shards[w].at[pl.ds(start, size), cols]

    def full(w, row, col, owner, first, size):
        start = pl.multiple_of(owner * cuts.shard_rows[w] + row * rows + first, 16)
        cols = pl.ds(pl.multiple_of(col * wide, 128), wide)
        return fulls[w].at[pl.ds(start, size), cols]

    def alike(size):
        return fulls[0].at[pl.ds(0, size), pl.ds(0, wide)]

    def place(c, x, z):
        return ((c * 2 + x) * nz + z) * unit

    def spread_copy(k, first, size, sems, device):
        def act_on(w, row, col):
            view = full(w, row, col, yours, first, size)
            remote(view, view, sems, k, device).start()

        cuts.weight_of(k, act_on)

    def settle(k, size, sems, device, received):
        view = alike(size)
        copy = remote(view, view, sems, k, device)
        if received:
            copy.wait_recv()
        else:
            copy.wait_send()

    def along(k, begin, size, sems, device):
        spread_copy(k, place(at.c, at.x, begin), size * unit, sems, device)

    def start_y(k):
        def act_on(w, row, col):
            first = place(at.c, at.x, at.z)
            remote(
                shard(w, row, col, first, unit),
                full(w, row, col, mine, first, unit),
                y_sem, k, at.to_y,
            ).start()
            first = plane + at.c * straight
            remote(
                shard(w, row, col, first, straight),
                full(w, row, col, mine, first, straight),
                d_sem, k, at.to_y,
            ).start()

        cuts.weight_of(k, act_on)

    def inner_send(k, depth):
        if depth == half - 1:
            along(k, jnp.where(at.low, 0, half), half, mid_sem, at.to_in)
        else:
            along(k, jnp.where(at.low, 0, nz - 1 - depth), depth + 1, in_sem, at.to_in)

    def back_start(k, depth):
        along(k, jnp.where(at.low, depth, 0), nz - depth, back_sem, at.to_out)

    def x_start(k):
        along(k, 0, nz, x_sem, at.to_x)

    def crossed(k):
        settle(k, unit, y_sem, at.to_y, True)

        @at.at_depth(0)
        def _():
            inner_send(k, 0)

        settle(k, straight, d_sem, at.to_y, True)
        spread_copy(k, plane + at.c * straight, straight, cd_sem, at.to_core)

    def pass_in(depth):
        def stage(k):
            @at.at_depth(depth)
            def _():
                settle(k, depth * unit, in_sem, at.to_in, True)
                inner_send(k, depth)

        return stage

    def middle(k):
        @at.at_depth(half - 1)
        def _():
            settle(k, half * unit, mid_sem, at.to_in, True)
            if half > 1:
                back_start(k, half - 1)
            x_start(k)

    def pass_out(depth):
        def stage(k):
            @at.at_depth(depth)
            def _():
                settle(k, (nz - depth - 1) * unit, back_sem, at.to_out, True)
                if depth > 0:
                    back_start(k, depth)
                x_start(k)

        return stage

    def crossed_x(k):
        settle(k, nz * unit, x_sem, at.to_x, True)
        spread_copy(k, place(at.c, 0, 0), 2 * nz * unit, c_sem, at.to_core)

    def own_load(k, view):
        return pltpu.make_async_copy(view, hold.at[k % 3], own_in.at[k])

    def own_store(k, view):
        return pltpu.make_async_copy(hold.at[k % 3], view, own_out.at[k])

    def take_own(k):
        cuts.weight_of(k, lambda w, row, col: own_load(k, shard(w, row, col, 0, rows)).start())

    def give_own(k):
        own_load(k, alike(rows)).wait()
        cuts.weight_of(
            k, lambda w, row, col: own_store(k, full(w, row, col, mine, 0, rows)).start()
        )

    def arrived(k):
        own_store(k, alike(rows)).wait()
        settle(k, 2 * nz * unit, c_sem, at.to_core, True)
        settle(k, straight, cd_sem, at.to_core, True)
        settle(k, unit, y_sem, at.to_y, False)
        settle(k, straight, d_sem, at.to_y, False)
        settle(k, nz * unit, x_sem, at.to_x, False)
        settle(k, 2 * nz * unit, c_sem, at.to_core, False)
        settle(k, straight, cd_sem, at.to_core, False)
        for depth in range(half):

            @at.at_depth(depth)
            def _():
                if depth == half - 1:
                    settle(k, half * unit, mid_sem, at.to_in, False)
                else:
                    settle(k, (depth + 1) * unit, in_sem, at.to_in, False)
                if depth > 0:
                    settle(k, (nz - depth) * unit, back_sem, at.to_out, False)

    def block_of(u, view):
        return pltpu.make_async_copy(view, w_block.at[u % 2], w_sem.at[0, u])

    def half_block(u, owner, view):
        spot = pl.ds(owner * (wide // 2), wide // 2)
        return pltpu.make_async_copy(view, w_block.at[u % 2, spot, :], w_sem.at[owner, u])

    def columns(w, col):
        return fulls[w].at[:, pl.ds(pl.multiple_of(col * wide, 128), wide)]

    def down_rows(i, owner):
        start = owner * cuts.shard_rows[3] + i * (wide // 2)
        return fulls[3].at[pl.ds(pl.multiple_of(start, 16), wide // 2), :]

    step = 256

    def qkv_step(b, u):
        block_of(u, columns(0, 0)).wait()

        @pl.loop(0, wide // step)
        def _(i):
            spot = pl.ds(pl.multiple_of(i * step, 128), step)
            part = contract(normed[...], w_block[u % 2, :, spot], 1, 0)
            part = part + vector(2, b * wide + i * step, step)
            turned[pl.ds(pl.multiple_of(i * step, 16), step), :] = part.T

        @pl.loop(0, n_heads)
        def _(h):
            part = turned[pl.ds(pl.multiple_of(h * head, 8), head), :]
            spot = pl.ds(pl.multiple_of(b * model + h * head, 16), head)

            @pl.when(b < 2)
            def _():
                swap[spot, :] = apply_rotary(part, cosine[...], sine[...]).astype(jnp.bfloat16)

            @pl.when(b == 2)
            def _():
                swap[spot, :] = part.astype(jnp.bfloat16)

    def head_step(h):
        def part(i):
            return swap[pl.ds(pl.multiple_of(i * model + h * head, 16), head), :]

        scores = contract(part(1), part(0), 0, 0) * score_scale
        scores = jnp.where(pic_key[...] == pic_query[...], scores, -1000000000.0)
        top = jnp.max(scores, axis=0, keepdims=True)
        exp_scores = jnp.exp(scores - top)
        total = jnp.sum(exp_scores, axis=0, keepdims=True)
        probs = (exp_scores / total).astype(jnp.bfloat16)
        attended = contract(part(2), probs, 1, 0)
        heads_out[pl.ds(pl.multiple_of(h * head, 16), head), :] = attended.astype(jnp.bfloat16)
        log_total[pl.ds(h, 1), :] = top + jnp.log(total)

    def proj_step(u):
        block_of(u, columns(0, 0)).wait()

        @pl.loop(0, tokens // step)
        def _(i):
            spot = pl.ds(pl.multiple_of(i * step, 16), step)
            lanes = pl.ds(pl.multiple_of(i * step, 128), step)
            branch = contract(heads_out[:, lanes], w_block[u % 2], 0, 0)
            rows_in = patches[spot, :].astype(jnp.float32) + branch + vector(3)
            hidden[spot, :] = rows_in
            out_sum[spot, :] = rows_in + vector(7)
            standard, _ = apply_layer_norm(rows_in)
            result = (standard * vector(4) + vector(5)).astype(jnp.bfloat16)
            normed_two[spot, :] = result
            two_turned[:, lanes] = result.T

    def up_step(c, u):
        block_of(u, columns(0, 0)).wait()

        @pl.loop(0, wide // step)
        def _(i):
            spot = pl.ds(pl.multiple_of(i * step, 128), step)
            col = pl.multiple_of(c * wide + i * step, 128)
            cols = pl.ds(col, step)
            pre = contract(normed_two[...], w_block[u % 2, :, spot], 1, 0)
            pre = pre + vector(6, c * wide + i * step, step)
            up_pre[:, cols] = pre
            result = (pre / (1.0 + jnp.exp(-quick_slope * pre))).astype(jnp.bfloat16)
            act[:, cols] = result
            act_turned[pl.ds(col, step), :] = result.T

    def down_step(i, u):
        for owner in range(2):
            half_block(u, owner, down_rows(0, 0)).wait()
            size = wide // 2
            col = pl.multiple_of(owner * cuts.shard_rows[3] + i * size, 128)

            @pl.loop(0, tokens // step)
            def _(j):
                spot = pl.ds(pl.multiple_of(j * step, 16), step)
                lanes = pl.ds(pl.multiple_of(j * step, 128), step)
                weight = w_block[u % 2, pl.ds(owner * size, size), :]
                pre = up_pre[spot, pl.ds(col, size)]
                sigmoid = 1.0 / (1.0 + jnp.exp(-quick_slope * pre))
                slope = sigmoid + quick_slope * pre * sigmoid * (1.0 - sigmoid)
                grad = contract(cotangent[spot, :], weight, 1, 1) * slope
                pre_turned[pl.ds(col, size), lanes] = grad.astype(jnp.bfloat16).T
                out_sum[spot, :] += contract(act[spot, pl.ds(col, size)], weight, 1, 0)

            pre_give(i, owner).start()

    pairs = [
        (one_turned, one_out), (cot_turned, cot_out), (swap, swap_out),
        (heads_out, heads_to), (hidden, hidden_out), (two_turned, two_out),
        (act_turned, act_out),
    ]
    gives = [pltpu.make_async_copy(a, b, give_sem.at[i]) for i, (a, b) in enumerate(pairs)]

    def pre_give(i, owner):
        start = owner * cuts.shard_rows[3] + i * (wide // 2)
        spot = pl.ds(pl.multiple_of(start, 16), wide // 2)
        return pltpu.make_async_copy(
            pre_turned.at[spot, :], pre_out.at[spot, :], pre_sem.at[owner, i]
        )

    vector_copy = remote(own_vectors, got_vectors, vec_sem, 0, at.to_y)
    slab = 128

    def join_vectors():
        vector_copy.wait()
        for i, size in enumerate(sizes):
            own, spot = size // 2, pl.ds(starts[i] // 2, size // 2)
            for y, part in ((mine, own_vectors), (yours, got_vectors)):
                start = pl.multiple_of(starts[i] + y * own, 128)
                vectors[:, pl.ds(start, own)] = part[:, spot]

    def norm_step(i):
        spot = pl.ds(pl.multiple_of(i * slab, 16), slab)
        lanes = pl.ds(pl.multiple_of(i * slab, 128), slab)
        standard, _ = apply_layer_norm(patches[spot, :].astype(jnp.float32))
        result = (standard * vector(0) + vector(1)).astype(jnp.bfloat16)
        normed[spot, :] = result
        one_turned[:, lanes] = result.T
        cot_turned[:, lanes] = cotangent[spot, :].T

    def cotangent_sums():
        ones = jnp.ones((8, tokens), jnp.bfloat16)
        sums = contract(ones, cot_turned[...], 1, 1)[0:1, :]
        vectors[:, pl.ds(starts[-1], model)] = sums

    gap = 2
    across = 1 + gap * 2 * half
    offset = across + 1
    stages = [(1, crossed)]
    stages += [(1 + gap * depth, pass_in(depth)) for depth in range(1, half)]
    stages += [(1 + gap * half, middle)]
    stages += [
        (1 + gap * (2 * half - 1 - depth), pass_out(depth)) for depth in range(half - 1)
    ]
    stages += [(across, crossed_x)]
    stages += [(offset - 2, take_own), (offset - 1, give_own), (offset, arrived)]
    stages.sort(key=lambda item: -item[0])
    n_up, n_down = cuts.across[2], cuts.down[3] // 2
    per_tick = 3
    first_head = cuts.first[1] + 1
    at_proj = first_head + -(-n_heads // per_tick)
    at_up = at_proj + 1
    at_down = max(at_up + n_up, cuts.first[3] + 2)
    n_steps = 4 + n_up + n_down

    at.meet(True)
    vector_copy.start()

    @pl.loop(0, count)
    def _(k):
        start_y(k)

    def tick_body(tick, carry):
        for lag, stage in stages:

            @pl.when((tick >= lag) & (tick < count + lag))
            def _():
                stage(tick - lag)

        @pl.when(tick == 0)
        def _():
            join_vectors()

        @pl.when((tick >= 2) & (tick % 2 == 0) & (tick <= tokens // slab * 2))
        def _():
            norm_step(tick // 2 - 1)

        @pl.when(tick == offset)
        def _():
            cotangent_sums()

        now = tick - offset

        @pl.when((now >= 2) & (now < first_head) & (now % 2 == 0))
        def _():
            qkv_step(now // 2 - 1, now // 2 - 1)

        @pl.when((now >= first_head) & (now < at_proj))
        def _():
            @pl.loop(0, per_tick)
            def _(i):
                h = (now - first_head) * per_tick + i

                @pl.when(h < n_heads)
                def _():
                    head_step(h)

        @pl.when(now == at_proj)
        def _():
            proj_step(3)

        @pl.when((now >= at_up) & (now < at_up + n_up))
        def _():
            up_step(now - at_up, now - at_up + 4)

        down_i = (now - at_down) // 2

        @pl.when((now >= at_down) & (down_i < n_down) & ((now - at_down) % 2 == 0))
        def _():
            down_step(down_i, down_i + 4 + n_up)

        for when, group in ((first_head, gives[:3]), (at_up, gives[3:6]), (at_down, gives[6:])):

            @pl.when(now == when)
            def _():
                for copy in group:
                    copy.start()

        soon = now + 1

        @pl.when((soon >= 2) & (soon < first_head) & (soon % 2 == 0))
        def _():
            block_of(soon // 2 - 1, columns(0, soon // 2 - 1)).start()

        @pl.when(soon == at_proj)
        def _():
            block_of(3, columns(1, 0)).start()

        @pl.when((soon >= at_up) & (soon < at_up + n_up))
        def _():
            block_of(soon - at_up + 4, columns(2, soon - at_up)).start()

        next_i = (soon - at_down) // 2

        @pl.when((soon >= at_down) & (next_i < n_down) & ((soon - at_down) % 2 == 0))
        def _():
            for owner in range(2):
                half_block(next_i + 4 + n_up, owner, down_rows(next_i, owner)).start()

        return carry

    lax.fori_loop(0, offset + at_down + 2 * n_down - 1, tick_body, 0)
    layer_out[...] = out_sum[...].astype(jnp.bfloat16)
    for copy in gives:
        copy.wait()
    for i in range(n_down):
        for owner in range(2):
            pre_give(i, owner).wait()


def vector_sizes(model, wide_two):
    return [model, model, 3 * model, model, model, model, wide_two, model]


def gather_forward(shards, inputs, n_rep, n_heads, score_scale):
    cuts = Cuts([(shard.shape[0] * 2, shard.shape[1]) for shard in shards], 2)
    tokens, model = inputs[0].shape
    wide_two = shards[2].shape[1]
    count, rows, wide = cuts.count, cuts.rows, cuts.wide
    low, dma = jnp.bfloat16, pltpu.SemaphoreType.DMA
    anywhere, local = pl.BlockSpec(memory_space=pl.ANY), pl.BlockSpec(memory_space=pltpu.VMEM)
    n_steps = 4 + cuts.across[2] + cuts.down[3] // 2
    n_vectors = sum(vector_sizes(model, wide_two))

    def shape(*sizes, kind=low):
        return jax.ShapeDtypeStruct(sizes, kind)

    results = pl.pallas_call(
        partial(forward_kernel, n_rep, cuts, n_heads, score_scale),
        out_shape=[shape(item.shape[0] * 2, item.shape[1]) for item in shards]
        + [
            shape(3 * model, tokens),
            shape(model, tokens),
            shape(n_heads, tokens, kind=jnp.float32),
            shape(tokens, model, kind=jnp.float32),
            shape(model, tokens),
            shape(wide_two, tokens),
            shape(wide_two, tokens),
            shape(tokens, model),
            shape(model, tokens),
            shape(model, tokens),
            shape(1, n_vectors + model, kind=jnp.float32),
        ],
        in_specs=[anywhere] * len(shards) + [local] * len(inputs),
        out_specs=[anywhere] * len(shards)
        + [anywhere] * 2 + [local] + [anywhere] * 4 + [local] + [anywhere] * 2 + [local],
        scratch_shapes=[
            pltpu.VMEM((3 * model, tokens), low),
            pltpu.VMEM((model, tokens), low),
            pltpu.VMEM((tokens, model), jnp.float32),
            pltpu.VMEM((model, tokens), low),
            pltpu.VMEM((wide_two, tokens), low),
            pltpu.VMEM((wide_two, tokens), low),
            pltpu.VMEM((model, tokens), low),
            pltpu.VMEM((model, tokens), low),
            pltpu.VMEM((3, rows, wide), low),
            pltpu.VMEM((2, model, wide), low),
            pltpu.VMEM((model, tokens), jnp.float32),
            pltpu.VMEM((tokens, wide_two), jnp.float32),
            pltpu.VMEM((tokens, wide_two), low),
            pltpu.VMEM((tokens, model), jnp.float32),
            pltpu.VMEM((tokens, model), low),
            pltpu.VMEM((tokens, model), low),
            pltpu.VMEM((1, n_vectors // 2), jnp.float32),
            dma((2, 1)),
            dma((7,)),
            dma((2, cuts.down[3] // 2)),
            dma((count,)),
            dma((count,)),
            dma((2, n_steps)),
        ]
        + [dma((2, count))] * 8,
        compiler_params=pltpu.CompilerParams(
            collective_id=0, has_side_effects=True, vmem_limit_bytes=63 << 20
        ),
        name="gather_forward",
    )(*shards, *inputs)
    return results[: len(shards)], results[len(shards) :]


class Links:
    def __init__(self, n_rep, n_shard):
        self.nz, self.ny, self.n_rep = n_rep // 4, n_shard, n_rep
        self.y = lax.axis_index("shard")

    def gather_vector(self, vector):
        return lax.all_gather(vector, "shard", axis=0, tiled=False)

    def sum_all(self, vector):
        for flip in (1, 2):
            vector = vector + lax.ppermute(
                vector, "rep", [(i, i ^ flip) for i in range(self.n_rep)]
            )
        step = 1
        while step < self.nz:
            pairs = [(i, i ^ (4 * step)) for i in range(self.n_rep)]
            vector = vector + lax.ppermute(vector, "rep", pairs)
            step *= 2
        step = 1
        while step < self.ny:
            pairs = [(i, i ^ step) for i in range(self.ny)]
            vector = vector + lax.ppermute(vector, "shard", pairs)
            step *= 2
        return vector


def per_device(
    patches,
    lengths,
    positions,
    ln1_gain,
    ln1_bias,
    qkv_weight,
    qkv_bias,
    proj_weight,
    proj_bias,
    ln2_gain,
    ln2_bias,
    fc1_weight,
    fc1_bias,
    fc2_weight,
    fc2_bias,
    cotangent,
    n_rep,
    n_shard,
):
    links = Links(n_rep, n_shard)
    pack_count = lengths.shape[0]
    row_count = patches.shape[0]
    length = row_count // pack_count
    model_width = patches.shape[1]
    head_count = HEADS
    head_size = model_width // head_count
    score_scale = head_size ** (-0.5)
    pic_ends = jnp.cumsum(lengths[:, :-1], axis=1)
    slot_index = jnp.arange(length, dtype=jnp.int32)
    idents = jnp.sum((slot_index[None, :, None] >= pic_ends[:, None, :]).astype(jnp.int32), axis=2)
    pack_index = jnp.arange(pack_count, dtype=jnp.int32)
    idents = (idents + pack_index[:, None] * lengths.shape[1]).reshape(-1)
    cosine, sine = rotary_tables(positions, head_size)

    shards = [qkv_weight, proj_weight, fc1_weight, fc2_weight]
    qkv_shape = (3 * model_width, row_count)
    small = [ln1_gain, ln1_bias, qkv_bias, proj_bias, ln2_gain, ln2_bias, fc1_bias, fc2_bias]
    spots = [0]
    for item in small:
        spots.append(spots[-1] + item.shape[0])
    packed = sum(
        jnp.pad(item, (spots[i], spots[-1] - spots[i + 1])) for i, item in enumerate(small)
    )
    if n_shard == 2:
        pictures = [idents[:, None], idents[None, :]]
        inputs = [patches, cotangent, packed.astype(jnp.float32)[None, :]]
        inputs += pictures + [cosine, sine]
        weights, results = gather_forward(shards, inputs, n_rep, head_count, score_scale)
        w_qkv, w_proj, w_up, w_down = weights
        qkv, heads_out, log_total, hidden_rows, second_turned = results[:5]
        activation, grad_pre, layer_out, first_turned, cotangent_turned, vectors = results[5:]
        others = [qkv, w_qkv, w_up, w_proj, hidden_rows, cotangent, patches]
        small_args = [log_total] + pictures + [cosine, sine, vectors]
        lefts = [activation, second_turned, heads_out, first_turned]
        rights = [cotangent_turned, grad_pre]
        products, d_patches, total = reduce_backward(
            lefts, rights, others, small_args, n_rep, head_count, score_scale
        )
    else:
        gathered = links.gather_vector(packed)
        (
            first_norm_gain, first_norm_bias, b_qkv, b_proj,
            second_norm_gain, second_norm_bias, b_up, b_down,
        ) = [
            gathered[:, spots[i] : spots[i + 1]].reshape(-1).astype(jnp.float32)
            for i in range(len(small))
        ]
        grad_out = cotangent.astype(jnp.float32)
        d_b_down = jnp.sum(grad_out, axis=0)
        input_rows = patches.astype(jnp.float32)
        first_centered_standard, first_inverse_spread = apply_layer_norm(input_rows)
        first_normalized = (first_centered_standard * first_norm_gain + first_norm_bias).astype(
            jnp.bfloat16
        )
        w_qkv, w_proj, w_up, w_down = [
            lax.all_gather(shard, "shard", axis=0, tiled=True) for shard in shards
        ]
        qkv_rows = contract(w_qkv, first_normalized, 0, 1) + b_qkv[:, None]
        qkv_rows = qkv_rows.reshape(3, head_count, head_size, row_count)
        queries = apply_rotary(qkv_rows[0], cosine, sine).astype(jnp.bfloat16)
        keys_rot = apply_rotary(qkv_rows[1], cosine, sine).astype(jnp.bfloat16)
        values_all = qkv_rows[2].astype(jnp.bfloat16)
        attended, log_total = attend(queries, keys_rot, values_all, idents, score_scale)
        heads_out = attended.reshape(model_width, row_count).astype(jnp.bfloat16)
        hidden_rows = input_rows + contract(heads_out, w_proj, 0, 0) + b_proj
        second_centered_standard, second_inverse_spread = apply_layer_norm(hidden_rows)
        second_normalized = (
            second_centered_standard * second_norm_gain + second_norm_bias
        ).astype(jnp.bfloat16)
        up_pre = contract(w_up, second_normalized, 0, 1) + b_up[:, None]
        sigmoid_up = 1.0 / (1.0 + jnp.exp(-quick_slope * up_pre))
        activation = (up_pre * sigmoid_up).astype(jnp.bfloat16)
        out_full = hidden_rows + contract(activation, w_down, 0, 0) + b_down
        layer_out = out_full.astype(jnp.bfloat16)
        grad_act = contract(w_down, cotangent, 1, 1)
        slope_up = sigmoid_up + quick_slope * up_pre * sigmoid_up * (1.0 - sigmoid_up)
        grad_pre = (grad_act * slope_up).astype(jnp.bfloat16)
        d_b_up = jnp.sum(grad_pre.astype(jnp.float32), axis=1)
        second_normalized_gradient = contract(grad_pre, w_up, 0, 1)
        second_gain_gradient = jnp.sum(
            second_normalized_gradient * second_centered_standard, axis=0
        )
        d_bias_two = jnp.sum(second_normalized_gradient, axis=0)
        grad_hidden = grad_out + norm_gradient_step(
            second_normalized_gradient,
            second_centered_standard,
            second_inverse_spread,
            second_norm_gain,
        )
        grad_branch = grad_hidden.astype(jnp.bfloat16)
        d_b_proj = jnp.sum(grad_branch.astype(jnp.float32), axis=0)
        grad_heads = contract(w_proj, grad_branch, 1, 1).astype(jnp.bfloat16)
        back = partial(head_back, score_scale=score_scale)
        grad_query, grad_key, grad_value = jax.vmap(back, in_axes=(0, 0, 0, 0, None, 0))(
            queries,
            keys_rot,
            values_all,
            grad_heads.reshape(head_count, head_size, row_count),
            idents[:, None] == idents[None, :],
            log_total[:, None, :],
        )
        grad_query = rotary_back(grad_query, cosine, sine)
        grad_key = rotary_back(grad_key, cosine, sine)
        grad_qkv = jnp.stack([grad_query, grad_key, grad_value]).reshape(qkv_shape)
        grad_qkv = grad_qkv.astype(jnp.bfloat16)
        first_normalized_gradient = contract(grad_qkv, w_qkv, 0, 1)
        lefts = [activation, second_normalized.T, heads_out, first_normalized.T]
        rights = [cotangent.T, grad_pre, grad_branch.T, grad_qkv]
        products = [
            contract(left, right, 1, 1).astype(jnp.bfloat16) for left, right in zip(lefts, rights)
        ]
        products = [
            item.astype(jnp.float32) for item in reduce_products(products, n_rep, n_shard)
        ]
        d_b_qkv = jnp.sum(grad_qkv.astype(jnp.float32), axis=1)
        first_gain_gradient = jnp.sum(first_normalized_gradient * first_centered_standard, axis=0)
        d_bias_one = jnp.sum(first_normalized_gradient, axis=0)
        d_patches = grad_hidden + norm_gradient_step(
            first_normalized_gradient,
            first_centered_standard,
            first_inverse_spread,
            first_norm_gain,
        )
        total = jnp.concatenate(
            [
                second_gain_gradient, d_bias_two, d_b_up, d_b_down,
                first_gain_gradient, d_bias_one, d_b_qkv, d_b_proj,
            ]
        )
        total = links.sum_all(total)
    d_w_down, d_w_up, d_w_proj, d_w_qkv = products

    ff = fc1_weight.shape[1]
    own_parts, start = [], 0
    for size in (
        model_width, model_width, ff, model_width,
        model_width, model_width, 3 * model_width, model_width,
    ):
        own = size // n_shard
        own_parts.append(lax.dynamic_slice_in_dim(total, start + links.y * own, own, 0))
        start += size
    m_gain, m_bias, m_upb, m_downb, a_gain, a_bias, a_qkvb, a_projb = own_parts
    return (
        layer_out,
        d_patches,
        a_gain,
        a_bias,
        d_w_qkv,
        a_qkvb,
        d_w_proj,
        a_projb,
        m_gain,
        m_bias,
        d_w_up,
        m_upb,
        d_w_down,
        m_downb,
    )


def solution(mesh):
    rows, whole = P(("rep", "shard"), None), P("shard")
    matrix = P("shard", None)
    in_specs = (
        rows,
        rows,
        P(None, ("rep", "shard")),
        whole,
        whole,
        matrix,
        whole,
        matrix,
        whole,
        whole,
        whole,
        matrix,
        whole,
        matrix,
        whole,
        rows,
    )
    out_specs = (
        rows,
        rows,
        whole,
        whole,
        matrix,
        whole,
        matrix,
        whole,
        whole,
        whole,
        matrix,
        whole,
        matrix,
        whole,
    )
    body = partial(per_device, n_rep=mesh.shape["rep"], n_shard=mesh.shape["shard"])
    return jax.shard_map(
        body, mesh=mesh, in_specs=in_specs, out_specs=out_specs, check_vma=False
    )
```
